32 devices in a mesh: grp: 4 (over y, x), tp: 8 (over z, core).
Axes of the slice: x: 2, y: 2, z: 4, core: 2. Of those that a mesh axis runs over, the one named last changes fastest.
Arguments:
- layer_input: bfloat16 [8192, 2048], P('grp'), may hold values from -6 to 6
- out_cotangent: bfloat16 [8192, 2048], P('grp'), may hold values from -6 to 6
- seq_group: int32 [6], replicated, may hold values from 0 to 3, as said below
- seq_len: int32 [6], replicated, may hold values from 512 to 2048, as said below
- w_qkv: float32 [2048, 6144], P('grp', 'tp'), may hold values from -0.1875 to 0.1875
- b_qv: float32 [4096], replicated, may hold values from -3 to 3
- w_out: float32 [2048, 2048], P('grp', 'tp'), may hold values from -0.75 to 0.75
- b_out: float32 [2048], replicated, may hold values from -2 to 2
- w_up: float32 [2048, 8192], P('grp', 'tp'), may hold values from -0.125 to 0.125
- b_up: float32 [8192], replicated, may hold values from -3 to 3
- w_down: float32 [2048, 8192], P('grp', 'tp'), may hold values from -0.0625 to 0.0625
- b_down: float32 [2048], replicated, may hold values from -2 to 2
- first_norm_gain: float32 [2048], replicated, may hold values from 0.1 to 1.9
- first_norm_bias: float32 [2048], replicated, may hold values from -2 to 2
- second_norm_gain: float32 [2048], replicated, may hold values from 0.1 to 1.9
- second_norm_bias: float32 [2048], replicated, may hold values from -2 to 2
Outputs:
- layer_output: bfloat16 [8192, 2048], P(('grp', 'tp'))
- grad_x: float32 [8192, 2048], P(('grp', 'tp'))
- grad_w_qkv: float32 [2048, 6144], P('grp', 'tp')
- grad_b_qv: float32 [4096], replicated
- grad_w_out: float32 [2048, 2048], P('grp', 'tp')
- grad_b_out: float32 [2048], replicated
- grad_w_up: float32 [2048, 8192], P('grp', 'tp')
- grad_b_up: float32 [8192], replicated
- grad_w_down: float32 [2048, 8192], P('grp', 'tp')
- grad_b_down: float32 [2048], replicated
- grad_ln1_gain: float32 [2048], replicated
- grad_ln1_bias: float32 [2048], replicated
- grad_ln2_gain: float32 [2048], replicated
- grad_ln2_bias: float32 [2048], replicated
The draws below stay inside these ranges and needn't reach their ends.
Inputs may be any that keep to these rules, and one draw needn't show every extreme that they name: `seq_group`: each group's sequences total at most 2048 tokens, and in every draw some group holds exactly 2048; every group holds at least one sequence. `seq_len`: each sequence has 2048 or 512 tokens.
All inputs are finite; a program needn't handle non-finite values.
Results may differ from the reference program's by a relative error of at most 0.023.
Values may be sent and summed in bfloat16 or wider, within the bound.
A program may use at most 320 MiB of HBM per device.

```python
import jax
import jax.numpy as jnp
from jax import lax

D = 2048
HEADS = 16
HD = 128
FF = 8192
LONG = 2048
SHORT = 512
NLONG = 2
NSHORT = 4
NSEQ = 6
TOKENS = 8192
N_GRP = 4
N_TP = 8


def sequence_layout(key):
    base = jax.random.fold_in(key, 7)
    group_key, shuffle_key = jax.random.split(base)
    group_order = jax.random.permutation(group_key, 2 * NLONG).astype(jnp.int32)
    short_index = jnp.arange(NSHORT, dtype=jnp.int32)
    short_rank = 2 * (short_index // 4) + (short_index % 4 > 0).astype(jnp.int32)
    groups = jnp.concatenate([group_order[:NLONG], group_order[NLONG + short_rank]])
    lengths = jnp.concatenate([jnp.full((NLONG,), LONG, jnp.int32), jnp.full((NSHORT,), SHORT, jnp.int32)])
    shuffle = jax.random.permutation(shuffle_key, NSEQ)
    return (groups[shuffle].astype(jnp.int32), lengths[shuffle].astype(jnp.int32))


def draw_seq_group(key, part):
    return sequence_layout(key)[0]


def draw_seq_len(key, part):
    return sequence_layout(key)[1]


def block_levels(stream_key, dims, pieces, smallest, high):
    def one(position, shards_of):
        draws = jax.random.uniform(jax.random.fold_in(jax.random.fold_in(stream_key, 6), position), (shards_of,), jnp.float32, smallest / len(pieces), high / len(pieces))
        return jnp.repeat(jnp.exp(draws), dims[position] // shards_of).reshape((-1,) + (1,) * (len(dims) - position - 1))

    loudness = one(*pieces[0])
    for cut in pieces[1:]:
        loudness = loudness * one(*cut)
    return loudness


def gaussian(own_key, extent, width, most, shards=(), kind=jnp.bfloat16):
    array = jax.random.normal(own_key, extent, jnp.float32) * width
    if len(shards) > 0:
        array = block_levels(own_key, extent, shards, -0.22, 0.18) * array
    return jnp.clip(array, min=-most, max=most).astype(kind)


def setup_inputs(seed: int = 0) -> dict:
    streams_of = jax.random.split(jax.random.key(seed), 17)
    layer_input = gaussian(streams_of[0], (TOKENS, D), 1.0, 6.0, ((0, 4),))
    out_cotangent = gaussian(streams_of[1], (TOKENS, D), 1.0, 6.0, ((0, 4),))
    seq_group = draw_seq_group(jax.random.fold_in(streams_of[16], 71), 0)
    seq_len = draw_seq_len(jax.random.fold_in(streams_of[16], 71), 0)
    w_qkv = gaussian(streams_of[4], (D, 3 * D), (D // 2) ** -0.5, 0.1875, ((0, 4), (1, 8)), jnp.float32)
    b_qv = gaussian(streams_of[5], (2 * D,), 0.5, 3.0, (), jnp.float32)
    w_out = gaussian(streams_of[6], (D, D), (D // 32) ** -0.5, 0.75, ((0, 4), (1, 8)), jnp.float32)
    b_out = gaussian(streams_of[7], (D,), 0.3, 2.0, (), jnp.float32)
    w_up = gaussian(streams_of[8], (D, FF), D ** -0.5, 0.125, ((0, 4), (1, 8)), jnp.float32)
    b_up = gaussian(streams_of[9], (FF,), 0.5, 3.0, (), jnp.float32)
    w_down = gaussian(streams_of[10], (D, FF), FF ** -0.5, 0.0625, ((0, 4), (1, 8)), jnp.float32)
    b_down = gaussian(streams_of[11], (D,), 0.3, 2.0, (), jnp.float32)
    first_norm_gain = jnp.clip(1.0 + 0.18 * jax.random.normal(streams_of[12], (D,), jnp.float32), 0.1, 1.9)
    first_norm_bias = gaussian(streams_of[13], (D,), 0.3, 2.0, (), jnp.float32)
    second_norm_gain = jnp.clip(1.0 + 0.18 * jax.random.normal(streams_of[14], (D,), jnp.float32), 0.1, 1.9)
    second_norm_bias = gaussian(streams_of[15], (D,), 0.3, 2.0, (), jnp.float32)
    return dict(layer_input=layer_input, out_cotangent=out_cotangent, seq_group=seq_group, seq_len=seq_len, w_qkv=w_qkv, b_qv=b_qv, w_out=w_out, b_out=b_out, w_up=w_up, b_up=b_up, w_down=w_down, b_down=b_down, first_norm_gain=first_norm_gain, first_norm_bias=first_norm_bias, second_norm_gain=second_norm_gain, second_norm_bias=second_norm_bias)


@jax.custom_vjp
def low(v):
    return lax.optimization_barrier(v.astype(jnp.bfloat16)).astype(jnp.float32)

@jax.custom_vjp
def low_back(v):
    return v

def low_keep(v):
    return (low(v), None)

def low_pass(kept, grad):
    return (grad,)

def back_keep(v):
    return (v, None)

def back_low(kept, grad):
    return (low(grad),)
low.defvjp(low_keep, low_pass)
low_back.defvjp(back_keep, back_low)

def norm_rows(rows, gain, bias):
    mean_row = lax.optimization_barrier(jnp.mean(rows, -1, keepdims=True))
    centred = rows - mean_row
    variance = lax.optimization_barrier(jnp.mean(centred * centred, -1, keepdims=True))
    return centred * lax.rsqrt(variance + 1e-05) * gain + bias

def segments(seq_group, seq_len):
    seq_order = jnp.arange(NSEQ, dtype=jnp.int32)
    group_ids = jnp.arange(N_GRP, dtype=jnp.int32)
    in_group = seq_group[None, :] == group_ids[:, None]
    lengths = jnp.where(in_group, seq_len[None, :], 0).astype(jnp.int32)
    earlier = seq_order[:, None] > seq_order[None, :]
    offsets = lax.optimization_barrier(jnp.sum(jnp.where(earlier[None, :, :], lengths[:, None, :], 0), -1)).astype(jnp.int32)
    places = jnp.arange(LONG, dtype=jnp.int32)[None, :, None]
    inside = in_group[:, None, :] & (places >= offsets[:, None, :]) & (places < (offsets + lengths)[:, None, :])
    return (lax.optimization_barrier(jnp.sum(jnp.where(inside, seq_order[None, None, :] + 1, 0), -1)) - 1).astype(jnp.int32)

def reference(layer_input, out_cotangent, seq_group, seq_len, w_qkv, b_qv, w_out, b_out, w_up, b_up, w_down, b_down, first_norm_gain, first_norm_bias, second_norm_gain, second_norm_bias):
    segment = segments(seq_group, seq_len)
    highest = lax.Precision.HIGHEST
    score_scale = HD ** (-0.5)
    positions = jnp.arange(LONG, dtype=jnp.int32)
    causal = positions[None, :] <= positions[:, None]

    def forward(params, inputs):
        w_qkv_f, b_qv_f, w_out_f, b_out_f, w_up_f, b_up_f, w_down_f, b_down_f, gain_one, bias_one, gain_two, bias_two = params
        w_attn = low(w_qkv_f).reshape(D, N_TP, -1)
        w_proj = low(w_out_f).reshape(D, N_TP, -1)
        w_expand = low(w_up_f).reshape(D, N_TP, -1)
        w_reduce = low(w_down_f).reshape(D, N_TP, -1)
        head_bias = b_qv_f.reshape(HEADS, 2, HD)
        bias_three = jnp.stack([head_bias[:, 0], jnp.zeros_like(head_bias[:, 0]), head_bias[:, 1]], 1)

        def group_pass(pair):
            group_rows, group_segment = pair
            live_rows = (group_segment >= 0).astype(jnp.float32)[:, None]
            normed = low(norm_rows(group_rows, gain_one, bias_one))
            copies = low_back(jnp.broadcast_to(normed[:, None, :], (LONG, N_TP, D)))
            projected = jnp.einsum('tgd,dgk->tgk', copies, w_attn, precision=highest).reshape(LONG, HEADS, 3, HD) + bias_three
            projected = low_back(low(projected))
            query = projected[:, :, 0]
            keys = projected[:, :, 1]
            values = projected[:, :, 2]
            scores = low_back(score_scale * jnp.einsum('qhe,khe->hqk', query, keys, precision=highest))
            allowed = (group_segment[:, None] == group_segment[None, :]) & causal
            scores = jnp.where(allowed[None], scores, -1e+30)
            highest_score = lax.optimization_barrier(jnp.max(scores, -1, keepdims=True))
            powers = jnp.exp(scores - highest_score)
            chances = low(powers / lax.optimization_barrier(jnp.sum(powers, -1, keepdims=True)))
            context = low_back(low(jnp.einsum('hqk,khe->qhe', chances, values, precision=highest)))
            partial_attn = jnp.einsum('tgk,dgk->tgd', context.reshape(LONG, N_TP, -1), w_proj, precision=highest)
            hidden = group_rows + low_back(lax.optimization_barrier(jnp.sum(low(partial_attn), 1))) + b_out_f
            second_normalized = low(norm_rows(hidden, gain_two, bias_two))
            copies_two = low_back(jnp.broadcast_to(second_normalized[:, None, :], (LONG, N_TP, D)))
            before = low_back(jnp.einsum('tgd,dgf->tgf', copies_two, w_expand, precision=highest) + b_up_f.reshape(N_TP, -1))
            active = low(jax.nn.gelu(before, approximate=True))
            partial_mlp = jnp.einsum('tgf,dgf->tgd', active, w_reduce, precision=highest)
            return live_rows * (hidden + low_back(lax.optimization_barrier(jnp.sum(low(partial_mlp), 1))) + b_down_f)
        outputs = lax.map(jax.checkpoint(group_pass), (inputs.reshape(N_GRP, LONG, D), segment))
        return outputs.reshape(TOKENS, D)
    params = tuple((item.astype(jnp.float32) for item in (w_qkv, b_qv, w_out, b_out, w_up, b_up, w_down, b_down, first_norm_gain, first_norm_bias, second_norm_gain, second_norm_bias)))
    result, pullback = jax.vjp(forward, params, layer_input.astype(jnp.float32))
    grad_params, input_gradient = pullback(out_cotangent.astype(jnp.float32))
    return (result.astype(jnp.bfloat16), input_gradient, grad_params[0], grad_params[1], grad_params[2], grad_params[3], grad_params[4], grad_params[5], grad_params[6], grad_params[7], grad_params[8], grad_params[9], grad_params[10], grad_params[11])
```

```python
import functools

import jax
import jax.numpy as jnp
from jax import lax
from jax.experimental import pallas as pl
from jax.experimental.pallas import tpu as pltpu
from jax.sharding import PartitionSpec as P

HD = 128
BLK=512
F32=jnp.float32
BF=jnp.bfloat16
LOG2E=1.4426950408889634

def dg(a,b,ca,cb):
    return lax.dot_general(a,b,(((ca,),(cb,)),((),())),preferred_element_type=F32)

def attn_fwd_kernel(info, q_ref, k_ref, v_ref, o_ref, lse_ref, *, nb):
    c = HD ** -0.5 * LOG2E
    for qi in range(nb):
        rows = pl.ds(qi*BLK, BLK)
        @pl.when(info[2, qi] > 0)
        def _():
            q = q_ref[rows, :]
            def step(j, carry, diag=False):
                m, l, acc = carry
                kr = pl.ds(pl.multiple_of(j*BLK, BLK), BLK)
                s = dg(k_ref[kr, :], q, 1, 1)
                if diag:
                    ki = lax.broadcasted_iota(jnp.int32, s.shape, 0)
                    qq = lax.broadcasted_iota(jnp.int32, s.shape, 1)
                    s = jnp.where(ki <= qq, s, -1e30)
                mn = jnp.maximum(m, jnp.max(s, 0, keepdims=True))
                p = jnp.exp2(s*c - mn*c)
                alpha = jnp.exp2((m - mn)*c)
                l = l*alpha + jnp.sum(p, 0, keepdims=True)
                acc = acc*alpha + dg(v_ref[kr, :], p.astype(BF), 0, 0)
                return mn, l, acc
            init = (jnp.full((1, BLK), -1e30, F32), jnp.zeros((1, BLK), F32), jnp.zeros((HD, BLK), F32))
            carry = step(qi, init, True)
            m, l, acc = lax.fori_loop(info[0, qi], qi, step, carry)
            o_ref[rows, :] = jnp.transpose(acc / l).astype(BF)
            lse_ref[0, :, rows] = m*c + jnp.log2(l)
        @pl.when(info[2, qi] <= 0)
        def _():
            o_ref[rows, :] = jnp.zeros((BLK, HD), BF)
            lse_ref[0, :, rows] = jnp.zeros((1, BLK), F32)

def attn_fwd(info, proj):
    length = proj.shape[0]; heads = proj.shape[1]//(3*HD); nb = length//BLK
    spec = lambda o: pl.BlockSpec((length, HD), lambda h, info: (0, 3*h+o))
    return pl.pallas_call(functools.partial(attn_fwd_kernel, nb=nb),
        grid_spec=pltpu.PrefetchScalarGridSpec(num_scalar_prefetch=1, grid=(heads,),
            in_specs=[spec(0), spec(1), spec(2)],
            out_specs=[pl.BlockSpec((length, HD), lambda h, info: (0, h)), pl.BlockSpec((1, 1, length), lambda h, info: (h, 0, 0))]),
        out_shape=[jax.ShapeDtypeStruct((length, heads*HD), BF), jax.ShapeDtypeStruct((heads, 1, length), F32)],
        compiler_params=pltpu.CompilerParams(vmem_limit_bytes=40<<20), name="attn_fwd",
        cost_estimate=pl.CostEstimate(flops=heads*length*length*HD*2, bytes_accessed=length*heads*HD*8, transcendentals=heads*length*length//2),
    )(info, proj, proj, proj)

def attn_bwd_kernel(info, q_ref, k_ref, v_ref, o_ref, do_ref, lse_ref, dp_ref, dq_sc, dl_sc, *, nb):
    sc = HD ** -0.5
    c = sc * LOG2E
    prod = do_ref[...].astype(F32) * o_ref[...].astype(F32)
    dl_sc[...] = jnp.sum(jnp.transpose(prod), 0, keepdims=True)
    dq_sc[...] = jnp.zeros_like(dq_sc)
    for j in range(nb):
        kr = pl.ds(j*BLK, BLK)
        @pl.when(info[2, j] > 0)
        def _():
            k = k_ref[kr, :]; v = v_ref[kr, :]
            def step(i, carry, diag=False):
                dk, dv = carry
                qr = pl.ds(pl.multiple_of(i*BLK, BLK), BLK)
                q = q_ref[qr, :]; do = do_ref[qr, :]
                s = dg(k, q, 1, 1)
                p = jnp.exp2(s*c - lse_ref[0, :, qr])
                if diag:
                    ki = lax.broadcasted_iota(jnp.int32, s.shape, 0)
                    qq = lax.broadcasted_iota(jnp.int32, s.shape, 1)
                    p = jnp.where(ki <= qq, p, 0.0)
                dp = dg(v, do, 1, 1)
                ds = (p * (dp - dl_sc[:, qr])).astype(BF)
                dv = dv + dg(p.astype(BF), do, 1, 0)
                dk = dk + dg(ds, q, 1, 0)
                dq_sc[qr, :] += dg(ds, k, 0, 0)
                return dk, dv
            z = jnp.zeros((BLK, HD), F32)
            carry = step(j, (z, z), True)
            dk, dv = lax.fori_loop(j+1, info[1, j]+1, step, carry)
            dp_ref[kr, HD:2*HD] = (dk*sc).astype(BF)
            dp_ref[kr, 2*HD:] = dv.astype(BF)
        @pl.when(info[2, j] <= 0)
        def _():
            dp_ref[kr, HD:] = jnp.zeros((BLK, 2*HD), BF)
    dp_ref[:, :HD] = (dq_sc[...]*sc).astype(BF)

def attn_bwd(info, proj, ctx, dctx, lse):
    length = proj.shape[0]; heads = proj.shape[1]//(3*HD); nb = length//BLK
    spec = lambda o: pl.BlockSpec((length, HD), lambda h, info: (0, 3*h+o))
    hs = pl.BlockSpec((length, HD), lambda h, info: (0, h))
    return pl.pallas_call(functools.partial(attn_bwd_kernel, nb=nb),
        grid_spec=pltpu.PrefetchScalarGridSpec(num_scalar_prefetch=1, grid=(heads,),
            in_specs=[spec(0), spec(1), spec(2), hs, hs, pl.BlockSpec((1, 1, length), lambda h, info: (h, 0, 0))],
            out_specs=pl.BlockSpec((length, 3*HD), lambda h, info: (0, h)),
            scratch_shapes=[pltpu.VMEM((length, HD), F32), pltpu.VMEM((1, length), F32)]),
        out_shape=jax.ShapeDtypeStruct((length, heads*3*HD), BF),
        compiler_params=pltpu.CompilerParams(vmem_limit_bytes=40<<20), name="attn_bwd",
        cost_estimate=pl.CostEstimate(flops=heads*length*length*HD*5, bytes_accessed=length*heads*HD*16, transcendentals=heads*length*length//2),
    )(info, proj, proj, proj, ctx, dctx, lse)

MESH = pl.DeviceIdType.MESH


def small_kernel(x_ref, a_ref, b_ref, gbuf, tbuf, gs, gr, ts, tr, *, n_grp, n_tp, a_rows):
    t = lax.axis_index("tp")
    g = lax.axis_index("grp")
    bar = pltpu.get_barrier_semaphore()
    for d in range(1, n_grp):
        pl.semaphore_signal(bar, inc=1, device_id=(lax.rem(g + d, n_grp), t), device_id_type=MESH)
    for d in range(1, n_tp):
        pl.semaphore_signal(bar, inc=1, device_id=(g, lax.rem(t + d, n_tp)), device_id_type=MESH)
    pl.semaphore_wait(bar, n_grp + n_tp - 2)
    copies = []
    for d in range(1, n_grp):
        cp = pltpu.make_async_remote_copy(
            x_ref, gbuf.at[g], gs.at[d], gr.at[d],
            device_id=(lax.rem(g + d, n_grp), t), device_id_type=MESH)
        cp.start()
        copies.append(cp)
    gbuf[g] = x_ref[...]
    for cp in copies:
        cp.wait()
    total = gbuf[0]
    for i in range(1, n_grp):
        total = total + gbuf[i]
    tbuf[t] = total
    copies = []
    for d in range(1, n_tp):
        cp = pltpu.make_async_remote_copy(
            tbuf.at[t], tbuf.at[t], ts.at[d], tr.at[d],
            device_id=(g, lax.rem(t + d, n_tp)), device_id_type=MESH)
        cp.start()
        copies.append(cp)
    for cp in copies:
        cp.wait()
    total = tbuf[0, :a_rows]
    for i in range(1, n_tp):
        total = total + tbuf[i, :a_rows]
    a_ref[...] = total
    b_ref[...] = tbuf[:, a_rows:]


def small_sum(common, own):
    n_grp, n_tp = lax.axis_size("grp"), lax.axis_size("tp")
    a_rows = common.shape[0] // 128
    own_rows = own.shape[0] // 128
    pad = -own_rows % 8
    x = jnp.concatenate([common, own, jnp.zeros((pad * 128,), F32)]).reshape(-1, 128)
    rows = x.shape[0]
    vm = pl.BlockSpec(memory_space=pltpu.VMEM)
    a, b = pl.pallas_call(
        functools.partial(small_kernel, n_grp=n_grp, n_tp=n_tp, a_rows=a_rows),
        in_specs=[vm], out_specs=[vm, vm],
        out_shape=[jax.ShapeDtypeStruct((a_rows, 128), F32),
                   jax.ShapeDtypeStruct((n_tp, rows - a_rows, 128), F32)],
        scratch_shapes=[pltpu.VMEM((n_grp, rows, 128), F32), pltpu.VMEM((n_tp, rows, 128), F32),
                        pltpu.SemaphoreType.DMA((n_grp,)), pltpu.SemaphoreType.DMA((n_grp,)),
                        pltpu.SemaphoreType.DMA((n_tp,)), pltpu.SemaphoreType.DMA((n_tp,))],
        compiler_params=pltpu.CompilerParams(collective_id=1, has_side_effects=True),
        name="small_sum",
    )(x)
    return a.reshape(-1), b.reshape(n_tp, -1)[:, : own.shape[0]]


def normalize(rows, gain, bias):
    mean_row = jnp.mean(rows, -1, keepdims=True)
    centred = rows - mean_row
    inverse = lax.rsqrt(jnp.mean(centred * centred, -1, keepdims=True) + 1e-05)
    normed = centred * inverse
    return normed * gain + bias, normed, inverse


def norm_back(grad_norm, normed, inverse, gain):
    scaled = grad_norm * gain
    inner = jnp.mean(scaled, -1, keepdims=True) + normed * jnp.mean(scaled * normed, -1, keepdims=True)
    return inverse * (scaled - inner)


def on_device(layer_input, out_cotangent, seq_group, seq_len, w_qkv, b_qv, w_out, b_out, w_up, b_up,
              w_down, b_down, first_norm_gain, first_norm_bias, second_norm_gain, second_norm_bias):
    tp = lax.axis_index("tp")
    n_tp = lax.axis_size("tp")
    grp = lax.axis_index("grp")
    length, width = layer_input.shape
    share = length // n_tp
    heads = w_out.shape[1] // HD
    hidden_here = w_up.shape[1]

    w_attn = lax.all_gather(w_qkv.astype(BF), "grp", axis=0, tiled=True)
    w_proj = lax.all_gather(w_out.astype(BF), "tp", axis=1, tiled=True)
    w_proj = lax.all_gather(w_proj, "grp", axis=0, tiled=True)
    w_expand = lax.all_gather(w_up.astype(BF), "grp", axis=0, tiled=True)
    w_reduce = lax.all_gather(w_down.astype(BF), "grp", axis=0, tiled=True)

    nb = length // BLK
    in_group = seq_group == grp
    lengths = jnp.where(in_group, seq_len, 0)
    order = jnp.arange(seq_group.shape[0], dtype=jnp.int32)
    offsets = jnp.sum(jnp.where(order[:, None] > order[None, :], lengths[None, :], 0), 1)
    starts = jnp.arange(nb, dtype=jnp.int32) * BLK
    inside = in_group[None] & (starts[:, None] >= offsets[None]) & (starts[:, None] < (offsets + lengths)[None])
    alive = jnp.any(inside, 1)
    first = jnp.sum(jnp.where(inside, (offsets // BLK)[None], 0), 1)
    last = jnp.sum(jnp.where(inside, ((offsets + lengths) // BLK - 1)[None], 0), 1)
    info = jnp.stack([first, last, alive.astype(jnp.int32)]).astype(jnp.int32)
    tokens = jnp.sum(lengths)
    row0 = tp * share
    live = (row0 + jnp.arange(share, dtype=jnp.int32) < tokens).astype(F32)[:, None]
    live_all = (jnp.arange(length, dtype=jnp.int32) < tokens)[:, None]

    def mine(x):
        return lax.dynamic_slice_in_dim(x, row0, share, 0)

    x = layer_input.astype(F32)
    n1 = normalize(x, first_norm_gain, first_norm_bias)[0].astype(BF)
    x_share = mine(layer_input).astype(F32)
    _, xhat1, inverse1 = normalize(x_share, first_norm_gain, first_norm_bias)

    head_bias = lax.dynamic_slice_in_dim(b_qv.reshape(-1, 2, HD), tp * heads, heads, 0)
    bias_three = jnp.stack(
        [head_bias[:, 0], jnp.zeros_like(head_bias[:, 0]), head_bias[:, 1]], 1).reshape(-1)
    proj = (jnp.dot(n1, w_attn, preferred_element_type=F32) + bias_three).astype(BF)
    context, lse = attn_fwd(info, proj)
    context_rows = lax.all_to_all(context, "tp", 0, 1, tiled=True)
    hidden = x_share + dg(context_rows, w_proj, 1, 1) + b_out
    n2_share, xhat2, inverse2 = normalize(hidden, second_norm_gain, second_norm_bias)
    n2 = lax.all_gather(n2_share.astype(BF), "tp", axis=0, tiled=True)

    up_bias = lax.dynamic_slice_in_dim(b_up, tp * hidden_here, hidden_here, 0)
    before = jnp.dot(n2, w_expand, preferred_element_type=F32) + up_bias
    act = functools.partial(jax.nn.gelu, approximate=True)
    active, gelu_back = jax.vjp(act, before)
    active = active.astype(BF)
    gradb = jnp.where(live_all, out_cotangent, jnp.zeros_like(out_cotangent))
    grad_active = jnp.dot(gradb, w_reduce, preferred_element_type=F32)
    dbefore = gelu_back(grad_active)[0].astype(BF)
    dn2 = lax.psum_scatter(dg(dbefore, w_expand, 1, 1).astype(BF), "tp", scatter_dimension=0, tiled=True).astype(F32)
    grad_share = mine(gradb).astype(F32)
    dh = grad_share + norm_back(dn2, xhat2, inverse2, second_norm_gain)
    dhb = dh.astype(BF)
    dcontext_rows = jnp.dot(dhb, w_proj, preferred_element_type=F32).astype(BF)
    dcontext = lax.all_to_all(dcontext_rows, "tp", 1, 0, tiled=True)

    mlp = lax.psum_scatter(dg(active, w_reduce, 1, 1).astype(BF), "tp", scatter_dimension=0, tiled=True).astype(F32)
    result = (live * (hidden + mlp + b_down)).astype(BF)
    scatter = functools.partial(lax.psum_scatter, axis_name="grp", scatter_dimension=0, tiled=True)
    grads_reduce = scatter(dg(gradb, active, 0, 0).astype(BF)).astype(F32)
    grads_expand = scatter(dg(n2, dbefore, 0, 0).astype(BF)).astype(F32)
    dh_all = lax.all_gather(dhb, "tp", axis=0, tiled=True)
    grads_proj = scatter(dg(dh_all, context, 0, 0).astype(BF)).astype(F32)

    dproj = attn_bwd(info, proj, context, dcontext, lse)
    grads_attn = scatter(dg(n1, dproj, 0, 0).astype(BF)).astype(F32)
    dn1 = lax.psum_scatter(dg(dproj, w_attn, 1, 1).astype(BF), "tp", scatter_dimension=0, tiled=True).astype(F32)
    grad_x = dh + norm_back(dn1, xhat1, inverse1, first_norm_gain)

    proj_sums = jnp.sum(dproj.astype(F32), 0).reshape(heads, 3, HD)
    own = jnp.concatenate([jnp.stack([proj_sums[:, 0], proj_sums[:, 2]], 1).reshape(-1),
                           jnp.sum(dbefore.astype(F32), 0)])
    common = jnp.concatenate([jnp.sum(v, 0) for v in
                              (dh, grad_share, dn1 * xhat1, dn1, dn2 * xhat2, dn2)])
    sums, owned = small_sum(common, own)
    sums = sums.reshape(6, width)
    qv = heads * 2 * HD
    return (result, grad_x, grads_attn, owned[:, :qv].reshape(-1), grads_proj, sums[0], grads_expand,
            owned[:, qv:].reshape(-1), grads_reduce, sums[1], sums[2], sums[3], sums[4], sums[5])


def solution(mesh):
    rows, both, flat = P("grp", None), P("grp", "tp"), P()
    in_specs = (rows, rows, flat, flat, both, flat, both, flat, both, flat, both, flat, flat, flat, flat, flat)
    spread = P(("grp", "tp"), None)
    out_specs = (spread, spread, both, flat, both, flat, both, flat, both, flat, flat, flat, flat, flat)
    return jax.shard_map(on_device, mesh=mesh, in_specs=in_specs, out_specs=out_specs, check_vma=False)
```

```python
import functools

import jax
import jax.numpy as jnp
from jax import lax
from jax.experimental import pallas as pl
from jax.experimental.pallas import tpu as pltpu
from jax.sharding import PartitionSpec as P

HD = 128
BLK=512
F32=jnp.float32
BF=jnp.bfloat16
LOG2E=1.4426950408889634

def dg(a,b,ca,cb):
    return lax.dot_general(a,b,(((ca,),(cb,)),((),())),preferred_element_type=F32)

def attn_fwd_kernel(info, q_ref, k_ref, v_ref, o_ref, lse_ref, *, nb):
    c = HD ** -0.5 * LOG2E
    for qi in range(nb):
        rows = pl.ds(qi*BLK, BLK)
        @pl.when(info[2, qi] > 0)
        def _():
            q = q_ref[rows, :]
            def step(j, carry, diag=False):
                m, l, acc = carry
                kr = pl.ds(pl.multiple_of(j*BLK, BLK), BLK)
                s = dg(k_ref[kr, :], q, 1, 1)
                if diag:
                    ki = lax.broadcasted_iota(jnp.int32, s.shape, 0)
                    qq = lax.broadcasted_iota(jnp.int32, s.shape, 1)
                    s = jnp.where(ki <= qq, s, -1e30)
                mn = jnp.maximum(m, jnp.max(s, 0, keepdims=True))
                p = jnp.exp2(s*c - mn*c)
                alpha = jnp.exp2((m - mn)*c)
                l = l*alpha + jnp.sum(p, 0, keepdims=True)
                acc = acc*alpha + dg(v_ref[kr, :], p.astype(BF), 0, 0)
                return mn, l, acc
            init = (jnp.full((1, BLK), -1e30, F32), jnp.zeros((1, BLK), F32), jnp.zeros((HD, BLK), F32))
            carry = step(qi, init, True)
            m, l, acc = lax.fori_loop(info[0, qi], qi, step, carry)
            o_ref[rows, :] = jnp.transpose(acc / l).astype(BF)
            lse_ref[0, :, rows] = m*c + jnp.log2(l)
        @pl.when(info[2, qi] <= 0)
        def _():
            o_ref[rows, :] = jnp.zeros((BLK, HD), BF)
            lse_ref[0, :, rows] = jnp.zeros((1, BLK), F32)

def attn_fwd(info, proj):
    length = proj.shape[0]; heads = proj.shape[1]//(3*HD); nb = length//BLK
    spec = lambda o: pl.BlockSpec((length, HD), lambda h, info: (0, 3*h+o))
    return pl.pallas_call(functools.partial(attn_fwd_kernel, nb=nb),
        grid_spec=pltpu.PrefetchScalarGridSpec(num_scalar_prefetch=1, grid=(heads,),
            in_specs=[spec(0), spec(1), spec(2)],
            out_specs=[pl.BlockSpec((length, HD), lambda h, info: (0, h)), pl.BlockSpec((1, 1, length), lambda h, info: (h, 0, 0))]),
        out_shape=[jax.ShapeDtypeStruct((length, heads*HD), BF), jax.ShapeDtypeStruct((heads, 1, length), F32)],
        compiler_params=pltpu.CompilerParams(vmem_limit_bytes=40<<20), name="attn_fwd",
        cost_estimate=pl.CostEstimate(flops=heads*length*length*HD*2, bytes_accessed=length*heads*HD*8, transcendentals=heads*length*length//2),
    )(info, proj, proj, proj)

def attn_bwd_kernel(info, q_ref, k_ref, v_ref, o_ref, do_ref, lse_ref, dp_ref, dq_sc, dl_sc, *, nb):
    sc = HD ** -0.5
    c = sc * LOG2E
    prod = do_ref[...].astype(F32) * o_ref[...].astype(F32)
    dl_sc[...] = jnp.sum(jnp.transpose(prod), 0, keepdims=True)
    dq_sc[...] = jnp.zeros_like(dq_sc)
    for j in range(nb):
        kr = pl.ds(j*BLK, BLK)
        @pl.when(info[2, j] > 0)
        def _():
            k = k_ref[kr, :]; v = v_ref[kr, :]
            def step(i, carry, diag=False):
                dk, dv = carry
                qr = pl.ds(pl.multiple_of(i*BLK, BLK), BLK)
                q = q_ref[qr, :]; do = do_ref[qr, :]
                s = dg(k, q, 1, 1)
                p = jnp.exp2(s*c - lse_ref[0, :, qr])
                if diag:
                    ki = lax.broadcasted_iota(jnp.int32, s.shape, 0)
                    qq = lax.broadcasted_iota(jnp.int32, s.shape, 1)
                    p = jnp.where(ki <= qq, p, 0.0)
                dp = dg(v, do, 1, 1)
                ds = (p * (dp - dl_sc[:, qr])).astype(BF)
                dv = dv + dg(p.astype(BF), do, 1, 0)
                dk = dk + dg(ds, q, 1, 0)
                dq_sc[qr, :] += dg(ds, k, 0, 0)
                return dk, dv
            z = jnp.zeros((BLK, HD), F32)
            carry = step(j, (z, z), True)
            dk, dv = lax.fori_loop(j+1, info[1, j]+1, step, carry)
            dp_ref[kr, HD:2*HD] = (dk*sc).astype(BF)
            dp_ref[kr, 2*HD:] = dv.astype(BF)
        @pl.when(info[2, j] <= 0)
        def _():
            dp_ref[kr, HD:] = jnp.zeros((BLK, 2*HD), BF)
    dp_ref[:, :HD] = (dq_sc[...]*sc).astype(BF)

def attn_bwd(info, proj, ctx, dctx, lse):
    length = proj.shape[0]; heads = proj.shape[1]//(3*HD); nb = length//BLK
    spec = lambda o: pl.BlockSpec((length, HD), lambda h, info: (0, 3*h+o))
    hs = pl.BlockSpec((length, HD), lambda h, info: (0, h))
    return pl.pallas_call(functools.partial(attn_bwd_kernel, nb=nb),
        grid_spec=pltpu.PrefetchScalarGridSpec(num_scalar_prefetch=1, grid=(heads,),
            in_specs=[spec(0), spec(1), spec(2), hs, hs, pl.BlockSpec((1, 1, length), lambda h, info: (h, 0, 0))],
            out_specs=pl.BlockSpec((length, 3*HD), lambda h, info: (0, h)),
            scratch_shapes=[pltpu.VMEM((length, HD), F32), pltpu.VMEM((1, length), F32)]),
        out_shape=jax.ShapeDtypeStruct((length, heads*3*HD), BF),
        compiler_params=pltpu.CompilerParams(vmem_limit_bytes=40<<20), name="attn_bwd",
        cost_estimate=pl.CostEstimate(flops=heads*length*length*HD*5, bytes_accessed=length*heads*HD*16, transcendentals=heads*length*length//2),
    )(info, proj, proj, proj, ctx, dctx, lse)


MESH = pl.DeviceIdType.MESH
TILE = 256


class Place:
    def __init__(self, n_tp):
        self.g = lax.axis_index("grp")
        t = lax.axis_index("tp")
        self.t, self.n, self.Z = t, n_tp, n_tp // 2
        self.z, self.k = t // 2, lax.rem(t, 2)
        self.right, self.left, self.sib = (self.g, t + 2), (self.g, t - 2), (self.g, t + 1 - 2 * self.k)
        self.has_right, self.has_left = self.z < self.Z - 1, self.z > 0

    def barrier(self):
        bar = pltpu.get_barrier_semaphore()
        pl.semaphore_signal(bar, inc=1, device_id=self.sib, device_id_type=MESH)

        @pl.when(self.has_right)
        def _():
            pl.semaphore_signal(bar, inc=1, device_id=self.right, device_id_type=MESH)

        @pl.when(self.has_left)
        def _():
            pl.semaphore_signal(bar, inc=1, device_id=self.left, device_id_type=MESH)

        amount = 1 + jnp.where(self.has_right, 1, 0) + jnp.where(self.has_left, 1, 0)
        pl.semaphore_wait(bar, amount)


def remote(src, dst, ssem, rsem, device):
    return pltpu.make_async_remote_copy(src, dst, ssem, rsem, device_id=device, device_id_type=MESH)


class Gather:
    def __init__(self, at, gat, rows, ls, lr, ss, sr):
        self.at, self.gat, self.rows = at, gat, rows
        self.ls, self.lr, self.ss, self.sr = ls, lr, ss, sr

    def block(self, zz, kk, c):
        return self.gat.at[2 * zz + kk, pl.ds(pl.multiple_of(c * self.rows, self.rows), self.rows), :]

    def line(self, c, side, d):
        at = self.at
        sign, device = (-1, at.right) if side == 0 else (1, at.left)
        b = self.block(at.z + sign * (d - 1), at.k, c)
        return remote(b, b, self.ls.at[c, side, d - 1], self.lr.at[c, side, d - 1], device)

    def line_in(self, c, side, d):
        at = self.at
        sign, device = (-1, at.right) if side == 0 else (1, at.left)
        b = self.block(at.z + sign * d, at.k, c)
        return remote(b, b, self.ls.at[c, side, d - 1], self.lr.at[c, side, d - 1], device)

    def across(self, c, zz):
        b = self.block(zz, self.at.k, c)
        return remote(b, b, self.ss.at[c, zz], self.sr.at[c, zz], self.at.sib)

    def across_in(self, c, zz):
        b = self.block(zz, 1 - self.at.k, c)
        return remote(b, b, self.ss.at[c, zz], self.sr.at[c, zz], self.at.sib)

    def start(self, c):
        at = self.at

        @pl.when(at.has_right)
        def _():
            self.line(c, 0, 1).start()

        @pl.when(at.has_left)
        def _():
            self.line(c, 1, 1).start()

        self.across(c, at.z).start()

    def hop(self, c, d):
        at = self.at

        @pl.when(at.z >= d)
        def _():
            self.line_in(c, 0, d).wait_recv()
            if d < at.Z - 1:
                @pl.when(at.has_right)
                def _():
                    self.line(c, 0, d + 1).start()
            self.across(c, at.z - d).start()

        @pl.when(at.z + d <= at.Z - 1)
        def _():
            self.line_in(c, 1, d).wait_recv()
            if d < at.Z - 1:
                @pl.when(at.has_left)
                def _():
                    self.line(c, 1, d + 1).start()
            self.across(c, at.z + d).start()

    def finish(self, c):
        at = self.at
        for zz in range(at.Z):
            self.across_in(c, zz).wait_recv()
            self.across(c, zz).wait_send()
        for d in range(1, at.Z):
            @pl.when(at.has_right & (at.z >= d - 1))
            def _():
                self.line(c, 0, d).wait_send()

            @pl.when(at.has_left & (at.z + d - 1 <= at.Z - 1))
            def _():
                self.line(c, 1, d).wait_send()


class Scatter:
    def __init__(self, at, parts, pair, hops, cs, cr, hs, hr):
        self.at, self.parts, self.pair, self.hops = at, parts, pair, hops
        self.cs, self.cr, self.hs, self.hr = cs, cr, hs, hr

    def across(self, c):
        return remote(self.parts.at[:, 1 - self.at.k], self.pair.at[c], self.cs.at[c], self.cr.at[c], self.at.sib)

    def line(self, c, side, h, target):
        device = self.at.right if side == 0 else self.at.left
        return remote(self.pair.at[c, target], self.hops.at[side, c, h - 1],
                      self.hs.at[c, side, h - 1], self.hr.at[c, side, h - 1], device)

    def start(self, c):
        self.across(c).start()

    def meet(self, c):
        self.across(c).wait()
        own = self.parts[:, pl.ds(self.at.k, 1)]
        own = own.reshape(own.shape[0], own.shape[2], own.shape[3])
        self.pair[c] = (self.pair[c].astype(F32) + own.astype(F32)).astype(BF)

    def hop(self, c, h):
        at = self.at
        for side in (0, 1):
            pos = at.z if side == 0 else at.Z - 1 - at.z
            target = at.z + at.Z - h if side == 0 else at.z - at.Z + h

            @pl.when((pos <= h - 1) & (pos < at.Z - 1))
            def _():
                if h >= 2:
                    @pl.when(pos >= 1)
                    def _():
                        self.line(c, side, h - 1, target).wait_recv()
                        self.pair[c, target] = (self.pair[c, target].astype(F32)
                                                + self.hops[side, c, h - 2].astype(F32)).astype(BF)
                self.line(c, side, h, target).start()

    def finish(self, c, total):
        at = self.at
        total[...] = self.pair[c, at.z].astype(F32)
        for side in (0, 1):
            pos = at.z if side == 0 else at.Z - 1 - at.z

            @pl.when(pos >= 1)
            def _():
                self.line(c, side, at.Z - 1, at.z).wait_recv()
                total[...] += self.hops[side, c, at.Z - 2].astype(F32)

            for h in range(1, at.Z):
                @pl.when((pos <= h - 1) & (pos < at.Z - 1))
                def _():
                    self.line(c, side, h, at.z).wait_send()


def gather_sems(chunks, Z):
    dma = pltpu.SemaphoreType.DMA
    return [dma((chunks, 2, Z - 1)), dma((chunks, 2, Z - 1)), dma((chunks, Z)), dma((chunks, Z))]


def scatter_scratch(chunks, Z, rows, width):
    dma = pltpu.SemaphoreType.DMA
    return [pltpu.VMEM((Z, 2, rows, width), BF), pltpu.VMEM((chunks, Z, rows, width), BF),
            pltpu.VMEM((2, chunks, Z - 1, rows, width), BF),
            dma((chunks,)), dma((chunks,)), dma((chunks, 2, Z - 1)), dma((chunks, 2, Z - 1))]


def inside(c, chunks):
    return (c >= 0) & (c < chunks)


def chunk_rows(c, rows):
    return pl.ds(pl.multiple_of(c * rows, rows), rows)


def tiles(count, body):
    def step(i, carry):
        body(i)
        return carry
    lax.fori_loop(0, count, step, 0)


def cols(i, size=TILE):
    return pl.ds(pl.multiple_of(i * size, size), size)


def rows_stats(rows):
    mean = jnp.mean(rows, -1, keepdims=True)
    centred = rows - mean
    inverse = lax.rsqrt(jnp.mean(centred * centred, -1, keepdims=True) + 1e-05)
    return centred * inverse, inverse


def out_kernel(ctx, w_out, x_share, vec, hidden, n2, *scratch, n, chunks, rows):
    total, *sc = scratch
    at = Place(n)
    at.barrier()
    rs = Scatter(at, *sc)
    width = w_out.shape[0]

    def product(c):
        lhs = ctx[:, chunk_rows(c, rows), :].reshape(n * rows, ctx.shape[2])

        def tile(i):
            y = dg(lhs, w_out[cols(i), :], 1, 1)
            rs.parts[:, :, :, cols(i)] = y.astype(BF).reshape(at.Z, 2, rows, TILE)
        tiles(width // TILE, tile)
        rs.start(c)

    def tick(i, carry):
        c = i - 1

        @pl.when(inside(c, chunks))
        def _():
            rs.meet(c)
            rs.hop(c, 1)

        @pl.when(inside(i, chunks))
        def _():
            product(i)

        @pl.when(inside(c, chunks))
        def _():
            for h in range(2, at.Z):
                rs.hop(c, h)

        e = i - 2

        @pl.when(inside(e, chunks))
        def _():
            rs.finish(e, total)
            r = chunk_rows(e, rows)
            h = x_share[r, :].astype(F32) + total[...] + vec[0:1, :]
            hidden[r, :] = h
            n2[r, :] = (rows_stats(h)[0] * vec[1:2, :] + vec[2:3, :]).astype(BF)
        return carry

    lax.fori_loop(0, chunks + 2, tick, 0)


def attn_out(ctx, w_out, x_share, vec, n, chunks):
    length, hw = ctx.shape
    share, width = x_share.shape
    rows = share // chunks
    vm = pl.BlockSpec(memory_space=pltpu.VMEM)
    return pl.pallas_call(
        functools.partial(out_kernel, n=n, chunks=chunks, rows=rows),
        in_specs=[vm] * 4, out_specs=[vm] * 2,
        out_shape=[jax.ShapeDtypeStruct((share, width), F32), jax.ShapeDtypeStruct((share, width), BF)],
        scratch_shapes=[pltpu.VMEM((rows, width), F32)] + scatter_scratch(chunks, n // 2, rows, width),
        compiler_params=pltpu.CompilerParams(collective_id=2, has_side_effects=True, vmem_limit_bytes=40 << 20),
        cost_estimate=pl.CostEstimate(flops=2 * length * hw * width, bytes_accessed=1 << 23, transcendentals=0),
        name="attn_out",
    )(ctx.reshape(n, share, hw), w_out, x_share, vec)


def ffn_kernel(n2_hbm, gradb_hbm, w_up, w_down, w_out, b_up, ctx, hidden, gshare, gain,
               mlp_hbm, gwu_hbm, gwd_hbm, gwo, dctx, dh, stats, bsum,
               gat, acc_up, acc_down, gbuf, mst, actb, dbb, total, lsem, gsem, msem, *scratch, n, chunks, rows):
    at = Place(n)
    s1, s2, sc = scratch[:4], scratch[4:8], scratch[8:]
    ag1, ag2 = Gather(at, gat, rows, *s1), Gather(at, gat, rows, *s2)
    rs = Scatter(at, *sc)
    width, hid = w_up.shape
    m = n * rows

    load = pltpu.make_async_copy(n2_hbm, gat.at[at.t], lsem)
    load.start()

    def fetch(c):
        slot = lax.rem(c, 2)
        return pltpu.make_async_copy(gradb_hbm.at[:, chunk_rows(c, rows), :], gbuf.at[slot], gsem.at[slot])

    def put_mlp(c):
        return pltpu.make_async_copy(mst, mlp_hbm.at[:, chunk_rows(c, rows), :], msem)

    fetch(0).start()
    acc_up[...] = jnp.zeros_like(acc_up)
    acc_down[...] = jnp.zeros_like(acc_down)
    stats[...] = jnp.zeros_like(stats)
    bsum[...] = jnp.zeros_like(bsum)
    load.wait()
    at.barrier()

    a0, a1 = 0.7978845608028654, 0.044715

    def wide(c):
        return gat[:, chunk_rows(c, rows), :].reshape(m, width)

    def forward(c):
        fetch(c).wait()

        @pl.when(c + 1 < chunks)
        def _():
            fetch(c + 1).start()
        slot = lax.rem(c, 2)

        def tile(i):
            v = dg(wide(c), w_up[:, cols(i)], 1, 0) + b_up[:, cols(i)]
            ga = dg(gbuf[slot].reshape(m, width), w_down[:, cols(i)], 1, 0)
            v2 = v * v
            th = jnp.tanh(a0 * (v + a1 * v2 * v))
            half = 0.5 * (1.0 + th)
            actb[:, cols(i)] = (v * half).astype(BF)
            slope = half + 0.5 * v * (1.0 - th * th) * (a0 * (1.0 + 3.0 * a1 * v2))
            db = (ga * slope).astype(BF)
            dbb[:, cols(i)] = db
            bsum[:, cols(i)] += jnp.sum(db.astype(F32), 0, keepdims=True)
        tiles(hid // TILE, tile)

    def back(c):
        def tile(i):
            y = dg(dbb[...], w_up[cols(i), :], 1, 1)
            rs.parts[:, :, :, cols(i)] = y.astype(BF).reshape(at.Z, 2, rows, TILE)
        tiles(width // TILE, tile)

    def down(c):
        @pl.when(c > 0)
        def _():
            put_mlp(c - 1).wait()

        def tile(i):
            y = dg(actb[...], w_down[cols(i), :], 1, 1)
            mst[:, :, cols(i)] = y.astype(BF).reshape(n, rows, TILE)
        tiles(width // TILE, tile)
        put_mlp(c).start()

    def weights(c):
        slot = lax.rem(c, 2)

        def tile(i):
            x = gat[:, chunk_rows(c, rows), cols(i)].reshape(m, TILE)
            acc_up[cols(i), :] += dg(x, dbb[...], 0, 0)
            y = gbuf[slot, :, :, cols(i)].reshape(m, TILE)
            acc_down[cols(i), :] += dg(y, actb[...], 0, 0)
        tiles(width // TILE, tile)

    def norm_grad(c):
        r = chunk_rows(c, rows)
        xhat, inverse = rows_stats(hidden[r, :])
        dn2 = total[...]
        e = dn2 * gain[...]
        inner = jnp.mean(e, -1, keepdims=True) + xhat * jnp.mean(e * xhat, -1, keepdims=True)
        d = gshare[r, :].astype(F32) + inverse * (e - inner)
        dh[r, :] = d
        gat[at.t, r, :] = d.astype(BF)
        stats[0:1, :] += jnp.sum(dn2 * xhat, 0, keepdims=True)
        stats[1:2, :] += jnp.sum(dn2, 0, keepdims=True)
        stats[2:3, :] += jnp.sum(d, 0, keepdims=True)

    def heads(c):
        y = dg(wide(c), w_out[...], 1, 0)
        dctx[:, chunk_rows(c, rows), :] = y.astype(BF).reshape(n, rows, y.shape[1])

    def at_stage(c, fn):
        @pl.when(inside(c, chunks))
        def _():
            fn(c)

    def hops(i, h):
        at_stage(i - 3, lambda c: rs.hop(c, h))
        at_stage(i - 4, lambda c: ag2.hop(c, h))
        at_stage(i - 1, lambda c: ag1.hop(c, h))

    def tick(i, carry):
        at_stage(i, ag1.start)
        at_stage(i - 3, rs.meet)
        hops(i, 1)
        at_stage(i - 2, forward)
        for h in range(2, at.Z):
            hops(i, h)
            if h == 2:
                at_stage(i - 2, back)

        def rest(c):
            weights(c)
            rs.start(c)
            down(c)
        at_stage(i - 2, rest)

        def gathered(c):
            ag2.finish(c)
            heads(c)
        at_stage(i - 4, gathered)

        def reduced(c):
            rs.finish(c, total)
            norm_grad(c)
            ag2.start(c)
        at_stage(i - 3, reduced)
        at_stage(i - 1, ag1.finish)
        return carry

    lax.fori_loop(0, chunks + 4, tick, 0)
    put_mlp(chunks - 1).wait()

    def final(i):
        x = gat[:, :, cols(i)].reshape(-1, TILE)
        gwo[cols(i), :] = dg(x, ctx[...], 0, 0).astype(BF)
    tiles(width // TILE, final)

    def store(i):
        r = cols(i, m)
        actb[...] = acc_up[r, :].astype(BF)
        one = pltpu.make_async_copy(actb, gwu_hbm.at[r, :], lsem)
        one.start()
        dbb[...] = acc_down[r, :].astype(BF)
        two = pltpu.make_async_copy(dbb, gwd_hbm.at[r, :], msem)
        two.start()
        one.wait()
        two.wait()
    tiles(width // m, store)


def feed_forward(n2, gradb, w_up, w_down, w_out, b_up, ctx, hidden, gshare, gain, n, chunks):
    length, width = gradb.shape
    hid, hw = w_up.shape[1], w_out.shape[1]
    share = length // n
    rows = share // chunks
    Z = n // 2
    vm, hbm = pl.BlockSpec(memory_space=pltpu.VMEM), pl.BlockSpec(memory_space=pl.ANY)
    S = jax.ShapeDtypeStruct
    m = n * rows
    return pl.pallas_call(
        functools.partial(ffn_kernel, n=n, chunks=chunks, rows=rows),
        in_specs=[hbm, hbm] + [vm] * 8,
        out_specs=[hbm, hbm, hbm] + [vm] * 5,
        out_shape=[S((n, share, width), BF), S((width, hid), BF), S((width, hid), BF), S((width, hw), BF),
                   S((n, share, hw), BF), S((share, width), F32), S((8, width), F32), S((1, hid), F32)],
        scratch_shapes=[pltpu.VMEM((n, share, width), BF), pltpu.VMEM((width, hid), F32), pltpu.VMEM((width, hid), F32),
                        pltpu.VMEM((2, n, rows, width), BF), pltpu.VMEM((n, rows, width), BF),
                        pltpu.VMEM((m, hid), BF), pltpu.VMEM((m, hid), BF), pltpu.VMEM((rows, width), F32),
                        pltpu.SemaphoreType.DMA, pltpu.SemaphoreType.DMA((2,)), pltpu.SemaphoreType.DMA]
                       + gather_sems(chunks, Z) + gather_sems(chunks, Z) + scatter_scratch(chunks, Z, rows, width),
        compiler_params=pltpu.CompilerParams(collective_id=3, has_side_effects=True, vmem_limit_bytes=62 << 20),
        cost_estimate=pl.CostEstimate(flops=12 * length * hid * width, bytes_accessed=1 << 26, transcendentals=0),
        name="feed_forward",
    )(n2, gradb.reshape(n, share, width), w_up, w_down, w_out, b_up, ctx, hidden, gshare, gain)


def small_kernel(x_ref, a_ref, b_ref, gbuf, tbuf, gs, gr, ts, tr, *, n_grp, n_tp, a_rows):
    t = lax.axis_index("tp")
    g = lax.axis_index("grp")
    bar = pltpu.get_barrier_semaphore()
    for d in range(1, n_grp):
        pl.semaphore_signal(bar, inc=1, device_id=(lax.rem(g + d, n_grp), t), device_id_type=MESH)
    for d in range(1, n_tp):
        pl.semaphore_signal(bar, inc=1, device_id=(g, lax.rem(t + d, n_tp)), device_id_type=MESH)
    pl.semaphore_wait(bar, n_grp + n_tp - 2)
    copies = []
    for d in range(1, n_grp):
        cp = pltpu.make_async_remote_copy(
            x_ref, gbuf.at[g], gs.at[d], gr.at[d],
            device_id=(lax.rem(g + d, n_grp), t), device_id_type=MESH)
        cp.start()
        copies.append(cp)
    gbuf[g] = x_ref[...]
    for cp in copies:
        cp.wait()
    total = gbuf[0]
    for i in range(1, n_grp):
        total = total + gbuf[i]
    tbuf[t] = total
    copies = []
    for d in range(1, n_tp):
        cp = pltpu.make_async_remote_copy(
            tbuf.at[t], tbuf.at[t], ts.at[d], tr.at[d],
            device_id=(g, lax.rem(t + d, n_tp)), device_id_type=MESH)
        cp.start()
        copies.append(cp)
    for cp in copies:
        cp.wait()
    total = tbuf[0, :a_rows]
    for i in range(1, n_tp):
        total = total + tbuf[i, :a_rows]
    a_ref[...] = total
    b_ref[...] = tbuf[:, a_rows:]


def small_sum(common, own):
    n_grp, n_tp = lax.axis_size("grp"), lax.axis_size("tp")
    a_rows = common.shape[0] // 128
    own_rows = own.shape[0] // 128
    pad = -own_rows % 8
    x = jnp.concatenate([common, own, jnp.zeros((pad * 128,), F32)]).reshape(-1, 128)
    rows = x.shape[0]
    vm = pl.BlockSpec(memory_space=pltpu.VMEM)
    a, b = pl.pallas_call(
        functools.partial(small_kernel, n_grp=n_grp, n_tp=n_tp, a_rows=a_rows),
        in_specs=[vm], out_specs=[vm, vm],
        out_shape=[jax.ShapeDtypeStruct((a_rows, 128), F32),
                   jax.ShapeDtypeStruct((n_tp, rows - a_rows, 128), F32)],
        scratch_shapes=[pltpu.VMEM((n_grp, rows, 128), F32), pltpu.VMEM((n_tp, rows, 128), F32),
                        pltpu.SemaphoreType.DMA((n_grp,)), pltpu.SemaphoreType.DMA((n_grp,)),
                        pltpu.SemaphoreType.DMA((n_tp,)), pltpu.SemaphoreType.DMA((n_tp,))],
        compiler_params=pltpu.CompilerParams(collective_id=1, has_side_effects=True),
        name="small_sum",
    )(x)
    return a.reshape(-1), b.reshape(n_tp, -1)[:, : own.shape[0]]


def normalize(rows, gain, bias):
    mean_row = jnp.mean(rows, -1, keepdims=True)
    centred = rows - mean_row
    inverse = lax.rsqrt(jnp.mean(centred * centred, -1, keepdims=True) + 1e-05)
    normed = centred * inverse
    return normed * gain + bias, normed, inverse


def norm_back(grad_norm, normed, inverse, gain):
    scaled = grad_norm * gain
    inner = jnp.mean(scaled, -1, keepdims=True) + normed * jnp.mean(scaled * normed, -1, keepdims=True)
    return inverse * (scaled - inner)


def on_device(layer_input, out_cotangent, seq_group, seq_len, w_qkv, b_qv, w_out, b_out, w_up, b_up,
              w_down, b_down, first_norm_gain, first_norm_bias, second_norm_gain, second_norm_bias):
    tp = lax.axis_index("tp")
    n_tp = lax.axis_size("tp")
    grp = lax.axis_index("grp")
    length, width = layer_input.shape
    share = length // n_tp
    heads = w_out.shape[1] // HD
    hidden_here = w_up.shape[1]

    w_attn = lax.all_gather(w_qkv.astype(BF), "grp", axis=0, tiled=True)
    w_proj = lax.all_gather(w_out.astype(BF), "grp", axis=0, tiled=True)
    w_expand = lax.all_gather(w_up.astype(BF), "grp", axis=0, tiled=True)
    w_reduce = lax.all_gather(w_down.astype(BF), "grp", axis=0, tiled=True)

    nb = length // BLK
    in_group = seq_group == grp
    lengths = jnp.where(in_group, seq_len, 0)
    order = jnp.arange(seq_group.shape[0], dtype=jnp.int32)
    offsets = jnp.sum(jnp.where(order[:, None] > order[None, :], lengths[None, :], 0), 1)
    starts = jnp.arange(nb, dtype=jnp.int32) * BLK
    inside = in_group[None] & (starts[:, None] >= offsets[None]) & (starts[:, None] < (offsets + lengths)[None])
    alive = jnp.any(inside, 1)
    first = jnp.sum(jnp.where(inside, (offsets // BLK)[None], 0), 1)
    last = jnp.sum(jnp.where(inside, ((offsets + lengths) // BLK - 1)[None], 0), 1)
    info = jnp.stack([first, last, alive.astype(jnp.int32)]).astype(jnp.int32)
    tokens = jnp.sum(lengths)
    row0 = tp * share
    live = (row0 + jnp.arange(share, dtype=jnp.int32) < tokens).astype(F32)[:, None]
    live_all = (jnp.arange(length, dtype=jnp.int32) < tokens)[:, None]

    def mine(x):
        return lax.dynamic_slice_in_dim(x, row0, share, 0)

    x = layer_input.astype(F32)
    n1 = normalize(x, first_norm_gain, first_norm_bias)[0].astype(BF)
    x_share_b = mine(layer_input)
    x_share = x_share_b.astype(F32)
    _, xhat1, inverse1 = normalize(x_share, first_norm_gain, first_norm_bias)

    head_bias = lax.dynamic_slice_in_dim(b_qv.reshape(-1, 2, HD), tp * heads, heads, 0)
    bias_three = jnp.stack(
        [head_bias[:, 0], jnp.zeros_like(head_bias[:, 0]), head_bias[:, 1]], 1).reshape(-1)
    proj = (jnp.dot(n1, w_attn, preferred_element_type=F32) + bias_three).astype(BF)
    context, lse = attn_fwd(info, proj)
    vec = jnp.stack([b_out, second_norm_gain, second_norm_bias])
    hidden, n2_share = attn_out(context, w_proj, x_share_b, vec, n_tp, 8)
    up_bias = lax.dynamic_slice_in_dim(b_up, tp * hidden_here, hidden_here, 0)[None]
    gradb = jnp.where(live_all, out_cotangent, jnp.zeros_like(out_cotangent))
    gradb_share = mine(gradb)
    grad_share = gradb_share.astype(F32)
    (mlp_parts, gw_expand, gw_reduce, gw_proj, dcontext, dh, stats, up_sum) = feed_forward(
        n2_share, gradb, w_expand, w_reduce, w_proj, up_bias, context, hidden, gradb_share,
        second_norm_gain[None], n_tp, 8)
    dcontext = dcontext.reshape(length, -1)
    scatter = functools.partial(lax.psum_scatter, axis_name="grp", scatter_dimension=0, tiled=True)
    grads_reduce = scatter(gw_reduce).astype(F32)
    grads_expand = scatter(gw_expand).astype(F32)
    grads_proj = scatter(gw_proj).astype(F32)
    mlp = lax.psum_scatter(mlp_parts.reshape(length, width), "tp", scatter_dimension=0, tiled=True).astype(F32)
    result = (live * (hidden + mlp + b_down)).astype(BF)

    dproj = attn_bwd(info, proj, context, dcontext, lse)
    grads_attn = scatter(dg(n1, dproj, 0, 0).astype(BF)).astype(F32)
    dn1 = lax.psum_scatter(dg(dproj, w_attn, 1, 1).astype(BF), "tp", scatter_dimension=0, tiled=True).astype(F32)
    grad_x = dh + norm_back(dn1, xhat1, inverse1, first_norm_gain)

    proj_sums = jnp.sum(dproj.astype(F32), 0).reshape(heads, 3, HD)
    own = jnp.concatenate([jnp.stack([proj_sums[:, 0], proj_sums[:, 2]], 1).reshape(-1),
                           up_sum[0]])
    common = jnp.concatenate([stats[2]] + [jnp.sum(v, 0) for v in (grad_share, dn1 * xhat1, dn1)]
                             + [stats[0], stats[1]])
    sums, owned = small_sum(common, own)
    sums = sums.reshape(6, width)
    qv = heads * 2 * HD
    return (result, grad_x, grads_attn, owned[:, :qv].reshape(-1), grads_proj, sums[0], grads_expand,
            owned[:, qv:].reshape(-1), grads_reduce, sums[1], sums[2], sums[3], sums[4], sums[5])


def solution(mesh):
    rows, both, flat = P("grp", None), P("grp", "tp"), P()
    in_specs = (rows, rows, flat, flat, both, flat, both, flat, both, flat, both, flat, flat, flat, flat, flat)
    spread = P(("grp", "tp"), None)
    out_specs = (spread, spread, both, flat, both, flat, both, flat, both, flat, flat, flat, flat, flat)
    return jax.shard_map(on_device, mesh=mesh, in_specs=in_specs, out_specs=out_specs, check_vma=False)
```

```python
import functools

import jax
import jax.numpy as jnp
from jax import lax
from jax.experimental import pallas as pl
from jax.experimental.pallas import tpu as pltpu
from jax.sharding import PartitionSpec as P

HD = 128
BLK=512
F32=jnp.float32
BF=jnp.bfloat16
LOG2E=1.4426950408889634

def dg(a,b,ca,cb):
    return lax.dot_general(a,b,(((ca,),(cb,)),((),())),preferred_element_type=F32)

def attn_fwd_kernel(info, q_ref, k_ref, v_ref, o_ref, lse_ref, *, nb):
    c = HD ** -0.5 * LOG2E
    for qi in range(nb):
        rows = pl.ds(qi*BLK, BLK)
        @pl.when(info[2, qi] > 0)
        def _():
            q = q_ref[rows, :]
            def step(j, carry, diag=False):
                m, l, acc = carry
                kr = pl.ds(pl.multiple_of(j*BLK, BLK), BLK)
                s = dg(k_ref[kr, :], q, 1, 1)
                if diag:
                    ki = lax.broadcasted_iota(jnp.int32, s.shape, 0)
                    qq = lax.broadcasted_iota(jnp.int32, s.shape, 1)
                    s = jnp.where(ki <= qq, s, -1e30)
                mn = jnp.maximum(m, jnp.max(s, 0, keepdims=True))
                p = jnp.exp2(s*c - mn*c)
                alpha = jnp.exp2((m - mn)*c)
                l = l*alpha + jnp.sum(p, 0, keepdims=True)
                acc = acc*alpha + dg(v_ref[kr, :], p.astype(BF), 0, 0)
                return mn, l, acc
            init = (jnp.full((1, BLK), -1e30, F32), jnp.zeros((1, BLK), F32), jnp.zeros((HD, BLK), F32))
            carry = step(qi, init, True)
            m, l, acc = lax.fori_loop(info[0, qi], qi, step, carry)
            o_ref[rows, :] = jnp.transpose(acc / l).astype(BF)
            lse_ref[0, :, rows] = m*c + jnp.log2(l)
        @pl.when(info[2, qi] <= 0)
        def _():
            o_ref[rows, :] = jnp.zeros((BLK, HD), BF)
            lse_ref[0, :, rows] = jnp.zeros((1, BLK), F32)

def attn_fwd(info, proj):
    length = proj.shape[0]; heads = proj.shape[1]//(3*HD); nb = length//BLK
    spec = lambda o: pl.BlockSpec((length, HD), lambda h, info: (0, 3*h+o))
    return pl.pallas_call(functools.partial(attn_fwd_kernel, nb=nb),
        grid_spec=pltpu.PrefetchScalarGridSpec(num_scalar_prefetch=1, grid=(heads,),
            in_specs=[spec(0), spec(1), spec(2)],
            out_specs=[pl.BlockSpec((length, HD), lambda h, info: (0, h)), pl.BlockSpec((1, 1, length), lambda h, info: (h, 0, 0))]),
        out_shape=[jax.ShapeDtypeStruct((length, heads*HD), BF), jax.ShapeDtypeStruct((heads, 1, length), F32)],
        compiler_params=pltpu.CompilerParams(vmem_limit_bytes=40<<20), name="attn_fwd",
        cost_estimate=pl.CostEstimate(flops=heads*length*length*HD*2, bytes_accessed=length*heads*HD*8, transcendentals=heads*length*length//2),
    )(info, proj, proj, proj)

def attn_bwd_kernel(info, q_ref, k_ref, v_ref, o_ref, do_ref, lse_ref, dp_ref, dq_sc, dl_sc, *, nb):
    sc = HD ** -0.5
    c = sc * LOG2E
    prod = do_ref[...].astype(F32) * o_ref[...].astype(F32)
    dl_sc[...] = jnp.sum(jnp.transpose(prod), 0, keepdims=True)
    dq_sc[...] = jnp.zeros_like(dq_sc)
    for j in range(nb):
        kr = pl.ds(j*BLK, BLK)
        @pl.when(info[2, j] > 0)
        def _():
            k = k_ref[kr, :]; v = v_ref[kr, :]
            def step(i, carry, diag=False):
                dk, dv = carry
                qr = pl.ds(pl.multiple_of(i*BLK, BLK), BLK)
                q = q_ref[qr, :]; do = do_ref[qr, :]
                s = dg(k, q, 1, 1)
                p = jnp.exp2(s*c - lse_ref[0, :, qr])
                if diag:
                    ki = lax.broadcasted_iota(jnp.int32, s.shape, 0)
                    qq = lax.broadcasted_iota(jnp.int32, s.shape, 1)
                    p = jnp.where(ki <= qq, p, 0.0)
                dp = dg(v, do, 1, 1)
                ds = (p * (dp - dl_sc[:, qr])).astype(BF)
                dv = dv + dg(p.astype(BF), do, 1, 0)
                dk = dk + dg(ds, q, 1, 0)
                dq_sc[qr, :] += dg(ds, k, 0, 0)
                return dk, dv
            z = jnp.zeros((BLK, HD), F32)
            carry = step(j, (z, z), True)
            dk, dv = lax.fori_loop(j+1, info[1, j]+1, step, carry)
            dp_ref[kr, HD:2*HD] = (dk*sc).astype(BF)
            dp_ref[kr, 2*HD:] = dv.astype(BF)
        @pl.when(info[2, j] <= 0)
        def _():
            dp_ref[kr, HD:] = jnp.zeros((BLK, 2*HD), BF)
    dp_ref[:, :HD] = (dq_sc[...]*sc).astype(BF)

def attn_bwd(info, proj, ctx, dctx, lse):
    length = proj.shape[0]; heads = proj.shape[1]//(3*HD); nb = length//BLK
    spec = lambda o: pl.BlockSpec((length, HD), lambda h, info: (0, 3*h+o))
    hs = pl.BlockSpec((length, HD), lambda h, info: (0, h))
    return pl.pallas_call(functools.partial(attn_bwd_kernel, nb=nb),
        grid_spec=pltpu.PrefetchScalarGridSpec(num_scalar_prefetch=1, grid=(heads,),
            in_specs=[spec(0), spec(1), spec(2), hs, hs, pl.BlockSpec((1, 1, length), lambda h, info: (h, 0, 0))],
            out_specs=pl.BlockSpec((length, 3*HD), lambda h, info: (0, h)),
            scratch_shapes=[pltpu.VMEM((length, HD), F32), pltpu.VMEM((1, length), F32)]),
        out_shape=jax.ShapeDtypeStruct((length, heads*3*HD), BF),
        compiler_params=pltpu.CompilerParams(vmem_limit_bytes=40<<20), name="attn_bwd",
        cost_estimate=pl.CostEstimate(flops=heads*length*length*HD*5, bytes_accessed=length*heads*HD*16, transcendentals=heads*length*length//2),
    )(info, proj, proj, proj, ctx, dctx, lse)


MESH = pl.DeviceIdType.MESH
TILE = 256


class Place:
    def __init__(self, n_tp):
        self.g = lax.axis_index("grp")
        t = lax.axis_index("tp")
        self.t, self.n, self.Z = t, n_tp, n_tp // 2
        self.z, self.k = t // 2, lax.rem(t, 2)
        self.right, self.left, self.sib = (self.g, t + 2), (self.g, t - 2), (self.g, t + 1 - 2 * self.k)
        self.has_right, self.has_left = self.z < self.Z - 1, self.z > 0

    def barrier(self):
        bar = pltpu.get_barrier_semaphore()
        pl.semaphore_signal(bar, inc=1, device_id=self.sib, device_id_type=MESH)

        @pl.when(self.has_right)
        def _():
            pl.semaphore_signal(bar, inc=1, device_id=self.right, device_id_type=MESH)

        @pl.when(self.has_left)
        def _():
            pl.semaphore_signal(bar, inc=1, device_id=self.left, device_id_type=MESH)

        amount = 1 + jnp.where(self.has_right, 1, 0) + jnp.where(self.has_left, 1, 0)
        pl.semaphore_wait(bar, amount)


def remote(src, dst, ssem, rsem, device):
    return pltpu.make_async_remote_copy(src, dst, ssem, rsem, device_id=device, device_id_type=MESH)


class Gather:
    def __init__(self, at, gat, rows, ls, lr, ss, sr):
        self.at, self.gat, self.rows = at, gat, rows
        self.ls, self.lr, self.ss, self.sr = ls, lr, ss, sr

    def block(self, zz, kk, c):
        return self.gat.at[2 * zz + kk, pl.ds(pl.multiple_of(c * self.rows, self.rows), self.rows), :]

    def line(self, c, side, d):
        at = self.at
        sign, device = (-1, at.right) if side == 0 else (1, at.left)
        b = self.block(at.z + sign * (d - 1), at.k, c)
        return remote(b, b, self.ls.at[c, side, d - 1], self.lr.at[c, side, d - 1], device)

    def line_in(self, c, side, d):
        at = self.at
        sign, device = (-1, at.right) if side == 0 else (1, at.left)
        b = self.block(at.z + sign * d, at.k, c)
        return remote(b, b, self.ls.at[c, side, d - 1], self.lr.at[c, side, d - 1], device)

    def across(self, c, zz):
        b = self.block(zz, self.at.k, c)
        return remote(b, b, self.ss.at[c, zz], self.sr.at[c, zz], self.at.sib)

    def across_in(self, c, zz):
        b = self.block(zz, 1 - self.at.k, c)
        return remote(b, b, self.ss.at[c, zz], self.sr.at[c, zz], self.at.sib)

    def start(self, c):
        at = self.at

        @pl.when(at.has_right)
        def _():
            self.line(c, 0, 1).start()

        @pl.when(at.has_left)
        def _():
            self.line(c, 1, 1).start()

        self.across(c, at.z).start()

    def hop(self, c, d):
        at = self.at

        @pl.when(at.z >= d)
        def _():
            self.line_in(c, 0, d).wait_recv()
            if d < at.Z - 1:
                @pl.when(at.has_right)
                def _():
                    self.line(c, 0, d + 1).start()
            self.across(c, at.z - d).start()

        @pl.when(at.z + d <= at.Z - 1)
        def _():
            self.line_in(c, 1, d).wait_recv()
            if d < at.Z - 1:
                @pl.when(at.has_left)
                def _():
                    self.line(c, 1, d + 1).start()
            self.across(c, at.z + d).start()

    def finish(self, c):
        at = self.at
        for zz in range(at.Z):
            self.across_in(c, zz).wait_recv()
            self.across(c, zz).wait_send()
        for d in range(1, at.Z):
            @pl.when(at.has_right & (at.z >= d - 1))
            def _():
                self.line(c, 0, d).wait_send()

            @pl.when(at.has_left & (at.z + d - 1 <= at.Z - 1))
            def _():
                self.line(c, 1, d).wait_send()


class Scatter:
    def __init__(self, at, parts, pair, hops, cs, cr, hs, hr):
        self.at, self.parts, self.pair, self.hops = at, parts, pair, hops
        self.slots = pair.shape[0]
        self.cs, self.cr, self.hs, self.hr = cs, cr, hs, hr

    def across(self, c):
        c = lax.rem(c, self.slots)
        return remote(self.parts.at[:, 1 - self.at.k], self.pair.at[c], self.cs.at[c], self.cr.at[c], self.at.sib)

    def line(self, c, side, h, target):
        c = lax.rem(c, self.slots)
        device = self.at.right if side == 0 else self.at.left
        return remote(self.pair.at[c, target], self.hops.at[side, c, h - 1],
                      self.hs.at[c, side, h - 1], self.hr.at[c, side, h - 1], device)

    def start(self, c):
        self.across(c).start()

    def meet(self, c):
        self.across(c).wait()
        own = self.parts[:, pl.ds(self.at.k, 1)]
        own = own.reshape(own.shape[0], own.shape[2], own.shape[3])
        c = lax.rem(c, self.slots)
        self.pair[c] = (self.pair[c].astype(F32) + own.astype(F32)).astype(BF)

    def hop(self, c, h):
        at = self.at
        for side in (0, 1):
            pos = at.z if side == 0 else at.Z - 1 - at.z
            target = at.z + at.Z - h if side == 0 else at.z - at.Z + h

            @pl.when((pos <= h - 1) & (pos < at.Z - 1))
            def _():
                if h >= 2:
                    @pl.when(pos >= 1)
                    def _():
                        self.line(c, side, h - 1, target).wait_recv()
                        b = lax.rem(c, self.slots)
                        self.pair[b, target] = (self.pair[b, target].astype(F32)
                                                + self.hops[side, b, h - 2].astype(F32)).astype(BF)
                self.line(c, side, h, target).start()

    def finish(self, c, total):
        at = self.at
        b = lax.rem(c, self.slots)
        total[...] = self.pair[b, at.z].astype(F32)
        for side in (0, 1):
            pos = at.z if side == 0 else at.Z - 1 - at.z

            @pl.when(pos >= 1)
            def _():
                self.line(c, side, at.Z - 1, at.z).wait_recv()
                total[...] += self.hops[side, b, at.Z - 2].astype(F32)

            for h in range(1, at.Z):
                @pl.when((pos <= h - 1) & (pos < at.Z - 1))
                def _():
                    self.line(c, side, h, at.z).wait_send()


def gather_sems(chunks, Z):
    dma = pltpu.SemaphoreType.DMA
    return [dma((chunks, 2, Z - 1)), dma((chunks, 2, Z - 1)), dma((chunks, Z)), dma((chunks, Z))]


def scatter_scratch(chunks, Z, rows, width):
    chunks = min(chunks, 4)
    dma = pltpu.SemaphoreType.DMA
    return [pltpu.VMEM((Z, 2, rows, width), BF), pltpu.VMEM((chunks, Z, rows, width), BF),
            pltpu.VMEM((2, chunks, Z - 1, rows, width), BF),
            dma((chunks,)), dma((chunks,)), dma((chunks, 2, Z - 1)), dma((chunks, 2, Z - 1))]


def inside(c, chunks):
    return (c >= 0) & (c < chunks)


def chunk_rows(c, rows):
    return pl.ds(pl.multiple_of(c * rows, rows), rows)


def tiles(count, body):
    def step(i, carry):
        body(i)
        return carry
    lax.fori_loop(0, count, step, 0)


def cols(i, size=TILE):
    return pl.ds(pl.multiple_of(i * size, size), size)


def rows_stats(rows):
    mean = jnp.mean(rows, -1, keepdims=True)
    centred = rows - mean
    inverse = lax.rsqrt(jnp.mean(centred * centred, -1, keepdims=True) + 1e-05)
    return centred * inverse, inverse


def product_scatter(at, rs, lhs_ref, w_ref, total, chunks, rows, epilogue):
    def product(c):
        lhs = lhs_ref[:, chunk_rows(c, rows), :].reshape(at.n * rows, lhs_ref.shape[2])

        def tile(i):
            y = dg(lhs, w_ref[cols(i), :], 1, 1)
            rs.parts[:, :, :, cols(i)] = y.astype(BF).reshape(at.Z, 2, rows, TILE)
        tiles(w_ref.shape[0] // TILE, tile)
        rs.start(c)

    def tick(i, carry):
        c = i - 1

        @pl.when(inside(c, chunks))
        def _():
            rs.meet(c)
            rs.hop(c, 1)

        @pl.when(inside(i, chunks))
        def _():
            product(i)

        @pl.when(inside(c, chunks))
        def _():
            for h in range(2, at.Z):
                rs.hop(c, h)

        e = i - 2

        @pl.when(inside(e, chunks))
        def _():
            rs.finish(e, total)
            epilogue(e)
        return carry

    lax.fori_loop(0, chunks + 2, tick, 0)


def out_kernel(ctx, w_out, x_share, vec, hidden, n2, total, *sc, n, chunks, rows):
    at = Place(n)
    at.barrier()

    def epilogue(c):
        r = chunk_rows(c, rows)
        h = x_share[r, :].astype(F32) + total[...] + vec[0:1, :]
        hidden[r, :] = h
        n2[r, :] = (rows_stats(h)[0] * vec[1:2, :] + vec[2:3, :]).astype(BF)

    product_scatter(at, Scatter(at, *sc), ctx, w_out, total, chunks, rows, epilogue)


def back_kernel(dproj, w_attn, dn1, total, *sc, n, chunks, rows):
    at = Place(n)
    at.barrier()

    def epilogue(c):
        dn1[chunk_rows(c, rows), :] = total[...]

    product_scatter(at, Scatter(at, *sc), dproj, w_attn, total, chunks, rows, epilogue)


def project_back(dproj, w_attn, n, chunks):
    length, hw = dproj.shape
    width = w_attn.shape[0]
    share = length // n
    rows = share // chunks
    vm = pl.BlockSpec(memory_space=pltpu.VMEM)
    return pl.pallas_call(
        functools.partial(back_kernel, n=n, chunks=chunks, rows=rows),
        in_specs=[vm] * 2, out_specs=vm, out_shape=jax.ShapeDtypeStruct((share, width), F32),
        scratch_shapes=[pltpu.VMEM((rows, width), F32)] + scatter_scratch(chunks, n // 2, rows, width),
        compiler_params=pltpu.CompilerParams(collective_id=4, has_side_effects=True, vmem_limit_bytes=40 << 20),
        cost_estimate=pl.CostEstimate(flops=2 * length * hw * width, bytes_accessed=1 << 23, transcendentals=0),
        name="project_back",
    )(dproj.reshape(n, share, hw), w_attn)


def attn_out(ctx, w_out, x_share, vec, n, chunks):
    length, hw = ctx.shape
    share, width = x_share.shape
    rows = share // chunks
    vm = pl.BlockSpec(memory_space=pltpu.VMEM)
    return pl.pallas_call(
        functools.partial(out_kernel, n=n, chunks=chunks, rows=rows),
        in_specs=[vm] * 4, out_specs=[vm] * 2,
        out_shape=[jax.ShapeDtypeStruct((share, width), F32), jax.ShapeDtypeStruct((share, width), BF)],
        scratch_shapes=[pltpu.VMEM((rows, width), F32)] + scatter_scratch(chunks, n // 2, rows, width),
        compiler_params=pltpu.CompilerParams(collective_id=2, has_side_effects=True, vmem_limit_bytes=40 << 20),
        cost_estimate=pl.CostEstimate(flops=2 * length * hw * width, bytes_accessed=1 << 23, transcendentals=0),
        name="attn_out",
    )(ctx.reshape(n, share, hw), w_out, x_share, vec)


def ffn_kernel(n2_hbm, gradb_hbm, w_up, w_down, w_out, b_up, ctx, hidden, gshare, vec, live,
               gw_hbm, gwo, dctx, dh, res, stats, bsum,
               gat, acc_up, acc_down, gbuf, actb, dbb, total, lsem, gsem, msem, *scratch, n, chunks, rows):
    at = Place(n)
    ag1, ag2 = Gather(at, gat, rows, *scratch[:4]), Gather(at, gat, rows, *scratch[4:8])
    rs, mlp = Scatter(at, *scratch[8:15]), Scatter(at, *scratch[15:])
    width, hid = w_up.shape
    m = n * rows

    load = pltpu.make_async_copy(n2_hbm, gat.at[at.t], lsem)
    load.start()

    def fetch(c):
        slot = lax.rem(c, 2)
        return pltpu.make_async_copy(gradb_hbm.at[:, chunk_rows(c, rows), :], gbuf.at[slot], gsem.at[slot])

    fetch(0).start()
    acc_up[...] = jnp.zeros_like(acc_up)
    acc_down[...] = jnp.zeros_like(acc_down)
    stats[...] = jnp.zeros_like(stats)
    bsum[...] = jnp.zeros_like(bsum)
    load.wait()
    at.barrier()

    a0, a1 = 0.7978845608028654, 0.044715

    def wide(c):
        return gat[:, chunk_rows(c, rows), :].reshape(m, width)

    def forward(c):
        fetch(c).wait()

        @pl.when(c + 1 < chunks)
        def _():
            fetch(c + 1).start()
        slot = lax.rem(c, 2)

        def tile(i):
            v = dg(wide(c), w_up[:, cols(i)], 1, 0) + b_up[:, cols(i)]
            ga = dg(gbuf[slot].reshape(m, width), w_down[:, cols(i)], 1, 0)
            v2 = v * v
            th = jnp.tanh(a0 * (v + a1 * v2 * v))
            half = 0.5 * (1.0 + th)
            actb[:, cols(i)] = (v * half).astype(BF)
            slope = half + 0.5 * v * (1.0 - th * th) * (a0 * (1.0 + 3.0 * a1 * v2))
            db = (ga * slope).astype(BF)
            dbb[:, cols(i)] = db
            bsum[:, cols(i)] += jnp.sum(db.astype(F32), 0, keepdims=True)
        tiles(hid // TILE, tile)

    def back(c):
        def tile(i):
            y = dg(dbb[...], w_up[cols(i), :], 1, 1)
            rs.parts[:, :, :, cols(i)] = y.astype(BF).reshape(at.Z, 2, rows, TILE)
        tiles(width // TILE, tile)

    def down(c):
        def tile(i):
            y = dg(actb[...], w_down[cols(i), :], 1, 1)
            mlp.parts[:, :, :, cols(i)] = y.astype(BF).reshape(at.Z, 2, rows, TILE)
        tiles(width // TILE, tile)

    def weights(c):
        slot = lax.rem(c, 2)

        def tile(i):
            x = gat[:, chunk_rows(c, rows), cols(i)].reshape(m, TILE)
            acc_up[cols(i), :] += dg(x, dbb[...], 0, 0)
            y = gbuf[slot, :, :, cols(i)].reshape(m, TILE)
            acc_down[cols(i), :] += dg(y, actb[...], 0, 0)
        tiles(width // TILE, tile)

    def norm_grad(c):
        r = chunk_rows(c, rows)
        xhat, inverse = rows_stats(hidden[r, :])
        dn2 = total[...]
        e = dn2 * vec[0:1, :]
        inner = jnp.mean(e, -1, keepdims=True) + xhat * jnp.mean(e * xhat, -1, keepdims=True)
        d = gshare[r, :].astype(F32) + inverse * (e - inner)
        dh[r, :] = d
        gat[at.t, r, :] = d.astype(BF)
        stats[0:1, :] += jnp.sum(dn2 * xhat, 0, keepdims=True)
        stats[1:2, :] += jnp.sum(dn2, 0, keepdims=True)
        stats[2:3, :] += jnp.sum(d, 0, keepdims=True)

    def heads(c):
        y = dg(wide(c), w_out[...], 1, 0)
        dctx[:, chunk_rows(c, rows), :] = y.astype(BF).reshape(n, rows, y.shape[1])

    def at_stage(c, fn):
        @pl.when(inside(c, chunks))
        def _():
            fn(c)

    def tick(i, carry):
        at_stage(i, ag1.start)
        at_stage(i - 3, rs.meet)
        for h in range(1, at.Z):
            at_stage(i - 3, lambda c: rs.hop(c, h))
            at_stage(i - 1, lambda c: ag1.hop(c, h))
            if h == 1:
                at_stage(i - 4, lambda c: mlp.hop(c, at.Z - 1))
                at_stage(i - 5, lambda c: ag2.hop(c, at.Z - 1))
                at_stage(i - 2, forward)
            else:
                if h == 2:
                    def served(c):
                        mlp.finish(c, total)
                        r = chunk_rows(c, rows)
                        res[r, :] = (live[r, :] * (hidden[r, :] + total[...] + vec[1:2, :])).astype(BF)
                    at_stage(i - 4, served)
                    at_stage(i - 3, mlp.meet)
                at_stage(i - 3, lambda c: mlp.hop(c, h - 1))
                at_stage(i - 4, lambda c: ag2.hop(c, h - 1))
                if h == 2:
                    at_stage(i - 2, back)

                    def gathered(c):
                        ag2.finish(c)
                        heads(c)
                    at_stage(i - 5, gathered)

        def rest(c):
            weights(c)
            rs.start(c)
        at_stage(i - 2, rest)

        def reduced(c):
            rs.finish(c, total)
            norm_grad(c)
            ag2.start(c)
        at_stage(i - 3, reduced)
        at_stage(i - 1, ag1.finish)

        def send_mlp(c):
            down(c)
            mlp.start(c)
        at_stage(i - 2, send_mlp)

        @pl.when(i == chunks + 2)
        def _():
            tiles(width // m, store)
        return carry

    def store(i):
        r = cols(i, m)
        actb[...] = acc_up[r, :].astype(BF)
        one = pltpu.make_async_copy(actb, gw_hbm.at[r, pl.ds(0, hid)], lsem)
        one.start()
        dbb[...] = acc_down[r, :].astype(BF)
        two = pltpu.make_async_copy(dbb, gw_hbm.at[r, pl.ds(hid, hid)], msem)
        two.start()
        one.wait()
        two.wait()

    lax.fori_loop(0, chunks + 5, tick, 0)

    def final(i):
        x = gat[:, :, cols(i)].reshape(-1, TILE)
        gwo[cols(i), :] = dg(x, ctx[...], 0, 0).astype(BF)
    tiles(width // TILE, final)


def feed_forward(n2, gradb, w_up, w_down, w_out, b_up, ctx, hidden, gshare, vec, live, n, chunks):
    length, width = gradb.shape
    hid, hw = w_up.shape[1], w_out.shape[1]
    share = length // n
    rows = share // chunks
    Z = n // 2
    vm, hbm = pl.BlockSpec(memory_space=pltpu.VMEM), pl.BlockSpec(memory_space=pl.ANY)
    S = jax.ShapeDtypeStruct
    m = n * rows
    return pl.pallas_call(
        functools.partial(ffn_kernel, n=n, chunks=chunks, rows=rows),
        in_specs=[hbm, hbm] + [vm] * 9,
        out_specs=[hbm] + [vm] * 6,
        out_shape=[S((width, 2 * hid), BF), S((width, hw), BF), S((n, share, hw), BF), S((share, width), F32),
                   S((share, width), BF), S((8, width), F32), S((1, hid), F32)],
        scratch_shapes=[pltpu.VMEM((n, share, width), BF), pltpu.VMEM((width, hid), F32), pltpu.VMEM((width, hid), F32),
                        pltpu.VMEM((2, n, rows, width), BF),
                        pltpu.VMEM((m, hid), BF), pltpu.VMEM((m, hid), BF), pltpu.VMEM((rows, width), F32),
                        pltpu.SemaphoreType.DMA, pltpu.SemaphoreType.DMA((2,)), pltpu.SemaphoreType.DMA]
                       + gather_sems(chunks, Z) + gather_sems(chunks, Z) + scatter_scratch(chunks, Z, rows, width) * 2,
        compiler_params=pltpu.CompilerParams(collective_id=3, has_side_effects=True, vmem_limit_bytes=62 << 20),
        cost_estimate=pl.CostEstimate(flops=12 * length * hid * width, bytes_accessed=1 << 26, transcendentals=0),
        name="feed_forward",
    )(n2, gradb.reshape(n, share, width), w_up, w_down, w_out, b_up, ctx, hidden, gshare, vec, live)


def small_kernel(x_ref, a_ref, b_ref, gbuf, tbuf, gs, gr, ts, tr, *, n_grp, n_tp, a_rows):
    t = lax.axis_index("tp")
    g = lax.axis_index("grp")
    bar = pltpu.get_barrier_semaphore()
    for d in range(1, n_grp):
        pl.semaphore_signal(bar, inc=1, device_id=(lax.rem(g + d, n_grp), t), device_id_type=MESH)
    for d in range(1, n_tp):
        pl.semaphore_signal(bar, inc=1, device_id=(g, lax.rem(t + d, n_tp)), device_id_type=MESH)
    pl.semaphore_wait(bar, n_grp + n_tp - 2)
    copies = []
    for d in range(1, n_grp):
        cp = pltpu.make_async_remote_copy(
            x_ref, gbuf.at[g], gs.at[d], gr.at[d],
            device_id=(lax.rem(g + d, n_grp), t), device_id_type=MESH)
        cp.start()
        copies.append(cp)
    gbuf[g] = x_ref[...]
    for cp in copies:
        cp.wait()
    total = gbuf[0]
    for i in range(1, n_grp):
        total = total + gbuf[i]
    tbuf[t] = total
    copies = []
    for d in range(1, n_tp):
        cp = pltpu.make_async_remote_copy(
            tbuf.at[t], tbuf.at[t], ts.at[d], tr.at[d],
            device_id=(g, lax.rem(t + d, n_tp)), device_id_type=MESH)
        cp.start()
        copies.append(cp)
    for cp in copies:
        cp.wait()
    total = tbuf[0, :a_rows]
    for i in range(1, n_tp):
        total = total + tbuf[i, :a_rows]
    a_ref[...] = total
    b_ref[...] = tbuf[:, a_rows:]


def small_sum(common, own):
    n_grp, n_tp = lax.axis_size("grp"), lax.axis_size("tp")
    a_rows = common.shape[0] // 128
    own_rows = own.shape[0] // 128
    pad = -own_rows % 8
    x = jnp.concatenate([common, own, jnp.zeros((pad * 128,), F32)]).reshape(-1, 128)
    rows = x.shape[0]
    vm = pl.BlockSpec(memory_space=pltpu.VMEM)
    a, b = pl.pallas_call(
        functools.partial(small_kernel, n_grp=n_grp, n_tp=n_tp, a_rows=a_rows),
        in_specs=[vm], out_specs=[vm, vm],
        out_shape=[jax.ShapeDtypeStruct((a_rows, 128), F32),
                   jax.ShapeDtypeStruct((n_tp, rows - a_rows, 128), F32)],
        scratch_shapes=[pltpu.VMEM((n_grp, rows, 128), F32), pltpu.VMEM((n_tp, rows, 128), F32),
                        pltpu.SemaphoreType.DMA((n_grp,)), pltpu.SemaphoreType.DMA((n_grp,)),
                        pltpu.SemaphoreType.DMA((n_tp,)), pltpu.SemaphoreType.DMA((n_tp,))],
        compiler_params=pltpu.CompilerParams(collective_id=1, has_side_effects=True),
        name="small_sum",
    )(x)
    return a.reshape(-1), b.reshape(n_tp, -1)[:, : own.shape[0]]


def normalize(rows, gain, bias):
    mean_row = jnp.mean(rows, -1, keepdims=True)
    centred = rows - mean_row
    inverse = lax.rsqrt(jnp.mean(centred * centred, -1, keepdims=True) + 1e-05)
    normed = centred * inverse
    return normed * gain + bias, normed, inverse


def norm_back(grad_norm, normed, inverse, gain):
    scaled = grad_norm * gain
    inner = jnp.mean(scaled, -1, keepdims=True) + normed * jnp.mean(scaled * normed, -1, keepdims=True)
    return inverse * (scaled - inner)


def on_device(layer_input, out_cotangent, seq_group, seq_len, w_qkv, b_qv, w_out, b_out, w_up, b_up,
              w_down, b_down, first_norm_gain, first_norm_bias, second_norm_gain, second_norm_bias):
    tp = lax.axis_index("tp")
    n_tp = lax.axis_size("tp")
    grp = lax.axis_index("grp")
    length, width = layer_input.shape
    share = length // n_tp
    heads = w_out.shape[1] // HD
    hidden_here = w_up.shape[1]

    w_attn = lax.all_gather(w_qkv.astype(BF), "grp", axis=0, tiled=True)
    w_proj = lax.all_gather(w_out.astype(BF), "grp", axis=0, tiled=True)
    w_expand = lax.all_gather(w_up.astype(BF), "grp", axis=0, tiled=True)
    w_reduce = lax.all_gather(w_down.astype(BF), "grp", axis=0, tiled=True)

    nb = length // BLK
    in_group = seq_group == grp
    lengths = jnp.where(in_group, seq_len, 0)
    order = jnp.arange(seq_group.shape[0], dtype=jnp.int32)
    offsets = jnp.sum(jnp.where(order[:, None] > order[None, :], lengths[None, :], 0), 1)
    starts = jnp.arange(nb, dtype=jnp.int32) * BLK
    inside = in_group[None] & (starts[:, None] >= offsets[None]) & (starts[:, None] < (offsets + lengths)[None])
    alive = jnp.any(inside, 1)
    first = jnp.sum(jnp.where(inside, (offsets // BLK)[None], 0), 1)
    last = jnp.sum(jnp.where(inside, ((offsets + lengths) // BLK - 1)[None], 0), 1)
    info = jnp.stack([first, last, alive.astype(jnp.int32)]).astype(jnp.int32)
    tokens = jnp.sum(lengths)
    row0 = tp * share
    live = (row0 + jnp.arange(share, dtype=jnp.int32) < tokens).astype(F32)[:, None]
    live_all = (jnp.arange(length, dtype=jnp.int32) < tokens)[:, None]

    def mine(x):
        return lax.dynamic_slice_in_dim(x, row0, share, 0)

    x = layer_input.astype(F32)
    n1 = normalize(x, first_norm_gain, first_norm_bias)[0].astype(BF)
    x_share_b = mine(layer_input)
    x_share = x_share_b.astype(F32)
    _, xhat1, inverse1 = normalize(x_share, first_norm_gain, first_norm_bias)

    head_bias = lax.dynamic_slice_in_dim(b_qv.reshape(-1, 2, HD), tp * heads, heads, 0)
    bias_three = jnp.stack(
        [head_bias[:, 0], jnp.zeros_like(head_bias[:, 0]), head_bias[:, 1]], 1).reshape(-1)
    proj = (jnp.dot(n1, w_attn, preferred_element_type=F32) + bias_three).astype(BF)
    context, lse = attn_fwd(info, proj)
    vec = jnp.stack([b_out, second_norm_gain, second_norm_bias])
    hidden, n2_share = attn_out(context, w_proj, x_share_b, vec, n_tp, 8)
    up_bias = lax.dynamic_slice_in_dim(b_up, tp * hidden_here, hidden_here, 0)[None]
    gradb = jnp.where(live_all, out_cotangent, jnp.zeros_like(out_cotangent))
    gradb_share = mine(gradb)
    grad_share = gradb_share.astype(F32)
    gw_ffn, gw_proj, dcontext, dh, result, stats, up_sum = feed_forward(
        n2_share, gradb, w_expand, w_reduce, w_proj, up_bias, context, hidden, gradb_share,
        jnp.stack([second_norm_gain, b_down]), live, n_tp, 8)
    dcontext = dcontext.reshape(length, -1)
    scatter = functools.partial(lax.psum_scatter, axis_name="grp", scatter_dimension=0, tiled=True)
    grads_ffn = scatter(gw_ffn).astype(F32)
    grads_expand, grads_reduce = grads_ffn[:, :hidden_here], grads_ffn[:, hidden_here:]

    dproj = attn_bwd(info, proj, context, dcontext, lse)
    gw_attn = dg(n1, dproj, 0, 0).astype(BF)
    grads_late = scatter(jnp.concatenate([gw_attn, gw_proj], 1)).astype(F32)
    grads_attn, grads_proj = grads_late[:, :gw_attn.shape[1]], grads_late[:, gw_attn.shape[1]:]
    dn1 = project_back(dproj, w_attn, n_tp, 8)
    grad_x = dh + norm_back(dn1, xhat1, inverse1, first_norm_gain)

    proj_sums = jnp.sum(dproj.astype(F32), 0).reshape(heads, 3, HD)
    own = jnp.concatenate([jnp.stack([proj_sums[:, 0], proj_sums[:, 2]], 1).reshape(-1),
                           up_sum[0]])
    common = jnp.concatenate([stats[2]] + [jnp.sum(v, 0) for v in (grad_share, dn1 * xhat1, dn1)]
                             + [stats[0], stats[1]])
    sums, owned = small_sum(common, own)
    sums = sums.reshape(6, width)
    qv = heads * 2 * HD
    return (result, grad_x, grads_attn, owned[:, :qv].reshape(-1), grads_proj, sums[0], grads_expand,
            owned[:, qv:].reshape(-1), grads_reduce, sums[1], sums[2], sums[3], sums[4], sums[5])


def solution(mesh):
    rows, both, flat = P("grp", None), P("grp", "tp"), P()
    in_specs = (rows, rows, flat, flat, both, flat, both, flat, both, flat, both, flat, flat, flat, flat, flat)
    spread = P(("grp", "tp"), None)
    out_specs = (spread, spread, both, flat, both, flat, both, flat, both, flat, flat, flat, flat, flat)
    return jax.shard_map(on_device, mesh=mesh, in_specs=in_specs, out_specs=out_specs, check_vma=False)
```

```python
import functools

import jax
import jax.numpy as jnp
from jax import lax
from jax.experimental import pallas as pl
from jax.experimental.pallas import tpu as pltpu
from jax.sharding import PartitionSpec as P

HD = 128
BLK=512
F32=jnp.float32
BF=jnp.bfloat16
LOG2E=1.4426950408889634

def dg(a,b,ca,cb):
    return lax.dot_general(a,b,(((ca,),(cb,)),((),())),preferred_element_type=F32)

def attn_fwd_kernel(info, q_ref, k_ref, v_ref, o_ref, lse_ref, *, nb):
    c = HD ** -0.5 * LOG2E
    for qi in range(nb):
        rows = pl.ds(qi*BLK, BLK)
        @pl.when(info[2, qi] > 0)
        def _():
            q = q_ref[rows, :]
            def step(j, carry, diag=False):
                m, l, acc = carry
                kr = pl.ds(pl.multiple_of(j*BLK, BLK), BLK)
                s = dg(k_ref[kr, :], q, 1, 1)
                if diag:
                    ki = lax.broadcasted_iota(jnp.int32, s.shape, 0)
                    qq = lax.broadcasted_iota(jnp.int32, s.shape, 1)
                    s = jnp.where(ki <= qq, s, -1e30)
                mn = jnp.maximum(m, jnp.max(s, 0, keepdims=True))
                p = jnp.exp2(s*c - mn*c)
                alpha = jnp.exp2((m - mn)*c)
                l = l*alpha + jnp.sum(p, 0, keepdims=True)
                acc = acc*alpha + dg(v_ref[kr, :], p.astype(BF), 0, 0)
                return mn, l, acc
            init = (jnp.full((1, BLK), -1e30, F32), jnp.zeros((1, BLK), F32), jnp.zeros((HD, BLK), F32))
            carry = step(qi, init, True)
            m, l, acc = lax.fori_loop(info[0, qi], qi, step, carry)
            o_ref[rows, :] = jnp.transpose(acc / l).astype(BF)
            lse_ref[0, :, rows] = m*c + jnp.log2(l)
        @pl.when(info[2, qi] <= 0)
        def _():
            o_ref[rows, :] = jnp.zeros((BLK, HD), BF)
            lse_ref[0, :, rows] = jnp.zeros((1, BLK), F32)

def attn_fwd(info, proj):
    length = proj.shape[0]; heads = proj.shape[1]//(3*HD); nb = length//BLK
    spec = lambda o: pl.BlockSpec((length, HD), lambda h, info: (0, 3*h+o))
    return pl.pallas_call(functools.partial(attn_fwd_kernel, nb=nb),
        grid_spec=pltpu.PrefetchScalarGridSpec(num_scalar_prefetch=1, grid=(heads,),
            in_specs=[spec(0), spec(1), spec(2)],
            out_specs=[pl.BlockSpec((length, HD), lambda h, info: (0, h)), pl.BlockSpec((1, 1, length), lambda h, info: (h, 0, 0))]),
        out_shape=[jax.ShapeDtypeStruct((length, heads*HD), BF), jax.ShapeDtypeStruct((heads, 1, length), F32)],
        compiler_params=pltpu.CompilerParams(vmem_limit_bytes=40<<20), name="attn_fwd",
        cost_estimate=pl.CostEstimate(flops=heads*length*length*HD*2, bytes_accessed=length*heads*HD*8, transcendentals=heads*length*length//2),
    )(info, proj, proj, proj)

def attn_bwd_kernel(info, q_ref, k_ref, v_ref, o_ref, do_ref, lse_ref, dp_ref, dq_sc, dl_sc, *, nb):
    sc = HD ** -0.5
    c = sc * LOG2E
    prod = do_ref[...].astype(F32) * o_ref[...].astype(F32)
    dl_sc[...] = jnp.sum(jnp.transpose(prod), 0, keepdims=True)
    dq_sc[...] = jnp.zeros_like(dq_sc)
    for j in range(nb):
        kr = pl.ds(j*BLK, BLK)
        @pl.when(info[2, j] > 0)
        def _():
            k = k_ref[kr, :]; v = v_ref[kr, :]
            def step(i, carry, diag=False):
                dk, dv = carry
                qr = pl.ds(pl.multiple_of(i*BLK, BLK), BLK)
                q = q_ref[qr, :]; do = do_ref[qr, :]
                s = dg(k, q, 1, 1)
                p = jnp.exp2(s*c - lse_ref[0, :, qr])
                if diag:
                    ki = lax.broadcasted_iota(jnp.int32, s.shape, 0)
                    qq = lax.broadcasted_iota(jnp.int32, s.shape, 1)
                    p = jnp.where(ki <= qq, p, 0.0)
                dp = dg(v, do, 1, 1)
                ds = (p * (dp - dl_sc[:, qr])).astype(BF)
                dv = dv + dg(p.astype(BF), do, 1, 0)
                dk = dk + dg(ds, q, 1, 0)
                dq_sc[qr, :] += dg(ds, k, 0, 0)
                return dk, dv
            z = jnp.zeros((BLK, HD), F32)
            carry = step(j, (z, z), True)
            dk, dv = lax.fori_loop(j+1, info[1, j]+1, step, carry)
            dp_ref[kr, HD:2*HD] = (dk*sc).astype(BF)
            dp_ref[kr, 2*HD:] = dv.astype(BF)
        @pl.when(info[2, j] <= 0)
        def _():
            dp_ref[kr, HD:] = jnp.zeros((BLK, 2*HD), BF)
    dp_ref[:, :HD] = (dq_sc[...]*sc).astype(BF)

def attn_bwd(info, proj, ctx, dctx, lse):
    length = proj.shape[0]; heads = proj.shape[1]//(3*HD); nb = length//BLK
    spec = lambda o: pl.BlockSpec((length, HD), lambda h, info: (0, 3*h+o))
    hs = pl.BlockSpec((length, HD), lambda h, info: (0, h))
    return pl.pallas_call(functools.partial(attn_bwd_kernel, nb=nb),
        grid_spec=pltpu.PrefetchScalarGridSpec(num_scalar_prefetch=1, grid=(heads,),
            in_specs=[spec(0), spec(1), spec(2), hs, hs, pl.BlockSpec((1, 1, length), lambda h, info: (h, 0, 0))],
            out_specs=pl.BlockSpec((length, 3*HD), lambda h, info: (0, h)),
            scratch_shapes=[pltpu.VMEM((length, HD), F32), pltpu.VMEM((1, length), F32)]),
        out_shape=jax.ShapeDtypeStruct((length, heads*3*HD), BF),
        compiler_params=pltpu.CompilerParams(vmem_limit_bytes=40<<20), name="attn_bwd",
        cost_estimate=pl.CostEstimate(flops=heads*length*length*HD*5, bytes_accessed=length*heads*HD*16, transcendentals=heads*length*length//2),
    )(info, proj, proj, proj, ctx, dctx, lse)


MESH = pl.DeviceIdType.MESH
TILE = 256


class Place:
    def __init__(self, n_tp):
        self.g = lax.axis_index("grp")
        t = lax.axis_index("tp")
        self.t, self.n, self.Z = t, n_tp, n_tp // 2
        self.z, self.k = t // 2, lax.rem(t, 2)
        self.right, self.left, self.sib = (self.g, t + 2), (self.g, t - 2), (self.g, t + 1 - 2 * self.k)
        self.has_right, self.has_left = self.z < self.Z - 1, self.z > 0

    def barrier(self):
        bar = pltpu.get_barrier_semaphore()
        pl.semaphore_signal(bar, inc=1, device_id=self.sib, device_id_type=MESH)

        @pl.when(self.has_right)
        def _():
            pl.semaphore_signal(bar, inc=1, device_id=self.right, device_id_type=MESH)

        @pl.when(self.has_left)
        def _():
            pl.semaphore_signal(bar, inc=1, device_id=self.left, device_id_type=MESH)

        amount = 1 + jnp.where(self.has_right, 1, 0) + jnp.where(self.has_left, 1, 0)
        pl.semaphore_wait(bar, amount)


def remote(src, dst, ssem, rsem, device):
    return pltpu.make_async_remote_copy(src, dst, ssem, rsem, device_id=device, device_id_type=MESH)


class Gather:
    def __init__(self, at, gat, rows, ls, lr, ss, sr):
        self.at, self.gat, self.rows = at, gat, rows
        self.ls, self.lr, self.ss, self.sr = ls, lr, ss, sr

    def block(self, zz, kk, c):
        return self.gat.at[2 * zz + kk, pl.ds(pl.multiple_of(c * self.rows, self.rows), self.rows), :]

    def line(self, c, side, d):
        at = self.at
        sign, device = (-1, at.right) if side == 0 else (1, at.left)
        b = self.block(at.z + sign * (d - 1), at.k, c)
        return remote(b, b, self.ls.at[c, side, d - 1], self.lr.at[c, side, d - 1], device)

    def line_in(self, c, side, d):
        at = self.at
        sign, device = (-1, at.right) if side == 0 else (1, at.left)
        b = self.block(at.z + sign * d, at.k, c)
        return remote(b, b, self.ls.at[c, side, d - 1], self.lr.at[c, side, d - 1], device)

    def across(self, c, zz):
        b = self.block(zz, self.at.k, c)
        return remote(b, b, self.ss.at[c, zz], self.sr.at[c, zz], self.at.sib)

    def across_in(self, c, zz):
        b = self.block(zz, 1 - self.at.k, c)
        return remote(b, b, self.ss.at[c, zz], self.sr.at[c, zz], self.at.sib)

    def start(self, c):
        at = self.at

        @pl.when(at.has_right)
        def _():
            self.line(c, 0, 1).start()

        @pl.when(at.has_left)
        def _():
            self.line(c, 1, 1).start()

        self.across(c, at.z).start()

    def hop(self, c, d):
        at = self.at

        @pl.when(at.z >= d)
        def _():
            self.line_in(c, 0, d).wait_recv()
            if d < at.Z - 1:
                @pl.when(at.has_right)
                def _():
                    self.line(c, 0, d + 1).start()
            self.across(c, at.z - d).start()

        @pl.when(at.z + d <= at.Z - 1)
        def _():
            self.line_in(c, 1, d).wait_recv()
            if d < at.Z - 1:
                @pl.when(at.has_left)
                def _():
                    self.line(c, 1, d + 1).start()
            self.across(c, at.z + d).start()

    def finish(self, c):
        at = self.at
        for zz in range(at.Z):
            self.across_in(c, zz).wait_recv()
            self.across(c, zz).wait_send()
        for d in range(1, at.Z):
            @pl.when(at.has_right & (at.z >= d - 1))
            def _():
                self.line(c, 0, d).wait_send()

            @pl.when(at.has_left & (at.z + d - 1 <= at.Z - 1))
            def _():
                self.line(c, 1, d).wait_send()


class Scatter:
    def __init__(self, at, parts, pair, hops, cs, cr, hs, hr):
        self.at, self.parts, self.pair, self.hops = at, parts, pair, hops
        self.slots = pair.shape[0]
        self.cs, self.cr, self.hs, self.hr = cs, cr, hs, hr

    def across(self, c):
        c = lax.rem(c, self.slots)
        return remote(self.parts.at[:, 1 - self.at.k], self.pair.at[c], self.cs.at[c], self.cr.at[c], self.at.sib)

    def line(self, c, side, h, target):
        c = lax.rem(c, self.slots)
        device = self.at.right if side == 0 else self.at.left
        return remote(self.pair.at[c, target], self.hops.at[side, c, h - 1],
                      self.hs.at[c, side, h - 1], self.hr.at[c, side, h - 1], device)

    def start(self, c):
        self.across(c).start()

    def meet(self, c):
        self.across(c).wait()
        own = self.parts[:, pl.ds(self.at.k, 1)]
        own = own.reshape(own.shape[0], own.shape[2], own.shape[3])
        c = lax.rem(c, self.slots)
        self.pair[c] = (self.pair[c].astype(F32) + own.astype(F32)).astype(BF)

    def hop(self, c, h):
        at = self.at
        for side in (0, 1):
            pos = at.z if side == 0 else at.Z - 1 - at.z
            target = at.z + at.Z - h if side == 0 else at.z - at.Z + h

            @pl.when((pos <= h - 1) & (pos < at.Z - 1))
            def _():
                if h >= 2:
                    @pl.when(pos >= 1)
                    def _():
                        self.line(c, side, h - 1, target).wait_recv()
                        b = lax.rem(c, self.slots)
                        self.pair[b, target] = (self.pair[b, target].astype(F32)
                                                + self.hops[side, b, h - 2].astype(F32)).astype(BF)
                self.line(c, side, h, target).start()

    def finish(self, c, total):
        at = self.at
        b = lax.rem(c, self.slots)
        total[...] = self.pair[b, at.z].astype(F32)
        for side in (0, 1):
            pos = at.z if side == 0 else at.Z - 1 - at.z

            @pl.when(pos >= 1)
            def _():
                self.line(c, side, at.Z - 1, at.z).wait_recv()
                total[...] += self.hops[side, b, at.Z - 2].astype(F32)

            for h in range(1, at.Z):
                @pl.when((pos <= h - 1) & (pos < at.Z - 1))
                def _():
                    self.line(c, side, h, at.z).wait_send()


def gather_sems(chunks, Z):
    dma = pltpu.SemaphoreType.DMA
    return [dma((chunks, 2, Z - 1)), dma((chunks, 2, Z - 1)), dma((chunks, Z)), dma((chunks, Z))]


def scatter_scratch(chunks, Z, rows, width):
    chunks = min(chunks, 4)
    dma = pltpu.SemaphoreType.DMA
    return [pltpu.VMEM((Z, 2, rows, width), BF), pltpu.VMEM((chunks, Z, rows, width), BF),
            pltpu.VMEM((2, chunks, Z - 1, rows, width), BF),
            dma((chunks,)), dma((chunks,)), dma((chunks, 2, Z - 1)), dma((chunks, 2, Z - 1))]


def inside(c, chunks):
    return (c >= 0) & (c < chunks)


def chunk_rows(c, rows):
    return pl.ds(pl.multiple_of(c * rows, rows), rows)


def tiles(count, body):
    def step(i, carry):
        body(i)
        return carry
    lax.fori_loop(0, count, step, 0)


def cols(i, size=TILE):
    return pl.ds(pl.multiple_of(i * size, size), size)


def rows_stats(rows):
    mean = jnp.mean(rows, -1, keepdims=True)
    centred = rows - mean
    inverse = lax.rsqrt(jnp.mean(centred * centred, -1, keepdims=True) + 1e-05)
    return centred * inverse, inverse


def product_scatter(at, rs, lhs_ref, w_ref, total, chunks, rows, epilogue):
    def product(c):
        lhs = lhs_ref[:, chunk_rows(c, rows), :].reshape(at.n * rows, lhs_ref.shape[2])

        def tile(i):
            y = dg(lhs, w_ref[cols(i), :], 1, 1)
            rs.parts[:, :, :, cols(i)] = y.astype(BF).reshape(at.Z, 2, rows, TILE)
        tiles(w_ref.shape[0] // TILE, tile)
        rs.start(c)

    def tick(i, carry):
        c = i - 1

        @pl.when(inside(c, chunks))
        def _():
            rs.meet(c)
            rs.hop(c, 1)

        @pl.when(inside(i, chunks))
        def _():
            product(i)

        @pl.when(inside(c, chunks))
        def _():
            for h in range(2, at.Z):
                rs.hop(c, h)

        e = i - 2

        @pl.when(inside(e, chunks))
        def _():
            rs.finish(e, total)
            epilogue(e)
        return carry

    lax.fori_loop(0, chunks + 2, tick, 0)


def out_kernel(ctx, w_out, x_share, vec, hidden, n2, total, *sc, n, chunks, rows):
    at = Place(n)
    at.barrier()

    def epilogue(c):
        r = chunk_rows(c, rows)
        h = x_share[r, :].astype(F32) + total[...] + vec[0:1, :]
        hidden[r, :] = h
        n2[r, :] = (rows_stats(h)[0] * vec[1:2, :] + vec[2:3, :]).astype(BF)

    product_scatter(at, Scatter(at, *sc), ctx, w_out, total, chunks, rows, epilogue)


class AllSum:
    def __init__(self, at, n_grp, x, gbuf, tbuf, gs, gr, ts, tr):
        self.at, self.n_grp, self.x, self.gbuf, self.tbuf = at, n_grp, x, gbuf, tbuf
        self.gs, self.gr, self.ts, self.tr = gs, gr, ts, tr

    def over_grp(self, d):
        at = self.at
        return remote(self.x, self.gbuf.at[at.g], self.gs.at[d - 1], self.gr.at[d - 1],
                      (lax.rem(at.g + d, self.n_grp), at.t))

    def over_tp(self, d):
        at = self.at
        return remote(self.tbuf.at[at.t], self.tbuf.at[at.t], self.ts.at[d - 1], self.tr.at[d - 1],
                      (at.g, lax.rem(at.t + d, at.n)))

    def start(self):
        for d in range(1, self.n_grp):
            self.over_grp(d).start()
        self.gbuf[self.at.g] = self.x[...]

    def turn(self):
        for d in range(1, self.n_grp):
            self.over_grp(d).wait()
        total = self.gbuf[0]
        for i in range(1, self.n_grp):
            total = total + self.gbuf[i]
        self.tbuf[self.at.t] = total
        for d in range(1, self.at.n):
            self.over_tp(d).start()

    def finish(self):
        for d in range(1, self.at.n):
            self.over_tp(d).wait()

    def total(self, lo, hi):
        out = self.tbuf[0, lo:hi, :]
        for i in range(1, self.at.n):
            out = out + self.tbuf[i, lo:hi, :]
        return out


def all_sum_scratch(n_grp, n, shape):
    dma = pltpu.SemaphoreType.DMA
    return [pltpu.VMEM(shape, F32), pltpu.VMEM((n_grp,) + shape, F32), pltpu.VMEM((n,) + shape, F32),
            dma((n_grp - 1,)), dma((n_grp - 1,)), dma((n - 1,)), dma((n - 1,))]


def back_kernel(dproj, w_attn, n1_hbm, gw_proj, x_share, dh, gain, stats, up_sum,
                grad_x, g_attn, g_proj, sums, owned,
                n1, gw, got, got_proj, total, qv, ln_sum, nsem, ws, wr, ps, pr, *scratch, n, n_grp, chunks, rows):
    at = Place(n)
    width, hw = w_attn.shape
    block = width // n_grp
    per = block // TILE
    heads = hw // (3 * HD)
    hid = up_sum.shape[1]
    load = pltpu.make_async_copy(n1_hbm, n1, nsem)
    load.start()
    rs, early, late = Scatter(at, *scratch[:7]), AllSum(at, n_grp, *scratch[7:14]), AllSum(at, n_grp, *scratch[14:])
    bar = pltpu.get_barrier_semaphore()
    for d in range(1, n_grp):
        pl.semaphore_signal(bar, inc=1, device_id=(lax.rem(at.g + d, n_grp), at.t), device_id_type=MESH)
    for d in range(1, n):
        pl.semaphore_signal(bar, inc=1, device_id=(at.g, lax.rem(at.t + d, n)), device_id_type=MESH)
    pl.semaphore_wait(bar, n_grp + n - 2)

    def owner(k):
        return lax.rem(at.g + 1 + k, n_grp)

    def send(k):
        r = chunk_rows(owner(k), block)
        return remote(gw.at[r, :], got.at[k], ws.at[k], wr.at[k], (owner(k), at.t))

    def send_proj(k):
        r = chunk_rows(owner(k), block)
        return remote(gw_proj.at[r, :], got_proj.at[k], ps.at[k], pr.at[k], (owner(k), at.t))

    for k in range(n_grp - 1):
        send_proj(k).start()
    qv[...] = jnp.zeros_like(qv)
    ln_sum[...] = jnp.zeros_like(ln_sum)

    def product(c):
        lhs = dproj[:, chunk_rows(c, rows), :].reshape(n * rows, hw)
        qv[...] += jnp.sum(lhs.astype(F32), 0, keepdims=True)

        def tile(i):
            y = dg(lhs, w_attn[cols(i), :], 1, 1)
            rs.parts[:, :, :, cols(i)] = y.astype(BF).reshape(at.Z, 2, rows, TILE)
        tiles(width // TILE, tile)
        rs.start(c)

    def weights(i):
        k = i // per
        first = pl.multiple_of(owner(k) * block + lax.rem(i, per) * TILE, TILE)
        y = dg(n1[:, pl.ds(first, TILE)], dproj[...].reshape(-1, hw), 0, 0)

        @pl.when(k < n_grp - 1)
        def _():
            gw[pl.ds(first, TILE), :] = y.astype(BF)

            @pl.when(lax.rem(i, per) == per - 1)
            def _():
                send(k).start()

        @pl.when(k == n_grp - 1)
        def _():
            g_attn[cols(lax.rem(i, per)), :] = y

    def norm_grad(c):
        r = chunk_rows(c, rows)
        xhat, inverse = rows_stats(x_share[r, :].astype(F32))
        dn = total[...]
        e = dn * gain[...]
        inner = jnp.mean(e, -1, keepdims=True) + xhat * jnp.mean(e * xhat, -1, keepdims=True)
        grad_x[r, :] = dh[r, :] + inverse * (e - inner)
        ln_sum[0:1, :] += jnp.sum(dn * xhat, 0, keepdims=True)
        ln_sum[1:2, :] += jnp.sum(dn, 0, keepdims=True)

    load.wait()

    def tick(i, carry):
        c = i - 1

        @pl.when(inside(c, chunks))
        def _():
            rs.meet(c)
            rs.hop(c, 1)

        @pl.when(inside(i, chunks))
        def _():
            product(i)

        @pl.when(inside(c, chunks))
        def _():
            rs.hop(c, 2)

        @pl.when(i < width // TILE)
        def _():
            weights(i)

        @pl.when(inside(c, chunks))
        def _():
            for h in range(3, at.Z):
                rs.hop(c, h)

        @pl.when(i == chunks)
        def _():
            early.x[...] = stats[...]
            early.x[4:5, 0:hid] = up_sum[...]
            for h in range(heads):
                for j, src in ((0, 3 * h), (1, 3 * h + 2)):
                    early.x[4:5, hid + (2 * h + j) * HD:hid + (2 * h + j + 1) * HD] = qv[:, src * HD:(src + 1) * HD]
            early.start()

        @pl.when(i == chunks + 1)
        def _():
            early.turn()
        e = i - 2

        @pl.when(inside(e, chunks))
        def _():
            rs.finish(e, total)
            norm_grad(e)
        return carry

    lax.fori_loop(0, chunks + 2, tick, 0)
    part = width // 4
    for j in range(4):
        late.x[j:j + 1, :] = ln_sum[0:1, j * part:(j + 1) * part]
        late.x[j + 4:j + 5, :] = ln_sum[1:2, j * part:(j + 1) * part]
    late.start()
    mine = chunk_rows(at.g, block)
    g_proj[...] = gw_proj[mine, :].astype(F32)
    for k in range(n_grp - 1):
        send(k).wait()
        send_proj(k).wait()
        g_attn[...] += got[k].astype(F32)
        g_proj[...] += got_proj[k].astype(F32)
    late.turn()
    early.finish()
    sums[0:4, :] = early.total(0, 4)
    owned[...] = early.tbuf[:, 4, :]
    late.finish()
    ln = late.total(0, 8)
    for j in range(4):
        sums[4:5, j * part:(j + 1) * part] = ln[j:j + 1, :]
        sums[5:6, j * part:(j + 1) * part] = ln[j + 4:j + 5, :]
    sums[6:8, :] = jnp.zeros_like(sums[6:8, :])


def project_back(dproj, w_attn, n1, gw_proj, x_share, dh, gain, stats, up_sum, n, n_grp, chunks):
    length, hw = dproj.shape
    width = w_attn.shape[0]
    share = length // n
    rows = share // chunks
    block = width // n_grp
    pw = gw_proj.shape[1]
    vm, hbm = pl.BlockSpec(memory_space=pltpu.VMEM), pl.BlockSpec(memory_space=pl.ANY)
    S, dma = jax.ShapeDtypeStruct, pltpu.SemaphoreType.DMA
    return pl.pallas_call(
        functools.partial(back_kernel, n=n, n_grp=n_grp, chunks=chunks, rows=rows),
        in_specs=[vm, vm, hbm] + [vm] * 6, out_specs=[vm] * 5,
        out_shape=[S((share, width), F32), S((block, hw), F32), S((block, pw), F32), S((8, width), F32),
                   S((n, width), F32)],
        scratch_shapes=[pltpu.VMEM((length, width), BF), pltpu.VMEM((width, hw), BF),
                        pltpu.VMEM((n_grp - 1, block, hw), BF), pltpu.VMEM((n_grp - 1, block, pw), BF),
                        pltpu.VMEM((rows, width), F32), pltpu.VMEM((1, hw), F32), pltpu.VMEM((8, width), F32), dma]
                       + [dma((n_grp - 1,))] * 4 + scatter_scratch(chunks, n // 2, rows, width)
                       + all_sum_scratch(n_grp, n, (8, width)) + all_sum_scratch(n_grp, n, (8, width // 4)),
        compiler_params=pltpu.CompilerParams(collective_id=4, has_side_effects=True, vmem_limit_bytes=50 << 20),
        cost_estimate=pl.CostEstimate(flops=4 * length * hw * width, bytes_accessed=1 << 24, transcendentals=0),
        name="project_back",
    )(dproj.reshape(n, share, hw), w_attn, n1, gw_proj, x_share, dh, gain, stats, up_sum)


def attn_out(ctx, w_out, x_share, vec, n, chunks):
    length, hw = ctx.shape
    share, width = x_share.shape
    rows = share // chunks
    vm = pl.BlockSpec(memory_space=pltpu.VMEM)
    return pl.pallas_call(
        functools.partial(out_kernel, n=n, chunks=chunks, rows=rows),
        in_specs=[vm] * 4, out_specs=[vm] * 2,
        out_shape=[jax.ShapeDtypeStruct((share, width), F32), jax.ShapeDtypeStruct((share, width), BF)],
        scratch_shapes=[pltpu.VMEM((rows, width), F32)] + scatter_scratch(chunks, n // 2, rows, width),
        compiler_params=pltpu.CompilerParams(collective_id=2, has_side_effects=True, vmem_limit_bytes=40 << 20),
        cost_estimate=pl.CostEstimate(flops=2 * length * hw * width, bytes_accessed=1 << 23, transcendentals=0),
        name="attn_out",
    )(ctx.reshape(n, share, hw), w_out, x_share, vec)


def ffn_kernel(n2_hbm, gradb_hbm, w_up, w_down, w_out, b_up, ctx, hidden, gshare, vec, live,
               gw_hbm, gwo, dctx, dh, res, stats, bsum,
               gat, acc_up, acc_down, gbuf, actb, dbb, total, lsem, gsem, msem, *scratch, n, chunks, rows):
    at = Place(n)
    ag1, ag2 = Gather(at, gat, rows, *scratch[:4]), Gather(at, gat, rows, *scratch[4:8])
    rs, mlp = Scatter(at, *scratch[8:15]), Scatter(at, *scratch[15:])
    width, hid = w_up.shape
    m = n * rows

    load = pltpu.make_async_copy(n2_hbm, gat.at[at.t], lsem)
    load.start()

    def fetch(c):
        slot = lax.rem(c, 2)
        return pltpu.make_async_copy(gradb_hbm.at[:, chunk_rows(c, rows), :], gbuf.at[slot], gsem.at[slot])

    fetch(0).start()
    acc_up[...] = jnp.zeros_like(acc_up)
    acc_down[...] = jnp.zeros_like(acc_down)
    stats[...] = jnp.zeros_like(stats)
    bsum[...] = jnp.zeros_like(bsum)
    load.wait()
    at.barrier()

    a0, a1 = 0.7978845608028654, 0.044715

    def wide(c):
        return gat[:, chunk_rows(c, rows), :].reshape(m, width)

    def forward(c):
        fetch(c).wait()

        @pl.when(c + 1 < chunks)
        def _():
            fetch(c + 1).start()
        slot = lax.rem(c, 2)

        def tile(i):
            v = dg(wide(c), w_up[:, cols(i)], 1, 0) + b_up[:, cols(i)]
            ga = dg(gbuf[slot].reshape(m, width), w_down[:, cols(i)], 1, 0)
            v2 = v * v
            th = jnp.tanh(a0 * (v + a1 * v2 * v))
            half = 0.5 * (1.0 + th)
            actb[:, cols(i)] = (v * half).astype(BF)
            slope = half + 0.5 * v * (1.0 - th * th) * (a0 * (1.0 + 3.0 * a1 * v2))
            db = (ga * slope).astype(BF)
            dbb[:, cols(i)] = db
            bsum[:, cols(i)] += jnp.sum(db.astype(F32), 0, keepdims=True)
        tiles(hid // TILE, tile)

    def back(c):
        def tile(i):
            y = dg(dbb[...], w_up[cols(i), :], 1, 1)
            rs.parts[:, :, :, cols(i)] = y.astype(BF).reshape(at.Z, 2, rows, TILE)
        tiles(width // TILE, tile)

    def down(c):
        def tile(i):
            y = dg(actb[...], w_down[cols(i), :], 1, 1)
            mlp.parts[:, :, :, cols(i)] = y.astype(BF).reshape(at.Z, 2, rows, TILE)
        tiles(width // TILE, tile)

    def weights(c):
        slot = lax.rem(c, 2)

        def tile(i):
            x = gat[:, chunk_rows(c, rows), cols(i)].reshape(m, TILE)
            acc_up[cols(i), :] += dg(x, dbb[...], 0, 0)
            y = gbuf[slot, :, :, cols(i)].reshape(m, TILE)
            acc_down[cols(i), :] += dg(y, actb[...], 0, 0)
        tiles(width // TILE, tile)

    def norm_grad(c):
        r = chunk_rows(c, rows)
        xhat, inverse = rows_stats(hidden[r, :])
        dn2 = total[...]
        e = dn2 * vec[0:1, :]
        inner = jnp.mean(e, -1, keepdims=True) + xhat * jnp.mean(e * xhat, -1, keepdims=True)
        d = gshare[r, :].astype(F32) + inverse * (e - inner)
        dh[r, :] = d
        gat[at.t, r, :] = d.astype(BF)
        stats[0:1, :] += jnp.sum(dn2 * xhat, 0, keepdims=True)
        stats[1:2, :] += jnp.sum(dn2, 0, keepdims=True)
        stats[2:3, :] += jnp.sum(d, 0, keepdims=True)
        stats[3:4, :] += jnp.sum(gshare[r, :].astype(F32), 0, keepdims=True)

    def heads(c):
        y = dg(wide(c), w_out[...], 1, 0)
        dctx[:, chunk_rows(c, rows), :] = y.astype(BF).reshape(n, rows, y.shape[1])

    def at_stage(c, fn):
        @pl.when(inside(c, chunks))
        def _():
            fn(c)

    def tick(i, carry):
        at_stage(i, ag1.start)
        at_stage(i - 3, rs.meet)
        for h in range(1, at.Z):
            at_stage(i - 3, lambda c: rs.hop(c, h))
            at_stage(i - 1, lambda c: ag1.hop(c, h))
            if h == 1:
                at_stage(i - 4, lambda c: mlp.hop(c, at.Z - 1))
                at_stage(i - 5, lambda c: ag2.hop(c, at.Z - 1))
                at_stage(i - 2, forward)
            else:
                if h == 2:
                    def served(c):
                        mlp.finish(c, total)
                        r = chunk_rows(c, rows)
                        res[r, :] = (live[r, :] * (hidden[r, :] + total[...] + vec[1:2, :])).astype(BF)
                    at_stage(i - 4, served)
                    at_stage(i - 3, mlp.meet)
                at_stage(i - 3, lambda c: mlp.hop(c, h - 1))
                at_stage(i - 4, lambda c: ag2.hop(c, h - 1))
                if h == 2:
                    at_stage(i - 2, back)

                    def gathered(c):
                        ag2.finish(c)
                        heads(c)
                    at_stage(i - 5, gathered)

        def rest(c):
            weights(c)
            rs.start(c)
        at_stage(i - 2, rest)

        def reduced(c):
            rs.finish(c, total)
            norm_grad(c)
            ag2.start(c)
        at_stage(i - 3, reduced)
        at_stage(i - 1, ag1.finish)

        def send_mlp(c):
            down(c)
            mlp.start(c)
        at_stage(i - 2, send_mlp)

        @pl.when(i == chunks + 2)
        def _():
            tiles(width // m, store)
        return carry

    def store(i):
        r = cols(i, m)
        actb[...] = acc_up[r, :].astype(BF)
        one = pltpu.make_async_copy(actb, gw_hbm.at[r, pl.ds(0, hid)], lsem)
        one.start()
        dbb[...] = acc_down[r, :].astype(BF)
        two = pltpu.make_async_copy(dbb, gw_hbm.at[r, pl.ds(hid, hid)], msem)
        two.start()
        one.wait()
        two.wait()

    lax.fori_loop(0, chunks + 5, tick, 0)

    def final(i):
        x = gat[:, :, cols(i)].reshape(-1, TILE)
        gwo[cols(i), :] = dg(x, ctx[...], 0, 0).astype(BF)
    tiles(width // TILE, final)


def feed_forward(n2, gradb, w_up, w_down, w_out, b_up, ctx, hidden, gshare, vec, live, n, chunks):
    length, width = gradb.shape
    hid, hw = w_up.shape[1], w_out.shape[1]
    share = length // n
    rows = share // chunks
    Z = n // 2
    vm, hbm = pl.BlockSpec(memory_space=pltpu.VMEM), pl.BlockSpec(memory_space=pl.ANY)
    S = jax.ShapeDtypeStruct
    m = n * rows
    return pl.pallas_call(
        functools.partial(ffn_kernel, n=n, chunks=chunks, rows=rows),
        in_specs=[hbm, hbm] + [vm] * 9,
        out_specs=[hbm] + [vm] * 6,
        out_shape=[S((width, 2 * hid), BF), S((width, hw), BF), S((n, share, hw), BF), S((share, width), F32),
                   S((share, width), BF), S((8, width), F32), S((1, hid), F32)],
        scratch_shapes=[pltpu.VMEM((n, share, width), BF), pltpu.VMEM((width, hid), F32), pltpu.VMEM((width, hid), F32),
                        pltpu.VMEM((2, n, rows, width), BF),
                        pltpu.VMEM((m, hid), BF), pltpu.VMEM((m, hid), BF), pltpu.VMEM((rows, width), F32),
                        pltpu.SemaphoreType.DMA, pltpu.SemaphoreType.DMA((2,)), pltpu.SemaphoreType.DMA]
                       + gather_sems(chunks, Z) + gather_sems(chunks, Z) + scatter_scratch(chunks, Z, rows, width) * 2,
        compiler_params=pltpu.CompilerParams(collective_id=3, has_side_effects=True, vmem_limit_bytes=62 << 20),
        cost_estimate=pl.CostEstimate(flops=12 * length * hid * width, bytes_accessed=1 << 26, transcendentals=0),
        name="feed_forward",
    )(n2, gradb.reshape(n, share, width), w_up, w_down, w_out, b_up, ctx, hidden, gshare, vec, live)


def normalize(rows, gain, bias):
    mean_row = jnp.mean(rows, -1, keepdims=True)
    centred = rows - mean_row
    return centred * lax.rsqrt(jnp.mean(centred * centred, -1, keepdims=True) + 1e-05) * gain + bias


def on_device(layer_input, out_cotangent, seq_group, seq_len, w_qkv, b_qv, w_out, b_out, w_up, b_up,
              w_down, b_down, first_norm_gain, first_norm_bias, second_norm_gain, second_norm_bias):
    tp = lax.axis_index("tp")
    n_tp = lax.axis_size("tp")
    grp = lax.axis_index("grp")
    length, width = layer_input.shape
    share = length // n_tp
    heads = w_out.shape[1] // HD
    hidden_here = w_up.shape[1]

    w_attn = lax.all_gather(w_qkv.astype(BF), "grp", axis=0, tiled=True)
    w_proj = lax.all_gather(w_out.astype(BF), "grp", axis=0, tiled=True)
    w_expand = lax.all_gather(w_up.astype(BF), "grp", axis=0, tiled=True)
    w_reduce = lax.all_gather(w_down.astype(BF), "grp", axis=0, tiled=True)

    nb = length // BLK
    in_group = seq_group == grp
    lengths = jnp.where(in_group, seq_len, 0)
    order = jnp.arange(seq_group.shape[0], dtype=jnp.int32)
    offsets = jnp.sum(jnp.where(order[:, None] > order[None, :], lengths[None, :], 0), 1)
    starts = jnp.arange(nb, dtype=jnp.int32) * BLK
    inside = in_group[None] & (starts[:, None] >= offsets[None]) & (starts[:, None] < (offsets + lengths)[None])
    alive = jnp.any(inside, 1)
    first = jnp.sum(jnp.where(inside, (offsets // BLK)[None], 0), 1)
    last = jnp.sum(jnp.where(inside, ((offsets + lengths) // BLK - 1)[None], 0), 1)
    info = jnp.stack([first, last, alive.astype(jnp.int32)]).astype(jnp.int32)
    tokens = jnp.sum(lengths)
    row0 = tp * share
    live = (row0 + jnp.arange(share, dtype=jnp.int32) < tokens).astype(F32)[:, None]
    live_all = (jnp.arange(length, dtype=jnp.int32) < tokens)[:, None]

    def mine(x):
        return lax.dynamic_slice_in_dim(x, row0, share, 0)

    x = layer_input.astype(F32)
    n1 = normalize(x, first_norm_gain, first_norm_bias).astype(BF)
    x_share_b = mine(layer_input)

    head_bias = lax.dynamic_slice_in_dim(b_qv.reshape(-1, 2, HD), tp * heads, heads, 0)
    bias_three = jnp.stack(
        [head_bias[:, 0], jnp.zeros_like(head_bias[:, 0]), head_bias[:, 1]], 1).reshape(-1)
    proj = (jnp.dot(n1, w_attn, preferred_element_type=F32) + bias_three).astype(BF)
    context, lse = attn_fwd(info, proj)
    vec = jnp.stack([b_out, second_norm_gain, second_norm_bias])
    hidden, n2_share = attn_out(context, w_proj, x_share_b, vec, n_tp, 8)
    up_bias = lax.dynamic_slice_in_dim(b_up, tp * hidden_here, hidden_here, 0)[None]
    gradb = jnp.where(live_all, out_cotangent, jnp.zeros_like(out_cotangent))
    gradb_share = mine(gradb)
    gw_ffn, gw_proj, dcontext, dh, result, stats, up_sum = feed_forward(
        n2_share, gradb, w_expand, w_reduce, w_proj, up_bias, context, hidden, gradb_share,
        jnp.stack([second_norm_gain, b_down]), live, n_tp, 8)
    dcontext = dcontext.reshape(length, -1)
    scatter = functools.partial(lax.psum_scatter, axis_name="grp", scatter_dimension=0, tiled=True)
    grads_ffn = scatter(gw_ffn).astype(F32)
    grads_expand, grads_reduce = grads_ffn[:, :hidden_here], grads_ffn[:, hidden_here:]

    dproj = attn_bwd(info, proj, context, dcontext, lse)
    grad_x, grads_attn, grads_proj, sums, owned = project_back(
        dproj, w_attn, n1, gw_proj, x_share_b, dh, first_norm_gain[None], stats, up_sum,
        n_tp, lax.axis_size("grp"), 8)
    qv = heads * 2 * HD
    return (result, grad_x, grads_attn, owned[:, hidden_here:hidden_here + qv].reshape(-1), grads_proj, sums[2],
            grads_expand, owned[:, :hidden_here].reshape(-1), grads_reduce, sums[3], sums[4], sums[5],
            sums[0], sums[1])


def solution(mesh):
    rows, both, flat = P("grp", None), P("grp", "tp"), P()
    in_specs = (rows, rows, flat, flat, both, flat, both, flat, both, flat, both, flat, flat, flat, flat, flat)
    spread = P(("grp", "tp"), None)
    out_specs = (spread, spread, both, flat, both, flat, both, flat, both, flat, flat, flat, flat, flat)
    return jax.shard_map(on_device, mesh=mesh, in_specs=in_specs, out_specs=out_specs, check_vma=False)
```

```python
import functools

import jax
import jax.numpy as jnp
from jax import lax
from jax.experimental import pallas as pl
from jax.experimental.pallas import tpu as pltpu
from jax.sharding import PartitionSpec as P

HD = 128
BLK=512
F32=jnp.float32
BF=jnp.bfloat16
LOG2E=1.4426950408889634

def dg(a,b,ca,cb):
    return lax.dot_general(a,b,(((ca,),(cb,)),((),())),preferred_element_type=F32)

def block_info(grps, lens, nb, seqs):
    g = lax.axis_index("grp")
    found = [[jnp.int32(0), jnp.int32(0), jnp.int32(0)] for _ in range(nb)]
    start = jnp.int32(0)
    for s in range(seqs):
        count = jnp.where(grps[s] == g, lens[s] // BLK, 0)
        for b in range(nb):
            hit = (start <= b) & (b < start + count)
            found[b] = [jnp.where(hit, start, found[b][0]), jnp.where(hit, start + count - 1, found[b][1]),
                        jnp.where(hit, 1, found[b][2])]
        start = start + count
    return found


def attn_fwd_kernel(grps, lens, q_ref, k_ref, v_ref, o_ref, lse_ref, *, nb, seqs):
    info = block_info(grps, lens, nb, seqs)
    c = HD ** -0.5 * LOG2E
    for qi in range(nb):
        rows = pl.ds(qi*BLK, BLK)
        @pl.when(info[qi][2] > 0)
        def _():
            q = q_ref[rows, :]
            def step(j, carry, diag=False):
                m, l, acc = carry
                kr = pl.ds(pl.multiple_of(j*BLK, BLK), BLK)
                s = dg(k_ref[kr, :], q, 1, 1)
                if diag:
                    ki = lax.broadcasted_iota(jnp.int32, s.shape, 0)
                    qq = lax.broadcasted_iota(jnp.int32, s.shape, 1)
                    s = jnp.where(ki <= qq, s, -1e30)
                mn = jnp.maximum(m, jnp.max(s, 0, keepdims=True))
                p = jnp.exp2(s*c - mn*c)
                alpha = jnp.exp2((m - mn)*c)
                l = l*alpha + jnp.sum(p, 0, keepdims=True)
                acc = acc*alpha + dg(v_ref[kr, :], p.astype(BF), 0, 0)
                return mn, l, acc
            init = (jnp.full((1, BLK), -1e30, F32), jnp.zeros((1, BLK), F32), jnp.zeros((HD, BLK), F32))
            carry = step(qi, init, True)
            m, l, acc = lax.fori_loop(info[qi][0], qi, step, carry)
            o_ref[rows, :] = jnp.transpose(acc / l).astype(BF)
            lse_ref[0, :, rows] = m*c + jnp.log2(l)
        @pl.when(info[qi][2] <= 0)
        def _():
            o_ref[rows, :] = jnp.zeros((BLK, HD), BF)
            lse_ref[0, :, rows] = jnp.zeros((1, BLK), F32)

def attn_fwd(grps, lens, proj):
    length = proj.shape[0]; heads = proj.shape[1]//(3*HD); nb = length//BLK
    spec = lambda o: pl.BlockSpec((length, HD), lambda h, grps, lens: (0, 3*h+o))
    return pl.pallas_call(functools.partial(attn_fwd_kernel, nb=nb, seqs=grps.shape[0]),
        grid_spec=pltpu.PrefetchScalarGridSpec(num_scalar_prefetch=2, grid=(heads,),
            in_specs=[spec(0), spec(1), spec(2)],
            out_specs=[pl.BlockSpec((length, HD), lambda h, grps, lens: (0, h)), pl.BlockSpec((1, 1, length), lambda h, grps, lens: (h, 0, 0))]),
        out_shape=[jax.ShapeDtypeStruct((length, heads*HD), BF), jax.ShapeDtypeStruct((heads, 1, length), F32)],
        compiler_params=pltpu.CompilerParams(vmem_limit_bytes=40<<20), name="attn_fwd",
        cost_estimate=pl.CostEstimate(flops=heads*length*length*HD*2, bytes_accessed=length*heads*HD*8, transcendentals=heads*length*length//2),
    )(grps, lens, proj, proj, proj)

def attn_bwd_kernel(grps, lens, q_ref, k_ref, v_ref, o_ref, do_ref, lse_ref, dp_ref, dq_sc, dl_sc, *, nb, seqs):
    info = block_info(grps, lens, nb, seqs)
    sc = HD ** -0.5
    c = sc * LOG2E
    prod = do_ref[...].astype(F32) * o_ref[...].astype(F32)
    dl_sc[...] = jnp.sum(jnp.transpose(prod), 0, keepdims=True)
    dq_sc[...] = jnp.zeros_like(dq_sc)
    for j in range(nb):
        kr = pl.ds(j*BLK, BLK)
        @pl.when(info[j][2] > 0)
        def _():
            k = k_ref[kr, :]; v = v_ref[kr, :]
            def step(i, carry, diag=False):
                dk, dv = carry
                qr = pl.ds(pl.multiple_of(i*BLK, BLK), BLK)
                q = q_ref[qr, :]; do = do_ref[qr, :]
                s = dg(k, q, 1, 1)
                p = jnp.exp2(s*c - lse_ref[0, :, qr])
                if diag:
                    ki = lax.broadcasted_iota(jnp.int32, s.shape, 0)
                    qq = lax.broadcasted_iota(jnp.int32, s.shape, 1)
                    p = jnp.where(ki <= qq, p, 0.0)
                dp = dg(v, do, 1, 1)
                ds = (p * (dp - dl_sc[:, qr])).astype(BF)
                dv = dv + dg(p.astype(BF), do, 1, 0)
                dk = dk + dg(ds, q, 1, 0)
                dq_sc[qr, :] += dg(ds, k, 0, 0)
                return dk, dv
            z = jnp.zeros((BLK, HD), F32)
            carry = step(j, (z, z), True)
            dk, dv = lax.fori_loop(j+1, info[j][1]+1, step, carry)
            dp_ref[kr, HD:2*HD] = (dk*sc).astype(BF)
            dp_ref[kr, 2*HD:] = dv.astype(BF)
        @pl.when(info[j][2] <= 0)
        def _():
            dp_ref[kr, HD:] = jnp.zeros((BLK, 2*HD), BF)
    dp_ref[:, :HD] = (dq_sc[...]*sc).astype(BF)

def attn_bwd(grps, lens, proj, ctx, dctx, lse):
    length = proj.shape[0]; heads = proj.shape[1]//(3*HD); nb = length//BLK
    spec = lambda o: pl.BlockSpec((length, HD), lambda h, grps, lens: (0, 3*h+o))
    hs = pl.BlockSpec((length, HD), lambda h, grps, lens: (0, h))
    return pl.pallas_call(functools.partial(attn_bwd_kernel, nb=nb, seqs=grps.shape[0]),
        grid_spec=pltpu.PrefetchScalarGridSpec(num_scalar_prefetch=2, grid=(heads,),
            in_specs=[spec(0), spec(1), spec(2), hs, hs, pl.BlockSpec((1, 1, length), lambda h, grps, lens: (h, 0, 0))],
            out_specs=pl.BlockSpec((length, 3*HD), lambda h, grps, lens: (0, h)),
            scratch_shapes=[pltpu.VMEM((length, HD), F32), pltpu.VMEM((1, length), F32)]),
        out_shape=jax.ShapeDtypeStruct((length, heads*3*HD), BF),
        compiler_params=pltpu.CompilerParams(vmem_limit_bytes=40<<20), name="attn_bwd",
        cost_estimate=pl.CostEstimate(flops=heads*length*length*HD*5, bytes_accessed=length*heads*HD*16, transcendentals=heads*length*length//2),
    )(grps, lens, proj, proj, proj, ctx, dctx, lse)


MESH = pl.DeviceIdType.MESH
TILE = 256


class Place:
    def __init__(self, n_tp):
        self.g = lax.axis_index("grp")
        t = lax.axis_index("tp")
        self.t, self.n, self.Z = t, n_tp, n_tp // 2
        self.z, self.k = t // 2, lax.rem(t, 2)
        self.right, self.left, self.sib = (self.g, t + 2), (self.g, t - 2), (self.g, t + 1 - 2 * self.k)
        self.has_right, self.has_left = self.z < self.Z - 1, self.z > 0

    def barrier(self, n_grp=0):
        bar = pltpu.get_barrier_semaphore()
        extra = grp_signal(self, n_grp) if n_grp else 0
        pl.semaphore_signal(bar, inc=1, device_id=self.sib, device_id_type=MESH)

        @pl.when(self.has_right)
        def _():
            pl.semaphore_signal(bar, inc=1, device_id=self.right, device_id_type=MESH)

        @pl.when(self.has_left)
        def _():
            pl.semaphore_signal(bar, inc=1, device_id=self.left, device_id_type=MESH)

        amount = 1 + extra + jnp.where(self.has_right, 1, 0) + jnp.where(self.has_left, 1, 0)
        pl.semaphore_wait(bar, amount)


def remote(src, dst, ssem, rsem, device):
    return pltpu.make_async_remote_copy(src, dst, ssem, rsem, device_id=device, device_id_type=MESH)


class Gather:
    def __init__(self, at, gat, rows, ls, lr, ss, sr):
        self.at, self.gat, self.rows = at, gat, rows
        self.ls, self.lr, self.ss, self.sr = ls, lr, ss, sr

    def block(self, zz, kk, c):
        return self.gat.at[2 * zz + kk, pl.ds(pl.multiple_of(c * self.rows, self.rows), self.rows), :]

    def line(self, c, side, d):
        at = self.at
        sign, device = (-1, at.right) if side == 0 else (1, at.left)
        b = self.block(at.z + sign * (d - 1), at.k, c)
        return remote(b, b, self.ls.at[c, side, d - 1], self.lr.at[c, side, d - 1], device)

    def line_in(self, c, side, d):
        at = self.at
        sign, device = (-1, at.right) if side == 0 else (1, at.left)
        b = self.block(at.z + sign * d, at.k, c)
        return remote(b, b, self.ls.at[c, side, d - 1], self.lr.at[c, side, d - 1], device)

    def across(self, c, zz):
        b = self.block(zz, self.at.k, c)
        return remote(b, b, self.ss.at[c, zz], self.sr.at[c, zz], self.at.sib)

    def across_in(self, c, zz):
        b = self.block(zz, 1 - self.at.k, c)
        return remote(b, b, self.ss.at[c, zz], self.sr.at[c, zz], self.at.sib)

    def start(self, c):
        at = self.at

        @pl.when(at.has_right)
        def _():
            self.line(c, 0, 1).start()

        @pl.when(at.has_left)
        def _():
            self.line(c, 1, 1).start()

        self.across(c, at.z).start()

    def hop(self, c, d):
        at = self.at

        @pl.when(at.z >= d)
        def _():
            self.line_in(c, 0, d).wait_recv()
            if d < at.Z - 1:
                @pl.when(at.has_right)
                def _():
                    self.line(c, 0, d + 1).start()
            self.across(c, at.z - d).start()

        @pl.when(at.z + d <= at.Z - 1)
        def _():
            self.line_in(c, 1, d).wait_recv()
            if d < at.Z - 1:
                @pl.when(at.has_left)
                def _():
                    self.line(c, 1, d + 1).start()
            self.across(c, at.z + d).start()

    def finish(self, c):
        at = self.at
        for zz in range(at.Z):
            self.across_in(c, zz).wait_recv()
            self.across(c, zz).wait_send()
        for d in range(1, at.Z):
            @pl.when(at.has_right & (at.z >= d - 1))
            def _():
                self.line(c, 0, d).wait_send()

            @pl.when(at.has_left & (at.z + d - 1 <= at.Z - 1))
            def _():
                self.line(c, 1, d).wait_send()


class Scatter:
    def __init__(self, at, parts, pair, hops, cs, cr, hs, hr):
        self.at, self.parts, self.pair, self.hops = at, parts, pair, hops
        self.slots = pair.shape[0]
        self.cs, self.cr, self.hs, self.hr = cs, cr, hs, hr

    def across(self, c):
        c = lax.rem(c, self.slots)
        return remote(self.parts.at[:, 1 - self.at.k], self.pair.at[c], self.cs.at[c], self.cr.at[c], self.at.sib)

    def line(self, c, side, h, target):
        c = lax.rem(c, self.slots)
        device = self.at.right if side == 0 else self.at.left
        return remote(self.pair.at[c, target], self.hops.at[side, c, h - 1],
                      self.hs.at[c, side, h - 1], self.hr.at[c, side, h - 1], device)

    def start(self, c):
        self.across(c).start()

    def meet(self, c):
        self.across(c).wait()
        own = self.parts[:, pl.ds(self.at.k, 1)]
        own = own.reshape(own.shape[0], own.shape[2], own.shape[3])
        c = lax.rem(c, self.slots)
        self.pair[c] = (self.pair[c].astype(F32) + own.astype(F32)).astype(BF)

    def hop(self, c, h):
        at = self.at
        for side in (0, 1):
            pos = at.z if side == 0 else at.Z - 1 - at.z
            target = at.z + at.Z - h if side == 0 else at.z - at.Z + h

            @pl.when((pos <= h - 1) & (pos < at.Z - 1))
            def _():
                if h >= 2:
                    @pl.when(pos >= 1)
                    def _():
                        self.line(c, side, h - 1, target).wait_recv()
                        b = lax.rem(c, self.slots)
                        self.pair[b, target] = (self.pair[b, target].astype(F32)
                                                + self.hops[side, b, h - 2].astype(F32)).astype(BF)
                self.line(c, side, h, target).start()

    def finish(self, c, total):
        at = self.at
        b = lax.rem(c, self.slots)
        total[...] = self.pair[b, at.z].astype(F32)
        for side in (0, 1):
            pos = at.z if side == 0 else at.Z - 1 - at.z

            @pl.when(pos >= 1)
            def _():
                self.line(c, side, at.Z - 1, at.z).wait_recv()
                total[...] += self.hops[side, b, at.Z - 2].astype(F32)

            for h in range(1, at.Z):
                @pl.when((pos <= h - 1) & (pos < at.Z - 1))
                def _():
                    self.line(c, side, h, at.z).wait_send()


class GroupGather:
    def __init__(self, at, n_grp, full, ss, sr):
        self.at, self.full, self.ss, self.sr = at, full, ss, sr
        self.P = n_grp // 2
        self.size = full.shape[0] // n_grp
        self.p, self.q = at.g // 2, lax.rem(at.g, 2)
        self.partner = (at.g + 1 - 2 * self.q, at.t)

    def peer(self, j):
        return lax.rem(self.p + j, self.P)

    def rows(self, p, q, half=None):
        size = self.size if half is None else self.size // 2
        first = (2 * p + q) * self.size + (size if half == 1 else 0)
        return self.full.at[pl.ds(pl.multiple_of(first, size), size), :]

    def copy(self, kind, j, incoming=False):
        p, q = self.p, self.q
        src = lax.rem(p + self.P - j, self.P)
        if kind == 0:
            b, k, dev = self.rows(p, 1 - q if incoming else q), 0, self.partner
        elif kind == 1:
            b, k, dev = self.rows(src if incoming else p, q), j, (2 * self.peer(j) + q, self.at.t)
        elif kind == 2:
            b, k = self.rows(src if incoming else p, 1 - q, 1), self.P - 1 + j
            dev = (2 * self.peer(j) + q, self.at.t)
        else:
            b, k = self.rows(src, 1 - q if incoming else q, 0), 2 * (self.P - 1) + j
            dev = self.partner
        return remote(b, b, self.ss.at[k], self.sr.at[k], dev)

    def start(self):
        self.copy(0, 0).start()
        for j in range(1, self.P):
            self.copy(1, j).start()

    def forward(self):
        self.copy(0, 0, True).wait_recv()
        for j in range(1, self.P):
            self.copy(2, j).start()
        for j in range(1, self.P):
            self.copy(1, j, True).wait_recv()
            self.copy(3, j).start()

    def finish(self):
        for j in range(1, self.P):
            for kind in (2, 3):
                self.copy(kind, j, True).wait_recv()
                self.copy(kind, j).wait_send()
            self.copy(1, j).wait_send()
        self.copy(0, 0).wait_send()


def group_sems(n_grp):
    k = 1 + 3 * (n_grp // 2 - 1)
    return [pltpu.SemaphoreType.DMA((k,)), pltpu.SemaphoreType.DMA((k,))]


def grp_signal(at, n_grp):
    bar = pltpu.get_barrier_semaphore()
    p, q = at.g // 2, lax.rem(at.g, 2)
    pl.semaphore_signal(bar, inc=1, device_id=(at.g + 1 - 2 * q, at.t), device_id_type=MESH)
    for j in range(1, n_grp // 2):
        pl.semaphore_signal(bar, inc=1, device_id=(2 * lax.rem(p + j, n_grp // 2) + q, at.t), device_id_type=MESH)
    return n_grp // 2


def gather_sems(chunks, Z):
    dma = pltpu.SemaphoreType.DMA
    return [dma((chunks, 2, Z - 1)), dma((chunks, 2, Z - 1)), dma((chunks, Z)), dma((chunks, Z))]


def scatter_scratch(chunks, Z, rows, width):
    chunks = min(chunks, 4)
    dma = pltpu.SemaphoreType.DMA
    return [pltpu.VMEM((Z, 2, rows, width), BF), pltpu.VMEM((chunks, Z, rows, width), BF),
            pltpu.VMEM((2, chunks, Z - 1, rows, width), BF),
            dma((chunks,)), dma((chunks,)), dma((chunks, 2, Z - 1)), dma((chunks, 2, Z - 1))]


def inside(c, chunks):
    return (c >= 0) & (c < chunks)


def chunk_rows(c, rows):
    return pl.ds(pl.multiple_of(c * rows, rows), rows)


def tiles(count, body):
    def step(i, carry):
        body(i)
        return carry
    lax.fori_loop(0, count, step, 0)


def cols(i, size=TILE):
    return pl.ds(pl.multiple_of(i * size, size), size)


def rows_stats(rows):
    mean = jnp.mean(rows, -1, keepdims=True)
    centred = rows - mean
    inverse = lax.rsqrt(jnp.mean(centred * centred, -1, keepdims=True) + 1e-05)
    return centred * inverse, inverse


def product_scatter(at, rs, lhs_ref, w_ref, total, chunks, rows, epilogue, extra):
    def product(c):
        lhs = lhs_ref[:, chunk_rows(c, rows), :].reshape(at.n * rows, lhs_ref.shape[2])

        def tile(i):
            y = dg(lhs, w_ref[cols(i), :], 1, 1)
            rs.parts[:, :, :, cols(i)] = y.astype(BF).reshape(at.Z, 2, rows, TILE)
        tiles(w_ref.shape[0] // TILE, tile)
        rs.start(c)

    def tick(i, carry):
        c = i - 1

        @pl.when(inside(c, chunks))
        def _():
            rs.meet(c)
            rs.hop(c, 1)

        @pl.when(inside(i, chunks))
        def _():
            product(i)

        @pl.when(inside(c, chunks))
        def _():
            for h in range(2, at.Z):
                rs.hop(c, h)

        e = i - 2

        @pl.when(inside(e, chunks))
        def _():
            rs.finish(e, total)
            epilogue(e)
        extra(i)
        return carry

    lax.fori_loop(0, chunks + 2, tick, 0)


def out_kernel(ctx, w_out, vec, x_hbm, up16, down16, hidden, n2, up_hbm, down_hbm,
               x_share, total, lsem, *sc, n, n_grp, chunks, rows):
    at = Place(n)
    load = pltpu.make_async_copy(x_hbm.at[at.t], x_share, lsem.at[0])
    load.start()
    up, down = GroupGather(at, n_grp, up_hbm, *sc[:2]), GroupGather(at, n_grp, down_hbm, *sc[2:4])
    own = chunk_rows(at.g, up.size)
    put_up = pltpu.make_async_copy(up16, up_hbm.at[own, :], lsem.at[1])
    put_down = pltpu.make_async_copy(down16, down_hbm.at[own, :], lsem.at[2])
    put_up.start()
    put_down.start()
    at.barrier(n_grp)
    load.wait()
    put_up.wait()
    put_down.wait()
    up.start()
    down.start()

    def epilogue(c):
        r = chunk_rows(c, rows)
        h = x_share[r, :].astype(F32) + total[...] + vec[0:1, :]
        hidden[r, :] = h
        n2[r, :] = (rows_stats(h)[0] * vec[1:2, :] + vec[2:3, :]).astype(BF)

    def extra(i):
        @pl.when(i == chunks // 2)
        def _():
            up.forward()

        @pl.when(i == chunks - 1)
        def _():
            down.forward()

    product_scatter(at, Scatter(at, *sc[4:]), ctx, w_out, total, chunks, rows, epilogue, extra)
    up.finish()
    down.finish()


def attn_out(ctx, w_out, vec, x, up16, down16, n, n_grp, chunks):
    length, hw = ctx.shape
    width = x.shape[1]
    share = length // n
    rows = share // chunks
    hid = up16.shape[1]
    vm, hbm = pl.BlockSpec(memory_space=pltpu.VMEM), pl.BlockSpec(memory_space=pl.ANY)
    S = jax.ShapeDtypeStruct
    return pl.pallas_call(
        functools.partial(out_kernel, n=n, n_grp=n_grp, chunks=chunks, rows=rows),
        in_specs=[vm] * 3 + [hbm] * 3, out_specs=[vm] * 2 + [hbm] * 2,
        out_shape=[S((share, width), F32), S((share, width), BF), S((width, hid), BF), S((width, hid), BF)],
        scratch_shapes=[pltpu.VMEM((share, width), BF), pltpu.VMEM((rows, width), F32), pltpu.SemaphoreType.DMA((3,))]
                       + group_sems(n_grp) * 2 + scatter_scratch(chunks, n // 2, rows, width),
        compiler_params=pltpu.CompilerParams(collective_id=2, has_side_effects=True, vmem_limit_bytes=40 << 20),
        cost_estimate=pl.CostEstimate(flops=2 * length * hw * width, bytes_accessed=1 << 23, transcendentals=0),
        name="attn_out",
    )(ctx.reshape(n, share, hw), w_out, vec, x.reshape(n, share, width), up16, down16)


def front_kernel(x_hbm, w_qkv, w_out, w_up, w_down, vec, bias_hbm, proj, n1_hbm, w_attn, w_proj, up16, down16,
                 xbuf, n1, acc, bias, xsem, osem, bsem, *sc, n, n_grp, parts):
    at = Place(n)
    width, hw = w_attn.shape
    block = width // n_grp
    length = n1.shape[0]
    rows = length // parts
    heads = hw // (3 * HD)

    def fetch(i):
        slot = lax.rem(i, 2)
        return pltpu.make_async_copy(x_hbm.at[chunk_rows(i, rows), :], xbuf.at[slot], xsem.at[slot])

    def put(i):
        r = chunk_rows(i, rows)
        return pltpu.make_async_copy(n1.at[r, :], n1_hbm.at[r, :], osem)

    get_bias = pltpu.make_async_copy(bias_hbm.at[at.t], bias, bsem)
    get_bias.start()
    fetch(0).start()
    own = chunk_rows(at.g, block)
    w_attn[own, :] = w_qkv[...].astype(BF)
    bar = pltpu.get_barrier_semaphore()
    pl.semaphore_wait(bar, grp_signal(at, n_grp))
    qkv, out = GroupGather(at, n_grp, w_attn, *sc[:2]), GroupGather(at, n_grp, w_proj, *sc[2:])
    qkv.start()
    w_proj[own, :] = w_out[...].astype(BF)
    up16[...] = w_up[...].astype(BF)
    down16[...] = w_down[...].astype(BF)

    def norm(i):
        fetch(i).wait()

        @pl.when(i + 1 < parts)
        def _():
            fetch(i + 1).start()
        y = rows_stats(xbuf[lax.rem(i, 2)].astype(F32))[0] * vec[0:1, :] + vec[1:2, :]
        n1[chunk_rows(i, rows), :] = y.astype(BF)
        put(i).start()
    tiles(parts, norm)

    def partial(b, first=False, last=False):
        r = chunk_rows(b, block)

        def tile(i):
            m = chunk_rows(i, rows)
            y = dg(n1[m, r], w_attn[r, :], 1, 0)
            if not first:
                y = y + acc[m, :]
            acc[m, :] = y
        tiles(parts, tile)

    p, q, P = at.g // 2, lax.rem(at.g, 2), n_grp // 2
    partial(at.g, True)
    qkv.forward()
    out.start()
    partial(2 * p + 1 - q)
    for j in range(1, P):
        partial(2 * lax.rem(p + j, P) + q)
    out.forward()
    qkv.finish()
    for j in range(1, P):
        partial(2 * lax.rem(p + j, P) + 1 - q)
    get_bias.wait()

    def write(i):
        m = chunk_rows(i, rows)
        for h in range(heads):
            c = 3 * h * HD
            proj[m, c:c + HD] = (acc[m, c:c + HD] + bias[:, 2 * h * HD:(2 * h + 1) * HD]).astype(BF)
            c += HD
            proj[m, c:c + HD] = acc[m, c:c + HD].astype(BF)
            c += HD
            proj[m, c:c + HD] = (acc[m, c:c + HD] + bias[:, (2 * h + 1) * HD:(2 * h + 2) * HD]).astype(BF)
        put(i).wait()
    tiles(parts, write)
    out.finish()


def front(x, w_qkv, w_out, w_up, w_down, vec, b_qv, n, n_grp):
    length, width = x.shape
    block, hw = w_qkv.shape
    pw, hid = w_out.shape[1], w_up.shape[1]
    parts = length // TILE
    vm, hbm = pl.BlockSpec(memory_space=pltpu.VMEM), pl.BlockSpec(memory_space=pl.ANY)
    S, dma = jax.ShapeDtypeStruct, pltpu.SemaphoreType.DMA
    return pl.pallas_call(
        functools.partial(front_kernel, n=n, n_grp=n_grp, parts=parts),
        in_specs=[hbm] + [vm] * 5 + [hbm], out_specs=[vm, hbm] + [vm] * 4,
        out_shape=[S((length, hw), BF), S((length, width), BF), S((width, hw), BF), S((width, pw), BF),
                   S((block, hid), BF), S((block, hid), BF)],
        scratch_shapes=[pltpu.VMEM((2, length // parts, width), BF), pltpu.VMEM((length, width), BF),
                        pltpu.VMEM((length, hw), F32), pltpu.VMEM((1, b_qv.shape[0] // n), F32),
                        dma((2,)), dma, dma] + group_sems(n_grp) * 2,
        compiler_params=pltpu.CompilerParams(collective_id=5, has_side_effects=True, vmem_limit_bytes=50 << 20),
        cost_estimate=pl.CostEstimate(flops=2 * length * hw * width, bytes_accessed=1 << 24, transcendentals=0),
        name="front",
    )(x, w_qkv, w_out, w_up, w_down, vec, b_qv.reshape(n, 1, -1))


class AllSum:
    def __init__(self, at, n_grp, x, gbuf, tbuf, gs, gr, ts, tr):
        self.at, self.n_grp, self.x, self.gbuf, self.tbuf = at, n_grp, x, gbuf, tbuf
        self.gs, self.gr, self.ts, self.tr = gs, gr, ts, tr

    def over_grp(self, d):
        at = self.at
        return remote(self.x, self.gbuf.at[at.g], self.gs.at[d - 1], self.gr.at[d - 1],
                      (lax.rem(at.g + d, self.n_grp), at.t))

    def over_tp(self, d):
        at = self.at
        return remote(self.tbuf.at[at.t], self.tbuf.at[at.t], self.ts.at[d - 1], self.tr.at[d - 1],
                      (at.g, lax.rem(at.t + d, at.n)))

    def start(self):
        for d in range(1, self.n_grp):
            self.over_grp(d).start()
        self.gbuf[self.at.g] = self.x[...]

    def turn(self):
        for d in range(1, self.n_grp):
            self.over_grp(d).wait()
        total = self.gbuf[0]
        for i in range(1, self.n_grp):
            total = total + self.gbuf[i]
        self.tbuf[self.at.t] = total
        for d in range(1, self.at.n):
            self.over_tp(d).start()

    def finish(self):
        for d in range(1, self.at.n):
            self.over_tp(d).wait()

    def total(self, lo, hi):
        out = self.tbuf[0, lo:hi, :]
        for i in range(1, self.at.n):
            out = out + self.tbuf[i, lo:hi, :]
        return out


def all_sum_scratch(n_grp, n, shape):
    dma = pltpu.SemaphoreType.DMA
    return [pltpu.VMEM(shape, F32), pltpu.VMEM((n_grp,) + shape, F32), pltpu.VMEM((n,) + shape, F32),
            dma((n_grp - 1,)), dma((n_grp - 1,)), dma((n - 1,)), dma((n - 1,))]


def back_kernel(dproj, w_attn, n1_hbm, gw_proj, x_hbm, dh, gain, stats, up_sum,
                grad_x, g_attn, g_proj, sums, owned,
                n1, x_share, gw, got, got_proj, total, qv, ln_sum, nsem, ws, wr, ps, pr, *scratch, n, n_grp, chunks, rows):
    at = Place(n)
    width, hw = w_attn.shape
    block = width // n_grp
    per = block // TILE
    heads = hw // (3 * HD)
    hid = up_sum.shape[1]
    load = pltpu.make_async_copy(n1_hbm, n1, nsem.at[0])
    load.start()
    load_x = pltpu.make_async_copy(x_hbm.at[at.t], x_share, nsem.at[1])
    load_x.start()
    rs, early, late = Scatter(at, *scratch[:7]), AllSum(at, n_grp, *scratch[7:14]), AllSum(at, n_grp, *scratch[14:])
    bar = pltpu.get_barrier_semaphore()
    for d in range(1, n_grp):
        pl.semaphore_signal(bar, inc=1, device_id=(lax.rem(at.g + d, n_grp), at.t), device_id_type=MESH)
    for d in range(1, n):
        pl.semaphore_signal(bar, inc=1, device_id=(at.g, lax.rem(at.t + d, n)), device_id_type=MESH)
    pl.semaphore_wait(bar, n_grp + n - 2)

    def owner(k):
        return lax.rem(at.g + 1 + k, n_grp)

    def send(k):
        r = chunk_rows(owner(k), block)
        return remote(gw.at[r, :], got.at[k], ws.at[k], wr.at[k], (owner(k), at.t))

    def send_proj(k):
        r = chunk_rows(owner(k), block)
        return remote(gw_proj.at[r, :], got_proj.at[k], ps.at[k], pr.at[k], (owner(k), at.t))

    for k in range(n_grp - 1):
        send_proj(k).start()
    qv[...] = jnp.zeros_like(qv)
    ln_sum[...] = jnp.zeros_like(ln_sum)

    def product(c):
        lhs = dproj[:, chunk_rows(c, rows), :].reshape(n * rows, hw)
        qv[...] += jnp.sum(lhs.astype(F32), 0, keepdims=True)

        def tile(i):
            y = dg(lhs, w_attn[cols(i), :], 1, 1)
            rs.parts[:, :, :, cols(i)] = y.astype(BF).reshape(at.Z, 2, rows, TILE)
        tiles(width // TILE, tile)
        rs.start(c)

    def weights(i):
        k = i // per
        first = pl.multiple_of(owner(k) * block + lax.rem(i, per) * TILE, TILE)
        y = dg(n1[:, pl.ds(first, TILE)], dproj[...].reshape(-1, hw), 0, 0)

        @pl.when(k < n_grp - 1)
        def _():
            gw[pl.ds(first, TILE), :] = y.astype(BF)

            @pl.when(lax.rem(i, per) == per - 1)
            def _():
                send(k).start()

        @pl.when(k == n_grp - 1)
        def _():
            g_attn[cols(lax.rem(i, per)), :] = y

    def norm_grad(c):
        r = chunk_rows(c, rows)
        xhat, inverse = rows_stats(x_share[r, :].astype(F32))
        dn = total[...]
        e = dn * gain[...]
        inner = jnp.mean(e, -1, keepdims=True) + xhat * jnp.mean(e * xhat, -1, keepdims=True)
        grad_x[r, :] = dh[r, :] + inverse * (e - inner)
        ln_sum[0:1, :] += jnp.sum(dn * xhat, 0, keepdims=True)
        ln_sum[1:2, :] += jnp.sum(dn, 0, keepdims=True)

    load.wait()
    load_x.wait()

    def tick(i, carry):
        c = i - 1

        @pl.when(inside(c, chunks))
        def _():
            rs.meet(c)
            rs.hop(c, 1)

        @pl.when(inside(i, chunks))
        def _():
            product(i)

        @pl.when(inside(c, chunks))
        def _():
            rs.hop(c, 2)

        @pl.when(i < width // TILE)
        def _():
            weights(i)

        @pl.when(inside(c, chunks))
        def _():
            for h in range(3, at.Z):
                rs.hop(c, h)

        @pl.when(i == chunks)
        def _():
            early.x[...] = stats[...]
            early.x[4:5, 0:hid] = up_sum[...]
            for h in range(heads):
                for j, src in ((0, 3 * h), (1, 3 * h + 2)):
                    early.x[4:5, hid + (2 * h + j) * HD:hid + (2 * h + j + 1) * HD] = qv[:, src * HD:(src + 1) * HD]
            early.start()

        @pl.when(i == chunks + 1)
        def _():
            early.turn()
        e = i - 2

        @pl.when(inside(e, chunks))
        def _():
            rs.finish(e, total)
            norm_grad(e)
        return carry

    lax.fori_loop(0, chunks + 2, tick, 0)
    part = width // 4
    for j in range(4):
        late.x[j:j + 1, :] = ln_sum[0:1, j * part:(j + 1) * part]
        late.x[j + 4:j + 5, :] = ln_sum[1:2, j * part:(j + 1) * part]
    late.start()
    mine = chunk_rows(at.g, block)
    g_proj[...] = gw_proj[mine, :].astype(F32)
    for k in range(n_grp - 1):
        send(k).wait()
        send_proj(k).wait()
        g_attn[...] += got[k].astype(F32)
        g_proj[...] += got_proj[k].astype(F32)
    late.turn()
    early.finish()
    sums[0:4, :] = early.total(0, 4)
    owned[...] = early.tbuf[:, 4, :]
    late.finish()
    ln = late.total(0, 8)
    for j in range(4):
        sums[4:5, j * part:(j + 1) * part] = ln[j:j + 1, :]
        sums[5:6, j * part:(j + 1) * part] = ln[j + 4:j + 5, :]
    sums[6:8, :] = jnp.zeros_like(sums[6:8, :])


def project_back(dproj, w_attn, n1, gw_proj, x, dh, gain, stats, up_sum, n, n_grp, chunks):
    length, hw = dproj.shape
    width = w_attn.shape[0]
    share = length // n
    rows = share // chunks
    block = width // n_grp
    pw = gw_proj.shape[1]
    vm, hbm = pl.BlockSpec(memory_space=pltpu.VMEM), pl.BlockSpec(memory_space=pl.ANY)
    S, dma = jax.ShapeDtypeStruct, pltpu.SemaphoreType.DMA
    return pl.pallas_call(
        functools.partial(back_kernel, n=n, n_grp=n_grp, chunks=chunks, rows=rows),
        in_specs=[vm, vm, hbm, vm, hbm] + [vm] * 4, out_specs=[vm] * 5,
        out_shape=[S((share, width), F32), S((block, hw), F32), S((block, pw), F32), S((8, width), F32),
                   S((n, width), F32)],
        scratch_shapes=[pltpu.VMEM((length, width), BF), pltpu.VMEM((share, width), BF), pltpu.VMEM((width, hw), BF),
                        pltpu.VMEM((n_grp - 1, block, hw), BF), pltpu.VMEM((n_grp - 1, block, pw), BF),
                        pltpu.VMEM((rows, width), F32), pltpu.VMEM((1, hw), F32), pltpu.VMEM((8, width), F32), dma((2,))]
                       + [dma((n_grp - 1,))] * 4 + scatter_scratch(chunks, n // 2, rows, width)
                       + all_sum_scratch(n_grp, n, (8, width)) + all_sum_scratch(n_grp, n, (8, width // 4)),
        compiler_params=pltpu.CompilerParams(collective_id=4, has_side_effects=True, vmem_limit_bytes=50 << 20),
        cost_estimate=pl.CostEstimate(flops=4 * length * hw * width, bytes_accessed=1 << 24, transcendentals=0),
        name="project_back",
    )(dproj.reshape(n, share, hw), w_attn, n1, gw_proj, x.reshape(n, share, width), dh, gain, stats, up_sum)


def ffn_kernel(n2_hbm, gradb_hbm, bias_hbm, w_up, w_down, w_out, ctx, hidden, vec, tokens,
               gw_hbm, gwo, dctx, dh, res, stats, bsum,
               gat, acc_up, acc_down, gbuf, actb, dbb, total, gshare, b_up, keep, lsem, gsem, msem, *scratch, n, chunks, rows):
    at = Place(n)
    ag1, ag2 = Gather(at, gat, rows, *scratch[:4]), Gather(at, gat, rows, *scratch[4:8])
    rs, mlp = Scatter(at, *scratch[8:15]), Scatter(at, *scratch[15:])
    width, hid = w_up.shape
    m = n * rows

    load = pltpu.make_async_copy(n2_hbm, gat.at[at.t], lsem)
    load.start()
    load_g = pltpu.make_async_copy(gradb_hbm.at[at.t], gshare, msem.at[0])
    load_g.start()
    load_b = pltpu.make_async_copy(bias_hbm.at[at.t], b_up, msem.at[1])
    load_b.start()
    share = hidden.shape[0]

    def alive(ranks, first, c):
        shape = (ranks, rows, 1)
        place = ((first + lax.broadcasted_iota(jnp.int32, shape, 0)) * share + c * rows
                 + lax.broadcasted_iota(jnp.int32, shape, 1))
        return jnp.where(place < tokens[...].reshape(1, 1, 1), 1.0, 0.0).reshape(ranks * rows, 1)

    def fetch(c):
        slot = lax.rem(c, 2)
        return pltpu.make_async_copy(gradb_hbm.at[:, chunk_rows(c, rows), :], gbuf.at[slot], gsem.at[slot])

    fetch(0).start()
    acc_up[...] = jnp.zeros_like(acc_up)
    acc_down[...] = jnp.zeros_like(acc_down)
    stats[...] = jnp.zeros_like(stats)
    bsum[...] = jnp.zeros_like(bsum)
    load.wait()
    load_g.wait()
    load_b.wait()
    at.barrier()

    a0, a1 = 0.7978845608028654, 0.044715

    def wide(c):
        return gat[:, chunk_rows(c, rows), :].reshape(m, width)

    def forward(c):
        fetch(c).wait()

        @pl.when(c + 1 < chunks)
        def _():
            fetch(c + 1).start()
        slot = lax.rem(c, 2)
        keep[...] = alive(n, 0, c)

        def tile(i):
            v = dg(wide(c), w_up[:, cols(i)], 1, 0) + b_up[:, cols(i)]
            ga = dg(gbuf[slot].reshape(m, width), w_down[:, cols(i)], 1, 0)
            v2 = v * v
            th = jnp.tanh(a0 * (v + a1 * v2 * v))
            half = 0.5 * (1.0 + th)
            actb[:, cols(i)] = (v * half * keep[...]).astype(BF)
            slope = half + 0.5 * v * (1.0 - th * th) * (a0 * (1.0 + 3.0 * a1 * v2))
            db = (ga * slope * keep[...]).astype(BF)
            dbb[:, cols(i)] = db
            bsum[:, cols(i)] += jnp.sum(db.astype(F32), 0, keepdims=True)
        tiles(hid // TILE, tile)

    def back(c):
        def tile(i):
            y = dg(dbb[...], w_up[cols(i), :], 1, 1)
            rs.parts[:, :, :, cols(i)] = y.astype(BF).reshape(at.Z, 2, rows, TILE)
        tiles(width // TILE, tile)

    def down(c):
        def tile(i):
            y = dg(actb[...], w_down[cols(i), :], 1, 1)
            mlp.parts[:, :, :, cols(i)] = y.astype(BF).reshape(at.Z, 2, rows, TILE)
        tiles(width // TILE, tile)

    def weights(c):
        slot = lax.rem(c, 2)

        def tile(i):
            x = gat[:, chunk_rows(c, rows), cols(i)].reshape(m, TILE)
            acc_up[cols(i), :] += dg(x, dbb[...], 0, 0)
            y = gbuf[slot, :, :, cols(i)].reshape(m, TILE)
            acc_down[cols(i), :] += dg(y, actb[...], 0, 0)
        tiles(width // TILE, tile)

    def norm_grad(c):
        r = chunk_rows(c, rows)
        xhat, inverse = rows_stats(hidden[r, :])
        dn2 = total[...]
        e = dn2 * vec[0:1, :]
        inner = jnp.mean(e, -1, keepdims=True) + xhat * jnp.mean(e * xhat, -1, keepdims=True)
        grad = gshare[r, :].astype(F32) * alive(1, at.t, c)
        d = grad + inverse * (e - inner)
        dh[r, :] = d
        gat[at.t, r, :] = d.astype(BF)
        stats[0:1, :] += jnp.sum(dn2 * xhat, 0, keepdims=True)
        stats[1:2, :] += jnp.sum(dn2, 0, keepdims=True)
        stats[2:3, :] += jnp.sum(d, 0, keepdims=True)
        stats[3:4, :] += jnp.sum(grad, 0, keepdims=True)

    def heads(c):
        y = dg(wide(c), w_out[...], 1, 0)
        dctx[:, chunk_rows(c, rows), :] = y.astype(BF).reshape(n, rows, y.shape[1])

    def at_stage(c, fn):
        @pl.when(inside(c, chunks))
        def _():
            fn(c)

    def tick(i, carry):
        at_stage(i, ag1.start)
        at_stage(i - 3, rs.meet)
        for h in range(1, at.Z):
            at_stage(i - 3, lambda c: rs.hop(c, h))
            at_stage(i - 1, lambda c: ag1.hop(c, h))
            if h == 1:
                at_stage(i - 4, lambda c: mlp.hop(c, at.Z - 1))
                at_stage(i - 5, lambda c: ag2.hop(c, at.Z - 1))
                at_stage(i - 2, forward)
            else:
                if h == 2:
                    def served(c):
                        mlp.finish(c, total)
                        r = chunk_rows(c, rows)
                        res[r, :] = (alive(1, at.t, c) * (hidden[r, :] + total[...] + vec[1:2, :])).astype(BF)
                    at_stage(i - 4, served)
                    at_stage(i - 3, mlp.meet)
                at_stage(i - 3, lambda c: mlp.hop(c, h - 1))
                at_stage(i - 4, lambda c: ag2.hop(c, h - 1))
                if h == 2:
                    at_stage(i - 2, back)

                    def gathered(c):
                        ag2.finish(c)
                        heads(c)
                    at_stage(i - 5, gathered)

        def rest(c):
            weights(c)
            rs.start(c)
        at_stage(i - 2, rest)

        def reduced(c):
            rs.finish(c, total)
            norm_grad(c)
            ag2.start(c)
        at_stage(i - 3, reduced)
        at_stage(i - 1, ag1.finish)

        def send_mlp(c):
            down(c)
            mlp.start(c)
        at_stage(i - 2, send_mlp)

        @pl.when(i == chunks + 2)
        def _():
            tiles(width // m, store)
        return carry

    def store(i):
        r = cols(i, m)
        actb[...] = acc_up[r, :].astype(BF)
        one = pltpu.make_async_copy(actb, gw_hbm.at[r, pl.ds(0, hid)], lsem)
        one.start()
        dbb[...] = acc_down[r, :].astype(BF)
        two = pltpu.make_async_copy(dbb, gw_hbm.at[r, pl.ds(hid, hid)], msem.at[0])
        two.start()
        one.wait()
        two.wait()

    lax.fori_loop(0, chunks + 5, tick, 0)

    def final(i):
        x = gat[:, :, cols(i)].reshape(-1, TILE)
        gwo[cols(i), :] = dg(x, ctx[...], 0, 0).astype(BF)
    tiles(width // TILE, final)


def feed_forward(n2, gradb, b_up, w_up, w_down, w_out, ctx, hidden, vec, tokens, n, chunks):
    length, width = gradb.shape
    hid, hw = w_up.shape[1], w_out.shape[1]
    share = length // n
    rows = share // chunks
    Z = n // 2
    vm, hbm = pl.BlockSpec(memory_space=pltpu.VMEM), pl.BlockSpec(memory_space=pl.ANY)
    S = jax.ShapeDtypeStruct
    m = n * rows
    return pl.pallas_call(
        functools.partial(ffn_kernel, n=n, chunks=chunks, rows=rows),
        in_specs=[hbm] * 3 + [vm] * 7,
        out_specs=[hbm] + [vm] * 6,
        out_shape=[S((width, 2 * hid), BF), S((width, hw), BF), S((n, share, hw), BF), S((share, width), F32),
                   S((share, width), BF), S((8, width), F32), S((1, hid), F32)],
        scratch_shapes=[pltpu.VMEM((n, share, width), BF), pltpu.VMEM((width, hid), F32), pltpu.VMEM((width, hid), F32),
                        pltpu.VMEM((2, n, rows, width), BF),
                        pltpu.VMEM((m, hid), BF), pltpu.VMEM((m, hid), BF), pltpu.VMEM((rows, width), F32),
                        pltpu.VMEM((share, width), BF), pltpu.VMEM((1, hid), F32), pltpu.VMEM((m, 1), F32),
                        pltpu.SemaphoreType.DMA, pltpu.SemaphoreType.DMA((2,)), pltpu.SemaphoreType.DMA((2,))]
                       + gather_sems(chunks, Z) + gather_sems(chunks, Z) + scatter_scratch(chunks, Z, rows, width) * 2,
        compiler_params=pltpu.CompilerParams(collective_id=3, has_side_effects=True, vmem_limit_bytes=62 << 20),
        cost_estimate=pl.CostEstimate(flops=12 * length * hid * width, bytes_accessed=1 << 26, transcendentals=0),
        name="feed_forward",
    )(n2, gradb.reshape(n, share, width), b_up.reshape(n, 1, hid), w_up, w_down, w_out, ctx, hidden, vec, tokens)


def on_device(layer_input, out_cotangent, seq_group, seq_len, w_qkv, b_qv, w_out, b_out, w_up, b_up,
              w_down, b_down, first_norm_gain, first_norm_bias, second_norm_gain, second_norm_bias):
    n_tp, n_grp = lax.axis_size("tp"), lax.axis_size("grp")
    grp = lax.axis_index("grp")
    length, width = layer_input.shape
    hid, qv = w_up.shape[1], b_qv.shape[0] // n_tp

    proj, n1, w_attn, w_proj, up16, down16 = front(
        layer_input, w_qkv, w_out, w_up, w_down, jnp.stack([first_norm_gain, first_norm_bias]), b_qv, n_tp, n_grp)
    context, lse = attn_fwd(seq_group, seq_len, proj)
    hidden, n2, w_expand, w_reduce = attn_out(
        context, w_proj, jnp.stack([b_out, second_norm_gain, second_norm_bias]), layer_input, up16, down16,
        n_tp, n_grp, 8)
    tokens = jnp.sum(jnp.where(seq_group == grp, seq_len, 0)).reshape(1, 1)
    gw_ffn, gw_proj, dcontext, dh, result, stats, up_sum = feed_forward(
        n2, out_cotangent, b_up, w_expand, w_reduce, w_proj, context, hidden,
        jnp.stack([second_norm_gain, b_down]), tokens, n_tp, 8)
    grads_ffn = lax.psum_scatter(gw_ffn, "grp", scatter_dimension=0, tiled=True).astype(F32)
    grads_expand, grads_reduce = grads_ffn[:, :hid], grads_ffn[:, hid:]

    dproj = attn_bwd(seq_group, seq_len, proj, context, dcontext.reshape(length, -1), lse)
    grad_x, grads_attn, grads_proj, sums, owned = project_back(
        dproj, w_attn, n1, gw_proj, layer_input, dh, first_norm_gain[None], stats, up_sum, n_tp, n_grp, 8)
    return (result, grad_x, grads_attn, owned[:, hid:hid + qv].reshape(-1), grads_proj, sums[2],
            grads_expand, owned[:, :hid].reshape(-1), grads_reduce, sums[3], sums[4], sums[5],
            sums[0], sums[1])


def solution(mesh):
    rows, both, flat = P("grp", None), P("grp", "tp"), P()
    in_specs = (rows, rows, flat, flat, both, flat, both, flat, both, flat, both, flat, flat, flat, flat, flat)
    spread = P(("grp", "tp"), None)
    out_specs = (spread, spread, both, flat, both, flat, both, flat, both, flat, flat, flat, flat, flat)
    return jax.shard_map(on_device, mesh=mesh, in_specs=in_specs, out_specs=out_specs, check_vma=False)
```

```python
import functools

import jax
import jax.numpy as jnp
from jax import lax
from jax.experimental import pallas as pl
from jax.experimental.pallas import tpu as pltpu
from jax.sharding import PartitionSpec as P

HD = 128
BLK=512
F32=jnp.float32
BF=jnp.bfloat16
LOG2E=1.4426950408889634

def dg(a,b,ca,cb):
    return lax.dot_general(a,b,(((ca,),(cb,)),((),())),preferred_element_type=F32)


def block_info(grps, lens, nb, seqs):
    g = lax.axis_index("grp")
    found = [[jnp.int32(0), jnp.int32(0), jnp.int32(0)] for _ in range(nb)]
    start = jnp.int32(0)
    for s in range(seqs):
        count = jnp.where(grps[s] == g, lens[s] // BLK, 0)
        for b in range(nb):
            hit = (start <= b) & (b < start + count)
            found[b] = [jnp.where(hit, start, found[b][0]), jnp.where(hit, start + count - 1, found[b][1]),
                        jnp.where(hit, 1, found[b][2])]
        start = start + count
    return found


def below(shape):
    return lax.broadcasted_iota(jnp.int32, shape, 0) <= lax.broadcasted_iota(jnp.int32, shape, 1)


def attn_fwd_kernel(grps, lens, proj, o_ref, lse_ref, *, nb, seqs, heads):
    info = block_info(grps, lens, nb, seqs)
    c = HD ** -0.5 * LOG2E

    def attend(qi, first):
        rows = slice(qi * BLK, (qi + 1) * BLK)
        early = slice(first * BLK, qi * BLK)
        for h in range(heads):
            col = 3 * h * HD
            q = proj[rows, col:col + HD]
            pieces = [(rows, jnp.where(below((BLK, BLK)), dg(proj[rows, col + HD:col + 2 * HD], q, 1, 1), -1e30))]
            if first < qi:
                pieces.append((early, dg(proj[early, col + HD:col + 2 * HD], q, 1, 1)))
            top = functools.reduce(jnp.maximum, [jnp.max(s, 0, keepdims=True) for _, s in pieces]) * c
            total, acc = 0.0, 0.0
            for keys, s in pieces:
                p = jnp.exp2(s * c - top)
                total = total + jnp.sum(p, 0, keepdims=True)
                acc = acc + dg(proj[keys, col + 2 * HD:col + 3 * HD], p.astype(BF), 0, 0)
            o_ref[rows, h * HD:(h + 1) * HD] = jnp.transpose(acc / total).astype(BF)
            lse_ref[h, :, rows] = top + jnp.log2(total)

    for qi in range(nb):
        for first in range(qi + 1):
            @pl.when((info[qi][2] > 0) & (info[qi][0] == first))
            def _():
                attend(qi, first)

        @pl.when(info[qi][2] <= 0)
        def _():
            o_ref[qi * BLK:(qi + 1) * BLK, :] = jnp.zeros((BLK, heads * HD), BF)
            lse_ref[:, :, qi * BLK:(qi + 1) * BLK] = jnp.zeros((heads, 1, BLK), F32)


def attn_fwd(grps, lens, proj):
    length = proj.shape[0]; heads = proj.shape[1]//(3*HD); nb = length//BLK
    vm, sm = pl.BlockSpec(memory_space=pltpu.VMEM), pl.BlockSpec(memory_space=pltpu.SMEM)
    return pl.pallas_call(functools.partial(attn_fwd_kernel, nb=nb, seqs=grps.shape[0], heads=heads),
        in_specs=[sm, sm, vm], out_specs=[vm, vm],
        out_shape=[jax.ShapeDtypeStruct((length, heads*HD), BF), jax.ShapeDtypeStruct((heads, 1, length), F32)],
        compiler_params=pltpu.CompilerParams(vmem_limit_bytes=40<<20), name="attn_fwd",
        cost_estimate=pl.CostEstimate(flops=heads*length*length*HD*2, bytes_accessed=length*heads*HD*8, transcendentals=heads*length*length//2),
    )(grps, lens, proj)


def attn_bwd_kernel(grps, lens, proj, o_ref, do_ref, lse_ref, dp_ref, dq_sc, dl_sc, *, nb, seqs, heads):
    info = block_info(grps, lens, nb, seqs)
    scale = HD ** -0.5
    c = scale * LOG2E
    for h in range(heads):
        hc = slice(h * HD, (h + 1) * HD)
        prod = do_ref[:, hc].astype(F32) * o_ref[:, hc].astype(F32)
        dl_sc[h] = jnp.sum(jnp.transpose(prod), 0, keepdims=True)
    dq_sc[...] = jnp.zeros_like(dq_sc)

    def attend(j, last):
        keys = slice(j * BLK, (j + 1) * BLK)
        for h in range(heads):
            col = 3 * h * HD
            hc = slice(h * HD, (h + 1) * HD)
            k, v = proj[keys, col + HD:col + 2 * HD], proj[keys, col + 2 * HD:col + 3 * HD]
            dk, dv = 0.0, 0.0
            for diag in (True, False):
                rows = keys if diag else slice((j + 1) * BLK, (last + 1) * BLK)
                if rows.start == rows.stop:
                    continue
                q, do = proj[rows, col:col + HD], do_ref[rows, hc]
                p = jnp.exp2(dg(k, q, 1, 1) * c - lse_ref[h, :, rows])
                if diag:
                    p = jnp.where(below((BLK, BLK)), p, 0.0)
                ds = (p * (dg(v, do, 1, 1) - dl_sc[h, :, rows])).astype(BF)
                dv = dv + dg(p.astype(BF), do, 1, 0)
                dk = dk + dg(ds, q, 1, 0)
                dq_sc[h, :, rows] += dg(k, ds, 0, 0)
            dp_ref[keys, col + HD:col + 2 * HD] = (dk * scale).astype(BF)
            dp_ref[keys, col + 2 * HD:col + 3 * HD] = dv.astype(BF)

    for j in range(nb):
        for last in range(j, nb):
            @pl.when((info[j][2] > 0) & (info[j][1] == last))
            def _():
                attend(j, last)

        @pl.when(info[j][2] <= 0)
        def _():
            dp_ref[j * BLK:(j + 1) * BLK, :] = jnp.zeros((BLK, heads * 3 * HD), BF)
    for h in range(heads):
        dp_ref[:, 3 * h * HD:(3 * h + 1) * HD] = jnp.transpose(dq_sc[h] * scale).astype(BF)


def attn_bwd(grps, lens, proj, ctx, dctx, lse):
    length = proj.shape[0]; heads = proj.shape[1]//(3*HD); nb = length//BLK
    vm, sm = pl.BlockSpec(memory_space=pltpu.VMEM), pl.BlockSpec(memory_space=pltpu.SMEM)
    return pl.pallas_call(functools.partial(attn_bwd_kernel, nb=nb, seqs=grps.shape[0], heads=heads),
        in_specs=[sm, sm] + [vm]*4, out_specs=vm,
        scratch_shapes=[pltpu.VMEM((heads, HD, length), F32), pltpu.VMEM((heads, 1, length), F32)],
        out_shape=jax.ShapeDtypeStruct((length, heads*3*HD), BF),
        compiler_params=pltpu.CompilerParams(vmem_limit_bytes=40<<20), name="attn_bwd",
        cost_estimate=pl.CostEstimate(flops=heads*length*length*HD*5, bytes_accessed=length*heads*HD*16, transcendentals=heads*length*length//2),
    )(grps, lens, proj, ctx, dctx, lse)


MESH = pl.DeviceIdType.MESH
TILE = 256


class Place:
    def __init__(self, n_tp):
        self.g = lax.axis_index("grp")
        t = lax.axis_index("tp")
        self.t, self.n, self.Z = t, n_tp, n_tp // 2
        self.z, self.k = t // 2, lax.rem(t, 2)
        self.right, self.left, self.sib = (self.g, t + 2), (self.g, t - 2), (self.g, t + 1 - 2 * self.k)
        self.has_right, self.has_left = self.z < self.Z - 1, self.z > 0

    def barrier(self, n_grp=0):
        bar = pltpu.get_barrier_semaphore()
        extra = grp_signal(self, n_grp) if n_grp else 0
        pl.semaphore_signal(bar, inc=1, device_id=self.sib, device_id_type=MESH)

        @pl.when(self.has_right)
        def _():
            pl.semaphore_signal(bar, inc=1, device_id=self.right, device_id_type=MESH)

        @pl.when(self.has_left)
        def _():
            pl.semaphore_signal(bar, inc=1, device_id=self.left, device_id_type=MESH)

        amount = 1 + extra + jnp.where(self.has_right, 1, 0) + jnp.where(self.has_left, 1, 0)
        pl.semaphore_wait(bar, amount)


def remote(src, dst, ssem, rsem, device):
    return pltpu.make_async_remote_copy(src, dst, ssem, rsem, device_id=device, device_id_type=MESH)


class Gather:
    def __init__(self, at, gat, rows, ls, lr, ss, sr):
        self.at, self.gat, self.rows = at, gat, rows
        self.ls, self.lr, self.ss, self.sr = ls, lr, ss, sr

    def block(self, zz, kk, c):
        return self.gat.at[2 * zz + kk, pl.ds(pl.multiple_of(c * self.rows, self.rows), self.rows), :]

    def line(self, c, side, d):
        at = self.at
        sign, device = (-1, at.right) if side == 0 else (1, at.left)
        b = self.block(at.z + sign * (d - 1), at.k, c)
        return remote(b, b, self.ls.at[c, side, d - 1], self.lr.at[c, side, d - 1], device)

    def line_in(self, c, side, d):
        at = self.at
        sign, device = (-1, at.right) if side == 0 else (1, at.left)
        b = self.block(at.z + sign * d, at.k, c)
        return remote(b, b, self.ls.at[c, side, d - 1], self.lr.at[c, side, d - 1], device)

    def across(self, c, zz):
        b = self.block(zz, self.at.k, c)
        return remote(b, b, self.ss.at[c, zz], self.sr.at[c, zz], self.at.sib)

    def across_in(self, c, zz):
        b = self.block(zz, 1 - self.at.k, c)
        return remote(b, b, self.ss.at[c, zz], self.sr.at[c, zz], self.at.sib)

    def start(self, c):
        at = self.at

        @pl.when(at.has_right)
        def _():
            self.line(c, 0, 1).start()

        @pl.when(at.has_left)
        def _():
            self.line(c, 1, 1).start()

        self.across(c, at.z).start()

    def hop(self, c, d):
        at = self.at

        @pl.when(at.z >= d)
        def _():
            self.line_in(c, 0, d).wait_recv()
            if d < at.Z - 1:
                @pl.when(at.has_right)
                def _():
                    self.line(c, 0, d + 1).start()
            self.across(c, at.z - d).start()

        @pl.when(at.z + d <= at.Z - 1)
        def _():
            self.line_in(c, 1, d).wait_recv()
            if d < at.Z - 1:
                @pl.when(at.has_left)
                def _():
                    self.line(c, 1, d + 1).start()
            self.across(c, at.z + d).start()

    def finish(self, c):
        at = self.at
        for zz in range(at.Z):
            self.across_in(c, zz).wait_recv()
            self.across(c, zz).wait_send()
        for d in range(1, at.Z):
            @pl.when(at.has_right & (at.z >= d - 1))
            def _():
                self.line(c, 0, d).wait_send()

            @pl.when(at.has_left & (at.z + d - 1 <= at.Z - 1))
            def _():
                self.line(c, 1, d).wait_send()


class Scatter:
    def __init__(self, at, parts, pair, hops, cs, cr, hs, hr):
        self.at, self.parts, self.pair, self.hops = at, parts, pair, hops
        self.slots = pair.shape[0]
        self.cs, self.cr, self.hs, self.hr = cs, cr, hs, hr

    def across(self, c):
        c = lax.rem(c, self.slots)
        return remote(self.parts.at[:, 1 - self.at.k], self.pair.at[c], self.cs.at[c], self.cr.at[c], self.at.sib)

    def line(self, c, side, h, target):
        c = lax.rem(c, self.slots)
        device = self.at.right if side == 0 else self.at.left
        return remote(self.pair.at[c, target], self.hops.at[side, c, h - 1],
                      self.hs.at[c, side, h - 1], self.hr.at[c, side, h - 1], device)

    def start(self, c):
        self.across(c).start()

    def meet(self, c):
        self.across(c).wait()
        own = self.parts[:, pl.ds(self.at.k, 1)]
        own = own.reshape(own.shape[0], own.shape[2], own.shape[3])
        c = lax.rem(c, self.slots)
        self.pair[c] = (self.pair[c].astype(F32) + own.astype(F32)).astype(BF)

    def hop(self, c, h):
        at = self.at
        for side in (0, 1):
            pos = at.z if side == 0 else at.Z - 1 - at.z
            target = at.z + at.Z - h if side == 0 else at.z - at.Z + h

            @pl.when((pos <= h - 1) & (pos < at.Z - 1))
            def _():
                if h >= 2:
                    @pl.when(pos >= 1)
                    def _():
                        self.line(c, side, h - 1, target).wait_recv()
                        b = lax.rem(c, self.slots)
                        self.pair[b, target] = (self.pair[b, target].astype(F32)
                                                + self.hops[side, b, h - 2].astype(F32)).astype(BF)
                self.line(c, side, h, target).start()

    def finish(self, c, total):
        at = self.at
        b = lax.rem(c, self.slots)
        total[...] = self.pair[b, at.z].astype(F32)
        for side in (0, 1):
            pos = at.z if side == 0 else at.Z - 1 - at.z

            @pl.when(pos >= 1)
            def _():
                self.line(c, side, at.Z - 1, at.z).wait_recv()
                total[...] += self.hops[side, b, at.Z - 2].astype(F32)

            for h in range(1, at.Z):
                @pl.when((pos <= h - 1) & (pos < at.Z - 1))
                def _():
                    self.line(c, side, h, at.z).wait_send()


class GroupGather:
    def __init__(self, at, n_grp, full, ss, sr):
        self.at, self.full, self.ss, self.sr = at, full, ss, sr
        self.P = n_grp // 2
        self.size = full.shape[0] // n_grp
        self.p, self.q = at.g // 2, lax.rem(at.g, 2)
        self.partner = (at.g + 1 - 2 * self.q, at.t)

    def peer(self, j):
        return lax.rem(self.p + j, self.P)

    def rows(self, p, q, half=None):
        size = self.size if half is None else self.size // 2
        first = (2 * p + q) * self.size + (size if half == 1 else 0)
        return self.full.at[pl.ds(pl.multiple_of(first, size), size), :]

    def copy(self, kind, j, incoming=False):
        p, q = self.p, self.q
        src = lax.rem(p + self.P - j, self.P)
        if kind == 0:
            b, k, dev = self.rows(p, 1 - q if incoming else q), 0, self.partner
        elif kind == 1:
            b, k, dev = self.rows(src if incoming else p, q), j, (2 * self.peer(j) + q, self.at.t)
        elif kind == 2:
            b, k = self.rows(src if incoming else p, 1 - q, 1), self.P - 1 + j
            dev = (2 * self.peer(j) + q, self.at.t)
        else:
            b, k = self.rows(src, 1 - q if incoming else q, 0), 2 * (self.P - 1) + j
            dev = self.partner
        return remote(b, b, self.ss.at[k], self.sr.at[k], dev)

    def start(self):
        self.copy(0, 0).start()
        for j in range(1, self.P):
            self.copy(1, j).start()

    def forward(self):
        self.copy(0, 0, True).wait_recv()
        for j in range(1, self.P):
            self.copy(2, j).start()
        for j in range(1, self.P):
            self.copy(1, j, True).wait_recv()
            self.copy(3, j).start()

    def finish(self):
        for j in range(1, self.P):
            for kind in (2, 3):
                self.copy(kind, j, True).wait_recv()
                self.copy(kind, j).wait_send()
            self.copy(1, j).wait_send()
        self.copy(0, 0).wait_send()


def group_sems(n_grp):
    k = 1 + 3 * (n_grp // 2 - 1)
    return [pltpu.SemaphoreType.DMA((k,)), pltpu.SemaphoreType.DMA((k,))]


def grp_signal(at, n_grp):
    bar = pltpu.get_barrier_semaphore()
    p, q = at.g // 2, lax.rem(at.g, 2)
    pl.semaphore_signal(bar, inc=1, device_id=(at.g + 1 - 2 * q, at.t), device_id_type=MESH)
    for j in range(1, n_grp // 2):
        pl.semaphore_signal(bar, inc=1, device_id=(2 * lax.rem(p + j, n_grp // 2) + q, at.t), device_id_type=MESH)
    return n_grp // 2


def gather_sems(chunks, Z):
    dma = pltpu.SemaphoreType.DMA
    return [dma((chunks, 2, Z - 1)), dma((chunks, 2, Z - 1)), dma((chunks, Z)), dma((chunks, Z))]


def scatter_scratch(chunks, Z, rows, width):
    chunks = min(chunks, 4)
    dma = pltpu.SemaphoreType.DMA
    return [pltpu.VMEM((Z, 2, rows, width), BF), pltpu.VMEM((chunks, Z, rows, width), BF),
            pltpu.VMEM((2, chunks, Z - 1, rows, width), BF),
            dma((chunks,)), dma((chunks,)), dma((chunks, 2, Z - 1)), dma((chunks, 2, Z - 1))]


def inside(c, chunks):
    return (c >= 0) & (c < chunks)


def chunk_rows(c, rows):
    return pl.ds(pl.multiple_of(c * rows, rows), rows)


def tiles(count, body):
    def step(i, carry):
        body(i)
        return carry
    lax.fori_loop(0, count, step, 0)


def cols(i, size=TILE):
    return pl.ds(pl.multiple_of(i * size, size), size)


def rows_stats(rows):
    mean = jnp.mean(rows, -1, keepdims=True)
    centred = rows - mean
    inverse = lax.rsqrt(jnp.mean(centred * centred, -1, keepdims=True) + 1e-05)
    return centred * inverse, inverse


def product_scatter(at, rs, lhs_ref, w_ref, total, chunks, rows, epilogue, extra):
    def product(c):
        lhs = lhs_ref[:, chunk_rows(c, rows), :].reshape(at.n * rows, lhs_ref.shape[2])

        def tile(i):
            y = dg(lhs, w_ref[cols(i), :], 1, 1)
            rs.parts[:, :, :, cols(i)] = y.astype(BF).reshape(at.Z, 2, rows, TILE)
        tiles(w_ref.shape[0] // TILE, tile)
        rs.start(c)

    def tick(i, carry):
        c = i - 1

        @pl.when(inside(c, chunks))
        def _():
            rs.meet(c)
            rs.hop(c, 1)

        @pl.when(inside(i, chunks))
        def _():
            product(i)

        @pl.when(inside(c, chunks))
        def _():
            for h in range(2, at.Z):
                rs.hop(c, h)

        e = i - 2

        @pl.when(inside(e, chunks))
        def _():
            rs.finish(e, total)
            epilogue(e)
        extra(i)
        return carry

    lax.fori_loop(0, chunks + 2, tick, 0)


def out_kernel(ctx, w_out, vec, x_hbm, up16, down16, hidden, n2, up_hbm, down_hbm,
               x_share, total, lsem, *sc, n, n_grp, chunks, rows):
    at = Place(n)
    load = pltpu.make_async_copy(x_hbm.at[at.t], x_share, lsem.at[0])
    load.start()
    up, down = GroupGather(at, n_grp, up_hbm, *sc[:2]), GroupGather(at, n_grp, down_hbm, *sc[2:4])
    own = chunk_rows(at.g, up.size)
    put_up = pltpu.make_async_copy(up16, up_hbm.at[own, :], lsem.at[1])
    put_down = pltpu.make_async_copy(down16, down_hbm.at[own, :], lsem.at[2])
    put_up.start()
    put_down.start()
    at.barrier(n_grp)
    load.wait()
    put_up.wait()
    put_down.wait()
    up.start()
    down.start()

    def epilogue(c):
        r = chunk_rows(c, rows)
        h = x_share[r, :].astype(F32) + total[...] + vec[0:1, :]
        hidden[r, :] = h
        n2[r, :] = (rows_stats(h)[0] * vec[1:2, :] + vec[2:3, :]).astype(BF)

    def extra(i):
        @pl.when(i == chunks // 2)
        def _():
            up.forward()

        @pl.when(i == chunks - 1)
        def _():
            down.forward()

    product_scatter(at, Scatter(at, *sc[4:]), ctx, w_out, total, chunks, rows, epilogue, extra)
    up.finish()
    down.finish()


def attn_out(ctx, w_out, vec, x, up16, down16, n, n_grp, chunks):
    length, hw = ctx.shape
    width = x.shape[1]
    share = length // n
    rows = share // chunks
    hid = up16.shape[1]
    vm, hbm = pl.BlockSpec(memory_space=pltpu.VMEM), pl.BlockSpec(memory_space=pl.ANY)
    S = jax.ShapeDtypeStruct
    return pl.pallas_call(
        functools.partial(out_kernel, n=n, n_grp=n_grp, chunks=chunks, rows=rows),
        in_specs=[vm] * 3 + [hbm] * 3, out_specs=[vm] * 2 + [hbm] * 2,
        out_shape=[S((share, width), F32), S((share, width), BF), S((width, hid), BF), S((width, hid), BF)],
        scratch_shapes=[pltpu.VMEM((share, width), BF), pltpu.VMEM((rows, width), F32), pltpu.SemaphoreType.DMA((3,))]
                       + group_sems(n_grp) * 2 + scatter_scratch(chunks, n // 2, rows, width),
        compiler_params=pltpu.CompilerParams(collective_id=2, has_side_effects=True, vmem_limit_bytes=40 << 20),
        cost_estimate=pl.CostEstimate(flops=2 * length * hw * width, bytes_accessed=1 << 23, transcendentals=0),
        name="attn_out",
    )(ctx.reshape(n, share, hw), w_out, vec, x.reshape(n, share, width), up16, down16)


def front_kernel(x_hbm, w_qkv, w_out, w_up, w_down, vec, bias_hbm, proj, n1_hbm, w_attn, w_proj, up16, down16,
                 xbuf, n1, acc, bias, xsem, osem, bsem, *sc, n, n_grp, parts):
    at = Place(n)
    width, hw = w_attn.shape
    block = width // n_grp
    length = n1.shape[0]
    rows = length // parts
    heads = hw // (3 * HD)

    def fetch(i):
        slot = lax.rem(i, 2)
        return pltpu.make_async_copy(x_hbm.at[chunk_rows(i, rows), :], xbuf.at[slot], xsem.at[slot])

    def put(i):
        r = chunk_rows(i, rows)
        return pltpu.make_async_copy(n1.at[r, :], n1_hbm.at[r, :], osem)

    get_bias = pltpu.make_async_copy(bias_hbm.at[at.t], bias, bsem)
    get_bias.start()
    fetch(0).start()
    own = chunk_rows(at.g, block)
    w_attn[own, :] = w_qkv[...].astype(BF)
    bar = pltpu.get_barrier_semaphore()
    pl.semaphore_wait(bar, grp_signal(at, n_grp))
    qkv, out = GroupGather(at, n_grp, w_attn, *sc[:2]), GroupGather(at, n_grp, w_proj, *sc[2:])
    qkv.start()
    w_proj[own, :] = w_out[...].astype(BF)
    up16[...] = w_up[...].astype(BF)
    down16[...] = w_down[...].astype(BF)

    def norm(i):
        fetch(i).wait()

        @pl.when(i + 1 < parts)
        def _():
            fetch(i + 1).start()
        y = rows_stats(xbuf[lax.rem(i, 2)].astype(F32))[0] * vec[0:1, :] + vec[1:2, :]
        n1[chunk_rows(i, rows), :] = y.astype(BF)
        put(i).start()
    tiles(parts, norm)

    def partial(b, first=False, last=False):
        r = chunk_rows(b, block)

        def tile(i):
            m = chunk_rows(i, rows)
            y = dg(n1[m, r], w_attn[r, :], 1, 0)
            if not first:
                y = y + acc[m, :]
            acc[m, :] = y
        tiles(parts, tile)

    p, q, P = at.g // 2, lax.rem(at.g, 2), n_grp // 2
    partial(at.g, True)
    qkv.forward()
    out.start()
    partial(2 * p + 1 - q)
    for j in range(1, P):
        partial(2 * lax.rem(p + j, P) + q)
    out.forward()
    qkv.finish()
    for j in range(1, P):
        partial(2 * lax.rem(p + j, P) + 1 - q)
    get_bias.wait()

    def write(i):
        m = chunk_rows(i, rows)
        for h in range(heads):
            c = 3 * h * HD
            proj[m, c:c + HD] = (acc[m, c:c + HD] + bias[:, 2 * h * HD:(2 * h + 1) * HD]).astype(BF)
            c += HD
            proj[m, c:c + HD] = acc[m, c:c + HD].astype(BF)
            c += HD
            proj[m, c:c + HD] = (acc[m, c:c + HD] + bias[:, (2 * h + 1) * HD:(2 * h + 2) * HD]).astype(BF)
        put(i).wait()
    tiles(parts, write)
    out.finish()


def front(x, w_qkv, w_out, w_up, w_down, vec, b_qv, n, n_grp):
    length, width = x.shape
    block, hw = w_qkv.shape
    pw, hid = w_out.shape[1], w_up.shape[1]
    parts = length // TILE
    vm, hbm = pl.BlockSpec(memory_space=pltpu.VMEM), pl.BlockSpec(memory_space=pl.ANY)
    S, dma = jax.ShapeDtypeStruct, pltpu.SemaphoreType.DMA
    return pl.pallas_call(
        functools.partial(front_kernel, n=n, n_grp=n_grp, parts=parts),
        in_specs=[hbm] + [vm] * 5 + [hbm], out_specs=[vm, hbm] + [vm] * 4,
        out_shape=[S((length, hw), BF), S((length, width), BF), S((width, hw), BF), S((width, pw), BF),
                   S((block, hid), BF), S((block, hid), BF)],
        scratch_shapes=[pltpu.VMEM((2, length // parts, width), BF), pltpu.VMEM((length, width), BF),
                        pltpu.VMEM((length, hw), F32), pltpu.VMEM((1, b_qv.shape[0] // n), F32),
                        dma((2,)), dma, dma] + group_sems(n_grp) * 2,
        compiler_params=pltpu.CompilerParams(collective_id=5, has_side_effects=True, vmem_limit_bytes=50 << 20),
        cost_estimate=pl.CostEstimate(flops=2 * length * hw * width, bytes_accessed=1 << 24, transcendentals=0),
        name="front",
    )(x, w_qkv, w_out, w_up, w_down, vec, b_qv.reshape(n, 1, -1))


class AllSum:
    def __init__(self, at, n_grp, x, gbuf, tbuf, gs, gr, ts, tr):
        self.at, self.n_grp, self.x, self.gbuf, self.tbuf = at, n_grp, x, gbuf, tbuf
        self.gs, self.gr, self.ts, self.tr = gs, gr, ts, tr

    def over_grp(self, d):
        at = self.at
        return remote(self.x, self.gbuf.at[at.g], self.gs.at[d - 1], self.gr.at[d - 1],
                      (lax.rem(at.g + d, self.n_grp), at.t))

    def over_tp(self, d):
        at = self.at
        return remote(self.tbuf.at[at.t], self.tbuf.at[at.t], self.ts.at[d - 1], self.tr.at[d - 1],
                      (at.g, lax.rem(at.t + d, at.n)))

    def start(self):
        for d in range(1, self.n_grp):
            self.over_grp(d).start()
        self.gbuf[self.at.g] = self.x[...]

    def turn(self):
        for d in range(1, self.n_grp):
            self.over_grp(d).wait()
        total = self.gbuf[0]
        for i in range(1, self.n_grp):
            total = total + self.gbuf[i]
        self.tbuf[self.at.t] = total
        for d in range(1, self.at.n):
            self.over_tp(d).start()

    def finish(self):
        for d in range(1, self.at.n):
            self.over_tp(d).wait()

    def total(self, lo, hi):
        out = self.tbuf[0, lo:hi, :]
        for i in range(1, self.at.n):
            out = out + self.tbuf[i, lo:hi, :]
        return out


def all_sum_scratch(n_grp, n, shape):
    dma = pltpu.SemaphoreType.DMA
    return [pltpu.VMEM(shape, F32), pltpu.VMEM((n_grp,) + shape, F32), pltpu.VMEM((n,) + shape, F32),
            dma((n_grp - 1,)), dma((n_grp - 1,)), dma((n - 1,)), dma((n - 1,))]


def back_kernel(dproj, w_attn, n1_hbm, gw_proj, x_hbm, dh, gain, stats, up_sum,
                grad_x, g_attn, g_proj, sums, owned,
                n1, x_share, gw, got, got_proj, total, qv, ln_sum, nsem, ws, wr, ps, pr, *scratch, n, n_grp, chunks, rows):
    at = Place(n)
    width, hw = w_attn.shape
    block = width // n_grp
    per = block // TILE
    heads = hw // (3 * HD)
    hid = up_sum.shape[1]
    load = pltpu.make_async_copy(n1_hbm, n1, nsem.at[0])
    load.start()
    load_x = pltpu.make_async_copy(x_hbm.at[at.t], x_share, nsem.at[1])
    load_x.start()
    rs, early, late = Scatter(at, *scratch[:7]), AllSum(at, n_grp, *scratch[7:14]), AllSum(at, n_grp, *scratch[14:])
    bar = pltpu.get_barrier_semaphore()
    for d in range(1, n_grp):
        pl.semaphore_signal(bar, inc=1, device_id=(lax.rem(at.g + d, n_grp), at.t), device_id_type=MESH)
    for d in range(1, n):
        pl.semaphore_signal(bar, inc=1, device_id=(at.g, lax.rem(at.t + d, n)), device_id_type=MESH)
    pl.semaphore_wait(bar, n_grp + n - 2)

    def owner(k):
        return lax.rem(at.g + 1 + k, n_grp)

    def send(k):
        r = chunk_rows(owner(k), block)
        return remote(gw.at[r, :], got.at[k], ws.at[k], wr.at[k], (owner(k), at.t))

    def send_proj(k):
        r = chunk_rows(owner(k), block)
        return remote(gw_proj.at[r, :], got_proj.at[k], ps.at[k], pr.at[k], (owner(k), at.t))

    for k in range(n_grp - 1):
        send_proj(k).start()
    qv[...] = jnp.zeros_like(qv)
    ln_sum[...] = jnp.zeros_like(ln_sum)

    def product(c):
        lhs = dproj[:, chunk_rows(c, rows), :].reshape(n * rows, hw)
        qv[...] += jnp.sum(lhs.astype(F32), 0, keepdims=True)

        def tile(i):
            y = dg(lhs, w_attn[cols(i), :], 1, 1)
            rs.parts[:, :, :, cols(i)] = y.astype(BF).reshape(at.Z, 2, rows, TILE)
        tiles(width // TILE, tile)
        rs.start(c)

    def weights(i):
        @pl.when(i == 0)
        def _():
            load.wait()
            load_x.wait()
        k = i // per
        first = pl.multiple_of(owner(k) * block + lax.rem(i, per) * TILE, TILE)
        y = dg(n1[:, pl.ds(first, TILE)], dproj[...].reshape(-1, hw), 0, 0)

        @pl.when(k < n_grp - 1)
        def _():
            gw[pl.ds(first, TILE), :] = y.astype(BF)

            @pl.when(lax.rem(i, per) == per - 1)
            def _():
                send(k).start()

        @pl.when(k == n_grp - 1)
        def _():
            g_attn[cols(lax.rem(i, per)), :] = y

    def norm_grad(c):
        r = chunk_rows(c, rows)
        xhat, inverse = rows_stats(x_share[r, :].astype(F32))
        dn = total[...]
        e = dn * gain[...]
        inner = jnp.mean(e, -1, keepdims=True) + xhat * jnp.mean(e * xhat, -1, keepdims=True)
        grad_x[r, :] = dh[r, :] + inverse * (e - inner)
        ln_sum[0:1, :] += jnp.sum(dn * xhat, 0, keepdims=True)
        ln_sum[1:2, :] += jnp.sum(dn, 0, keepdims=True)

    def tick(i, carry):
        c = i - 1

        @pl.when(inside(c, chunks))
        def _():
            rs.meet(c)
            rs.hop(c, 1)

        @pl.when(inside(i, chunks))
        def _():
            product(i)

        @pl.when(inside(c, chunks))
        def _():
            rs.hop(c, 2)

        @pl.when(i < width // TILE)
        def _():
            weights(i)

        @pl.when(inside(c, chunks))
        def _():
            for h in range(3, at.Z):
                rs.hop(c, h)

        @pl.when(i == chunks)
        def _():
            early.x[...] = stats[...]
            early.x[4:5, 0:hid] = up_sum[...]
            for h in range(heads):
                for j, src in ((0, 3 * h), (1, 3 * h + 2)):
                    early.x[4:5, hid + (2 * h + j) * HD:hid + (2 * h + j + 1) * HD] = qv[:, src * HD:(src + 1) * HD]
            early.start()

        @pl.when(i == chunks + 1)
        def _():
            early.turn()
        e = i - 2

        @pl.when(inside(e, chunks))
        def _():
            rs.finish(e, total)
            norm_grad(e)
        return carry

    lax.fori_loop(0, chunks + 2, tick, 0)
    part = width // 4
    for j in range(4):
        late.x[j:j + 1, :] = ln_sum[0:1, j * part:(j + 1) * part]
        late.x[j + 4:j + 5, :] = ln_sum[1:2, j * part:(j + 1) * part]
    late.start()
    mine = chunk_rows(at.g, block)
    g_proj[...] = gw_proj[mine, :].astype(F32)
    for k in range(n_grp - 1):
        send(k).wait()
        send_proj(k).wait()
        g_attn[...] += got[k].astype(F32)
        g_proj[...] += got_proj[k].astype(F32)
    late.turn()
    early.finish()
    sums[0:4, :] = early.total(0, 4)
    owned[...] = early.tbuf[:, 4, :]
    late.finish()
    ln = late.total(0, 8)
    for j in range(4):
        sums[4:5, j * part:(j + 1) * part] = ln[j:j + 1, :]
        sums[5:6, j * part:(j + 1) * part] = ln[j + 4:j + 5, :]
    sums[6:8, :] = jnp.zeros_like(sums[6:8, :])


def project_back(dproj, w_attn, n1, gw_proj, x, dh, gain, stats, up_sum, n, n_grp, chunks):
    length, hw = dproj.shape
    width = w_attn.shape[0]
    share = length // n
    rows = share // chunks
    block = width // n_grp
    pw = gw_proj.shape[1]
    vm, hbm = pl.BlockSpec(memory_space=pltpu.VMEM), pl.BlockSpec(memory_space=pl.ANY)
    S, dma = jax.ShapeDtypeStruct, pltpu.SemaphoreType.DMA
    return pl.pallas_call(
        functools.partial(back_kernel, n=n, n_grp=n_grp, chunks=chunks, rows=rows),
        in_specs=[vm, vm, hbm, vm, hbm] + [vm] * 4, out_specs=[vm] * 5,
        out_shape=[S((share, width), F32), S((block, hw), F32), S((block, pw), F32), S((8, width), F32),
                   S((n, width), F32)],
        scratch_shapes=[pltpu.VMEM((length, width), BF), pltpu.VMEM((share, width), BF), pltpu.VMEM((width, hw), BF),
                        pltpu.VMEM((n_grp - 1, block, hw), BF), pltpu.VMEM((n_grp - 1, block, pw), BF),
                        pltpu.VMEM((rows, width), F32), pltpu.VMEM((1, hw), F32), pltpu.VMEM((8, width), F32), dma((2,))]
                       + [dma((n_grp - 1,))] * 4 + scatter_scratch(chunks, n // 2, rows, width)
                       + all_sum_scratch(n_grp, n, (8, width)) + all_sum_scratch(n_grp, n, (8, width // 4)),
        compiler_params=pltpu.CompilerParams(collective_id=4, has_side_effects=True, vmem_limit_bytes=50 << 20),
        cost_estimate=pl.CostEstimate(flops=4 * length * hw * width, bytes_accessed=1 << 24, transcendentals=0),
        name="project_back",
    )(dproj.reshape(n, share, hw), w_attn, n1, gw_proj, x.reshape(n, share, width), dh, gain, stats, up_sum)


def ffn_kernel(n2_hbm, gradb_hbm, bias_hbm, up_hbm, down_hbm, out_hbm, ctx_hbm, hidden_hbm, vec, tokens,
               gw_hbm, gwo, dctx, dh, res, stats, bsum,
               w_up, w_down, w_out, ctx, hidden, wsem, acc_out, gat, acc_up, acc_down, gbuf, actb, dbb, total, gshare, b_up, keep, lsem, gsem, msem, *scratch, n, chunks, rows):
    at = Place(n)
    ag1, ag2 = Gather(at, gat, rows, *scratch[:4]), Gather(at, gat, rows, *scratch[4:8])
    rs, mlp = Scatter(at, *scratch[8:15]), Scatter(at, *scratch[15:])
    width, hid = w_up.shape
    m = n * rows

    load = pltpu.make_async_copy(n2_hbm, gat.at[at.t], lsem)
    load.start()
    load_g = pltpu.make_async_copy(gradb_hbm.at[at.t], gshare, msem.at[0])
    load_g.start()
    big = [pltpu.make_async_copy(src, dst, wsem.at[j]) for j, (src, dst) in enumerate(
        ((up_hbm, w_up), (down_hbm, w_down), (hidden_hbm, hidden), (out_hbm, w_out), (ctx_hbm, ctx)))]
    for copy in big:
        copy.start()
    load_b = pltpu.make_async_copy(bias_hbm.at[at.t], b_up, msem.at[1])
    load_b.start()
    share = hidden.shape[0]

    def alive(ranks, first, c):
        shape = (ranks, rows, 1)
        place = ((first + lax.broadcasted_iota(jnp.int32, shape, 0)) * share + c * rows
                 + lax.broadcasted_iota(jnp.int32, shape, 1))
        return jnp.where(place < tokens[...].reshape(1, 1, 1), 1.0, 0.0).reshape(ranks * rows, 1)

    def fetch(c):
        slot = lax.rem(c, 2)
        return pltpu.make_async_copy(gradb_hbm.at[:, chunk_rows(c, rows), :], gbuf.at[slot], gsem.at[slot])

    fetch(0).start()
    stats[...] = jnp.zeros_like(stats)
    bsum[...] = jnp.zeros_like(bsum)
    load.wait()
    load_g.wait()
    load_b.wait()
    at.barrier()

    a0, a1 = 0.7978845608028654, 0.044715

    def wide(c):
        return gat[:, chunk_rows(c, rows), :].reshape(m, width)

    def forward(c):
        @pl.when(c == 0)
        def _():
            for copy in big:
                copy.wait()
        fetch(c).wait()

        @pl.when(c + 1 < chunks)
        def _():
            fetch(c + 1).start()
        slot = lax.rem(c, 2)
        keep[...] = alive(n, 0, c)

        def tile(i):
            v = dg(wide(c), w_up[:, cols(i)], 1, 0) + b_up[:, cols(i)]
            ga = dg(gbuf[slot].reshape(m, width), w_down[:, cols(i)], 1, 0)
            v2 = v * v
            th = jnp.tanh(a0 * (v + a1 * v2 * v))
            half = 0.5 * (1.0 + th)
            actb[:, cols(i)] = (v * half * keep[...]).astype(BF)
            slope = half + 0.5 * v * (1.0 - th * th) * (a0 * (1.0 + 3.0 * a1 * v2))
            db = (ga * slope * keep[...]).astype(BF)
            dbb[:, cols(i)] = db
            bsum[:, cols(i)] += jnp.sum(db.astype(F32), 0, keepdims=True)
        tiles(hid // TILE, tile)

    def back(c):
        def tile(i):
            y = dg(dbb[...], w_up[cols(i), :], 1, 1)
            rs.parts[:, :, :, cols(i)] = y.astype(BF).reshape(at.Z, 2, rows, TILE)
        tiles(width // TILE, tile)

    def down(c):
        def tile(i):
            y = dg(actb[...], w_down[cols(i), :], 1, 1)
            mlp.parts[:, :, :, cols(i)] = y.astype(BF).reshape(at.Z, 2, rows, TILE)
        tiles(width // TILE, tile)

    def weights(c):
        slot = lax.rem(c, 2)

        def tile(i):
            x = gat[:, chunk_rows(c, rows), cols(i)].reshape(m, TILE)
            acc_up[cols(i), :] += dg(x, dbb[...], 0, 0)
            y = gbuf[slot, :, :, cols(i)].reshape(m, TILE)
            acc_down[cols(i), :] += dg(y, actb[...], 0, 0)
        tiles(width // TILE, tile)

    def norm_grad(c):
        r = chunk_rows(c, rows)
        xhat, inverse = rows_stats(hidden[r, :])
        dn2 = total[...]
        e = dn2 * vec[0:1, :]
        inner = jnp.mean(e, -1, keepdims=True) + xhat * jnp.mean(e * xhat, -1, keepdims=True)
        grad = gshare[r, :].astype(F32) * alive(1, at.t, c)
        d = grad + inverse * (e - inner)
        dh[r, :] = d
        gat[at.t, r, :] = d.astype(BF)
        stats[0:1, :] += jnp.sum(dn2 * xhat, 0, keepdims=True)
        stats[1:2, :] += jnp.sum(dn2, 0, keepdims=True)
        stats[2:3, :] += jnp.sum(d, 0, keepdims=True)
        stats[3:4, :] += jnp.sum(grad, 0, keepdims=True)

    def heads(c):
        def tile(i):
            x = gat[:, chunk_rows(c, rows), cols(i)].reshape(m, TILE)
            acc_out[cols(i), :] += dg(x, ctx[:, chunk_rows(c, rows), :].reshape(m, -1), 0, 0)
        tiles(width // TILE, tile)
        y = dg(wide(c), w_out[...], 1, 0)
        dctx[:, chunk_rows(c, rows), :] = y.astype(BF).reshape(n, rows, y.shape[1])

    def at_stage(c, fn):
        @pl.when(inside(c, chunks))
        def _():
            fn(c)

    def store_copies(j):
        r = chunk_rows(j, m)
        return (pltpu.make_async_copy(actb, gw_hbm.at[r, pl.ds(0, hid)], lsem),
                pltpu.make_async_copy(dbb, gw_hbm.at[r, pl.ds(hid, hid)], msem.at[0]))

    def store_wait(j):
        for copy in store_copies(j):
            copy.wait()

    def store(j):
        @pl.when((j >= 0) & (j < width // m))
        def _():
            @pl.when(j > 0)
            def _():
                store_wait(j - 1)
            r = chunk_rows(j, m)
            actb[...] = acc_up[r, :].astype(BF)
            dbb[...] = acc_down[r, :].astype(BF)
            for copy in store_copies(j):
                copy.start()

    per_slot = -(-(width // m) // (3 * (at.Z - 1)))

    def tick(i, carry):
        def stores(slot):
            for j in range(per_slot):
                store(((i - chunks - 2) * (at.Z - 1) + slot) * per_slot + j)
        at_stage(i, ag1.start)

        @pl.when(i == 0)
        def _():
            acc_up[...] = jnp.zeros_like(acc_up)
            acc_down[...] = jnp.zeros_like(acc_down)
            acc_out[...] = jnp.zeros_like(acc_out)
        at_stage(i - 3, rs.meet)
        for h in range(1, at.Z):
            at_stage(i - 3, lambda c: rs.hop(c, h))
            at_stage(i - 1, lambda c: ag1.hop(c, h))
            if h == 1:
                at_stage(i - 4, lambda c: mlp.hop(c, at.Z - 1))
                at_stage(i - 5, lambda c: ag2.hop(c, at.Z - 1))
                at_stage(i - 2, forward)
                stores(0)
            else:
                if h == 2:
                    def served(c):
                        mlp.finish(c, total)
                        r = chunk_rows(c, rows)
                        res[r, :] = (alive(1, at.t, c) * (hidden[r, :] + total[...] + vec[1:2, :])).astype(BF)
                    at_stage(i - 4, served)
                    at_stage(i - 3, mlp.meet)
                at_stage(i - 3, lambda c: mlp.hop(c, h - 1))
                at_stage(i - 4, lambda c: ag2.hop(c, h - 1))
                stores(h - 1)
                if h == 2:
                    at_stage(i - 2, back)

                    def gathered(c):
                        ag2.finish(c)
                        heads(c)
                    at_stage(i - 5, gathered)

        def rest(c):
            weights(c)
            rs.start(c)
        at_stage(i - 2, rest)

        def reduced(c):
            rs.finish(c, total)
            norm_grad(c)
            ag2.start(c)
        at_stage(i - 3, reduced)
        at_stage(i - 1, ag1.finish)

        def send_mlp(c):
            down(c)
            mlp.start(c)
        at_stage(i - 2, send_mlp)

        return carry

    lax.fori_loop(0, chunks + 5, tick, 0)

    store_wait(width // m - 1)
    gwo[...] = acc_out[...].astype(BF)


def feed_forward(n2, gradb, b_up, w_up, w_down, w_out, ctx, hidden, vec, tokens, n, chunks):
    length, width = gradb.shape
    hid, hw = w_up.shape[1], w_out.shape[1]
    share = length // n
    rows = share // chunks
    Z = n // 2
    vm, hbm = pl.BlockSpec(memory_space=pltpu.VMEM), pl.BlockSpec(memory_space=pl.ANY)
    S = jax.ShapeDtypeStruct
    m = n * rows
    return pl.pallas_call(
        functools.partial(ffn_kernel, n=n, chunks=chunks, rows=rows),
        in_specs=[hbm] * 8 + [vm] * 2,
        out_specs=[hbm] + [vm] * 6,
        out_shape=[S((width, 2 * hid), BF), S((width, hw), BF), S((n, share, hw), BF), S((share, width), F32),
                   S((share, width), BF), S((8, width), F32), S((1, hid), F32)],
        scratch_shapes=[pltpu.VMEM((width, hid), BF), pltpu.VMEM((width, hid), BF), pltpu.VMEM((width, hw), BF),
                        pltpu.VMEM((n, share, hw), BF), pltpu.VMEM((share, width), F32), pltpu.SemaphoreType.DMA((5,)),
                        pltpu.VMEM((width, hw), F32), pltpu.VMEM((n, share, width), BF), pltpu.VMEM((width, hid), F32), pltpu.VMEM((width, hid), F32),
                        pltpu.VMEM((2, n, rows, width), BF),
                        pltpu.VMEM((m, hid), BF), pltpu.VMEM((m, hid), BF), pltpu.VMEM((rows, width), F32),
                        pltpu.VMEM((share, width), BF), pltpu.VMEM((1, hid), F32), pltpu.VMEM((m, 1), F32),
                        pltpu.SemaphoreType.DMA, pltpu.SemaphoreType.DMA((2,)), pltpu.SemaphoreType.DMA((2,))]
                       + gather_sems(chunks, Z) + gather_sems(chunks, Z) + scatter_scratch(chunks, Z, rows, width) * 2,
        compiler_params=pltpu.CompilerParams(collective_id=3, has_side_effects=True, vmem_limit_bytes=62 << 20),
        cost_estimate=pl.CostEstimate(flops=12 * length * hid * width, bytes_accessed=1 << 26, transcendentals=0),
        name="feed_forward",
    )(n2, gradb.reshape(n, share, width), b_up.reshape(n, 1, hid), w_up, w_down, w_out, ctx.reshape(n, share, hw),
      hidden, vec, tokens)


def on_device(layer_input, out_cotangent, seq_group, seq_len, w_qkv, b_qv, w_out, b_out, w_up, b_up,
              w_down, b_down, first_norm_gain, first_norm_bias, second_norm_gain, second_norm_bias):
    n_tp, n_grp = lax.axis_size("tp"), lax.axis_size("grp")
    grp = lax.axis_index("grp")
    length, width = layer_input.shape
    hid, qv = w_up.shape[1], b_qv.shape[0] // n_tp

    proj, n1, w_attn, w_proj, up16, down16 = front(
        layer_input, w_qkv, w_out, w_up, w_down, jnp.stack([first_norm_gain, first_norm_bias]), b_qv, n_tp, n_grp)
    context, lse = attn_fwd(seq_group, seq_len, proj)
    hidden, n2, w_expand, w_reduce = attn_out(
        context, w_proj, jnp.stack([b_out, second_norm_gain, second_norm_bias]), layer_input, up16, down16,
        n_tp, n_grp, 8)
    tokens = jnp.sum(jnp.where(seq_group == grp, seq_len, 0)).reshape(1, 1)
    gw_ffn, gw_proj, dcontext, dh, result, stats, up_sum = feed_forward(
        n2, out_cotangent, b_up, w_expand, w_reduce, w_proj, context, hidden,
        jnp.stack([second_norm_gain, b_down]), tokens, n_tp, 8)
    grads_ffn = lax.psum_scatter(gw_ffn, "grp", scatter_dimension=0, tiled=True).astype(F32)
    grads_expand, grads_reduce = grads_ffn[:, :hid], grads_ffn[:, hid:]

    dproj = attn_bwd(seq_group, seq_len, proj, context, dcontext.reshape(length, -1), lse)
    grad_x, grads_attn, grads_proj, sums, owned = project_back(
        dproj, w_attn, n1, gw_proj, layer_input, dh, first_norm_gain[None], stats, up_sum, n_tp, n_grp, 8)
    return (result, grad_x, grads_attn, owned[:, hid:hid + qv].reshape(-1), grads_proj, sums[2],
            grads_expand, owned[:, :hid].reshape(-1), grads_reduce, sums[3], sums[4], sums[5],
            sums[0], sums[1])


def solution(mesh):
    rows, both, flat = P("grp", None), P("grp", "tp"), P()
    in_specs = (rows, rows, flat, flat, both, flat, both, flat, both, flat, both, flat, flat, flat, flat, flat)
    spread = P(("grp", "tp"), None)
    out_specs = (spread, spread, both, flat, both, flat, both, flat, both, flat, flat, flat, flat, flat)
    return jax.shard_map(on_device, mesh=mesh, in_specs=in_specs, out_specs=out_specs, check_vma=False)
```

```python
import functools

import jax
import jax.numpy as jnp
from jax import lax
from jax.experimental import pallas as pl
from jax.experimental.pallas import tpu as pltpu
from jax.sharding import PartitionSpec as P

HD = 128
BLK=512
F32=jnp.float32
BF=jnp.bfloat16
LOG2E=1.4426950408889634

def dg(a,b,ca,cb):
    return lax.dot_general(a,b,(((ca,),(cb,)),((),())),preferred_element_type=F32)


def group_tokens(grps, lens, seqs):
    g = lax.axis_index("grp")
    tokens, longest = jnp.int32(0), jnp.int32(0)
    for s in range(seqs):
        count = jnp.where(grps[s] == g, lens[s], 0)
        tokens, longest = tokens + count, jnp.maximum(longest, count)
    return tokens, longest > BLK


def below(shape):
    return lax.broadcasted_iota(jnp.int32, shape, 0) <= lax.broadcasted_iota(jnp.int32, shape, 1)


def attn_fwd_kernel(grps, lens, q_ref, k_ref, v_ref, o_ref, lse_ref, *, nb, seqs):
    tokens, is_long = group_tokens(grps, lens, seqs)
    c = HD ** -0.5 * LOG2E

    def attend(rows, early):
        q = q_ref[rows, :]
        pieces = [(rows, jnp.where(below((BLK, BLK)), dg(k_ref[rows, :], q, 1, 1), -1e30))]
        if early is not None:
            pieces.append((early, dg(k_ref[early, :], q, 1, 1)))
        top = functools.reduce(jnp.maximum, [jnp.max(s, 0, keepdims=True) for _, s in pieces]) * c
        total, acc = 0.0, 0.0
        for keys, s in pieces:
            p = jnp.exp2(s * c - top)
            total = total + jnp.sum(p, 0, keepdims=True)
            acc = acc + dg(v_ref[keys, :], p.astype(BF), 0, 0)
        o_ref[rows, :] = jnp.transpose(acc / total).astype(BF)
        lse_ref[0, :, rows] = top + jnp.log2(total)

    @pl.when(is_long)
    def _():
        for i in range(nb):
            attend(slice(i * BLK, (i + 1) * BLK), slice(0, i * BLK) if i else None)

    @pl.when(jnp.logical_not(is_long))
    def _():
        def block(i, carry):
            rows = pl.ds(pl.multiple_of(i * BLK, BLK), BLK)

            @pl.when(i * BLK < tokens)
            def _():
                attend(rows, None)

            @pl.when(i * BLK >= tokens)
            def _():
                o_ref[rows, :] = jnp.zeros((BLK, HD), BF)
                lse_ref[0, :, rows] = jnp.zeros((1, BLK), F32)
            return carry
        lax.fori_loop(0, nb, block, 0)


def attn_fwd(grps, lens, proj):
    length, heads = proj.shape[0], proj.shape[1] // (3 * HD)
    spec = lambda o: pl.BlockSpec((length, HD), lambda h, grps, lens: (0, 3 * h + o))
    return pl.pallas_call(
        functools.partial(attn_fwd_kernel, nb=length // BLK, seqs=grps.shape[0]),
        grid_spec=pltpu.PrefetchScalarGridSpec(
            num_scalar_prefetch=2, grid=(heads,), in_specs=[spec(0), spec(1), spec(2)],
            out_specs=[pl.BlockSpec((length, HD), lambda h, grps, lens: (0, h)),
                       pl.BlockSpec((1, 1, length), lambda h, grps, lens: (h, 0, 0))]),
        out_shape=[jax.ShapeDtypeStruct((length, heads * HD), BF), jax.ShapeDtypeStruct((heads, 1, length), F32)],
        compiler_params=pltpu.CompilerParams(vmem_limit_bytes=40 << 20),
        cost_estimate=pl.CostEstimate(flops=heads * length * length * HD * 2, bytes_accessed=length * heads * HD * 8,
                                      transcendentals=heads * length * length // 2),
        name="attn_fwd",
    )(grps, lens, proj, proj, proj)


def attn_bwd_kernel(grps, lens, q_ref, k_ref, v_ref, o_ref, do_ref, lse_ref, dp_ref, dq_sc, dl_sc, *, nb, seqs):
    tokens, is_long = group_tokens(grps, lens, seqs)
    scale = HD ** -0.5
    c = scale * LOG2E
    prod = do_ref[...].astype(F32) * o_ref[...].astype(F32)
    dl_sc[...] = jnp.sum(jnp.transpose(prod), 0, keepdims=True)

    def attend(keys, later, first):
        k, v = k_ref[keys, :], v_ref[keys, :]
        dk, dv = 0.0, 0.0
        for diag, rows in ((True, keys), (False, later)):
            if rows is None:
                continue
            q, do = q_ref[rows, :], do_ref[rows, :]
            p = jnp.exp2(dg(k, q, 1, 1) * c - lse_ref[0, :, rows])
            if diag:
                p = jnp.where(below((BLK, BLK)), p, 0.0)
            ds = (p * (dg(v, do, 1, 1) - dl_sc[:, rows])).astype(BF)
            dv = dv + dg(p.astype(BF), do, 1, 0)
            dk = dk + dg(ds, q, 1, 0)
            dq = dg(k, ds, 0, 0)
            dq_sc[:, rows] = dq if first else dq_sc[:, rows] + dq
        dp_ref[keys, HD:2 * HD] = (dk * scale).astype(BF)
        dp_ref[keys, 2 * HD:] = dv.astype(BF)

    @pl.when(is_long)
    def _():
        for j in range(nb):
            attend(slice(j * BLK, (j + 1) * BLK), slice((j + 1) * BLK, nb * BLK) if j < nb - 1 else None, j == 0)

    @pl.when(jnp.logical_not(is_long))
    def _():
        def block(i, carry):
            rows = pl.ds(pl.multiple_of(i * BLK, BLK), BLK)

            @pl.when(i * BLK < tokens)
            def _():
                attend(rows, None, True)

            @pl.when(i * BLK >= tokens)
            def _():
                dp_ref[rows, :] = jnp.zeros((BLK, 3 * HD), BF)
                dq_sc[:, rows] = jnp.zeros((HD, BLK), F32)
            return carry
        lax.fori_loop(0, nb, block, 0)
    dp_ref[:, :HD] = jnp.transpose(dq_sc[...] * scale).astype(BF)


def attn_bwd(grps, lens, proj, ctx, dctx, lse):
    length, heads = proj.shape[0], proj.shape[1] // (3 * HD)
    spec = lambda o: pl.BlockSpec((length, HD), lambda h, grps, lens: (0, 3 * h + o))
    head = pl.BlockSpec((length, HD), lambda h, grps, lens: (0, h))
    return pl.pallas_call(
        functools.partial(attn_bwd_kernel, nb=length // BLK, seqs=grps.shape[0]),
        grid_spec=pltpu.PrefetchScalarGridSpec(
            num_scalar_prefetch=2, grid=(heads,),
            in_specs=[spec(0), spec(1), spec(2), head, head,
                      pl.BlockSpec((1, 1, length), lambda h, grps, lens: (h, 0, 0))],
            out_specs=pl.BlockSpec((length, 3 * HD), lambda h, grps, lens: (0, h)),
            scratch_shapes=[pltpu.VMEM((HD, length), F32), pltpu.VMEM((1, length), F32)]),
        out_shape=jax.ShapeDtypeStruct((length, heads * 3 * HD), BF),
        compiler_params=pltpu.CompilerParams(vmem_limit_bytes=40 << 20),
        cost_estimate=pl.CostEstimate(flops=heads * length * length * HD * 5, bytes_accessed=length * heads * HD * 16,
                                      transcendentals=heads * length * length // 2),
        name="attn_bwd",
    )(grps, lens, proj, proj, proj, ctx, dctx, lse)


MESH = pl.DeviceIdType.MESH
TILE = 256


class Place:
    def __init__(self, n_tp):
        self.g = lax.axis_index("grp")
        t = lax.axis_index("tp")
        self.t, self.n, self.Z = t, n_tp, n_tp // 2
        self.z, self.k = t // 2, lax.rem(t, 2)
        self.right, self.left, self.sib = (self.g, t + 2), (self.g, t - 2), (self.g, t + 1 - 2 * self.k)
        self.has_right, self.has_left = self.z < self.Z - 1, self.z > 0

    def barrier(self, n_grp=0):
        bar = pltpu.get_barrier_semaphore()
        extra = grp_signal(self, n_grp) if n_grp else 0
        pl.semaphore_signal(bar, inc=1, device_id=self.sib, device_id_type=MESH)

        @pl.when(self.has_right)
        def _():
            pl.semaphore_signal(bar, inc=1, device_id=self.right, device_id_type=MESH)

        @pl.when(self.has_left)
        def _():
            pl.semaphore_signal(bar, inc=1, device_id=self.left, device_id_type=MESH)

        amount = 1 + extra + jnp.where(self.has_right, 1, 0) + jnp.where(self.has_left, 1, 0)
        pl.semaphore_wait(bar, amount)


def remote(src, dst, ssem, rsem, device):
    return pltpu.make_async_remote_copy(src, dst, ssem, rsem, device_id=device, device_id_type=MESH)


class Gather:
    def __init__(self, at, gat, rows, ls, lr, ss, sr):
        self.at, self.gat, self.rows = at, gat, rows
        self.ls, self.lr, self.ss, self.sr = ls, lr, ss, sr

    def block(self, zz, kk, c):
        return self.gat.at[2 * zz + kk, pl.ds(pl.multiple_of(c * self.rows, self.rows), self.rows), :]

    def line(self, c, side, d):
        at = self.at
        sign, device = (-1, at.right) if side == 0 else (1, at.left)
        b = self.block(at.z + sign * (d - 1), at.k, c)
        return remote(b, b, self.ls.at[c, side, d - 1], self.lr.at[c, side, d - 1], device)

    def line_in(self, c, side, d):
        at = self.at
        sign, device = (-1, at.right) if side == 0 else (1, at.left)
        b = self.block(at.z + sign * d, at.k, c)
        return remote(b, b, self.ls.at[c, side, d - 1], self.lr.at[c, side, d - 1], device)

    def across(self, c, zz):
        b = self.block(zz, self.at.k, c)
        return remote(b, b, self.ss.at[c, zz], self.sr.at[c, zz], self.at.sib)

    def across_in(self, c, zz):
        b = self.block(zz, 1 - self.at.k, c)
        return remote(b, b, self.ss.at[c, zz], self.sr.at[c, zz], self.at.sib)

    def start(self, c):
        at = self.at

        @pl.when(at.has_right)
        def _():
            self.line(c, 0, 1).start()

        @pl.when(at.has_left)
        def _():
            self.line(c, 1, 1).start()

        self.across(c, at.z).start()

    def hop(self, c, d):
        at = self.at

        @pl.when(at.z >= d)
        def _():
            self.line_in(c, 0, d).wait_recv()
            if d < at.Z - 1:
                @pl.when(at.has_right)
                def _():
                    self.line(c, 0, d + 1).start()
            self.across(c, at.z - d).start()

        @pl.when(at.z + d <= at.Z - 1)
        def _():
            self.line_in(c, 1, d).wait_recv()
            if d < at.Z - 1:
                @pl.when(at.has_left)
                def _():
                    self.line(c, 1, d + 1).start()
            self.across(c, at.z + d).start()

    def finish(self, c):
        at = self.at
        for zz in range(at.Z):
            self.across_in(c, zz).wait_recv()
            self.across(c, zz).wait_send()
        for d in range(1, at.Z):
            @pl.when(at.has_right & (at.z >= d - 1))
            def _():
                self.line(c, 0, d).wait_send()

            @pl.when(at.has_left & (at.z + d - 1 <= at.Z - 1))
            def _():
                self.line(c, 1, d).wait_send()


class Scatter:
    def __init__(self, at, parts, pair, hops, cs, cr, hs, hr):
        self.at, self.parts, self.pair, self.hops = at, parts, pair, hops
        self.slots = pair.shape[0]
        self.cs, self.cr, self.hs, self.hr = cs, cr, hs, hr

    def across(self, c):
        c = lax.rem(c, self.slots)
        return remote(self.parts.at[:, 1 - self.at.k], self.pair.at[c], self.cs.at[c], self.cr.at[c], self.at.sib)

    def line(self, c, side, h, target):
        c = lax.rem(c, self.slots)
        device = self.at.right if side == 0 else self.at.left
        return remote(self.pair.at[c, target], self.hops.at[side, c, h - 1],
                      self.hs.at[c, side, h - 1], self.hr.at[c, side, h - 1], device)

    def start(self, c):
        self.across(c).start()

    def meet(self, c):
        self.across(c).wait()
        own = self.parts[:, pl.ds(self.at.k, 1)]
        own = own.reshape(own.shape[0], own.shape[2], own.shape[3])
        c = lax.rem(c, self.slots)
        self.pair[c] = (self.pair[c].astype(F32) + own.astype(F32)).astype(BF)

    def hop(self, c, h):
        at = self.at
        for side in (0, 1):
            pos = at.z if side == 0 else at.Z - 1 - at.z
            target = at.z + at.Z - h if side == 0 else at.z - at.Z + h

            @pl.when((pos <= h - 1) & (pos < at.Z - 1))
            def _():
                if h >= 2:
                    @pl.when(pos >= 1)
                    def _():
                        self.line(c, side, h - 1, target).wait_recv()
                        b = lax.rem(c, self.slots)
                        self.pair[b, target] = (self.pair[b, target].astype(F32)
                                                + self.hops[side, b, h - 2].astype(F32)).astype(BF)
                self.line(c, side, h, target).start()

    def finish(self, c, total):
        at = self.at
        b = lax.rem(c, self.slots)
        total[...] = self.pair[b, at.z].astype(F32)
        for side in (0, 1):
            pos = at.z if side == 0 else at.Z - 1 - at.z

            @pl.when(pos >= 1)
            def _():
                self.line(c, side, at.Z - 1, at.z).wait_recv()
                total[...] += self.hops[side, b, at.Z - 2].astype(F32)

            for h in range(1, at.Z):
                @pl.when((pos <= h - 1) & (pos < at.Z - 1))
                def _():
                    self.line(c, side, h, at.z).wait_send()


class GroupGather:
    def __init__(self, at, n_grp, full, ss, sr):
        self.at, self.full, self.ss, self.sr = at, full, ss, sr
        self.P = n_grp // 2
        self.size = full.shape[0] // n_grp
        self.p, self.q = at.g // 2, lax.rem(at.g, 2)
        self.partner = (at.g + 1 - 2 * self.q, at.t)

    def peer(self, j):
        return lax.rem(self.p + j, self.P)

    def rows(self, p, q, half=None):
        size = self.size if half is None else self.size // 2
        first = (2 * p + q) * self.size + (size if half == 1 else 0)
        return self.full.at[pl.ds(pl.multiple_of(first, size), size), :]

    def copy(self, kind, j, incoming=False):
        p, q = self.p, self.q
        src = lax.rem(p + self.P - j, self.P)
        if kind == 0:
            b, k, dev = self.rows(p, 1 - q if incoming else q), 0, self.partner
        elif kind == 1:
            b, k, dev = self.rows(src if incoming else p, q), j, (2 * self.peer(j) + q, self.at.t)
        elif kind == 2:
            b, k = self.rows(src if incoming else p, 1 - q, 1), self.P - 1 + j
            dev = (2 * self.peer(j) + q, self.at.t)
        else:
            b, k = self.rows(src, 1 - q if incoming else q, 0), 2 * (self.P - 1) + j
            dev = self.partner
        return remote(b, b, self.ss.at[k], self.sr.at[k], dev)

    def start(self):
        self.copy(0, 0).start()
        for j in range(1, self.P):
            self.copy(1, j).start()

    def forward(self):
        self.copy(0, 0, True).wait_recv()
        for j in range(1, self.P):
            self.copy(2, j).start()
        for j in range(1, self.P):
            self.copy(1, j, True).wait_recv()
            self.copy(3, j).start()

    def finish(self):
        for j in range(1, self.P):
            for kind in (2, 3):
                self.copy(kind, j, True).wait_recv()
                self.copy(kind, j).wait_send()
            self.copy(1, j).wait_send()
        self.copy(0, 0).wait_send()


def group_sems(n_grp):
    k = 1 + 3 * (n_grp // 2 - 1)
    return [pltpu.SemaphoreType.DMA((k,)), pltpu.SemaphoreType.DMA((k,))]


def grp_signal(at, n_grp):
    bar = pltpu.get_barrier_semaphore()
    p, q = at.g // 2, lax.rem(at.g, 2)
    pl.semaphore_signal(bar, inc=1, device_id=(at.g + 1 - 2 * q, at.t), device_id_type=MESH)
    for j in range(1, n_grp // 2):
        pl.semaphore_signal(bar, inc=1, device_id=(2 * lax.rem(p + j, n_grp // 2) + q, at.t), device_id_type=MESH)
    return n_grp // 2


def gather_sems(chunks, Z):
    dma = pltpu.SemaphoreType.DMA
    return [dma((chunks, 2, Z - 1)), dma((chunks, 2, Z - 1)), dma((chunks, Z)), dma((chunks, Z))]


def scatter_scratch(chunks, Z, rows, width):
    chunks = min(chunks, 4)
    dma = pltpu.SemaphoreType.DMA
    return [pltpu.VMEM((Z, 2, rows, width), BF), pltpu.VMEM((chunks, Z, rows, width), BF),
            pltpu.VMEM((2, chunks, Z - 1, rows, width), BF),
            dma((chunks,)), dma((chunks,)), dma((chunks, 2, Z - 1)), dma((chunks, 2, Z - 1))]


def inside(c, chunks):
    return (c >= 0) & (c < chunks)


def chunk_rows(c, rows):
    return pl.ds(pl.multiple_of(c * rows, rows), rows)


def tiles(count, body):
    def step(i, carry):
        body(i)
        return carry
    lax.fori_loop(0, count, step, 0)


def cols(i, size=TILE):
    return pl.ds(pl.multiple_of(i * size, size), size)


def rows_stats(rows):
    mean = jnp.mean(rows, -1, keepdims=True)
    centred = rows - mean
    inverse = lax.rsqrt(jnp.mean(centred * centred, -1, keepdims=True) + 1e-05)
    return centred * inverse, inverse


def product_scatter(at, rs, lhs_ref, w_ref, total, chunks, rows, epilogue, extra):
    def product(c):
        lhs = lhs_ref[:, chunk_rows(c, rows), :].reshape(at.n * rows, lhs_ref.shape[2])

        def tile(i):
            y = dg(lhs, w_ref[cols(i), :], 1, 1)
            rs.parts[:, :, :, cols(i)] = y.astype(BF).reshape(at.Z, 2, rows, TILE)
        tiles(w_ref.shape[0] // TILE, tile)
        rs.start(c)

    def tick(i, carry):
        c = i - 1

        @pl.when(inside(c, chunks))
        def _():
            rs.meet(c)
            rs.hop(c, 1)

        @pl.when(inside(i, chunks))
        def _():
            product(i)

        @pl.when(inside(c, chunks))
        def _():
            for h in range(2, at.Z):
                rs.hop(c, h)

        e = i - 2

        @pl.when(inside(e, chunks))
        def _():
            rs.finish(e, total)
            epilogue(e)
        extra(i)
        return carry

    lax.fori_loop(0, chunks + 2, tick, 0)


def out_kernel(ctx, w_out, vec, x_hbm, up16, down16, hidden, n2, up_hbm, down_hbm,
               x_share, total, lsem, *sc, n, n_grp, chunks, rows):
    at = Place(n)
    load = pltpu.make_async_copy(x_hbm.at[at.t], x_share, lsem.at[0])
    load.start()
    up, down = GroupGather(at, n_grp, up_hbm, *sc[:2]), GroupGather(at, n_grp, down_hbm, *sc[2:4])
    own = chunk_rows(at.g, up.size)
    put_up = pltpu.make_async_copy(up16, up_hbm.at[own, :], lsem.at[1])
    put_down = pltpu.make_async_copy(down16, down_hbm.at[own, :], lsem.at[2])
    put_up.start()
    put_down.start()
    at.barrier(n_grp)
    load.wait()
    put_up.wait()
    put_down.wait()
    up.start()
    down.start()

    def epilogue(c):
        r = chunk_rows(c, rows)
        h = x_share[r, :].astype(F32) + total[...] + vec[0:1, :]
        hidden[r, :] = h
        n2[r, :] = (rows_stats(h)[0] * vec[1:2, :] + vec[2:3, :]).astype(BF)

    def extra(i):
        @pl.when(i == chunks // 2)
        def _():
            up.forward()

        @pl.when(i == chunks - 1)
        def _():
            down.forward()

    product_scatter(at, Scatter(at, *sc[4:]), ctx, w_out, total, chunks, rows, epilogue, extra)
    up.finish()
    down.finish()


def attn_out(ctx, w_out, vec, x, up16, down16, n, n_grp, chunks):
    length, hw = ctx.shape
    width = x.shape[1]
    share = length // n
    rows = share // chunks
    hid = up16.shape[1]
    vm, hbm = pl.BlockSpec(memory_space=pltpu.VMEM), pl.BlockSpec(memory_space=pl.ANY)
    S = jax.ShapeDtypeStruct
    return pl.pallas_call(
        functools.partial(out_kernel, n=n, n_grp=n_grp, chunks=chunks, rows=rows),
        in_specs=[vm] * 3 + [hbm] * 3, out_specs=[vm] * 2 + [hbm] * 2,
        out_shape=[S((share, width), F32), S((share, width), BF), S((width, hid), BF), S((width, hid), BF)],
        scratch_shapes=[pltpu.VMEM((share, width), BF), pltpu.VMEM((rows, width), F32), pltpu.SemaphoreType.DMA((3,))]
                       + group_sems(n_grp) * 2 + scatter_scratch(chunks, n // 2, rows, width),
        compiler_params=pltpu.CompilerParams(collective_id=2, has_side_effects=True, vmem_limit_bytes=40 << 20),
        cost_estimate=pl.CostEstimate(flops=2 * length * hw * width, bytes_accessed=1 << 23, transcendentals=0),
        name="attn_out",
    )(ctx.reshape(n, share, hw), w_out, vec, x.reshape(n, share, width), up16, down16)


def front_kernel(x_hbm, w_qkv, w_out, w_up, w_down, vec, bias_hbm, proj, n1_hbm, w_attn, w_proj, up16, down16,
                 xbuf, n1, acc, bias, xsem, osem, bsem, *sc, n, n_grp, parts):
    at = Place(n)
    width, hw = w_attn.shape
    block = width // n_grp
    length = n1.shape[0]
    rows = length // parts
    heads = hw // (3 * HD)

    def fetch(i):
        slot = lax.rem(i, 2)
        return pltpu.make_async_copy(x_hbm.at[chunk_rows(i, rows), :], xbuf.at[slot], xsem.at[slot])

    def put(i):
        r = chunk_rows(i, rows)
        return pltpu.make_async_copy(n1.at[r, :], n1_hbm.at[r, :], osem)

    get_bias = pltpu.make_async_copy(bias_hbm.at[at.t], bias, bsem)
    get_bias.start()
    fetch(0).start()
    own = chunk_rows(at.g, block)
    w_attn[own, :] = w_qkv[...].astype(BF)
    bar = pltpu.get_barrier_semaphore()
    pl.semaphore_wait(bar, grp_signal(at, n_grp))
    qkv, out = GroupGather(at, n_grp, w_attn, *sc[:2]), GroupGather(at, n_grp, w_proj, *sc[2:])
    qkv.start()
    w_proj[own, :] = w_out[...].astype(BF)
    up16[...] = w_up[...].astype(BF)
    down16[...] = w_down[...].astype(BF)

    def norm(i):
        fetch(i).wait()

        @pl.when(i + 1 < parts)
        def _():
            fetch(i + 1).start()
        y = rows_stats(xbuf[lax.rem(i, 2)].astype(F32))[0] * vec[0:1, :] + vec[1:2, :]
        n1[chunk_rows(i, rows), :] = y.astype(BF)
        put(i).start()
    tiles(parts, norm)

    def partial(b, first=False, last=False):
        r = chunk_rows(b, block)

        def tile(i):
            m = chunk_rows(i, rows)
            y = dg(n1[m, r], w_attn[r, :], 1, 0)
            if not first:
                y = y + acc[m, :]
            acc[m, :] = y
        tiles(parts, tile)

    p, q, P = at.g // 2, lax.rem(at.g, 2), n_grp // 2
    partial(at.g, True)
    qkv.forward()
    out.start()
    partial(2 * p + 1 - q)
    for j in range(1, P):
        partial(2 * lax.rem(p + j, P) + q)
    out.forward()
    qkv.finish()
    for j in range(1, P):
        partial(2 * lax.rem(p + j, P) + 1 - q)
    get_bias.wait()

    def write(i):
        m = chunk_rows(i, rows)
        for h in range(heads):
            c = 3 * h * HD
            proj[m, c:c + HD] = (acc[m, c:c + HD] + bias[:, 2 * h * HD:(2 * h + 1) * HD]).astype(BF)
            c += HD
            proj[m, c:c + HD] = acc[m, c:c + HD].astype(BF)
            c += HD
            proj[m, c:c + HD] = (acc[m, c:c + HD] + bias[:, (2 * h + 1) * HD:(2 * h + 2) * HD]).astype(BF)
        put(i).wait()
    tiles(parts, write)
    out.finish()


def front(x, w_qkv, w_out, w_up, w_down, vec, b_qv, n, n_grp):
    length, width = x.shape
    block, hw = w_qkv.shape
    pw, hid = w_out.shape[1], w_up.shape[1]
    parts = length // TILE
    vm, hbm = pl.BlockSpec(memory_space=pltpu.VMEM), pl.BlockSpec(memory_space=pl.ANY)
    S, dma = jax.ShapeDtypeStruct, pltpu.SemaphoreType.DMA
    return pl.pallas_call(
        functools.partial(front_kernel, n=n, n_grp=n_grp, parts=parts),
        in_specs=[hbm] + [vm] * 5 + [hbm], out_specs=[vm, hbm] + [vm] * 4,
        out_shape=[S((length, hw), BF), S((length, width), BF), S((width, hw), BF), S((width, pw), BF),
                   S((block, hid), BF), S((block, hid), BF)],
        scratch_shapes=[pltpu.VMEM((2, length // parts, width), BF), pltpu.VMEM((length, width), BF),
                        pltpu.VMEM((length, hw), F32), pltpu.VMEM((1, b_qv.shape[0] // n), F32),
                        dma((2,)), dma, dma] + group_sems(n_grp) * 2,
        compiler_params=pltpu.CompilerParams(collective_id=5, has_side_effects=True, vmem_limit_bytes=50 << 20),
        cost_estimate=pl.CostEstimate(flops=2 * length * hw * width, bytes_accessed=1 << 24, transcendentals=0),
        name="front",
    )(x, w_qkv, w_out, w_up, w_down, vec, b_qv.reshape(n, 1, -1))


class AllSum:
    def __init__(self, at, n_grp, x, gbuf, tbuf, gs, gr, ts, tr):
        self.at, self.n_grp, self.x, self.gbuf, self.tbuf = at, n_grp, x, gbuf, tbuf
        self.gs, self.gr, self.ts, self.tr = gs, gr, ts, tr

    def over_grp(self, d):
        at = self.at
        return remote(self.x, self.gbuf.at[at.g], self.gs.at[d - 1], self.gr.at[d - 1],
                      (lax.rem(at.g + d, self.n_grp), at.t))

    def over_tp(self, d):
        at = self.at
        return remote(self.tbuf.at[at.t], self.tbuf.at[at.t], self.ts.at[d - 1], self.tr.at[d - 1],
                      (at.g, lax.rem(at.t + d, at.n)))

    def start(self):
        for d in range(1, self.n_grp):
            self.over_grp(d).start()
        self.gbuf[self.at.g] = self.x[...]

    def turn(self):
        for d in range(1, self.n_grp):
            self.over_grp(d).wait()
        total = self.gbuf[0]
        for i in range(1, self.n_grp):
            total = total + self.gbuf[i]
        self.tbuf[self.at.t] = total
        for d in range(1, self.at.n):
            self.over_tp(d).start()

    def finish(self):
        for d in range(1, self.at.n):
            self.over_tp(d).wait()

    def total(self, lo, hi):
        out = self.tbuf[0, lo:hi, :]
        for i in range(1, self.at.n):
            out = out + self.tbuf[i, lo:hi, :]
        return out


def all_sum_scratch(n_grp, n, shape):
    dma = pltpu.SemaphoreType.DMA
    return [pltpu.VMEM(shape, F32), pltpu.VMEM((n_grp,) + shape, F32), pltpu.VMEM((n,) + shape, F32),
            dma((n_grp - 1,)), dma((n_grp - 1,)), dma((n - 1,)), dma((n - 1,))]


def back_kernel(dproj, w_attn, n1_hbm, gw_proj, x_hbm, dh, gain, stats, up_sum,
                grad_x, g_attn, g_proj, sums, owned,
                n1, x_share, gw, got, got_proj, total, qv, ln_sum, nsem, ws, wr, ps, pr, *scratch, n, n_grp, chunks, rows):
    at = Place(n)
    width, hw = w_attn.shape
    block = width // n_grp
    per = block // TILE
    heads = hw // (3 * HD)
    hid = up_sum.shape[1]
    load = pltpu.make_async_copy(n1_hbm, n1, nsem.at[0])
    load.start()
    load_x = pltpu.make_async_copy(x_hbm.at[at.t], x_share, nsem.at[1])
    load_x.start()
    rs, early, late = Scatter(at, *scratch[:7]), AllSum(at, n_grp, *scratch[7:14]), AllSum(at, n_grp, *scratch[14:])
    bar = pltpu.get_barrier_semaphore()
    for d in range(1, n_grp):
        pl.semaphore_signal(bar, inc=1, device_id=(lax.rem(at.g + d, n_grp), at.t), device_id_type=MESH)
    for d in range(1, n):
        pl.semaphore_signal(bar, inc=1, device_id=(at.g, lax.rem(at.t + d, n)), device_id_type=MESH)
    pl.semaphore_wait(bar, n_grp + n - 2)

    def owner(k):
        return lax.rem(at.g + 1 + k, n_grp)

    def send(k):
        r = chunk_rows(owner(k), block)
        return remote(gw.at[r, :], got.at[k], ws.at[k], wr.at[k], (owner(k), at.t))

    def send_proj(k):
        r = chunk_rows(owner(k), block)
        return remote(gw_proj.at[r, :], got_proj.at[k], ps.at[k], pr.at[k], (owner(k), at.t))

    for k in range(n_grp - 1):
        send_proj(k).start()
    qv[...] = jnp.zeros_like(qv)
    ln_sum[...] = jnp.zeros_like(ln_sum)

    def product(c):
        lhs = dproj[:, chunk_rows(c, rows), :].reshape(n * rows, hw)
        qv[...] += jnp.sum(lhs.astype(F32), 0, keepdims=True)

        def tile(i):
            y = dg(lhs, w_attn[cols(i), :], 1, 1)
            rs.parts[:, :, :, cols(i)] = y.astype(BF).reshape(at.Z, 2, rows, TILE)
        tiles(width // TILE, tile)
        rs.start(c)

    def weights(i):
        @pl.when(i == 0)
        def _():
            load.wait()
            load_x.wait()
        k = i // per
        first = pl.multiple_of(owner(k) * block + lax.rem(i, per) * TILE, TILE)
        y = dg(n1[:, pl.ds(first, TILE)], dproj[...].reshape(-1, hw), 0, 0)

        @pl.when(k < n_grp - 1)
        def _():
            gw[pl.ds(first, TILE), :] = y.astype(BF)

            @pl.when(lax.rem(i, per) == per - 1)
            def _():
                send(k).start()

        @pl.when(k == n_grp - 1)
        def _():
            g_attn[cols(lax.rem(i, per)), :] = y

    def norm_grad(c):
        r = chunk_rows(c, rows)
        xhat, inverse = rows_stats(x_share[r, :].astype(F32))
        dn = total[...]
        e = dn * gain[...]
        inner = jnp.mean(e, -1, keepdims=True) + xhat * jnp.mean(e * xhat, -1, keepdims=True)
        grad_x[r, :] = dh[r, :] + inverse * (e - inner)
        ln_sum[0:1, :] += jnp.sum(dn * xhat, 0, keepdims=True)
        ln_sum[1:2, :] += jnp.sum(dn, 0, keepdims=True)

    def tick(i, carry):
        c = i - 1

        @pl.when(inside(c, chunks))
        def _():
            rs.meet(c)
            rs.hop(c, 1)

        @pl.when(inside(i, chunks))
        def _():
            product(i)

        @pl.when(inside(c, chunks))
        def _():
            rs.hop(c, 2)

        @pl.when(i < width // TILE)
        def _():
            weights(i)

        @pl.when(inside(c, chunks))
        def _():
            for h in range(3, at.Z):
                rs.hop(c, h)

        @pl.when(i == chunks)
        def _():
            early.x[...] = stats[...]
            early.x[4:5, 0:hid] = up_sum[...]
            for h in range(heads):
                for j, src in ((0, 3 * h), (1, 3 * h + 2)):
                    early.x[4:5, hid + (2 * h + j) * HD:hid + (2 * h + j + 1) * HD] = qv[:, src * HD:(src + 1) * HD]
            early.start()

        @pl.when(i == chunks + 1)
        def _():
            early.turn()
        e = i - 2

        @pl.when(inside(e, chunks))
        def _():
            rs.finish(e, total)
            norm_grad(e)
        return carry

    lax.fori_loop(0, chunks + 2, tick, 0)
    part = width // 4
    for j in range(4):
        late.x[j:j + 1, :] = ln_sum[0:1, j * part:(j + 1) * part]
        late.x[j + 4:j + 5, :] = ln_sum[1:2, j * part:(j + 1) * part]
    late.start()
    mine = chunk_rows(at.g, block)
    g_proj[...] = gw_proj[mine, :].astype(F32)
    for k in range(n_grp - 1):
        send(k).wait()
        send_proj(k).wait()
        g_attn[...] += got[k].astype(F32)
        g_proj[...] += got_proj[k].astype(F32)
    late.turn()
    early.finish()
    sums[0:4, :] = early.total(0, 4)
    owned[...] = early.tbuf[:, 4, :]
    late.finish()
    ln = late.total(0, 8)
    for j in range(4):
        sums[4:5, j * part:(j + 1) * part] = ln[j:j + 1, :]
        sums[5:6, j * part:(j + 1) * part] = ln[j + 4:j + 5, :]
    sums[6:8, :] = jnp.zeros_like(sums[6:8, :])


def project_back(dproj, w_attn, n1, gw_proj, x, dh, gain, stats, up_sum, n, n_grp, chunks):
    length, hw = dproj.shape
    width = w_attn.shape[0]
    share = length // n
    rows = share // chunks
    block = width // n_grp
    pw = gw_proj.shape[1]
    vm, hbm = pl.BlockSpec(memory_space=pltpu.VMEM), pl.BlockSpec(memory_space=pl.ANY)
    S, dma = jax.ShapeDtypeStruct, pltpu.SemaphoreType.DMA
    return pl.pallas_call(
        functools.partial(back_kernel, n=n, n_grp=n_grp, chunks=chunks, rows=rows),
        in_specs=[vm, vm, hbm, vm, hbm] + [vm] * 4, out_specs=[vm] * 5,
        out_shape=[S((share, width), F32), S((block, hw), F32), S((block, pw), F32), S((8, width), F32),
                   S((n, width), F32)],
        scratch_shapes=[pltpu.VMEM((length, width), BF), pltpu.VMEM((share, width), BF), pltpu.VMEM((width, hw), BF),
                        pltpu.VMEM((n_grp - 1, block, hw), BF), pltpu.VMEM((n_grp - 1, block, pw), BF),
                        pltpu.VMEM((rows, width), F32), pltpu.VMEM((1, hw), F32), pltpu.VMEM((8, width), F32), dma((2,))]
                       + [dma((n_grp - 1,))] * 4 + scatter_scratch(chunks, n // 2, rows, width)
                       + all_sum_scratch(n_grp, n, (8, width)) + all_sum_scratch(n_grp, n, (8, width // 4)),
        compiler_params=pltpu.CompilerParams(collective_id=4, has_side_effects=True, vmem_limit_bytes=50 << 20),
        cost_estimate=pl.CostEstimate(flops=4 * length * hw * width, bytes_accessed=1 << 24, transcendentals=0),
        name="project_back",
    )(dproj.reshape(n, share, hw), w_attn, n1, gw_proj, x.reshape(n, share, width), dh, gain, stats, up_sum)


def ffn_kernel(n2_hbm, gradb_hbm, bias_hbm, up_hbm, down_hbm, out_hbm, ctx_hbm, hidden_hbm, vec, tokens,
               gw_hbm, gwo, dctx, dh, res, stats, bsum,
               w_up, w_down, w_out, ctx, hidden, wsem, acc_out, gat, acc_up, acc_down, gbuf, actb, dbb, total, gshare, b_up, keep, lsem, gsem, msem, *scratch, n, chunks, rows):
    at = Place(n)
    ag1, ag2 = Gather(at, gat, rows, *scratch[:4]), Gather(at, gat, rows, *scratch[4:8])
    rs, mlp = Scatter(at, *scratch[8:15]), Scatter(at, *scratch[15:])
    width, hid = w_up.shape
    m = n * rows

    load = pltpu.make_async_copy(n2_hbm, gat.at[at.t], lsem)
    load.start()
    load_g = pltpu.make_async_copy(gradb_hbm.at[at.t], gshare, msem.at[0])
    load_g.start()
    big = [pltpu.make_async_copy(src, dst, wsem.at[j]) for j, (src, dst) in enumerate(
        ((up_hbm, w_up), (down_hbm, w_down), (hidden_hbm, hidden), (out_hbm, w_out), (ctx_hbm, ctx)))]
    for copy in big:
        copy.start()
    load_b = pltpu.make_async_copy(bias_hbm.at[at.t], b_up, msem.at[1])
    load_b.start()
    share = hidden.shape[0]

    def alive(ranks, first, c):
        shape = (ranks, rows, 1)
        place = ((first + lax.broadcasted_iota(jnp.int32, shape, 0)) * share + c * rows
                 + lax.broadcasted_iota(jnp.int32, shape, 1))
        return jnp.where(place < tokens[...].reshape(1, 1, 1), 1.0, 0.0).reshape(ranks * rows, 1)

    def fetch(c):
        slot = lax.rem(c, 2)
        return pltpu.make_async_copy(gradb_hbm.at[:, chunk_rows(c, rows), :], gbuf.at[slot], gsem.at[slot])

    fetch(0).start()
    stats[...] = jnp.zeros_like(stats)
    bsum[...] = jnp.zeros_like(bsum)
    load.wait()
    load_g.wait()
    load_b.wait()
    at.barrier()

    a0, a1 = 0.7978845608028654, 0.044715

    def wide(c):
        return gat[:, chunk_rows(c, rows), :].reshape(m, width)

    def forward(c):
        @pl.when(c == 0)
        def _():
            for copy in big:
                copy.wait()
        fetch(c).wait()

        @pl.when(c + 1 < chunks)
        def _():
            fetch(c + 1).start()
        slot = lax.rem(c, 2)
        keep[...] = alive(n, 0, c)

        def tile(i):
            v = dg(wide(c), w_up[:, cols(i)], 1, 0) + b_up[:, cols(i)]
            ga = dg(gbuf[slot].reshape(m, width), w_down[:, cols(i)], 1, 0)
            v2 = v * v
            th = jnp.tanh(a0 * (v + a1 * v2 * v))
            half = 0.5 * (1.0 + th)
            actb[:, cols(i)] = (v * half * keep[...]).astype(BF)
            slope = half + 0.5 * v * (1.0 - th * th) * (a0 * (1.0 + 3.0 * a1 * v2))
            db = (ga * slope * keep[...]).astype(BF)
            dbb[:, cols(i)] = db
            bsum[:, cols(i)] += jnp.sum(db.astype(F32), 0, keepdims=True)
        tiles(hid // TILE, tile)

    def back(c):
        def tile(i):
            y = dg(dbb[...], w_up[cols(i), :], 1, 1)
            rs.parts[:, :, :, cols(i)] = y.astype(BF).reshape(at.Z, 2, rows, TILE)
        tiles(width // TILE, tile)

    def down(c):
        def tile(i):
            y = dg(actb[...], w_down[cols(i), :], 1, 1)
            mlp.parts[:, :, :, cols(i)] = y.astype(BF).reshape(at.Z, 2, rows, TILE)
        tiles(width // TILE, tile)

    def weights(c):
        slot = lax.rem(c, 2)

        def tile(i):
            x = gat[:, chunk_rows(c, rows), cols(i)].reshape(m, TILE)
            acc_up[cols(i), :] += dg(x, dbb[...], 0, 0)
            y = gbuf[slot, :, :, cols(i)].reshape(m, TILE)
            acc_down[cols(i), :] += dg(y, actb[...], 0, 0)
        tiles(width // TILE, tile)

    def norm_grad(c):
        r = chunk_rows(c, rows)
        xhat, inverse = rows_stats(hidden[r, :])
        dn2 = total[...]
        e = dn2 * vec[0:1, :]
        inner = jnp.mean(e, -1, keepdims=True) + xhat * jnp.mean(e * xhat, -1, keepdims=True)
        grad = gshare[r, :].astype(F32) * alive(1, at.t, c)
        d = grad + inverse * (e - inner)
        dh[r, :] = d
        gat[at.t, r, :] = d.astype(BF)
        stats[0:1, :] += jnp.sum(dn2 * xhat, 0, keepdims=True)
        stats[1:2, :] += jnp.sum(dn2, 0, keepdims=True)
        stats[2:3, :] += jnp.sum(d, 0, keepdims=True)
        stats[3:4, :] += jnp.sum(grad, 0, keepdims=True)

    def heads(c):
        def tile(i):
            x = gat[:, chunk_rows(c, rows), cols(i)].reshape(m, TILE)
            acc_out[cols(i), :] += dg(x, ctx[:, chunk_rows(c, rows), :].reshape(m, -1), 0, 0)
        tiles(width // TILE, tile)
        y = dg(wide(c), w_out[...], 1, 0)
        dctx[:, chunk_rows(c, rows), :] = y.astype(BF).reshape(n, rows, y.shape[1])

    def at_stage(c, fn):
        @pl.when(inside(c, chunks))
        def _():
            fn(c)

    def store_copies(j):
        r = chunk_rows(j, m)
        return (pltpu.make_async_copy(actb, gw_hbm.at[r, pl.ds(0, hid)], lsem),
                pltpu.make_async_copy(dbb, gw_hbm.at[r, pl.ds(hid, hid)], msem.at[0]))

    def store_wait(j):
        for copy in store_copies(j):
            copy.wait()

    def store(j):
        @pl.when((j >= 0) & (j < width // m))
        def _():
            @pl.when(j > 0)
            def _():
                store_wait(j - 1)
            r = chunk_rows(j, m)
            actb[...] = acc_up[r, :].astype(BF)
            dbb[...] = acc_down[r, :].astype(BF)
            for copy in store_copies(j):
                copy.start()

    per_slot = -(-(width // m) // (3 * (at.Z - 1)))

    def tick(i, carry):
        def stores(slot):
            for j in range(per_slot):
                store(((i - chunks - 2) * (at.Z - 1) + slot) * per_slot + j)
        at_stage(i, ag1.start)

        @pl.when(i == 0)
        def _():
            acc_up[...] = jnp.zeros_like(acc_up)
            acc_down[...] = jnp.zeros_like(acc_down)
            acc_out[...] = jnp.zeros_like(acc_out)
        at_stage(i - 3, rs.meet)
        for h in range(1, at.Z):
            at_stage(i - 3, lambda c: rs.hop(c, h))
            at_stage(i - 1, lambda c: ag1.hop(c, h))
            if h == 1:
                at_stage(i - 4, lambda c: mlp.hop(c, at.Z - 1))
                at_stage(i - 5, lambda c: ag2.hop(c, at.Z - 1))
                at_stage(i - 2, forward)
                stores(0)
            else:
                if h == 2:
                    def served(c):
                        mlp.finish(c, total)
                        r = chunk_rows(c, rows)
                        res[r, :] = (alive(1, at.t, c) * (hidden[r, :] + total[...] + vec[1:2, :])).astype(BF)
                    at_stage(i - 4, served)
                    at_stage(i - 3, mlp.meet)
                at_stage(i - 3, lambda c: mlp.hop(c, h - 1))
                at_stage(i - 4, lambda c: ag2.hop(c, h - 1))
                stores(h - 1)
                if h == 2:
                    at_stage(i - 2, back)

                    def gathered(c):
                        ag2.finish(c)
                        heads(c)
                    at_stage(i - 5, gathered)

        def rest(c):
            weights(c)
            rs.start(c)
        at_stage(i - 2, rest)

        def reduced(c):
            rs.finish(c, total)
            norm_grad(c)
            ag2.start(c)
        at_stage(i - 3, reduced)
        at_stage(i - 1, ag1.finish)

        def send_mlp(c):
            down(c)
            mlp.start(c)
        at_stage(i - 2, send_mlp)

        return carry

    lax.fori_loop(0, chunks + 5, tick, 0)

    store_wait(width // m - 1)
    gwo[...] = acc_out[...].astype(BF)


def feed_forward(n2, gradb, b_up, w_up, w_down, w_out, ctx, hidden, vec, tokens, n, chunks):
    length, width = gradb.shape
    hid, hw = w_up.shape[1], w_out.shape[1]
    share = length // n
    rows = share // chunks
    Z = n // 2
    vm, hbm = pl.BlockSpec(memory_space=pltpu.VMEM), pl.BlockSpec(memory_space=pl.ANY)
    S = jax.ShapeDtypeStruct
    m = n * rows
    return pl.pallas_call(
        functools.partial(ffn_kernel, n=n, chunks=chunks, rows=rows),
        in_specs=[hbm] * 8 + [vm] * 2,
        out_specs=[hbm] + [vm] * 6,
        out_shape=[S((width, 2 * hid), BF), S((width, hw), BF), S((n, share, hw), BF), S((share, width), F32),
                   S((share, width), BF), S((8, width), F32), S((1, hid), F32)],
        scratch_shapes=[pltpu.VMEM((width, hid), BF), pltpu.VMEM((width, hid), BF), pltpu.VMEM((width, hw), BF),
                        pltpu.VMEM((n, share, hw), BF), pltpu.VMEM((share, width), F32), pltpu.SemaphoreType.DMA((5,)),
                        pltpu.VMEM((width, hw), F32), pltpu.VMEM((n, share, width), BF), pltpu.VMEM((width, hid), F32), pltpu.VMEM((width, hid), F32),
                        pltpu.VMEM((2, n, rows, width), BF),
                        pltpu.VMEM((m, hid), BF), pltpu.VMEM((m, hid), BF), pltpu.VMEM((rows, width), F32),
                        pltpu.VMEM((share, width), BF), pltpu.VMEM((1, hid), F32), pltpu.VMEM((m, 1), F32),
                        pltpu.SemaphoreType.DMA, pltpu.SemaphoreType.DMA((2,)), pltpu.SemaphoreType.DMA((2,))]
                       + gather_sems(chunks, Z) + gather_sems(chunks, Z) + scatter_scratch(chunks, Z, rows, width) * 2,
        compiler_params=pltpu.CompilerParams(collective_id=3, has_side_effects=True, vmem_limit_bytes=62 << 20),
        cost_estimate=pl.CostEstimate(flops=12 * length * hid * width, bytes_accessed=1 << 26, transcendentals=0),
        name="feed_forward",
    )(n2, gradb.reshape(n, share, width), b_up.reshape(n, 1, hid), w_up, w_down, w_out, ctx.reshape(n, share, hw),
      hidden, vec, tokens)


def on_device(layer_input, out_cotangent, seq_group, seq_len, w_qkv, b_qv, w_out, b_out, w_up, b_up,
              w_down, b_down, first_norm_gain, first_norm_bias, second_norm_gain, second_norm_bias):
    n_tp, n_grp = lax.axis_size("tp"), lax.axis_size("grp")
    grp = lax.axis_index("grp")
    length, width = layer_input.shape
    hid, qv = w_up.shape[1], b_qv.shape[0] // n_tp

    proj, n1, w_attn, w_proj, up16, down16 = front(
        layer_input, w_qkv, w_out, w_up, w_down, jnp.stack([first_norm_gain, first_norm_bias]), b_qv, n_tp, n_grp)
    context, lse = attn_fwd(seq_group, seq_len, proj)
    hidden, n2, w_expand, w_reduce = attn_out(
        context, w_proj, jnp.stack([b_out, second_norm_gain, second_norm_bias]), layer_input, up16, down16,
        n_tp, n_grp, 8)
    tokens = jnp.sum(jnp.where(seq_group == grp, seq_len, 0)).reshape(1, 1)
    gw_ffn, gw_proj, dcontext, dh, result, stats, up_sum = feed_forward(
        n2, out_cotangent, b_up, w_expand, w_reduce, w_proj, context, hidden,
        jnp.stack([second_norm_gain, b_down]), tokens, n_tp, 8)
    grads_ffn = lax.psum_scatter(gw_ffn, "grp", scatter_dimension=0, tiled=True).astype(F32)
    grads_expand, grads_reduce = grads_ffn[:, :hid], grads_ffn[:, hid:]

    dproj = attn_bwd(seq_group, seq_len, proj, context, dcontext.reshape(length, -1), lse)
    grad_x, grads_attn, grads_proj, sums, owned = project_back(
        dproj, w_attn, n1, gw_proj, layer_input, dh, first_norm_gain[None], stats, up_sum, n_tp, n_grp, 8)
    return (result, grad_x, grads_attn, owned[:, hid:hid + qv].reshape(-1), grads_proj, sums[2],
            grads_expand, owned[:, :hid].reshape(-1), grads_reduce, sums[3], sums[4], sums[5],
            sums[0], sums[1])


def solution(mesh):
    rows, both, flat = P("grp", None), P("grp", "tp"), P()
    in_specs = (rows, rows, flat, flat, both, flat, both, flat, both, flat, both, flat, flat, flat, flat, flat)
    spread = P(("grp", "tp"), None)
    out_specs = (spread, spread, both, flat, both, flat, both, flat, both, flat, flat, flat, flat, flat)
    return jax.shard_map(on_device, mesh=mesh, in_specs=in_specs, out_specs=out_specs, check_vma=False)
```

```python
import functools

import jax
import jax.numpy as jnp
from jax import lax
from jax.experimental import pallas as pl
from jax.experimental.pallas import tpu as pltpu
from jax.sharding import PartitionSpec as P

HD = 128
BLK=512
F32=jnp.float32
BF=jnp.bfloat16
LOG2E=1.4426950408889634

def dg(a,b,ca,cb):
    return lax.dot_general(a,b,(((ca,),(cb,)),((),())),preferred_element_type=F32)


def group_tokens(grps, lens, seqs):
    g = lax.axis_index("grp")
    tokens, longest = jnp.int32(0), jnp.int32(0)
    for s in range(seqs):
        count = jnp.where(grps[s] == g, lens[s], 0)
        tokens, longest = tokens + count, jnp.maximum(longest, count)
    return tokens, longest > BLK


def below(shape):
    return lax.broadcasted_iota(jnp.int32, shape, 0) <= lax.broadcasted_iota(jnp.int32, shape, 1)


def attn_fwd_kernel(grps, lens, q_ref, k_ref, v_ref, o_ref, lse_ref, *, nb, seqs):
    tokens, is_long = group_tokens(grps, lens, seqs)
    c = HD ** -0.5 * LOG2E

    def attend(rows, early):
        q = q_ref[rows, :]
        pieces = [(rows, jnp.where(below((BLK, BLK)), dg(k_ref[rows, :], q, 1, 1), -1e30))]
        if early is not None:
            pieces.append((early, dg(k_ref[early, :], q, 1, 1)))
        top = functools.reduce(jnp.maximum, [jnp.max(s, 0, keepdims=True) for _, s in pieces]) * c
        total, acc = 0.0, 0.0
        for keys, s in pieces:
            p = jnp.exp2(s * c - top)
            total = total + jnp.sum(p, 0, keepdims=True)
            acc = acc + dg(v_ref[keys, :], p.astype(BF), 0, 0)
        o_ref[rows, :] = jnp.transpose(acc / total).astype(BF)
        lse_ref[0, :, rows] = top + jnp.log2(total)

    @pl.when(is_long)
    def _():
        for i in range(nb):
            attend(slice(i * BLK, (i + 1) * BLK), slice(0, i * BLK) if i else None)

    @pl.when(jnp.logical_not(is_long))
    def _():
        def block(i, carry):
            rows = pl.ds(pl.multiple_of(i * BLK, BLK), BLK)

            @pl.when(i * BLK < tokens)
            def _():
                attend(rows, None)

            @pl.when(i * BLK >= tokens)
            def _():
                o_ref[rows, :] = jnp.zeros((BLK, HD), BF)
                lse_ref[0, :, rows] = jnp.zeros((1, BLK), F32)
            return carry
        lax.fori_loop(0, nb, block, 0)


def attn_fwd(grps, lens, proj):
    length, heads = proj.shape[0], proj.shape[1] // (3 * HD)
    spec = lambda o: pl.BlockSpec((length, HD), lambda h, grps, lens: (0, 3 * h + o))
    return pl.pallas_call(
        functools.partial(attn_fwd_kernel, nb=length // BLK, seqs=grps.shape[0]),
        grid_spec=pltpu.PrefetchScalarGridSpec(
            num_scalar_prefetch=2, grid=(heads,), in_specs=[spec(0), spec(1), spec(2)],
            out_specs=[pl.BlockSpec((length, HD), lambda h, grps, lens: (0, h)),
                       pl.BlockSpec((1, 1, length), lambda h, grps, lens: (h, 0, 0))]),
        out_shape=[jax.ShapeDtypeStruct((length, heads * HD), BF), jax.ShapeDtypeStruct((heads, 1, length), F32)],
        compiler_params=pltpu.CompilerParams(vmem_limit_bytes=40 << 20),
        cost_estimate=pl.CostEstimate(flops=heads * length * length * HD * 2, bytes_accessed=length * heads * HD * 8,
                                      transcendentals=heads * length * length // 2),
        name="attn_fwd",
    )(grps, lens, proj, proj, proj)


def attn_bwd_kernel(grps, lens, q_ref, k_ref, v_ref, o_ref, do_ref, lse_ref, dp_ref, dq_sc, dl_sc, *, nb, seqs):
    tokens, is_long = group_tokens(grps, lens, seqs)
    scale = HD ** -0.5
    c = scale * LOG2E
    prod = do_ref[...].astype(F32) * o_ref[...].astype(F32)
    dl_sc[...] = jnp.sum(jnp.transpose(prod), 0, keepdims=True)

    def attend(keys, later, first):
        k, v = k_ref[keys, :], v_ref[keys, :]
        dk, dv = 0.0, 0.0
        for diag, rows in ((True, keys), (False, later)):
            if rows is None:
                continue
            q, do = q_ref[rows, :], do_ref[rows, :]
            p = jnp.exp2(dg(k, q, 1, 1) * c - lse_ref[0, :, rows])
            if diag:
                p = jnp.where(below((BLK, BLK)), p, 0.0)
            ds = (p * (dg(v, do, 1, 1) - dl_sc[:, rows])).astype(BF)
            dv = dv + dg(p.astype(BF), do, 1, 0)
            dk = dk + dg(ds, q, 1, 0)
            dq = dg(k, ds, 0, 0)
            dq_sc[:, rows] = dq if first else dq_sc[:, rows] + dq
        dp_ref[keys, HD:2 * HD] = (dk * scale).astype(BF)
        dp_ref[keys, 2 * HD:] = dv.astype(BF)

    @pl.when(is_long)
    def _():
        for j in range(nb):
            attend(slice(j * BLK, (j + 1) * BLK), slice((j + 1) * BLK, nb * BLK) if j < nb - 1 else None, j == 0)

    @pl.when(jnp.logical_not(is_long))
    def _():
        def block(i, carry):
            rows = pl.ds(pl.multiple_of(i * BLK, BLK), BLK)

            @pl.when(i * BLK < tokens)
            def _():
                attend(rows, None, True)

            @pl.when(i * BLK >= tokens)
            def _():
                dp_ref[rows, :] = jnp.zeros((BLK, 3 * HD), BF)
                dq_sc[:, rows] = jnp.zeros((HD, BLK), F32)
            return carry
        lax.fori_loop(0, nb, block, 0)
    dp_ref[:, :HD] = jnp.transpose(dq_sc[...] * scale).astype(BF)


def attn_bwd(grps, lens, proj, ctx, dctx, lse):
    length, heads = proj.shape[0], proj.shape[1] // (3 * HD)
    spec = lambda o: pl.BlockSpec((length, HD), lambda h, grps, lens: (0, 3 * h + o))
    head = pl.BlockSpec((length, HD), lambda h, grps, lens: (0, h))
    return pl.pallas_call(
        functools.partial(attn_bwd_kernel, nb=length // BLK, seqs=grps.shape[0]),
        grid_spec=pltpu.PrefetchScalarGridSpec(
            num_scalar_prefetch=2, grid=(heads,),
            in_specs=[spec(0), spec(1), spec(2), head, head,
                      pl.BlockSpec((1, 1, length), lambda h, grps, lens: (h, 0, 0))],
            out_specs=pl.BlockSpec((length, 3 * HD), lambda h, grps, lens: (0, h)),
            scratch_shapes=[pltpu.VMEM((HD, length), F32), pltpu.VMEM((1, length), F32)]),
        out_shape=jax.ShapeDtypeStruct((length, heads * 3 * HD), BF),
        compiler_params=pltpu.CompilerParams(vmem_limit_bytes=40 << 20),
        cost_estimate=pl.CostEstimate(flops=heads * length * length * HD * 5, bytes_accessed=length * heads * HD * 16,
                                      transcendentals=heads * length * length // 2),
        name="attn_bwd",
    )(grps, lens, proj, proj, proj, ctx, dctx, lse)


MESH = pl.DeviceIdType.MESH
TILE = 256


class Place:
    def __init__(self, n_tp):
        self.g = lax.axis_index("grp")
        t = lax.axis_index("tp")
        self.t, self.n, self.Z = t, n_tp, n_tp // 2
        self.z, self.k = t // 2, lax.rem(t, 2)
        self.right, self.left, self.sib = (self.g, t + 2), (self.g, t - 2), (self.g, t + 1 - 2 * self.k)
        self.has_right, self.has_left = self.z < self.Z - 1, self.z > 0

    def barrier(self, n_grp=0):
        bar = pltpu.get_barrier_semaphore()
        extra = grp_signal(self, n_grp) if n_grp else 0
        pl.semaphore_signal(bar, inc=1, device_id=self.sib, device_id_type=MESH)

        @pl.when(self.has_right)
        def _():
            pl.semaphore_signal(bar, inc=1, device_id=self.right, device_id_type=MESH)

        @pl.when(self.has_left)
        def _():
            pl.semaphore_signal(bar, inc=1, device_id=self.left, device_id_type=MESH)

        amount = 1 + extra + jnp.where(self.has_right, 1, 0) + jnp.where(self.has_left, 1, 0)
        pl.semaphore_wait(bar, amount)


def remote(src, dst, ssem, rsem, device):
    return pltpu.make_async_remote_copy(src, dst, ssem, rsem, device_id=device, device_id_type=MESH)


class Gather:
    def __init__(self, at, gat, rows, ls, lr, ss, sr):
        self.at, self.gat, self.rows = at, gat, rows
        self.ls, self.lr, self.ss, self.sr = ls, lr, ss, sr

    def block(self, zz, kk, c):
        return self.gat.at[2 * zz + kk, pl.ds(pl.multiple_of(c * self.rows, self.rows), self.rows), :]

    def line(self, c, side, d):
        at = self.at
        sign, device = (-1, at.right) if side == 0 else (1, at.left)
        b = self.block(at.z + sign * (d - 1), at.k, c)
        return remote(b, b, self.ls.at[c, side, d - 1], self.lr.at[c, side, d - 1], device)

    def line_in(self, c, side, d):
        at = self.at
        sign, device = (-1, at.right) if side == 0 else (1, at.left)
        b = self.block(at.z + sign * d, at.k, c)
        return remote(b, b, self.ls.at[c, side, d - 1], self.lr.at[c, side, d - 1], device)

    def across(self, c, zz):
        b = self.block(zz, self.at.k, c)
        return remote(b, b, self.ss.at[c, zz], self.sr.at[c, zz], self.at.sib)

    def across_in(self, c, zz):
        b = self.block(zz, 1 - self.at.k, c)
        return remote(b, b, self.ss.at[c, zz], self.sr.at[c, zz], self.at.sib)

    def start(self, c):
        at = self.at

        @pl.when(at.has_right)
        def _():
            self.line(c, 0, 1).start()

        @pl.when(at.has_left)
        def _():
            self.line(c, 1, 1).start()

        self.across(c, at.z).start()

    def hop(self, c, d):
        at = self.at

        @pl.when(at.z >= d)
        def _():
            self.line_in(c, 0, d).wait_recv()
            if d < at.Z - 1:
                @pl.when(at.has_right)
                def _():
                    self.line(c, 0, d + 1).start()
            self.across(c, at.z - d).start()

        @pl.when(at.z + d <= at.Z - 1)
        def _():
            self.line_in(c, 1, d).wait_recv()
            if d < at.Z - 1:
                @pl.when(at.has_left)
                def _():
                    self.line(c, 1, d + 1).start()
            self.across(c, at.z + d).start()

    def finish(self, c):
        at = self.at
        for zz in range(at.Z):
            self.across_in(c, zz).wait_recv()
            self.across(c, zz).wait_send()
        for d in range(1, at.Z):
            @pl.when(at.has_right & (at.z >= d - 1))
            def _():
                self.line(c, 0, d).wait_send()

            @pl.when(at.has_left & (at.z + d - 1 <= at.Z - 1))
            def _():
                self.line(c, 1, d).wait_send()


class Scatter:
    def __init__(self, at, parts, pair, hops, cs, cr, hs, hr):
        self.at, self.parts, self.pair, self.hops = at, parts, pair, hops
        self.slots = pair.shape[0]
        self.cs, self.cr, self.hs, self.hr = cs, cr, hs, hr

    def across(self, c):
        c = lax.rem(c, self.slots)
        return remote(self.parts.at[:, 1 - self.at.k], self.pair.at[c], self.cs.at[c], self.cr.at[c], self.at.sib)

    def line(self, c, side, h, target):
        c = lax.rem(c, self.slots)
        device = self.at.right if side == 0 else self.at.left
        return remote(self.pair.at[c, target], self.hops.at[side, c, h - 1],
                      self.hs.at[c, side, h - 1], self.hr.at[c, side, h - 1], device)

    def start(self, c):
        self.across(c).start()

    def meet(self, c):
        self.across(c).wait()
        own = self.parts[:, pl.ds(self.at.k, 1)]
        own = own.reshape(own.shape[0], own.shape[2], own.shape[3])
        c = lax.rem(c, self.slots)
        self.pair[c] = (self.pair[c].astype(F32) + own.astype(F32)).astype(BF)

    def hop(self, c, h):
        at = self.at
        for side in (0, 1):
            pos = at.z if side == 0 else at.Z - 1 - at.z
            target = at.z + at.Z - h if side == 0 else at.z - at.Z + h

            @pl.when((pos <= h - 1) & (pos < at.Z - 1))
            def _():
                if h >= 2:
                    @pl.when(pos >= 1)
                    def _():
                        self.line(c, side, h - 1, target).wait_recv()
                        b = lax.rem(c, self.slots)
                        self.pair[b, target] = (self.pair[b, target].astype(F32)
                                                + self.hops[side, b, h - 2].astype(F32)).astype(BF)
                self.line(c, side, h, target).start()

    def finish(self, c, total):
        at = self.at
        b = lax.rem(c, self.slots)
        total[...] = self.pair[b, at.z].astype(F32)
        for side in (0, 1):
            pos = at.z if side == 0 else at.Z - 1 - at.z

            @pl.when(pos >= 1)
            def _():
                self.line(c, side, at.Z - 1, at.z).wait_recv()
                total[...] += self.hops[side, b, at.Z - 2].astype(F32)

            for h in range(1, at.Z):
                @pl.when((pos <= h - 1) & (pos < at.Z - 1))
                def _():
                    self.line(c, side, h, at.z).wait_send()


class GroupGather:
    def __init__(self, at, n_grp, full, ss, sr):
        self.at, self.full, self.ss, self.sr = at, full, ss, sr
        self.P = n_grp // 2
        self.size = full.shape[0] // n_grp
        self.p, self.q = at.g // 2, lax.rem(at.g, 2)
        self.partner = (at.g + 1 - 2 * self.q, at.t)

    def peer(self, j):
        return lax.rem(self.p + j, self.P)

    def rows(self, p, q, half=None):
        size = self.size if half is None else self.size // 2
        first = (2 * p + q) * self.size + (size if half == 1 else 0)
        return self.full.at[pl.ds(pl.multiple_of(first, size), size), :]

    def copy(self, kind, j, incoming=False):
        p, q = self.p, self.q
        src = lax.rem(p + self.P - j, self.P)
        if kind == 0:
            b, k, dev = self.rows(p, 1 - q if incoming else q), 0, self.partner
        elif kind == 1:
            b, k, dev = self.rows(src if incoming else p, q), j, (2 * self.peer(j) + q, self.at.t)
        elif kind == 2:
            b, k = self.rows(src if incoming else p, 1 - q, 1), self.P - 1 + j
            dev = (2 * self.peer(j) + q, self.at.t)
        else:
            b, k = self.rows(src, 1 - q if incoming else q, 0), 2 * (self.P - 1) + j
            dev = self.partner
        return remote(b, b, self.ss.at[k], self.sr.at[k], dev)

    def start(self):
        self.copy(0, 0).start()
        for j in range(1, self.P):
            self.copy(1, j).start()

    def forward(self):
        self.copy(0, 0, True).wait_recv()
        for j in range(1, self.P):
            self.copy(2, j).start()
        for j in range(1, self.P):
            self.copy(1, j, True).wait_recv()
            self.copy(3, j).start()

    def finish(self):
        for j in range(1, self.P):
            for kind in (2, 3):
                self.copy(kind, j, True).wait_recv()
                self.copy(kind, j).wait_send()
            self.copy(1, j).wait_send()
        self.copy(0, 0).wait_send()


def group_sems(n_grp):
    k = 1 + 3 * (n_grp // 2 - 1)
    return [pltpu.SemaphoreType.DMA((k,)), pltpu.SemaphoreType.DMA((k,))]


def grp_signal(at, n_grp):
    bar = pltpu.get_barrier_semaphore()
    p, q = at.g // 2, lax.rem(at.g, 2)
    pl.semaphore_signal(bar, inc=1, device_id=(at.g + 1 - 2 * q, at.t), device_id_type=MESH)
    for j in range(1, n_grp // 2):
        pl.semaphore_signal(bar, inc=1, device_id=(2 * lax.rem(p + j, n_grp // 2) + q, at.t), device_id_type=MESH)
    return n_grp // 2


def gather_sems(chunks, Z):
    dma = pltpu.SemaphoreType.DMA
    return [dma((chunks, 2, Z - 1)), dma((chunks, 2, Z - 1)), dma((chunks, Z)), dma((chunks, Z))]


def scatter_scratch(chunks, Z, rows, width):
    chunks = min(chunks, 4)
    dma = pltpu.SemaphoreType.DMA
    return [pltpu.VMEM((Z, 2, rows, width), BF), pltpu.VMEM((chunks, Z, rows, width), BF),
            pltpu.VMEM((2, chunks, Z - 1, rows, width), BF),
            dma((chunks,)), dma((chunks,)), dma((chunks, 2, Z - 1)), dma((chunks, 2, Z - 1))]


def inside(c, chunks):
    return (c >= 0) & (c < chunks)


def chunk_rows(c, rows):
    return pl.ds(pl.multiple_of(c * rows, rows), rows)


def tiles(count, body):
    def step(i, carry):
        body(i)
        return carry
    lax.fori_loop(0, count, step, 0)


def cols(i, size=TILE):
    return pl.ds(pl.multiple_of(i * size, size), size)


def rows_stats(rows):
    mean = jnp.mean(rows, -1, keepdims=True)
    centred = rows - mean
    inverse = lax.rsqrt(jnp.mean(centred * centred, -1, keepdims=True) + 1e-05)
    return centred * inverse, inverse


def product_scatter(at, rs, lhs_ref, w_ref, total, chunks, rows, epilogue, extra):
    def product(c):
        lhs = lhs_ref[:, chunk_rows(c, rows), :].reshape(at.n * rows, lhs_ref.shape[2])

        def tile(i):
            y = dg(lhs, w_ref[cols(i, 1024), :], 1, 1)
            rs.parts[:, :, :, cols(i, 1024)] = y.astype(BF).reshape(at.Z, 2, rows, 1024)
        tiles(w_ref.shape[0] // 1024, tile)
        rs.start(c)

    def tick(i, carry):
        c = i - 1

        @pl.when(inside(c, chunks))
        def _():
            rs.meet(c)
            rs.hop(c, 1)

        @pl.when(inside(i, chunks))
        def _():
            product(i)

        @pl.when(inside(c, chunks))
        def _():
            for h in range(2, at.Z):
                rs.hop(c, h)

        e = i - 2

        @pl.when(inside(e, chunks))
        def _():
            rs.finish(e, total)
            epilogue(e)
        extra(i)
        return carry

    lax.fori_loop(0, chunks + 2, tick, 0)


def out_kernel(ctx, w_out, vec, x_hbm, up16, down16, hidden, n2, up_hbm, down_hbm,
               x_share, total, lsem, *sc, n, n_grp, chunks, rows):
    at = Place(n)
    load = pltpu.make_async_copy(x_hbm.at[at.t], x_share, lsem.at[0])
    load.start()
    up, down = GroupGather(at, n_grp, up_hbm, *sc[:2]), GroupGather(at, n_grp, down_hbm, *sc[2:4])
    own = chunk_rows(at.g, up.size)
    put_up = pltpu.make_async_copy(up16, up_hbm.at[own, :], lsem.at[1])
    put_down = pltpu.make_async_copy(down16, down_hbm.at[own, :], lsem.at[2])
    put_up.start()
    put_down.start()
    at.barrier(n_grp)
    load.wait()
    put_up.wait()
    put_down.wait()
    up.start()
    down.start()

    def epilogue(c):
        r = chunk_rows(c, rows)
        h = x_share[r, :].astype(F32) + total[...] + vec[0:1, :]
        hidden[r, :] = h
        n2[r, :] = (rows_stats(h)[0] * vec[1:2, :] + vec[2:3, :]).astype(BF)

    def extra(i):
        @pl.when(i == chunks // 2)
        def _():
            up.forward()

        @pl.when(i == chunks - 1)
        def _():
            down.forward()

    product_scatter(at, Scatter(at, *sc[4:]), ctx, w_out, total, chunks, rows, epilogue, extra)
    up.finish()
    down.finish()


def attn_out(ctx, w_out, vec, x, up16, down16, n, n_grp, chunks):
    length, hw = ctx.shape
    width = x.shape[1]
    share = length // n
    rows = share // chunks
    hid = up16.shape[1]
    vm, hbm = pl.BlockSpec(memory_space=pltpu.VMEM), pl.BlockSpec(memory_space=pl.ANY)
    S = jax.ShapeDtypeStruct
    return pl.pallas_call(
        functools.partial(out_kernel, n=n, n_grp=n_grp, chunks=chunks, rows=rows),
        in_specs=[vm] * 3 + [hbm] * 3, out_specs=[vm] * 2 + [hbm] * 2,
        out_shape=[S((share, width), F32), S((share, width), BF), S((width, hid), BF), S((width, hid), BF)],
        scratch_shapes=[pltpu.VMEM((share, width), BF), pltpu.VMEM((rows, width), F32), pltpu.SemaphoreType.DMA((3,))]
                       + group_sems(n_grp) * 2 + scatter_scratch(chunks, n // 2, rows, width),
        compiler_params=pltpu.CompilerParams(collective_id=2, has_side_effects=True, vmem_limit_bytes=40 << 20),
        cost_estimate=pl.CostEstimate(flops=2 * length * hw * width, bytes_accessed=1 << 23, transcendentals=0),
        name="attn_out",
    )(ctx.reshape(n, share, hw), w_out, vec, x.reshape(n, share, width), up16, down16)


def front_kernel(x_hbm, w_qkv, w_out, w_up, w_down, vec, bias_hbm, proj, n1_hbm, w_attn, w_proj, up16, down16,
                 xbuf, n1, acc, bias, xsem, osem, bsem, *sc, n, n_grp, parts):
    at = Place(n)
    width, hw = w_attn.shape
    block = width // n_grp
    length = n1.shape[0]
    rows = length // parts
    heads = hw // (3 * HD)

    def fetch(i):
        slot = lax.rem(i, 2)
        return pltpu.make_async_copy(x_hbm.at[chunk_rows(i, rows), :], xbuf.at[slot], xsem.at[slot])

    def put(i):
        r = chunk_rows(i, rows)
        return pltpu.make_async_copy(n1.at[r, :], n1_hbm.at[r, :], osem)

    get_bias = pltpu.make_async_copy(bias_hbm.at[at.t], bias, bsem)
    get_bias.start()
    fetch(0).start()
    own = chunk_rows(at.g, block)
    w_attn[own, :] = w_qkv[...].astype(BF)
    bar = pltpu.get_barrier_semaphore()
    pl.semaphore_wait(bar, grp_signal(at, n_grp))
    qkv, out = GroupGather(at, n_grp, w_attn, *sc[:2]), GroupGather(at, n_grp, w_proj, *sc[2:])
    qkv.start()
    w_proj[own, :] = w_out[...].astype(BF)
    up16[...] = w_up[...].astype(BF)
    down16[...] = w_down[...].astype(BF)

    def norm(i):
        fetch(i).wait()

        @pl.when(i + 1 < parts)
        def _():
            fetch(i + 1).start()
        y = rows_stats(xbuf[lax.rem(i, 2)].astype(F32))[0] * vec[0:1, :] + vec[1:2, :]
        n1[chunk_rows(i, rows), :] = y.astype(BF)
        put(i).start()
    tiles(parts, norm)

    def partial(b, first=False, last=False):
        r = chunk_rows(b, block)

        def tile(i):
            m = chunk_rows(i, 2 * rows)
            y = dg(n1[m, r], w_attn[r, :], 1, 0)
            if not first:
                y = y + acc[m, :]
            acc[m, :] = y
        tiles(parts // 2, tile)

    p, q, P = at.g // 2, lax.rem(at.g, 2), n_grp // 2
    partial(at.g, True)
    qkv.forward()
    out.start()
    partial(2 * p + 1 - q)
    for j in range(1, P):
        partial(2 * lax.rem(p + j, P) + q)
    out.forward()
    qkv.finish()
    for j in range(1, P):
        partial(2 * lax.rem(p + j, P) + 1 - q)
    get_bias.wait()

    def write(i):
        m = chunk_rows(i, rows)
        for h in range(heads):
            c = 3 * h * HD
            proj[m, c:c + HD] = (acc[m, c:c + HD] + bias[:, 2 * h * HD:(2 * h + 1) * HD]).astype(BF)
            c += HD
            proj[m, c:c + HD] = acc[m, c:c + HD].astype(BF)
            c += HD
            proj[m, c:c + HD] = (acc[m, c:c + HD] + bias[:, (2 * h + 1) * HD:(2 * h + 2) * HD]).astype(BF)
        put(i).wait()
    tiles(parts, write)
    out.finish()


def front(x, w_qkv, w_out, w_up, w_down, vec, b_qv, n, n_grp):
    length, width = x.shape
    block, hw = w_qkv.shape
    pw, hid = w_out.shape[1], w_up.shape[1]
    parts = length // TILE
    vm, hbm = pl.BlockSpec(memory_space=pltpu.VMEM), pl.BlockSpec(memory_space=pl.ANY)
    S, dma = jax.ShapeDtypeStruct, pltpu.SemaphoreType.DMA
    return pl.pallas_call(
        functools.partial(front_kernel, n=n, n_grp=n_grp, parts=parts),
        in_specs=[hbm] + [vm] * 5 + [hbm], out_specs=[vm, hbm] + [vm] * 4,
        out_shape=[S((length, hw), BF), S((length, width), BF), S((width, hw), BF), S((width, pw), BF),
                   S((block, hid), BF), S((block, hid), BF)],
        scratch_shapes=[pltpu.VMEM((2, length // parts, width), BF), pltpu.VMEM((length, width), BF),
                        pltpu.VMEM((length, hw), F32), pltpu.VMEM((1, b_qv.shape[0] // n), F32),
                        dma((2,)), dma, dma] + group_sems(n_grp) * 2,
        compiler_params=pltpu.CompilerParams(collective_id=5, has_side_effects=True, vmem_limit_bytes=50 << 20),
        cost_estimate=pl.CostEstimate(flops=2 * length * hw * width, bytes_accessed=1 << 24, transcendentals=0),
        name="front",
    )(x, w_qkv, w_out, w_up, w_down, vec, b_qv.reshape(n, 1, -1))


class AllSum:
    def __init__(self, at, n_grp, x, gbuf, tbuf, gs, gr, ts, tr):
        self.at, self.n_grp, self.x, self.gbuf, self.tbuf = at, n_grp, x, gbuf, tbuf
        self.gs, self.gr, self.ts, self.tr = gs, gr, ts, tr

    def over_grp(self, d):
        at = self.at
        return remote(self.x, self.gbuf.at[at.g], self.gs.at[d - 1], self.gr.at[d - 1],
                      (lax.rem(at.g + d, self.n_grp), at.t))

    def over_tp(self, d):
        at = self.at
        return remote(self.tbuf.at[at.t], self.tbuf.at[at.t], self.ts.at[d - 1], self.tr.at[d - 1],
                      (at.g, lax.rem(at.t + d, at.n)))

    def start(self):
        for d in range(1, self.n_grp):
            self.over_grp(d).start()
        self.gbuf[self.at.g] = self.x[...]

    def turn(self):
        for d in range(1, self.n_grp):
            self.over_grp(d).wait()
        total = self.gbuf[0]
        for i in range(1, self.n_grp):
            total = total + self.gbuf[i]
        self.tbuf[self.at.t] = total
        for d in range(1, self.at.n):
            self.over_tp(d).start()

    def finish(self):
        for d in range(1, self.at.n):
            self.over_tp(d).wait()

    def total(self, lo, hi):
        out = self.tbuf[0, lo:hi, :]
        for i in range(1, self.at.n):
            out = out + self.tbuf[i, lo:hi, :]
        return out


def all_sum_scratch(n_grp, n, shape):
    dma = pltpu.SemaphoreType.DMA
    return [pltpu.VMEM(shape, F32), pltpu.VMEM((n_grp,) + shape, F32), pltpu.VMEM((n,) + shape, F32),
            dma((n_grp - 1,)), dma((n_grp - 1,)), dma((n - 1,)), dma((n - 1,))]


def back_kernel(dproj, w_attn, n1_hbm, gw_proj, x_hbm, dh, gain, stats, up_sum,
                grad_x, g_attn, g_proj, sums, owned,
                n1, x_share, gw, got, got_proj, total, qv, ln_sum, nsem, ws, wr, ps, pr, *scratch, n, n_grp, chunks, rows):
    at = Place(n)
    width, hw = w_attn.shape
    block = width // n_grp
    per = block // TILE
    heads = hw // (3 * HD)
    hid = up_sum.shape[1]
    load = pltpu.make_async_copy(n1_hbm, n1, nsem.at[0])
    load.start()
    load_x = pltpu.make_async_copy(x_hbm.at[at.t], x_share, nsem.at[1])
    load_x.start()
    rs, early, late = Scatter(at, *scratch[:7]), AllSum(at, n_grp, *scratch[7:14]), AllSum(at, n_grp, *scratch[14:])
    bar = pltpu.get_barrier_semaphore()
    for d in range(1, n_grp):
        pl.semaphore_signal(bar, inc=1, device_id=(lax.rem(at.g + d, n_grp), at.t), device_id_type=MESH)
    for d in range(1, n):
        pl.semaphore_signal(bar, inc=1, device_id=(at.g, lax.rem(at.t + d, n)), device_id_type=MESH)
    pl.semaphore_wait(bar, n_grp + n - 2)

    def owner(k):
        return lax.rem(at.g + 1 + k, n_grp)

    def send(k):
        r = chunk_rows(owner(k), block)
        return remote(gw.at[r, :], got.at[k], ws.at[k], wr.at[k], (owner(k), at.t))

    def send_proj(k):
        r = chunk_rows(owner(k), block)
        return remote(gw_proj.at[r, :], got_proj.at[k], ps.at[k], pr.at[k], (owner(k), at.t))

    for k in range(n_grp - 1):
        send_proj(k).start()
    qv[...] = jnp.zeros_like(qv)
    ln_sum[...] = jnp.zeros_like(ln_sum)

    def product(c):
        lhs = dproj[:, chunk_rows(c, rows), :].reshape(n * rows, hw)
        qv[...] += jnp.sum(lhs.astype(F32), 0, keepdims=True)

        def tile(i):
            y = dg(lhs, w_attn[cols(i, 1024), :], 1, 1)
            rs.parts[:, :, :, cols(i, 1024)] = y.astype(BF).reshape(at.Z, 2, rows, 1024)
        tiles(width // 1024, tile)
        rs.start(c)

    def weights(i):
        @pl.when(i == 0)
        def _():
            load.wait()
            load_x.wait()
        k = i // per
        first = pl.multiple_of(owner(k) * block + lax.rem(i, per) * TILE, TILE)
        y = dg(n1[:, pl.ds(first, TILE)], dproj[...].reshape(-1, hw), 0, 0)

        @pl.when(k < n_grp - 1)
        def _():
            gw[pl.ds(first, TILE), :] = y.astype(BF)

            @pl.when(lax.rem(i, per) == per - 1)
            def _():
                send(k).start()

        @pl.when(k == n_grp - 1)
        def _():
            g_attn[cols(lax.rem(i, per)), :] = y

    def norm_grad(c):
        r = chunk_rows(c, rows)
        xhat, inverse = rows_stats(x_share[r, :].astype(F32))
        dn = total[...]
        e = dn * gain[...]
        inner = jnp.mean(e, -1, keepdims=True) + xhat * jnp.mean(e * xhat, -1, keepdims=True)
        grad_x[r, :] = dh[r, :] + inverse * (e - inner)
        ln_sum[0:1, :] += jnp.sum(dn * xhat, 0, keepdims=True)
        ln_sum[1:2, :] += jnp.sum(dn, 0, keepdims=True)

    def tick(i, carry):
        c = i - 1

        @pl.when(inside(c, chunks))
        def _():
            rs.meet(c)
            rs.hop(c, 1)

        @pl.when(inside(i, chunks))
        def _():
            product(i)

        @pl.when(inside(c, chunks))
        def _():
            rs.hop(c, 2)

        @pl.when(i < width // TILE)
        def _():
            weights(i)

        @pl.when(inside(c, chunks))
        def _():
            for h in range(3, at.Z):
                rs.hop(c, h)

        @pl.when(i == chunks)
        def _():
            early.x[...] = stats[...]
            early.x[4:5, 0:hid] = up_sum[...]
            for h in range(heads):
                for j, src in ((0, 3 * h), (1, 3 * h + 2)):
                    early.x[4:5, hid + (2 * h + j) * HD:hid + (2 * h + j + 1) * HD] = qv[:, src * HD:(src + 1) * HD]
            early.start()

        @pl.when(i == chunks + 1)
        def _():
            early.turn()
        e = i - 2

        @pl.when(inside(e, chunks))
        def _():
            rs.finish(e, total)
            norm_grad(e)
        return carry

    lax.fori_loop(0, chunks + 2, tick, 0)
    part = width // 4
    for j in range(4):
        late.x[j:j + 1, :] = ln_sum[0:1, j * part:(j + 1) * part]
        late.x[j + 4:j + 5, :] = ln_sum[1:2, j * part:(j + 1) * part]
    late.start()
    mine = chunk_rows(at.g, block)
    g_proj[...] = gw_proj[mine, :].astype(F32)
    for k in range(n_grp - 1):
        send(k).wait()
        send_proj(k).wait()
        g_attn[...] += got[k].astype(F32)
        g_proj[...] += got_proj[k].astype(F32)
    late.turn()
    early.finish()
    sums[0:4, :] = early.total(0, 4)
    owned[...] = early.tbuf[:, 4, :]
    late.finish()
    ln = late.total(0, 8)
    for j in range(4):
        sums[4:5, j * part:(j + 1) * part] = ln[j:j + 1, :]
        sums[5:6, j * part:(j + 1) * part] = ln[j + 4:j + 5, :]
    sums[6:8, :] = jnp.zeros_like(sums[6:8, :])


def project_back(dproj, w_attn, n1, gw_proj, x, dh, gain, stats, up_sum, n, n_grp, chunks):
    length, hw = dproj.shape
    width = w_attn.shape[0]
    share = length // n
    rows = share // chunks
    block = width // n_grp
    pw = gw_proj.shape[1]
    vm, hbm = pl.BlockSpec(memory_space=pltpu.VMEM), pl.BlockSpec(memory_space=pl.ANY)
    S, dma = jax.ShapeDtypeStruct, pltpu.SemaphoreType.DMA
    return pl.pallas_call(
        functools.partial(back_kernel, n=n, n_grp=n_grp, chunks=chunks, rows=rows),
        in_specs=[vm, vm, hbm, vm, hbm] + [vm] * 4, out_specs=[vm] * 5,
        out_shape=[S((share, width), F32), S((block, hw), F32), S((block, pw), F32), S((8, width), F32),
                   S((n, width), F32)],
        scratch_shapes=[pltpu.VMEM((length, width), BF), pltpu.VMEM((share, width), BF), pltpu.VMEM((width, hw), BF),
                        pltpu.VMEM((n_grp - 1, block, hw), BF), pltpu.VMEM((n_grp - 1, block, pw), BF),
                        pltpu.VMEM((rows, width), F32), pltpu.VMEM((1, hw), F32), pltpu.VMEM((8, width), F32), dma((2,))]
                       + [dma((n_grp - 1,))] * 4 + scatter_scratch(chunks, n // 2, rows, width)
                       + all_sum_scratch(n_grp, n, (8, width)) + all_sum_scratch(n_grp, n, (8, width // 4)),
        compiler_params=pltpu.CompilerParams(collective_id=4, has_side_effects=True, vmem_limit_bytes=50 << 20),
        cost_estimate=pl.CostEstimate(flops=4 * length * hw * width, bytes_accessed=1 << 24, transcendentals=0),
        name="project_back",
    )(dproj.reshape(n, share, hw), w_attn, n1, gw_proj, x.reshape(n, share, width), dh, gain, stats, up_sum)


def ffn_kernel(n2_hbm, gradb_hbm, bias_hbm, up_hbm, down_hbm, out_hbm, ctx_hbm, hidden_hbm, vec, tokens,
               gw_hbm, gwo, dctx, dh, res, stats, bsum,
               w_up, w_down, w_out, ctx, hidden, wsem, acc_out, gat, acc_up, acc_down, gbuf, actb, dbb, total, gshare, b_up, keep, lsem, gsem, msem, *scratch, n, chunks, rows):
    at = Place(n)
    ag1, ag2 = Gather(at, gat, rows, *scratch[:4]), Gather(at, gat, rows, *scratch[4:8])
    rs, mlp = Scatter(at, *scratch[8:15]), Scatter(at, *scratch[15:])
    width, hid = w_up.shape
    m = n * rows

    load = pltpu.make_async_copy(n2_hbm, gat.at[at.t], lsem)
    load.start()
    load_g = pltpu.make_async_copy(gradb_hbm.at[at.t], gshare, msem.at[0])
    load_g.start()
    big = [pltpu.make_async_copy(src, dst, wsem.at[j]) for j, (src, dst) in enumerate(
        ((up_hbm, w_up), (down_hbm, w_down), (hidden_hbm, hidden), (out_hbm, w_out), (ctx_hbm, ctx)))]
    for copy in big:
        copy.start()
    load_b = pltpu.make_async_copy(bias_hbm.at[at.t], b_up, msem.at[1])
    load_b.start()
    share = hidden.shape[0]

    def alive(ranks, first, c):
        shape = (ranks, rows, 1)
        place = ((first + lax.broadcasted_iota(jnp.int32, shape, 0)) * share + c * rows
                 + lax.broadcasted_iota(jnp.int32, shape, 1))
        return jnp.where(place < tokens[...].reshape(1, 1, 1), 1.0, 0.0).reshape(ranks * rows, 1)

    def fetch(c):
        slot = lax.rem(c, 2)
        return pltpu.make_async_copy(gradb_hbm.at[:, chunk_rows(c, rows), :], gbuf.at[slot], gsem.at[slot])

    fetch(0).start()
    stats[...] = jnp.zeros_like(stats)
    bsum[...] = jnp.zeros_like(bsum)
    load.wait()
    load_g.wait()
    load_b.wait()
    at.barrier()

    a0, a1 = 0.7978845608028654, 0.044715

    def wide(c):
        return gat[:, chunk_rows(c, rows), :].reshape(m, width)

    def forward(c):
        @pl.when(c == 0)
        def _():
            for copy in big:
                copy.wait()
        fetch(c).wait()

        @pl.when(c + 1 < chunks)
        def _():
            fetch(c + 1).start()
        slot = lax.rem(c, 2)
        keep[...] = alive(n, 0, c)

        def tile(i):
            v = dg(wide(c), w_up[:, cols(i, 512)], 1, 0) + b_up[:, cols(i, 512)]
            ga = dg(gbuf[slot].reshape(m, width), w_down[:, cols(i, 512)], 1, 0)
            v2 = v * v
            th = jnp.tanh(a0 * (v + a1 * v2 * v))
            half = 0.5 * (1.0 + th)
            actb[:, cols(i, 512)] = (v * half * keep[...]).astype(BF)
            slope = half + 0.5 * v * (1.0 - th * th) * (a0 * (1.0 + 3.0 * a1 * v2))
            db = (ga * slope * keep[...]).astype(BF)
            dbb[:, cols(i, 512)] = db
            bsum[:, cols(i, 512)] += jnp.sum(db.astype(F32), 0, keepdims=True)
        tiles(hid // 512, tile)

    def back(c):
        def tile(i):
            y = dg(dbb[...], w_up[cols(i, 1024), :], 1, 1)
            rs.parts[:, :, :, cols(i, 1024)] = y.astype(BF).reshape(at.Z, 2, rows, 1024)
        tiles(width // 1024, tile)

    def down(c):
        def tile(i):
            y = dg(actb[...], w_down[cols(i, 1024), :], 1, 1)
            mlp.parts[:, :, :, cols(i, 1024)] = y.astype(BF).reshape(at.Z, 2, rows, 1024)
        tiles(width // 1024, tile)

    def weights(c):
        slot = lax.rem(c, 2)

        def tile(i):
            x = gat[:, chunk_rows(c, rows), cols(i, 512)].reshape(m, 512)
            acc_up[cols(i, 512), :] += dg(x, dbb[...], 0, 0)
            y = gbuf[slot, :, :, cols(i, 512)].reshape(m, 512)
            acc_down[cols(i, 512), :] += dg(y, actb[...], 0, 0)
        tiles(width // 512, tile)

    def norm_grad(c):
        r = chunk_rows(c, rows)
        xhat, inverse = rows_stats(hidden[r, :])
        dn2 = total[...]
        e = dn2 * vec[0:1, :]
        inner = jnp.mean(e, -1, keepdims=True) + xhat * jnp.mean(e * xhat, -1, keepdims=True)
        grad = gshare[r, :].astype(F32) * alive(1, at.t, c)
        d = grad + inverse * (e - inner)
        dh[r, :] = d
        gat[at.t, r, :] = d.astype(BF)
        stats[0:1, :] += jnp.sum(dn2 * xhat, 0, keepdims=True)
        stats[1:2, :] += jnp.sum(dn2, 0, keepdims=True)
        stats[2:3, :] += jnp.sum(d, 0, keepdims=True)
        stats[3:4, :] += jnp.sum(grad, 0, keepdims=True)

    def heads(c):
        def tile(i):
            x = gat[:, chunk_rows(c, rows), cols(i, 512)].reshape(m, 512)
            acc_out[cols(i, 512), :] += dg(x, ctx[:, chunk_rows(c, rows), :].reshape(m, -1), 0, 0)
        tiles(width // 512, tile)
        y = dg(wide(c), w_out[...], 1, 0)
        dctx[:, chunk_rows(c, rows), :] = y.astype(BF).reshape(n, rows, y.shape[1])

    def at_stage(c, fn):
        @pl.when(inside(c, chunks))
        def _():
            fn(c)

    def store_copies(j):
        r = chunk_rows(j, m)
        return (pltpu.make_async_copy(actb, gw_hbm.at[r, pl.ds(0, hid)], lsem),
                pltpu.make_async_copy(dbb, gw_hbm.at[r, pl.ds(hid, hid)], msem.at[0]))

    def store_wait(j):
        for copy in store_copies(j):
            copy.wait()

    def store(j):
        @pl.when((j >= 0) & (j < width // m))
        def _():
            @pl.when(j > 0)
            def _():
                store_wait(j - 1)
            r = chunk_rows(j, m)
            actb[...] = acc_up[r, :].astype(BF)
            dbb[...] = acc_down[r, :].astype(BF)
            for copy in store_copies(j):
                copy.start()

    per_slot = -(-(width // m) // (3 * (at.Z - 1)))

    def tick(i, carry):
        def stores(slot):
            for j in range(per_slot):
                store(((i - chunks - 2) * (at.Z - 1) + slot) * per_slot + j)
        at_stage(i, ag1.start)

        @pl.when(i == 0)
        def _():
            acc_up[...] = jnp.zeros_like(acc_up)
            acc_down[...] = jnp.zeros_like(acc_down)
            acc_out[...] = jnp.zeros_like(acc_out)
        at_stage(i - 3, rs.meet)
        for h in range(1, at.Z):
            at_stage(i - 3, lambda c: rs.hop(c, h))
            at_stage(i - 1, lambda c: ag1.hop(c, h))
            if h == 1:
                at_stage(i - 4, lambda c: mlp.hop(c, at.Z - 1))
                at_stage(i - 5, lambda c: ag2.hop(c, at.Z - 1))
                at_stage(i - 2, forward)
                stores(0)
            else:
                if h == 2:
                    def served(c):
                        mlp.finish(c, total)
                        r = chunk_rows(c, rows)
                        res[r, :] = (alive(1, at.t, c) * (hidden[r, :] + total[...] + vec[1:2, :])).astype(BF)
                    at_stage(i - 4, served)
                    at_stage(i - 3, mlp.meet)
                at_stage(i - 3, lambda c: mlp.hop(c, h - 1))
                at_stage(i - 4, lambda c: ag2.hop(c, h - 1))
                stores(h - 1)
                if h == 2:
                    at_stage(i - 2, back)

                    def gathered(c):
                        ag2.finish(c)
                        heads(c)
                    at_stage(i - 5, gathered)

        def rest(c):
            weights(c)
            rs.start(c)
        at_stage(i - 2, rest)

        def reduced(c):
            rs.finish(c, total)
            norm_grad(c)
            ag2.start(c)
        at_stage(i - 3, reduced)
        at_stage(i - 1, ag1.finish)

        def send_mlp(c):
            down(c)
            mlp.start(c)
        at_stage(i - 2, send_mlp)

        return carry

    lax.fori_loop(0, chunks + 5, tick, 0)

    store_wait(width // m - 1)
    gwo[...] = acc_out[...].astype(BF)


def feed_forward(n2, gradb, b_up, w_up, w_down, w_out, ctx, hidden, vec, tokens, n, chunks):
    length, width = gradb.shape
    hid, hw = w_up.shape[1], w_out.shape[1]
    share = length // n
    rows = share // chunks
    Z = n // 2
    vm, hbm = pl.BlockSpec(memory_space=pltpu.VMEM), pl.BlockSpec(memory_space=pl.ANY)
    S = jax.ShapeDtypeStruct
    m = n * rows
    return pl.pallas_call(
        functools.partial(ffn_kernel, n=n, chunks=chunks, rows=rows),
        in_specs=[hbm] * 8 + [vm] * 2,
        out_specs=[hbm] + [vm] * 6,
        out_shape=[S((width, 2 * hid), BF), S((width, hw), BF), S((n, share, hw), BF), S((share, width), F32),
                   S((share, width), BF), S((8, width), F32), S((1, hid), F32)],
        scratch_shapes=[pltpu.VMEM((width, hid), BF), pltpu.VMEM((width, hid), BF), pltpu.VMEM((width, hw), BF),
                        pltpu.VMEM((n, share, hw), BF), pltpu.VMEM((share, width), F32), pltpu.SemaphoreType.DMA((5,)),
                        pltpu.VMEM((width, hw), F32), pltpu.VMEM((n, share, width), BF), pltpu.VMEM((width, hid), F32), pltpu.VMEM((width, hid), F32),
                        pltpu.VMEM((2, n, rows, width), BF),
                        pltpu.VMEM((m, hid), BF), pltpu.VMEM((m, hid), BF), pltpu.VMEM((rows, width), F32),
                        pltpu.VMEM((share, width), BF), pltpu.VMEM((1, hid), F32), pltpu.VMEM((m, 1), F32),
                        pltpu.SemaphoreType.DMA, pltpu.SemaphoreType.DMA((2,)), pltpu.SemaphoreType.DMA((2,))]
                       + gather_sems(chunks, Z) + gather_sems(chunks, Z) + scatter_scratch(chunks, Z, rows, width) * 2,
        compiler_params=pltpu.CompilerParams(collective_id=3, has_side_effects=True, vmem_limit_bytes=62 << 20),
        cost_estimate=pl.CostEstimate(flops=12 * length * hid * width, bytes_accessed=1 << 26, transcendentals=0),
        name="feed_forward",
    )(n2, gradb.reshape(n, share, width), b_up.reshape(n, 1, hid), w_up, w_down, w_out, ctx.reshape(n, share, hw),
      hidden, vec, tokens)


def on_device(layer_input, out_cotangent, seq_group, seq_len, w_qkv, b_qv, w_out, b_out, w_up, b_up,
              w_down, b_down, first_norm_gain, first_norm_bias, second_norm_gain, second_norm_bias):
    n_tp, n_grp = lax.axis_size("tp"), lax.axis_size("grp")
    grp = lax.axis_index("grp")
    length, width = layer_input.shape
    hid, qv = w_up.shape[1], b_qv.shape[0] // n_tp

    proj, n1, w_attn, w_proj, up16, down16 = front(
        layer_input, w_qkv, w_out, w_up, w_down, jnp.stack([first_norm_gain, first_norm_bias]), b_qv, n_tp, n_grp)
    context, lse = attn_fwd(seq_group, seq_len, proj)
    hidden, n2, w_expand, w_reduce = attn_out(
        context, w_proj, jnp.stack([b_out, second_norm_gain, second_norm_bias]), layer_input, up16, down16,
        n_tp, n_grp, 8)
    tokens = jnp.sum(jnp.where(seq_group == grp, seq_len, 0)).reshape(1, 1)
    gw_ffn, gw_proj, dcontext, dh, result, stats, up_sum = feed_forward(
        n2, out_cotangent, b_up, w_expand, w_reduce, w_proj, context, hidden,
        jnp.stack([second_norm_gain, b_down]), tokens, n_tp, 8)
    grads_ffn = lax.psum_scatter(gw_ffn, "grp", scatter_dimension=0, tiled=True).astype(F32)
    grads_expand, grads_reduce = grads_ffn[:, :hid], grads_ffn[:, hid:]

    dproj = attn_bwd(seq_group, seq_len, proj, context, dcontext.reshape(length, -1), lse)
    grad_x, grads_attn, grads_proj, sums, owned = project_back(
        dproj, w_attn, n1, gw_proj, layer_input, dh, first_norm_gain[None], stats, up_sum, n_tp, n_grp, 8)
    return (result, grad_x, grads_attn, owned[:, hid:hid + qv].reshape(-1), grads_proj, sums[2],
            grads_expand, owned[:, :hid].reshape(-1), grads_reduce, sums[3], sums[4], sums[5],
            sums[0], sums[1])


def solution(mesh):
    rows, both, flat = P("grp", None), P("grp", "tp"), P()
    in_specs = (rows, rows, flat, flat, both, flat, both, flat, both, flat, both, flat, flat, flat, flat, flat)
    spread = P(("grp", "tp"), None)
    out_specs = (spread, spread, both, flat, both, flat, both, flat, both, flat, flat, flat, flat, flat)
    return jax.shard_map(on_device, mesh=mesh, in_specs=in_specs, out_specs=out_specs, check_vma=False)
```

```python
import functools

import jax
import jax.numpy as jnp
from jax import lax
from jax.experimental import pallas as pl
from jax.experimental.pallas import tpu as pltpu
from jax.sharding import PartitionSpec as P

HD = 128
BLK=512
F32=jnp.float32
BF=jnp.bfloat16
LOG2E=1.4426950408889634

def dg(a,b,ca,cb):
    return lax.dot_general(a,b,(((ca,),(cb,)),((),())),preferred_element_type=F32)


def group_tokens(grps, lens, seqs):
    g = lax.axis_index("grp")
    tokens, longest = jnp.int32(0), jnp.int32(0)
    for s in range(seqs):
        count = jnp.where(grps[s] == g, lens[s], 0)
        tokens, longest = tokens + count, jnp.maximum(longest, count)
    return tokens, longest > BLK


def below(shape):
    return lax.broadcasted_iota(jnp.int32, shape, 0) <= lax.broadcasted_iota(jnp.int32, shape, 1)


def attn_fwd_kernel(grps, lens, q_ref, k_ref, v_ref, o_ref, lse_ref, *, nb, seqs):
    tokens, is_long = group_tokens(grps, lens, seqs)
    c = HD ** -0.5 * LOG2E

    def attend(rows, early):
        q = q_ref[rows, :]
        pieces = [(rows, jnp.where(below((BLK, BLK)), dg(k_ref[rows, :], q, 1, 1), -1e30))]
        if early is not None:
            pieces.append((early, dg(k_ref[early, :], q, 1, 1)))
        top = functools.reduce(jnp.maximum, [jnp.max(s, 0, keepdims=True) for _, s in pieces]) * c
        total, acc = 0.0, 0.0
        for keys, s in pieces:
            p = jnp.exp2(s * c - top)
            total = total + jnp.sum(p, 0, keepdims=True)
            acc = acc + dg(v_ref[keys, :], p.astype(BF), 0, 0)
        o_ref[rows, :] = jnp.transpose(acc / total).astype(BF)
        lse_ref[0, :, rows] = top + jnp.log2(total)

    @pl.when(is_long)
    def _():
        for i in range(nb):
            attend(slice(i * BLK, (i + 1) * BLK), slice(0, i * BLK) if i else None)

    @pl.when(jnp.logical_not(is_long))
    def _():
        def block(i, carry):
            rows = pl.ds(pl.multiple_of(i * BLK, BLK), BLK)

            @pl.when(i * BLK < tokens)
            def _():
                attend(rows, None)

            @pl.when(i * BLK >= tokens)
            def _():
                o_ref[rows, :] = jnp.zeros((BLK, HD), BF)
                lse_ref[0, :, rows] = jnp.zeros((1, BLK), F32)
            return carry
        lax.fori_loop(0, nb, block, 0)


def attn_fwd(grps, lens, proj):
    length, heads = proj.shape[0], proj.shape[1] // (3 * HD)
    spec = lambda o: pl.BlockSpec((length, HD), lambda h, grps, lens: (0, 3 * h + o))
    return pl.pallas_call(
        functools.partial(attn_fwd_kernel, nb=length // BLK, seqs=grps.shape[0]),
        grid_spec=pltpu.PrefetchScalarGridSpec(
            num_scalar_prefetch=2, grid=(heads,), in_specs=[spec(0), spec(1), spec(2)],
            out_specs=[pl.BlockSpec((length, HD), lambda h, grps, lens: (0, h)),
                       pl.BlockSpec((1, 1, length), lambda h, grps, lens: (h, 0, 0))]),
        out_shape=[jax.ShapeDtypeStruct((length, heads * HD), BF), jax.ShapeDtypeStruct((heads, 1, length), F32)],
        compiler_params=pltpu.CompilerParams(vmem_limit_bytes=62 << 20),
        cost_estimate=pl.CostEstimate(flops=heads * length * length * HD * 2, bytes_accessed=length * heads * HD * 8,
                                      transcendentals=heads * length * length // 2),
        name="attn_fwd",
    )(grps, lens, proj, proj, proj)


def attn_bwd_kernel(grps, lens, q_ref, k_ref, v_ref, o_ref, do_ref, lse_ref, dp_ref, dq_sc, dl_sc, *, nb, seqs):
    tokens, is_long = group_tokens(grps, lens, seqs)
    scale = HD ** -0.5
    c = scale * LOG2E
    prod = do_ref[...].astype(F32) * o_ref[...].astype(F32)
    dl_sc[...] = jnp.sum(jnp.transpose(prod), 0, keepdims=True)

    def attend(keys, later, first):
        k, v = k_ref[keys, :], v_ref[keys, :]
        dk, dv = 0.0, 0.0
        for diag, rows in ((True, keys), (False, later)):
            if rows is None:
                continue
            q, do = q_ref[rows, :], do_ref[rows, :]
            p = jnp.exp2(dg(k, q, 1, 1) * c - lse_ref[0, :, rows])
            if diag:
                p = jnp.where(below((BLK, BLK)), p, 0.0)
            ds = (p * (dg(v, do, 1, 1) - dl_sc[:, rows])).astype(BF)
            dv = dv + dg(p.astype(BF), do, 1, 0)
            dk = dk + dg(ds, q, 1, 0)
            dq = dg(k, ds, 0, 0)
            dq_sc[:, rows] = dq if first else dq_sc[:, rows] + dq
        dp_ref[keys, HD:2 * HD] = (dk * scale).astype(BF)
        dp_ref[keys, 2 * HD:] = dv.astype(BF)

    @pl.when(is_long)
    def _():
        for j in range(nb):
            attend(slice(j * BLK, (j + 1) * BLK), slice((j + 1) * BLK, nb * BLK) if j < nb - 1 else None, j == 0)

    @pl.when(jnp.logical_not(is_long))
    def _():
        def block(i, carry):
            rows = pl.ds(pl.multiple_of(i * BLK, BLK), BLK)

            @pl.when(i * BLK < tokens)
            def _():
                attend(rows, None, True)

            @pl.when(i * BLK >= tokens)
            def _():
                dp_ref[rows, :] = jnp.zeros((BLK, 3 * HD), BF)
                dq_sc[:, rows] = jnp.zeros((HD, BLK), F32)
            return carry
        lax.fori_loop(0, nb, block, 0)
    dp_ref[:, :HD] = jnp.transpose(dq_sc[...] * scale).astype(BF)


def attn_bwd(grps, lens, proj, ctx, dctx, lse):
    length, heads = proj.shape[0], proj.shape[1] // (3 * HD)
    spec = lambda o: pl.BlockSpec((length, HD), lambda h, grps, lens: (0, 3 * h + o))
    head = pl.BlockSpec((length, HD), lambda h, grps, lens: (0, h))
    return pl.pallas_call(
        functools.partial(attn_bwd_kernel, nb=length // BLK, seqs=grps.shape[0]),
        grid_spec=pltpu.PrefetchScalarGridSpec(
            num_scalar_prefetch=2, grid=(heads,),
            in_specs=[spec(0), spec(1), spec(2), head, head,
                      pl.BlockSpec((1, 1, length), lambda h, grps, lens: (h, 0, 0))],
            out_specs=pl.BlockSpec((length, 3 * HD), lambda h, grps, lens: (0, h)),
            scratch_shapes=[pltpu.VMEM((HD, length), F32), pltpu.VMEM((1, length), F32)]),
        out_shape=jax.ShapeDtypeStruct((length, heads * 3 * HD), BF),
        compiler_params=pltpu.CompilerParams(vmem_limit_bytes=62 << 20),
        cost_estimate=pl.CostEstimate(flops=heads * length * length * HD * 5, bytes_accessed=length * heads * HD * 16,
                                      transcendentals=heads * length * length // 2),
        name="attn_bwd",
    )(grps, lens, proj, proj, proj, ctx, dctx, lse)


MESH = pl.DeviceIdType.MESH
TILE = 256


class Place:
    def __init__(self, n_tp):
        self.g = lax.axis_index("grp")
        t = lax.axis_index("tp")
        self.t, self.n, self.Z = t, n_tp, n_tp // 2
        self.z, self.k = t // 2, lax.rem(t, 2)
        self.right, self.left, self.sib = (self.g, t + 2), (self.g, t - 2), (self.g, t + 1 - 2 * self.k)
        self.has_right, self.has_left = self.z < self.Z - 1, self.z > 0

    def barrier(self, n_grp=0):
        bar = pltpu.get_barrier_semaphore()
        extra = grp_signal(self, n_grp) if n_grp else 0
        pl.semaphore_signal(bar, inc=1, device_id=self.sib, device_id_type=MESH)

        @pl.when(self.has_right)
        def _():
            pl.semaphore_signal(bar, inc=1, device_id=self.right, device_id_type=MESH)

        @pl.when(self.has_left)
        def _():
            pl.semaphore_signal(bar, inc=1, device_id=self.left, device_id_type=MESH)

        amount = 1 + extra + jnp.where(self.has_right, 1, 0) + jnp.where(self.has_left, 1, 0)
        pl.semaphore_wait(bar, amount)


def remote(src, dst, ssem, rsem, device):
    return pltpu.make_async_remote_copy(src, dst, ssem, rsem, device_id=device, device_id_type=MESH)


class Gather:
    def __init__(self, at, gat, rows, ls, lr, ss, sr):
        self.at, self.gat, self.rows = at, gat, rows
        self.ls, self.lr, self.ss, self.sr = ls, lr, ss, sr

    def block(self, zz, kk, c):
        return self.gat.at[2 * zz + kk, pl.ds(pl.multiple_of(c * self.rows, self.rows), self.rows), :]

    def line(self, c, side, d):
        at = self.at
        sign, device = (-1, at.right) if side == 0 else (1, at.left)
        b = self.block(at.z + sign * (d - 1), at.k, c)
        return remote(b, b, self.ls.at[c, side, d - 1], self.lr.at[c, side, d - 1], device)

    def line_in(self, c, side, d):
        at = self.at
        sign, device = (-1, at.right) if side == 0 else (1, at.left)
        b = self.block(at.z + sign * d, at.k, c)
        return remote(b, b, self.ls.at[c, side, d - 1], self.lr.at[c, side, d - 1], device)

    def across(self, c, zz):
        b = self.block(zz, self.at.k, c)
        return remote(b, b, self.ss.at[c, zz], self.sr.at[c, zz], self.at.sib)

    def across_in(self, c, zz):
        b = self.block(zz, 1 - self.at.k, c)
        return remote(b, b, self.ss.at[c, zz], self.sr.at[c, zz], self.at.sib)

    def start(self, c):
        at = self.at

        @pl.when(at.has_right)
        def _():
            self.line(c, 0, 1).start()

        @pl.when(at.has_left)
        def _():
            self.line(c, 1, 1).start()

        self.across(c, at.z).start()

    def hop(self, c, d):
        at = self.at

        @pl.when(at.z >= d)
        def _():
            self.line_in(c, 0, d).wait_recv()
            if d < at.Z - 1:
                @pl.when(at.has_right)
                def _():
                    self.line(c, 0, d + 1).start()
            self.across(c, at.z - d).start()

        @pl.when(at.z + d <= at.Z - 1)
        def _():
            self.line_in(c, 1, d).wait_recv()
            if d < at.Z - 1:
                @pl.when(at.has_left)
                def _():
                    self.line(c, 1, d + 1).start()
            self.across(c, at.z + d).start()

    def finish(self, c):
        at = self.at
        for zz in range(at.Z):
            self.across_in(c, zz).wait_recv()
            self.across(c, zz).wait_send()
        for d in range(1, at.Z):
            @pl.when(at.has_right & (at.z >= d - 1))
            def _():
                self.line(c, 0, d).wait_send()

            @pl.when(at.has_left & (at.z + d - 1 <= at.Z - 1))
            def _():
                self.line(c, 1, d).wait_send()


class Scatter:
    def __init__(self, at, parts, pair, hops, cs, cr, hs, hr):
        self.at, self.parts, self.pair, self.hops = at, parts, pair, hops
        self.slots = pair.shape[0]
        self.cs, self.cr, self.hs, self.hr = cs, cr, hs, hr

    def across(self, c):
        c = lax.rem(c, self.slots)
        return remote(self.parts.at[:, 1 - self.at.k], self.pair.at[c], self.cs.at[c], self.cr.at[c], self.at.sib)

    def line(self, c, side, h, target):
        c = lax.rem(c, self.slots)
        device = self.at.right if side == 0 else self.at.left
        return remote(self.pair.at[c, target], self.hops.at[side, c, h - 1],
                      self.hs.at[c, side, h - 1], self.hr.at[c, side, h - 1], device)

    def start(self, c):
        self.across(c).start()

    def meet(self, c):
        self.across(c).wait()
        own = self.parts[:, pl.ds(self.at.k, 1)]
        own = own.reshape(own.shape[0], own.shape[2], own.shape[3])
        c = lax.rem(c, self.slots)
        self.pair[c] = (self.pair[c].astype(F32) + own.astype(F32)).astype(BF)

    def hop(self, c, h):
        at = self.at
        for side in (0, 1):
            pos = at.z if side == 0 else at.Z - 1 - at.z
            target = at.z + at.Z - h if side == 0 else at.z - at.Z + h

            @pl.when((pos <= h - 1) & (pos < at.Z - 1))
            def _():
                if h >= 2:
                    @pl.when(pos >= 1)
                    def _():
                        self.line(c, side, h - 1, target).wait_recv()
                        b = lax.rem(c, self.slots)
                        self.pair[b, target] = (self.pair[b, target].astype(F32)
                                                + self.hops[side, b, h - 2].astype(F32)).astype(BF)
                self.line(c, side, h, target).start()

    def finish(self, c, total):
        at = self.at
        b = lax.rem(c, self.slots)
        total[...] = self.pair[b, at.z].astype(F32)
        for side in (0, 1):
            pos = at.z if side == 0 else at.Z - 1 - at.z

            @pl.when(pos >= 1)
            def _():
                self.line(c, side, at.Z - 1, at.z).wait_recv()
                total[...] += self.hops[side, b, at.Z - 2].astype(F32)

            for h in range(1, at.Z):
                @pl.when((pos <= h - 1) & (pos < at.Z - 1))
                def _():
                    self.line(c, side, h, at.z).wait_send()


class GroupGather:
    def __init__(self, at, n_grp, full, ss, sr):
        self.at, self.full, self.ss, self.sr = at, full, ss, sr
        self.P = n_grp // 2
        self.size = full.shape[0] // n_grp
        self.p, self.q = at.g // 2, lax.rem(at.g, 2)
        self.partner = (at.g + 1 - 2 * self.q, at.t)

    def peer(self, j):
        return lax.rem(self.p + j, self.P)

    def rows(self, p, q, half=None):
        size = self.size if half is None else self.size // 2
        first = (2 * p + q) * self.size + (size if half == 1 else 0)
        return self.full.at[pl.ds(pl.multiple_of(first, size), size), :]

    def copy(self, kind, j, incoming=False):
        p, q = self.p, self.q
        src = lax.rem(p + self.P - j, self.P)
        if kind == 0:
            b, k, dev = self.rows(p, 1 - q if incoming else q), 0, self.partner
        elif kind == 1:
            b, k, dev = self.rows(src if incoming else p, q), j, (2 * self.peer(j) + q, self.at.t)
        elif kind == 2:
            b, k = self.rows(src if incoming else p, 1 - q, 1), self.P - 1 + j
            dev = (2 * self.peer(j) + q, self.at.t)
        else:
            b, k = self.rows(src, 1 - q if incoming else q, 0), 2 * (self.P - 1) + j
            dev = self.partner
        return remote(b, b, self.ss.at[k], self.sr.at[k], dev)

    def start(self):
        self.copy(0, 0).start()
        for j in range(1, self.P):
            self.copy(1, j).start()

    def forward(self):
        self.copy(0, 0, True).wait_recv()
        for j in range(1, self.P):
            self.copy(2, j).start()
        for j in range(1, self.P):
            self.copy(1, j, True).wait_recv()
            self.copy(3, j).start()

    def finish(self):
        for j in range(1, self.P):
            for kind in (2, 3):
                self.copy(kind, j, True).wait_recv()
                self.copy(kind, j).wait_send()
            self.copy(1, j).wait_send()
        self.copy(0, 0).wait_send()


def group_sems(n_grp):
    k = 1 + 3 * (n_grp // 2 - 1)
    return [pltpu.SemaphoreType.DMA((k,)), pltpu.SemaphoreType.DMA((k,))]


def grp_signal(at, n_grp):
    bar = pltpu.get_barrier_semaphore()
    p, q = at.g // 2, lax.rem(at.g, 2)
    pl.semaphore_signal(bar, inc=1, device_id=(at.g + 1 - 2 * q, at.t), device_id_type=MESH)
    for j in range(1, n_grp // 2):
        pl.semaphore_signal(bar, inc=1, device_id=(2 * lax.rem(p + j, n_grp // 2) + q, at.t), device_id_type=MESH)
    return n_grp // 2


def gather_sems(chunks, Z):
    dma = pltpu.SemaphoreType.DMA
    return [dma((chunks, 2, Z - 1)), dma((chunks, 2, Z - 1)), dma((chunks, Z)), dma((chunks, Z))]


def scatter_scratch(chunks, Z, rows, width):
    chunks = min(chunks, 4)
    dma = pltpu.SemaphoreType.DMA
    return [pltpu.VMEM((Z, 2, rows, width), BF), pltpu.VMEM((chunks, Z, rows, width), BF),
            pltpu.VMEM((2, chunks, Z - 1, rows, width), BF),
            dma((chunks,)), dma((chunks,)), dma((chunks, 2, Z - 1)), dma((chunks, 2, Z - 1))]


def inside(c, chunks):
    return (c >= 0) & (c < chunks)


def chunk_rows(c, rows):
    return pl.ds(pl.multiple_of(c * rows, rows), rows)


def tiles(count, body):
    def step(i, carry):
        body(i)
        return carry
    lax.fori_loop(0, count, step, 0)


def cols(i, size=TILE):
    return pl.ds(pl.multiple_of(i * size, size), size)


def rows_stats(rows):
    mean = jnp.mean(rows, -1, keepdims=True)
    centred = rows - mean
    inverse = lax.rsqrt(jnp.mean(centred * centred, -1, keepdims=True) + 1e-05)
    return centred * inverse, inverse


def product_scatter(at, rs, lhs_ref, w_ref, total, chunks, rows, epilogue, extra):
    def product(c):
        lhs = lhs_ref[:, chunk_rows(c, rows), :].reshape(at.n * rows, lhs_ref.shape[2])

        def tile(i):
            y = dg(lhs, w_ref[cols(i, 1024), :], 1, 1)
            rs.parts[:, :, :, cols(i, 1024)] = y.astype(BF).reshape(at.Z, 2, rows, 1024)
        tiles(w_ref.shape[0] // 1024, tile)
        rs.start(c)

    def tick(i, carry):
        c = i - 1

        @pl.when(inside(c, chunks))
        def _():
            rs.meet(c)
            rs.hop(c, 1)

        @pl.when(inside(i, chunks))
        def _():
            product(i)

        @pl.when(inside(c, chunks))
        def _():
            for h in range(2, at.Z):
                rs.hop(c, h)

        e = i - 2

        @pl.when(inside(e, chunks))
        def _():
            rs.finish(e, total)
            epilogue(e)
        extra(i)
        return carry

    lax.fori_loop(0, chunks + 2, tick, 0)


def out_kernel(ctx, w_out, b_out, gain, shift, x_hbm, up16, down16, hidden, n2, up_hbm, down_hbm,
               x_share, total, up_own, down_own, lsem, *sc, n, n_grp, chunks, rows):
    at = Place(n)
    fetches = [pltpu.make_async_copy(up16, up_own, lsem.at[3]), pltpu.make_async_copy(down16, down_own, lsem.at[4])]
    for copy in fetches:
        copy.start()
    load = pltpu.make_async_copy(x_hbm.at[at.t], x_share, lsem.at[0])
    load.start()
    up, down = GroupGather(at, n_grp, up_hbm, *sc[:2]), GroupGather(at, n_grp, down_hbm, *sc[2:4])
    own = chunk_rows(at.g, up.size)
    put_up = pltpu.make_async_copy(up_own, up_hbm.at[own, :], lsem.at[1])
    put_down = pltpu.make_async_copy(down_own, down_hbm.at[own, :], lsem.at[2])
    for copy in fetches:
        copy.wait()
    put_up.start()
    put_down.start()
    at.barrier(n_grp)
    load.wait()
    put_up.wait()
    put_down.wait()
    up.start()
    down.start()

    def epilogue(c):
        r = chunk_rows(c, rows)
        h = x_share[r, :].astype(F32) + total[...] + b_out[...]
        hidden[r, :] = h
        n2[r, :] = (rows_stats(h)[0] * gain[...] + shift[...]).astype(BF)

    def extra(i):
        @pl.when(i == chunks // 2)
        def _():
            up.forward()

        @pl.when(i == chunks - 1)
        def _():
            down.forward()

    product_scatter(at, Scatter(at, *sc[4:]), ctx, w_out, total, chunks, rows, epilogue, extra)
    up.finish()
    down.finish()


def attn_out(ctx, w_out, b_out, gain, shift, x, up16, down16, n, n_grp, chunks):
    length, hw = ctx.shape
    width = x.shape[1]
    share = length // n
    rows = share // chunks
    hid = up16.shape[1]
    vm, hbm = pl.BlockSpec(memory_space=pltpu.VMEM), pl.BlockSpec(memory_space=pl.ANY)
    S = jax.ShapeDtypeStruct
    return pl.pallas_call(
        functools.partial(out_kernel, n=n, n_grp=n_grp, chunks=chunks, rows=rows),
        in_specs=[vm] * 5 + [hbm] * 3, out_specs=[vm] * 2 + [hbm] * 2,
        out_shape=[S((share, width), F32), S((share, width), BF), S((width, hid), BF), S((width, hid), BF)],
        scratch_shapes=[pltpu.VMEM((share, width), BF), pltpu.VMEM((rows, width), F32), pltpu.VMEM(up16.shape, BF),
                        pltpu.VMEM(up16.shape, BF), pltpu.SemaphoreType.DMA((5,))]
                       + group_sems(n_grp) * 2 + scatter_scratch(chunks, n // 2, rows, width),
        compiler_params=pltpu.CompilerParams(collective_id=2, has_side_effects=True, vmem_limit_bytes=62 << 20),
        cost_estimate=pl.CostEstimate(flops=2 * length * hw * width, bytes_accessed=1 << 23, transcendentals=0),
        name="attn_out",
    )(ctx.reshape(n, share, hw), w_out, b_out[None], gain[None], shift[None], x.reshape(n, share, width), up16, down16)


def front_kernel(x_hbm, w_qkv, w_out, w_up, w_down, gain, shift, bias_hbm, proj, n1_hbm, w_attn, w_proj, up16, down16,
                 xbuf, n1, acc, bias, xsem, osem, bsem, *sc, n, n_grp, parts):
    at = Place(n)
    width, hw = w_attn.shape
    block = width // n_grp
    length = n1.shape[0]
    rows = length // parts
    heads = hw // (3 * HD)

    def fetch(i):
        slot = lax.rem(i, 2)
        return pltpu.make_async_copy(x_hbm.at[chunk_rows(i, rows), :], xbuf.at[slot], xsem.at[slot])

    def put(i):
        r = chunk_rows(i, rows)
        return pltpu.make_async_copy(n1.at[r, :], n1_hbm.at[r, :], osem)

    get_bias = pltpu.make_async_copy(bias_hbm.at[at.t], bias, bsem)
    get_bias.start()
    fetch(0).start()
    own = chunk_rows(at.g, block)
    w_attn[own, :] = w_qkv[...].astype(BF)
    bar = pltpu.get_barrier_semaphore()
    pl.semaphore_wait(bar, grp_signal(at, n_grp))
    qkv, out = GroupGather(at, n_grp, w_attn, *sc[:2]), GroupGather(at, n_grp, w_proj, *sc[2:])
    qkv.start()
    w_proj[own, :] = w_out[...].astype(BF)
    out.start()
    up16[...] = w_up[...].astype(BF)
    down16[...] = w_down[...].astype(BF)

    def norm(i):
        fetch(i).wait()

        @pl.when(i + 1 < parts)
        def _():
            fetch(i + 1).start()
        y = rows_stats(xbuf[lax.rem(i, 2)].astype(F32))[0] * gain[...] + shift[...]
        n1[chunk_rows(i, rows), :] = y.astype(BF)
        put(i).start()
    tiles(parts, norm)

    def partial(b, first=False, last=False):
        r = chunk_rows(b, block)

        def tile(i):
            m = chunk_rows(i, 2 * rows)
            y = dg(n1[m, r], w_attn[r, :], 1, 0)
            if not first:
                y = y + acc[m, :]
            acc[m, :] = y
        tiles(parts // 2, tile)

    p, q, P = at.g // 2, lax.rem(at.g, 2), n_grp // 2
    partial(at.g, True)
    qkv.forward()
    partial(2 * p + 1 - q)
    for j in range(1, P):
        partial(2 * lax.rem(p + j, P) + q)
    out.forward()
    qkv.finish()
    for j in range(1, P):
        partial(2 * lax.rem(p + j, P) + 1 - q)
    get_bias.wait()

    def write(i):
        m = chunk_rows(i, rows)
        for h in range(heads):
            c = 3 * h * HD
            proj[m, c:c + HD] = (acc[m, c:c + HD] + bias[:, 2 * h * HD:(2 * h + 1) * HD]).astype(BF)
            c += HD
            proj[m, c:c + HD] = acc[m, c:c + HD].astype(BF)
            c += HD
            proj[m, c:c + HD] = (acc[m, c:c + HD] + bias[:, (2 * h + 1) * HD:(2 * h + 2) * HD]).astype(BF)
        put(i).wait()
    tiles(parts, write)
    out.finish()


def front(x, w_qkv, w_out, w_up, w_down, gain, shift, b_qv, n, n_grp):
    length, width = x.shape
    block, hw = w_qkv.shape
    pw, hid = w_out.shape[1], w_up.shape[1]
    parts = length // TILE
    vm, hbm = pl.BlockSpec(memory_space=pltpu.VMEM), pl.BlockSpec(memory_space=pl.ANY)
    S, dma = jax.ShapeDtypeStruct, pltpu.SemaphoreType.DMA
    return pl.pallas_call(
        functools.partial(front_kernel, n=n, n_grp=n_grp, parts=parts),
        in_specs=[hbm] + [vm] * 6 + [hbm], out_specs=[vm, hbm] + [vm] * 4,
        out_shape=[S((length, hw), BF), S((length, width), BF), S((width, hw), BF), S((width, pw), BF),
                   S((block, hid), BF), S((block, hid), BF)],
        scratch_shapes=[pltpu.VMEM((2, length // parts, width), BF), pltpu.VMEM((length, width), BF),
                        pltpu.VMEM((length, hw), F32), pltpu.VMEM((1, b_qv.shape[0] // n), F32),
                        dma((2,)), dma, dma] + group_sems(n_grp) * 2,
        compiler_params=pltpu.CompilerParams(collective_id=5, has_side_effects=True, vmem_limit_bytes=62 << 20),
        cost_estimate=pl.CostEstimate(flops=2 * length * hw * width, bytes_accessed=1 << 24, transcendentals=0),
        name="front",
    )(x, w_qkv, w_out, w_up, w_down, gain[None], shift[None], b_qv.reshape(n, 1, -1))


class AllSum:
    def __init__(self, at, n_grp, x, gbuf, tbuf, gs, gr, ts, tr):
        self.at, self.n_grp, self.x, self.gbuf, self.tbuf = at, n_grp, x, gbuf, tbuf
        self.gs, self.gr, self.ts, self.tr = gs, gr, ts, tr

    def over_grp(self, d):
        at = self.at
        return remote(self.x, self.gbuf.at[at.g], self.gs.at[d - 1], self.gr.at[d - 1],
                      (lax.rem(at.g + d, self.n_grp), at.t))

    def over_tp(self, d):
        at = self.at
        return remote(self.tbuf.at[at.t], self.tbuf.at[at.t], self.ts.at[d - 1], self.tr.at[d - 1],
                      (at.g, lax.rem(at.t + d, at.n)))

    def start(self):
        for d in range(1, self.n_grp):
            self.over_grp(d).start()
        self.gbuf[self.at.g] = self.x[...]

    def turn(self):
        for d in range(1, self.n_grp):
            self.over_grp(d).wait()
        total = self.gbuf[0]
        for i in range(1, self.n_grp):
            total = total + self.gbuf[i]
        self.tbuf[self.at.t] = total
        for d in range(1, self.at.n):
            self.over_tp(d).start()

    def finish(self):
        for d in range(1, self.at.n):
            self.over_tp(d).wait()

    def total(self, lo, hi):
        out = self.tbuf[0, lo:hi, :]
        for i in range(1, self.at.n):
            out = out + self.tbuf[i, lo:hi, :]
        return out


def all_sum_scratch(n_grp, n, shape):
    dma = pltpu.SemaphoreType.DMA
    return [pltpu.VMEM(shape, F32), pltpu.VMEM((n_grp,) + shape, F32), pltpu.VMEM((n,) + shape, F32),
            dma((n_grp - 1,)), dma((n_grp - 1,)), dma((n - 1,)), dma((n - 1,))]


def back_kernel(dproj, w_attn, n1_hbm, gw_proj, x_hbm, gain, stats, up_sum,
                grad_x, g_attn, g_proj, a_rest, p_rest, sums, owned,
                n1, x_share, gw, got, got_proj, total, qv, ln_sum, nsem, ws, wr, ps, pr, *scratch, n, n_grp, chunks, rows):
    at = Place(n)
    width, hw = w_attn.shape
    block = width // n_grp
    per = block // TILE
    heads = hw // (3 * HD)
    hid = up_sum.shape[1]
    load = pltpu.make_async_copy(n1_hbm, n1, nsem.at[0])
    load.start()
    load_x = pltpu.make_async_copy(x_hbm.at[at.t], x_share, nsem.at[1])
    load_x.start()
    rs, early, late = Scatter(at, *scratch[:7]), AllSum(at, n_grp, *scratch[7:14]), AllSum(at, n_grp, *scratch[14:])
    bar = pltpu.get_barrier_semaphore()
    for d in range(1, n_grp):
        pl.semaphore_signal(bar, inc=1, device_id=(lax.rem(at.g + d, n_grp), at.t), device_id_type=MESH)
    for d in range(1, n):
        pl.semaphore_signal(bar, inc=1, device_id=(at.g, lax.rem(at.t + d, n)), device_id_type=MESH)
    pl.semaphore_wait(bar, n_grp + n - 2)

    def owner(k):
        return lax.rem(at.g + 1 + k, n_grp)

    def send(k):
        r = chunk_rows(owner(k), block)
        return remote(gw.at[r, :], got.at[k], ws.at[k], wr.at[k], (owner(k), at.t))

    def send_proj(k):
        r = chunk_rows(owner(k), block)
        return remote(gw_proj.at[r, :], got_proj.at[k], ps.at[k], pr.at[k], (owner(k), at.t))

    for k in range(n_grp - 1):
        send_proj(k).start()
    qv[...] = jnp.zeros_like(qv)
    ln_sum[...] = jnp.zeros_like(ln_sum)

    def product(c):
        lhs = dproj[:, chunk_rows(c, rows), :].reshape(n * rows, hw)
        qv[...] += jnp.sum(lhs.astype(F32), 0, keepdims=True)

        def tile(i):
            y = dg(lhs, w_attn[cols(i, 1024), :], 1, 1)
            rs.parts[:, :, :, cols(i, 1024)] = y.astype(BF).reshape(at.Z, 2, rows, 1024)
        tiles(width // 1024, tile)
        rs.start(c)

    def weights(i):
        @pl.when(i == 0)
        def _():
            load.wait()
            load_x.wait()
        k = i // per
        first = pl.multiple_of(owner(k) * block + lax.rem(i, per) * TILE, TILE)
        y = dg(n1[:, pl.ds(first, TILE)], dproj[...].reshape(-1, hw), 0, 0)

        @pl.when(k < n_grp - 1)
        def _():
            gw[pl.ds(first, TILE), :] = y.astype(BF)

            @pl.when(lax.rem(i, per) == per - 1)
            def _():
                send(k).start()

        @pl.when(k == n_grp - 1)
        def _():
            g_attn[cols(lax.rem(i, per)), :] = y

    def norm_grad(c):
        r = chunk_rows(c, rows)
        xhat, inverse = rows_stats(x_share[r, :].astype(F32))
        dn = total[...]
        e = dn * gain[...]
        inner = jnp.mean(e, -1, keepdims=True) + xhat * jnp.mean(e * xhat, -1, keepdims=True)
        grad_x[r, :] = inverse * (e - inner)
        ln_sum[0:1, :] += jnp.sum(dn * xhat, 0, keepdims=True)
        ln_sum[1:2, :] += jnp.sum(dn, 0, keepdims=True)

    def tick(i, carry):
        c = i - 1

        @pl.when(inside(c, chunks))
        def _():
            rs.meet(c)
            rs.hop(c, 1)

        @pl.when(inside(i, chunks))
        def _():
            product(i)

        @pl.when(inside(c, chunks))
        def _():
            rs.hop(c, 2)

        @pl.when(i < width // TILE)
        def _():
            weights(i)

        @pl.when(inside(c, chunks))
        def _():
            for h in range(3, at.Z):
                rs.hop(c, h)

        @pl.when(i == chunks)
        def _():
            early.x[...] = stats[...]
            early.x[4:5, 0:hid] = up_sum[...]
            for h in range(heads):
                for j, src in ((0, 3 * h), (1, 3 * h + 2)):
                    early.x[4:5, hid + (2 * h + j) * HD:hid + (2 * h + j + 1) * HD] = qv[:, src * HD:(src + 1) * HD]
            early.start()

        @pl.when(i == chunks + 1)
        def _():
            early.turn()
        e = i - 2

        @pl.when(inside(e, chunks))
        def _():
            rs.finish(e, total)
            norm_grad(e)
        return carry

    lax.fori_loop(0, chunks + 2, tick, 0)
    part = width // 4
    for j in range(4):
        late.x[j:j + 1, :] = ln_sum[0:1, j * part:(j + 1) * part]
        late.x[j + 4:j + 5, :] = ln_sum[1:2, j * part:(j + 1) * part]
    late.start()
    mine = chunk_rows(at.g, block)
    g_proj[...] = gw_proj[mine, :].astype(F32)
    for k in range(n_grp - 1):
        send(k).wait()
        send_proj(k).wait()
    a_rest[...] = sum(got[k].astype(F32) for k in range(n_grp - 1))
    p_rest[...] = sum(got_proj[k].astype(F32) for k in range(n_grp - 1))
    late.turn()
    early.finish()
    sums[0:4, :] = early.total(0, 4)
    owned[...] = early.tbuf[:, 4, :]
    late.finish()
    ln = late.total(0, 8)
    for j in range(4):
        sums[4:5, j * part:(j + 1) * part] = ln[j:j + 1, :]
        sums[5:6, j * part:(j + 1) * part] = ln[j + 4:j + 5, :]
    sums[6:8, :] = jnp.zeros_like(sums[6:8, :])


def project_back(dproj, w_attn, n1, gw_proj, x, gain, stats, up_sum, n, n_grp, chunks):
    length, hw = dproj.shape
    width = w_attn.shape[0]
    share = length // n
    rows = share // chunks
    block = width // n_grp
    pw = gw_proj.shape[1]
    vm, hbm = pl.BlockSpec(memory_space=pltpu.VMEM), pl.BlockSpec(memory_space=pl.ANY)
    S, dma = jax.ShapeDtypeStruct, pltpu.SemaphoreType.DMA
    return pl.pallas_call(
        functools.partial(back_kernel, n=n, n_grp=n_grp, chunks=chunks, rows=rows),
        in_specs=[vm, vm, hbm, vm, hbm] + [vm] * 3, out_specs=[vm] * 7,
        out_shape=[S((share, width), F32), S((block, hw), F32), S((block, pw), F32), S((block, hw), F32),
                   S((block, pw), F32), S((8, width), F32),
                   S((n, width), F32)],
        scratch_shapes=[pltpu.VMEM((length, width), BF), pltpu.VMEM((share, width), BF), pltpu.VMEM((width, hw), BF),
                        pltpu.VMEM((n_grp - 1, block, hw), BF), pltpu.VMEM((n_grp - 1, block, pw), BF),
                        pltpu.VMEM((rows, width), F32), pltpu.VMEM((1, hw), F32), pltpu.VMEM((8, width), F32), dma((2,))]
                       + [dma((n_grp - 1,))] * 4 + scatter_scratch(chunks, n // 2, rows, width)
                       + all_sum_scratch(n_grp, n, (8, width)) + all_sum_scratch(n_grp, n, (8, width // 4)),
        compiler_params=pltpu.CompilerParams(collective_id=4, has_side_effects=True, vmem_limit_bytes=50 << 20),
        cost_estimate=pl.CostEstimate(flops=4 * length * hw * width, bytes_accessed=1 << 24, transcendentals=0),
        name="project_back",
    )(dproj.reshape(n, share, hw), w_attn, n1, gw_proj, x.reshape(n, share, width), gain, stats, up_sum)


def ffn_kernel(n2_hbm, gradb_hbm, bias_hbm, up_hbm, down_hbm, out_hbm, ctx_hbm, hidden_hbm, gain, b_down, groups, lens,
               gw_hbm, gwo, dctx, dh, res, stats, bsum,
               w_up, w_down, w_out, ctx, hidden, wsem, acc_out, gat, acc_up, acc_down, gbuf, actb, dbb, total, gshare, b_up, keep, lsem, gsem, msem, *scratch, n, chunks, rows):
    at = Place(n)
    ag1, ag2 = Gather(at, gat, rows, *scratch[:4]), Gather(at, gat, rows, *scratch[4:8])
    rs, mlp = Scatter(at, *scratch[8:15]), Scatter(at, *scratch[15:])
    width, hid = w_up.shape
    m = n * rows

    load = pltpu.make_async_copy(n2_hbm, gat.at[at.t], lsem)
    load.start()
    load_g = pltpu.make_async_copy(gradb_hbm.at[at.t], gshare, msem.at[0])
    load_g.start()
    big = [pltpu.make_async_copy(src, dst, wsem.at[j]) for j, (src, dst) in enumerate(
        ((up_hbm, w_up), (down_hbm, w_down), (hidden_hbm, hidden), (out_hbm, w_out), (ctx_hbm, ctx)))]
    for copy in big:
        copy.start()
    load_b = pltpu.make_async_copy(bias_hbm.at[at.t], b_up, msem.at[1])
    load_b.start()
    share = hidden.shape[0]
    tokens = jnp.sum(jnp.where(groups[...] == at.g, lens[...], 0), 1, keepdims=True)

    def alive(ranks, first, c):
        shape = (ranks, rows, 1)
        place = ((first + lax.broadcasted_iota(jnp.int32, shape, 0)) * share + c * rows
                 + lax.broadcasted_iota(jnp.int32, shape, 1))
        return jnp.where(place < tokens.reshape(1, 1, 1), 1.0, 0.0).reshape(ranks * rows, 1)

    def fetch(c):
        slot = lax.rem(c, 2)
        return pltpu.make_async_copy(gradb_hbm.at[:, chunk_rows(c, rows), :], gbuf.at[slot], gsem.at[slot])

    fetch(0).start()
    stats[...] = jnp.zeros_like(stats)
    bsum[...] = jnp.zeros_like(bsum)
    load.wait()
    load_g.wait()
    load_b.wait()
    at.barrier()

    a0, a1 = 0.7978845608028654, 0.044715

    def wide(c):
        return gat[:, chunk_rows(c, rows), :].reshape(m, width)

    def forward(c):
        @pl.when(c == 0)
        def _():
            for copy in big:
                copy.wait()
        fetch(c).wait()

        @pl.when(c + 1 < chunks)
        def _():
            fetch(c + 1).start()
        slot = lax.rem(c, 2)
        keep[...] = alive(n, 0, c)

        def tile(i):
            v = dg(wide(c), w_up[:, cols(i, 512)], 1, 0) + b_up[:, cols(i, 512)]
            ga = dg(gbuf[slot].reshape(m, width), w_down[:, cols(i, 512)], 1, 0)
            v2 = v * v
            th = jnp.tanh(a0 * (v + a1 * v2 * v))
            half = 0.5 * (1.0 + th)
            actb[:, cols(i, 512)] = (v * half * keep[...]).astype(BF)
            slope = half + 0.5 * v * (1.0 - th * th) * (a0 * (1.0 + 3.0 * a1 * v2))
            db = (ga * slope * keep[...]).astype(BF)
            dbb[:, cols(i, 512)] = db
            bsum[:, cols(i, 512)] += jnp.sum(db.astype(F32), 0, keepdims=True)
        tiles(hid // 512, tile)

    def back(c):
        def tile(i):
            y = dg(dbb[...], w_up[cols(i, 1024), :], 1, 1)
            rs.parts[:, :, :, cols(i, 1024)] = y.astype(BF).reshape(at.Z, 2, rows, 1024)
        tiles(width // 1024, tile)

    def down(c):
        def tile(i):
            y = dg(actb[...], w_down[cols(i, 1024), :], 1, 1)
            mlp.parts[:, :, :, cols(i, 1024)] = y.astype(BF).reshape(at.Z, 2, rows, 1024)
        tiles(width // 1024, tile)

    def weights(c):
        slot = lax.rem(c, 2)

        def tile(i):
            x = gat[:, chunk_rows(c, rows), cols(i, 512)].reshape(m, 512)
            acc_up[cols(i, 512), :] += dg(x, dbb[...], 0, 0)
            y = gbuf[slot, :, :, cols(i, 512)].reshape(m, 512)
            acc_down[cols(i, 512), :] += dg(y, actb[...], 0, 0)
        tiles(width // 512, tile)

    def norm_grad(c):
        r = chunk_rows(c, rows)
        xhat, inverse = rows_stats(hidden[r, :])
        dn2 = total[...]
        e = dn2 * gain[...]
        inner = jnp.mean(e, -1, keepdims=True) + xhat * jnp.mean(e * xhat, -1, keepdims=True)
        grad = gshare[r, :].astype(F32) * alive(1, at.t, c)
        d = grad + inverse * (e - inner)
        dh[r, :] = d
        gat[at.t, r, :] = d.astype(BF)
        stats[0:1, :] += jnp.sum(dn2 * xhat, 0, keepdims=True)
        stats[1:2, :] += jnp.sum(dn2, 0, keepdims=True)
        stats[2:3, :] += jnp.sum(d, 0, keepdims=True)
        stats[3:4, :] += jnp.sum(grad, 0, keepdims=True)

    def heads(c):
        def tile(i):
            x = gat[:, chunk_rows(c, rows), cols(i, 512)].reshape(m, 512)
            acc_out[cols(i, 512), :] += dg(x, ctx[:, chunk_rows(c, rows), :].reshape(m, -1), 0, 0)
        tiles(width // 512, tile)
        y = dg(wide(c), w_out[...], 1, 0)
        dctx[:, chunk_rows(c, rows), :] = y.astype(BF).reshape(n, rows, y.shape[1])

    def at_stage(c, fn):
        @pl.when(inside(c, chunks))
        def _():
            fn(c)

    def store_copies(j):
        r = chunk_rows(j, m)
        return (pltpu.make_async_copy(actb, gw_hbm.at[r, pl.ds(0, hid)], lsem),
                pltpu.make_async_copy(dbb, gw_hbm.at[r, pl.ds(hid, hid)], msem.at[0]))

    def store_wait(j):
        for copy in store_copies(j):
            copy.wait()

    def store(j):
        @pl.when((j >= 0) & (j < width // m))
        def _():
            @pl.when(j > 0)
            def _():
                store_wait(j - 1)
            r = chunk_rows(j, m)
            actb[...] = acc_up[r, :].astype(BF)
            dbb[...] = acc_down[r, :].astype(BF)
            for copy in store_copies(j):
                copy.start()

    per_slot = -(-(width // m) // (3 * (at.Z - 1)))

    def tick(i, carry):
        def stores(slot):
            for j in range(per_slot):
                store(((i - chunks - 2) * (at.Z - 1) + slot) * per_slot + j)
        at_stage(i, ag1.start)

        @pl.when(i == 0)
        def _():
            acc_up[...] = jnp.zeros_like(acc_up)
            acc_down[...] = jnp.zeros_like(acc_down)
            acc_out[...] = jnp.zeros_like(acc_out)
        at_stage(i - 3, rs.meet)
        for h in range(1, at.Z):
            at_stage(i - 3, lambda c: rs.hop(c, h))
            at_stage(i - 1, lambda c: ag1.hop(c, h))
            if h == 1:
                at_stage(i - 4, lambda c: mlp.hop(c, at.Z - 1))
                at_stage(i - 5, lambda c: ag2.hop(c, at.Z - 1))
                at_stage(i - 2, forward)
                stores(0)
            else:
                if h == 2:
                    def served(c):
                        mlp.finish(c, total)
                        r = chunk_rows(c, rows)
                        res[r, :] = (alive(1, at.t, c) * (hidden[r, :] + total[...] + b_down[...])).astype(BF)
                    at_stage(i - 4, served)
                    at_stage(i - 3, mlp.meet)
                at_stage(i - 3, lambda c: mlp.hop(c, h - 1))
                at_stage(i - 4, lambda c: ag2.hop(c, h - 1))
                stores(h - 1)
                if h == 2:
                    at_stage(i - 2, back)

                    def gathered(c):
                        ag2.finish(c)
                        heads(c)
                    at_stage(i - 5, gathered)

        def rest(c):
            weights(c)
            rs.start(c)
        at_stage(i - 2, rest)

        def reduced(c):
            rs.finish(c, total)
            norm_grad(c)
            ag2.start(c)
        at_stage(i - 3, reduced)
        at_stage(i - 1, ag1.finish)

        def send_mlp(c):
            down(c)
            mlp.start(c)
        at_stage(i - 2, send_mlp)

        return carry

    lax.fori_loop(0, chunks + 5, tick, 0)

    store_wait(width // m - 1)
    gwo[...] = acc_out[...].astype(BF)


def feed_forward(n2, gradb, b_up, w_up, w_down, w_out, ctx, hidden, gain, b_down, groups, lens, n, chunks):
    length, width = gradb.shape
    hid, hw = w_up.shape[1], w_out.shape[1]
    share = length // n
    rows = share // chunks
    Z = n // 2
    vm, hbm = pl.BlockSpec(memory_space=pltpu.VMEM), pl.BlockSpec(memory_space=pl.ANY)
    S = jax.ShapeDtypeStruct
    m = n * rows
    return pl.pallas_call(
        functools.partial(ffn_kernel, n=n, chunks=chunks, rows=rows),
        in_specs=[hbm] * 8 + [vm] * 4,
        out_specs=[hbm] + [vm] * 6,
        out_shape=[S((width, 2 * hid), BF), S((width, hw), BF), S((n, share, hw), BF), S((share, width), F32),
                   S((share, width), BF), S((8, width), F32), S((1, hid), F32)],
        scratch_shapes=[pltpu.VMEM((width, hid), BF), pltpu.VMEM((width, hid), BF), pltpu.VMEM((width, hw), BF),
                        pltpu.VMEM((n, share, hw), BF), pltpu.VMEM((share, width), F32), pltpu.SemaphoreType.DMA((5,)),
                        pltpu.VMEM((width, hw), F32), pltpu.VMEM((n, share, width), BF), pltpu.VMEM((width, hid), F32), pltpu.VMEM((width, hid), F32),
                        pltpu.VMEM((2, n, rows, width), BF),
                        pltpu.VMEM((m, hid), BF), pltpu.VMEM((m, hid), BF), pltpu.VMEM((rows, width), F32),
                        pltpu.VMEM((share, width), BF), pltpu.VMEM((1, hid), F32), pltpu.VMEM((m, 1), F32),
                        pltpu.SemaphoreType.DMA, pltpu.SemaphoreType.DMA((2,)), pltpu.SemaphoreType.DMA((2,))]
                       + gather_sems(chunks, Z) + gather_sems(chunks, Z) + scatter_scratch(chunks, Z, rows, width) * 2,
        compiler_params=pltpu.CompilerParams(collective_id=3, has_side_effects=True, vmem_limit_bytes=62 << 20),
        cost_estimate=pl.CostEstimate(flops=12 * length * hid * width, bytes_accessed=1 << 26, transcendentals=0),
        name="feed_forward",
    )(n2, gradb.reshape(n, share, width), b_up.reshape(n, 1, hid), w_up, w_down, w_out, ctx.reshape(n, share, hw),
      hidden, gain[None], b_down[None], groups[None], lens[None])


def on_device(layer_input, out_cotangent, seq_group, seq_len, w_qkv, b_qv, w_out, b_out, w_up, b_up,
              w_down, b_down, first_norm_gain, first_norm_bias, second_norm_gain, second_norm_bias):
    n_tp, n_grp = lax.axis_size("tp"), lax.axis_size("grp")
    length = layer_input.shape[0]
    hid, qv = w_up.shape[1], b_qv.shape[0] // n_tp

    proj, n1, w_attn, w_proj, up16, down16 = front(
        layer_input, w_qkv, w_out, w_up, w_down, first_norm_gain, first_norm_bias, b_qv, n_tp, n_grp)
    context, lse = attn_fwd(seq_group, seq_len, proj)
    hidden, n2, w_expand, w_reduce = attn_out(
        context, w_proj, b_out, second_norm_gain, second_norm_bias, layer_input, up16, down16,
        n_tp, n_grp, 8)
    gw_ffn, gw_proj, dcontext, dh, result, stats, up_sum = feed_forward(
        n2, out_cotangent, b_up, w_expand, w_reduce, w_proj, context, hidden,
        second_norm_gain, b_down, seq_group, seq_len, n_tp, 8)
    grads_ffn = lax.psum_scatter(gw_ffn, "grp", scatter_dimension=0, tiled=True).astype(F32)
    grads_expand, grads_reduce = grads_ffn[:, :hid], grads_ffn[:, hid:]

    dproj = attn_bwd(seq_group, seq_len, proj, context, dcontext.reshape(length, -1), lse)
    grad_x, grads_attn, grads_proj, attn_rest, proj_rest, sums, owned = project_back(
        dproj, w_attn, n1, gw_proj, layer_input, first_norm_gain[None], stats, up_sum, n_tp, n_grp, 8)
    grad_x, grads_attn, grads_proj = dh + grad_x, grads_attn + attn_rest, grads_proj + proj_rest
    return (result, grad_x, grads_attn, owned[:, hid:hid + qv].reshape(-1), grads_proj, sums[2],
            grads_expand, owned[:, :hid].reshape(-1), grads_reduce, sums[3], sums[4], sums[5],
            sums[0], sums[1])


def solution(mesh):
    rows, both, flat = P("grp", None), P("grp", "tp"), P()
    in_specs = (rows, rows, flat, flat, both, flat, both, flat, both, flat, both, flat, flat, flat, flat, flat)
    spread = P(("grp", "tp"), None)
    out_specs = (spread, spread, both, flat, both, flat, both, flat, both, flat, flat, flat, flat, flat)
    return jax.shard_map(on_device, mesh=mesh, in_specs=in_specs, out_specs=out_specs, check_vma=False)
```

```python
import functools

import jax
import jax.numpy as jnp
from jax import lax
from jax.experimental import pallas as pl
from jax.experimental.pallas import tpu as pltpu
from jax.sharding import PartitionSpec as P

HD = 128
BLK=512
F32=jnp.float32
BF=jnp.bfloat16
LOG2E=1.4426950408889634

def dg(a,b,ca,cb):
    return lax.dot_general(a,b,(((ca,),(cb,)),((),())),preferred_element_type=F32)


def group_tokens(grps, lens, seqs):
    g = lax.axis_index("grp")
    tokens, longest = jnp.int32(0), jnp.int32(0)
    for s in range(seqs):
        count = jnp.where(grps[s] == g, lens[s], 0)
        tokens, longest = tokens + count, jnp.maximum(longest, count)
    return tokens, longest > BLK


def below(shape):
    return lax.broadcasted_iota(jnp.int32, shape, 0) <= lax.broadcasted_iota(jnp.int32, shape, 1)


def attn_fwd_kernel(grps, lens, q_ref, k_ref, v_ref, o_ref, lse_ref, *, nb, seqs):
    tokens, is_long = group_tokens(grps, lens, seqs)
    c = HD ** -0.5 * LOG2E

    def attend(rows, early):
        q = q_ref[rows, :]
        pieces = [(rows, jnp.where(below((BLK, BLK)), dg(k_ref[rows, :], q, 1, 1), -1e30))]
        if early is not None:
            pieces.append((early, dg(k_ref[early, :], q, 1, 1)))
        top = functools.reduce(jnp.maximum, [jnp.max(s, 0, keepdims=True) for _, s in pieces]) * c
        total, acc = 0.0, 0.0
        for keys, s in pieces:
            p = jnp.exp2(s * c - top)
            total = total + jnp.sum(p, 0, keepdims=True)
            acc = acc + dg(v_ref[keys, :], p.astype(BF), 0, 0)
        o_ref[rows, :] = jnp.transpose(acc / total).astype(BF)
        lse_ref[0, :, rows] = top + jnp.log2(total)

    @pl.when(is_long)
    def _():
        for i in range(nb):
            attend(slice(i * BLK, (i + 1) * BLK), slice(0, i * BLK) if i else None)

    @pl.when(jnp.logical_not(is_long))
    def _():
        def block(i, carry):
            rows = pl.ds(pl.multiple_of(i * BLK, BLK), BLK)

            @pl.when(i * BLK < tokens)
            def _():
                attend(rows, None)

            @pl.when(i * BLK >= tokens)
            def _():
                o_ref[rows, :] = jnp.zeros((BLK, HD), BF)
                lse_ref[0, :, rows] = jnp.zeros((1, BLK), F32)
            return carry
        lax.fori_loop(0, nb, block, 0)


def attn_fwd(grps, lens, proj):
    length, heads = proj.shape[0], proj.shape[1] // (3 * HD)
    spec = lambda o: pl.BlockSpec((length, HD), lambda h, grps, lens: (0, 3 * h + o))
    return pl.pallas_call(
        functools.partial(attn_fwd_kernel, nb=length // BLK, seqs=grps.shape[0]),
        grid_spec=pltpu.PrefetchScalarGridSpec(
            num_scalar_prefetch=2, grid=(heads,), in_specs=[spec(0), spec(1), spec(2)],
            out_specs=[pl.BlockSpec((length, HD), lambda h, grps, lens: (0, h)),
                       pl.BlockSpec((1, 1, length), lambda h, grps, lens: (h, 0, 0))]),
        out_shape=[jax.ShapeDtypeStruct((length, heads * HD), BF), jax.ShapeDtypeStruct((heads, 1, length), F32)],
        compiler_params=pltpu.CompilerParams(vmem_limit_bytes=62 << 20),
        cost_estimate=pl.CostEstimate(flops=heads * length * length * HD * 2, bytes_accessed=length * heads * HD * 8,
                                      transcendentals=heads * length * length // 2),
        name="attn_fwd",
    )(grps, lens, proj, proj, proj)


def attn_bwd_kernel(grps, lens, q_ref, k_ref, v_ref, o_ref, do_ref, lse_ref, dp_ref, dq_sc, dl_sc, *, nb, seqs):
    tokens, is_long = group_tokens(grps, lens, seqs)
    scale = HD ** -0.5
    c = scale * LOG2E
    prod = do_ref[...].astype(F32) * o_ref[...].astype(F32)
    dl_sc[...] = jnp.sum(jnp.transpose(prod), 0, keepdims=True)

    def attend(keys, later, first):
        k, v = k_ref[keys, :], v_ref[keys, :]
        dk, dv = 0.0, 0.0
        for diag, rows in ((True, keys), (False, later)):
            if rows is None:
                continue
            q, do = q_ref[rows, :], do_ref[rows, :]
            p = jnp.exp2(dg(k, q, 1, 1) * c - lse_ref[0, :, rows])
            if diag:
                p = jnp.where(below((BLK, BLK)), p, 0.0)
            ds = (p * (dg(v, do, 1, 1) - dl_sc[:, rows])).astype(BF)
            dv = dv + dg(p.astype(BF), do, 1, 0)
            dk = dk + dg(ds, q, 1, 0)
            dq = dg(k, ds, 0, 0)
            dq_sc[:, rows] = dq if first else dq_sc[:, rows] + dq
        dp_ref[keys, HD:2 * HD] = (dk * scale).astype(BF)
        dp_ref[keys, 2 * HD:] = dv.astype(BF)

    @pl.when(is_long)
    def _():
        for j in range(nb):
            attend(slice(j * BLK, (j + 1) * BLK), slice((j + 1) * BLK, nb * BLK) if j < nb - 1 else None, j == 0)

    @pl.when(jnp.logical_not(is_long))
    def _():
        def block(i, carry):
            rows = pl.ds(pl.multiple_of(i * BLK, BLK), BLK)

            @pl.when(i * BLK < tokens)
            def _():
                attend(rows, None, True)

            @pl.when(i * BLK >= tokens)
            def _():
                dp_ref[rows, :] = jnp.zeros((BLK, 3 * HD), BF)
                dq_sc[:, rows] = jnp.zeros((HD, BLK), F32)
            return carry
        lax.fori_loop(0, nb, block, 0)
    dp_ref[:, :HD] = jnp.transpose(dq_sc[...] * scale).astype(BF)


def attn_bwd(grps, lens, proj, ctx, dctx, lse):
    length, heads = proj.shape[0], proj.shape[1] // (3 * HD)
    spec = lambda o: pl.BlockSpec((length, HD), lambda h, grps, lens: (0, 3 * h + o))
    head = pl.BlockSpec((length, HD), lambda h, grps, lens: (0, h))
    return pl.pallas_call(
        functools.partial(attn_bwd_kernel, nb=length // BLK, seqs=grps.shape[0]),
        grid_spec=pltpu.PrefetchScalarGridSpec(
            num_scalar_prefetch=2, grid=(heads,),
            in_specs=[spec(0), spec(1), spec(2), head, head,
                      pl.BlockSpec((1, 1, length), lambda h, grps, lens: (h, 0, 0))],
            out_specs=pl.BlockSpec((length, 3 * HD), lambda h, grps, lens: (0, h)),
            scratch_shapes=[pltpu.VMEM((HD, length), F32), pltpu.VMEM((1, length), F32)]),
        out_shape=jax.ShapeDtypeStruct((length, heads * 3 * HD), BF),
        compiler_params=pltpu.CompilerParams(vmem_limit_bytes=62 << 20),
        cost_estimate=pl.CostEstimate(flops=heads * length * length * HD * 5, bytes_accessed=length * heads * HD * 16,
                                      transcendentals=heads * length * length // 2),
        name="attn_bwd",
    )(grps, lens, proj, proj, proj, ctx, dctx, lse)


MESH = pl.DeviceIdType.MESH
TILE = 256


class Place:
    def __init__(self, n_tp):
        self.g = lax.axis_index("grp")
        t = lax.axis_index("tp")
        self.t, self.n, self.Z = t, n_tp, n_tp // 2
        self.z, self.k = t // 2, lax.rem(t, 2)
        self.right, self.left, self.sib = (self.g, t + 2), (self.g, t - 2), (self.g, t + 1 - 2 * self.k)
        self.has_right, self.has_left = self.z < self.Z - 1, self.z > 0

    def barrier(self, n_grp=0):
        bar = pltpu.get_barrier_semaphore()
        extra = grp_signal(self, n_grp) if n_grp else 0
        pl.semaphore_signal(bar, inc=1, device_id=self.sib, device_id_type=MESH)

        @pl.when(self.has_right)
        def _():
            pl.semaphore_signal(bar, inc=1, device_id=self.right, device_id_type=MESH)

        @pl.when(self.has_left)
        def _():
            pl.semaphore_signal(bar, inc=1, device_id=self.left, device_id_type=MESH)

        amount = 1 + extra + jnp.where(self.has_right, 1, 0) + jnp.where(self.has_left, 1, 0)
        pl.semaphore_wait(bar, amount)


def remote(src, dst, ssem, rsem, device):
    return pltpu.make_async_remote_copy(src, dst, ssem, rsem, device_id=device, device_id_type=MESH)


class Gather:
    def __init__(self, at, gat, rows, ls, lr, ss, sr):
        self.at, self.gat, self.rows = at, gat, rows
        self.ls, self.lr, self.ss, self.sr = ls, lr, ss, sr

    def block(self, zz, kk, c):
        return self.gat.at[2 * zz + kk, pl.ds(pl.multiple_of(c * self.rows, self.rows), self.rows), :]

    def line(self, c, side, d):
        at = self.at
        sign, device = (-1, at.right) if side == 0 else (1, at.left)
        b = self.block(at.z + sign * (d - 1), at.k, c)
        return remote(b, b, self.ls.at[c, side, d - 1], self.lr.at[c, side, d - 1], device)

    def line_in(self, c, side, d):
        at = self.at
        sign, device = (-1, at.right) if side == 0 else (1, at.left)
        b = self.block(at.z + sign * d, at.k, c)
        return remote(b, b, self.ls.at[c, side, d - 1], self.lr.at[c, side, d - 1], device)

    def across(self, c, zz):
        b = self.block(zz, self.at.k, c)
        return remote(b, b, self.ss.at[c, zz], self.sr.at[c, zz], self.at.sib)

    def across_in(self, c, zz):
        b = self.block(zz, 1 - self.at.k, c)
        return remote(b, b, self.ss.at[c, zz], self.sr.at[c, zz], self.at.sib)

    def start(self, c):
        at = self.at

        @pl.when(at.has_right)
        def _():
            self.line(c, 0, 1).start()

        @pl.when(at.has_left)
        def _():
            self.line(c, 1, 1).start()

        self.across(c, at.z).start()

    def hop(self, c, d):
        at = self.at

        @pl.when(at.z >= d)
        def _():
            self.line_in(c, 0, d).wait_recv()
            if d < at.Z - 1:
                @pl.when(at.has_right)
                def _():
                    self.line(c, 0, d + 1).start()
            self.across(c, at.z - d).start()

        @pl.when(at.z + d <= at.Z - 1)
        def _():
            self.line_in(c, 1, d).wait_recv()
            if d < at.Z - 1:
                @pl.when(at.has_left)
                def _():
                    self.line(c, 1, d + 1).start()
            self.across(c, at.z + d).start()

    def finish(self, c):
        at = self.at
        for zz in range(at.Z):
            self.across_in(c, zz).wait_recv()
            self.across(c, zz).wait_send()
        for d in range(1, at.Z):
            @pl.when(at.has_right & (at.z >= d - 1))
            def _():
                self.line(c, 0, d).wait_send()

            @pl.when(at.has_left & (at.z + d - 1 <= at.Z - 1))
            def _():
                self.line(c, 1, d).wait_send()


class Scatter:
    def __init__(self, at, parts, pair, hops, cs, cr, hs, hr):
        self.at, self.parts, self.pair, self.hops = at, parts, pair, hops
        self.slots = pair.shape[0]
        self.cs, self.cr, self.hs, self.hr = cs, cr, hs, hr

    def across(self, c):
        c = lax.rem(c, self.slots)
        return remote(self.parts.at[:, 1 - self.at.k], self.pair.at[c], self.cs.at[c], self.cr.at[c], self.at.sib)

    def line(self, c, side, h, target):
        c = lax.rem(c, self.slots)
        device = self.at.right if side == 0 else self.at.left
        return remote(self.pair.at[c, target], self.hops.at[side, c, h - 1],
                      self.hs.at[c, side, h - 1], self.hr.at[c, side, h - 1], device)

    def start(self, c):
        self.across(c).start()

    def meet(self, c):
        self.across(c).wait()
        own = self.parts[:, pl.ds(self.at.k, 1)]
        own = own.reshape(own.shape[0], own.shape[2], own.shape[3])
        c = lax.rem(c, self.slots)
        self.pair[c] = (self.pair[c].astype(F32) + own.astype(F32)).astype(BF)

    def hop(self, c, h):
        at = self.at
        for side in (0, 1):
            pos = at.z if side == 0 else at.Z - 1 - at.z
            target = at.z + at.Z - h if side == 0 else at.z - at.Z + h

            @pl.when((pos <= h - 1) & (pos < at.Z - 1))
            def _():
                if h >= 2:
                    @pl.when(pos >= 1)
                    def _():
                        self.line(c, side, h - 1, target).wait_recv()
                        b = lax.rem(c, self.slots)
                        self.pair[b, target] = (self.pair[b, target].astype(F32)
                                                + self.hops[side, b, h - 2].astype(F32)).astype(BF)
                self.line(c, side, h, target).start()

    def finish(self, c, total):
        at = self.at
        b = lax.rem(c, self.slots)
        total[...] = self.pair[b, at.z].astype(F32)
        for side in (0, 1):
            pos = at.z if side == 0 else at.Z - 1 - at.z

            @pl.when(pos >= 1)
            def _():
                self.line(c, side, at.Z - 1, at.z).wait_recv()
                total[...] += self.hops[side, b, at.Z - 2].astype(F32)

            for h in range(1, at.Z):
                @pl.when((pos <= h - 1) & (pos < at.Z - 1))
                def _():
                    self.line(c, side, h, at.z).wait_send()


class GroupGather:
    def __init__(self, at, n_grp, full, ss, sr):
        self.at, self.full, self.ss, self.sr = at, full, ss, sr
        self.P = n_grp // 2
        self.size = full.shape[0] // n_grp
        self.p, self.q = at.g // 2, lax.rem(at.g, 2)
        self.partner = (at.g + 1 - 2 * self.q, at.t)

    def peer(self, j):
        return lax.rem(self.p + j, self.P)

    def rows(self, p, q, half=None):
        size = self.size if half is None else self.size // 2
        first = (2 * p + q) * self.size + (size if half == 1 else 0)
        return self.full.at[pl.ds(pl.multiple_of(first, size), size), :]

    def copy(self, kind, j, incoming=False):
        p, q = self.p, self.q
        src = lax.rem(p + self.P - j, self.P)
        if kind == 0:
            b, k, dev = self.rows(p, 1 - q if incoming else q), 0, self.partner
        elif kind == 1:
            b, k, dev = self.rows(src if incoming else p, q), j, (2 * self.peer(j) + q, self.at.t)
        elif kind == 2:
            b, k = self.rows(src if incoming else p, 1 - q, 1), self.P - 1 + j
            dev = (2 * self.peer(j) + q, self.at.t)
        else:
            b, k = self.rows(src, 1 - q if incoming else q, 0), 2 * (self.P - 1) + j
            dev = self.partner
        return remote(b, b, self.ss.at[k], self.sr.at[k], dev)

    def start(self):
        self.copy(0, 0).start()
        for j in range(1, self.P):
            self.copy(1, j).start()

    def forward(self):
        self.copy(0, 0, True).wait_recv()
        for j in range(1, self.P):
            self.copy(2, j).start()
        for j in range(1, self.P):
            self.copy(1, j, True).wait_recv()
            self.copy(3, j).start()

    def finish(self):
        for j in range(1, self.P):
            for kind in (2, 3):
                self.copy(kind, j, True).wait_recv()
                self.copy(kind, j).wait_send()
            self.copy(1, j).wait_send()
        self.copy(0, 0).wait_send()


def group_sems(n_grp):
    k = 1 + 3 * (n_grp // 2 - 1)
    return [pltpu.SemaphoreType.DMA((k,)), pltpu.SemaphoreType.DMA((k,))]


def grp_signal(at, n_grp):
    bar = pltpu.get_barrier_semaphore()
    p, q = at.g // 2, lax.rem(at.g, 2)
    pl.semaphore_signal(bar, inc=1, device_id=(at.g + 1 - 2 * q, at.t), device_id_type=MESH)
    for j in range(1, n_grp // 2):
        pl.semaphore_signal(bar, inc=1, device_id=(2 * lax.rem(p + j, n_grp // 2) + q, at.t), device_id_type=MESH)
    return n_grp // 2


def gather_sems(chunks, Z):
    dma = pltpu.SemaphoreType.DMA
    return [dma((chunks, 2, Z - 1)), dma((chunks, 2, Z - 1)), dma((chunks, Z)), dma((chunks, Z))]


def scatter_scratch(chunks, Z, rows, width):
    chunks = min(chunks, 4)
    dma = pltpu.SemaphoreType.DMA
    return [pltpu.VMEM((Z, 2, rows, width), BF), pltpu.VMEM((chunks, Z, rows, width), BF),
            pltpu.VMEM((2, chunks, Z - 1, rows, width), BF),
            dma((chunks,)), dma((chunks,)), dma((chunks, 2, Z - 1)), dma((chunks, 2, Z - 1))]


def inside(c, chunks):
    return (c >= 0) & (c < chunks)


def chunk_rows(c, rows):
    return pl.ds(pl.multiple_of(c * rows, rows), rows)


def tiles(count, body):
    def step(i, carry):
        body(i)
        return carry
    lax.fori_loop(0, count, step, 0)


def cols(i, size=TILE):
    return pl.ds(pl.multiple_of(i * size, size), size)


def rows_stats(rows):
    mean = jnp.mean(rows, -1, keepdims=True)
    centred = rows - mean
    inverse = lax.rsqrt(jnp.mean(centred * centred, -1, keepdims=True) + 1e-05)
    return centred * inverse, inverse


def product_scatter(at, rs, lhs_ref, w_ref, total, chunks, rows, epilogue, extra):
    def product(c):
        lhs = lhs_ref[:, chunk_rows(c, rows), :].reshape(at.n * rows, lhs_ref.shape[2])

        def tile(i):
            y = dg(lhs, w_ref[cols(i, 1024), :], 1, 1)
            rs.parts[:, :, :, cols(i, 1024)] = y.astype(BF).reshape(at.Z, 2, rows, 1024)
        tiles(w_ref.shape[0] // 1024, tile)
        rs.start(c)

    def tick(i, carry):
        c = i - 1

        @pl.when(inside(c, chunks))
        def _():
            rs.meet(c)
            rs.hop(c, 1)

        @pl.when(inside(i, chunks))
        def _():
            product(i)

        @pl.when(inside(c, chunks))
        def _():
            for h in range(2, at.Z):
                rs.hop(c, h)

        e = i - 2

        @pl.when(inside(e, chunks))
        def _():
            rs.finish(e, total)
            epilogue(e)
        extra(i)
        return carry

    lax.fori_loop(0, chunks + 2, tick, 0)


def out_kernel(ctx, w_out, b_out, gain, shift, x_hbm, up16, down16, hidden, n2, up_hbm, down_hbm,
               x_share, total, up_own, down_own, lsem, *sc, n, n_grp, chunks, rows):
    at = Place(n)
    fetches = [pltpu.make_async_copy(up16, up_own, lsem.at[3]), pltpu.make_async_copy(down16, down_own, lsem.at[4])]
    for copy in fetches:
        copy.start()
    load = pltpu.make_async_copy(x_hbm.at[at.t], x_share, lsem.at[0])
    load.start()
    up, down = GroupGather(at, n_grp, up_hbm, *sc[:2]), GroupGather(at, n_grp, down_hbm, *sc[2:4])
    own = chunk_rows(at.g, up.size)
    put_up = pltpu.make_async_copy(up_own, up_hbm.at[own, :], lsem.at[1])
    put_down = pltpu.make_async_copy(down_own, down_hbm.at[own, :], lsem.at[2])
    for copy in fetches:
        copy.wait()
    put_up.start()
    put_down.start()
    at.barrier(n_grp)
    load.wait()
    put_up.wait()
    put_down.wait()
    up.start()
    down.start()

    def epilogue(c):
        r = chunk_rows(c, rows)
        h = x_share[r, :].astype(F32) + total[...] + b_out[...]
        hidden[r, :] = h
        n2[r, :] = (rows_stats(h)[0] * gain[...] + shift[...]).astype(BF)

    def extra(i):
        @pl.when(i == chunks // 2)
        def _():
            up.forward()

        @pl.when(i == chunks - 1)
        def _():
            down.forward()

    product_scatter(at, Scatter(at, *sc[4:]), ctx, w_out, total, chunks, rows, epilogue, extra)
    up.finish()
    down.finish()


def attn_out(ctx, w_out, b_out, gain, shift, x, up16, down16, n, n_grp, chunks):
    length, hw = ctx.shape
    width = x.shape[1]
    share = length // n
    rows = share // chunks
    hid = up16.shape[1]
    vm, hbm = pl.BlockSpec(memory_space=pltpu.VMEM), pl.BlockSpec(memory_space=pl.ANY)
    S = jax.ShapeDtypeStruct
    return pl.pallas_call(
        functools.partial(out_kernel, n=n, n_grp=n_grp, chunks=chunks, rows=rows),
        in_specs=[vm] * 5 + [hbm] * 3, out_specs=[vm] * 2 + [hbm] * 2,
        out_shape=[S((share, width), F32), S((share, width), BF), S((width, hid), BF), S((width, hid), BF)],
        scratch_shapes=[pltpu.VMEM((share, width), BF), pltpu.VMEM((rows, width), F32), pltpu.VMEM(up16.shape, BF),
                        pltpu.VMEM(up16.shape, BF), pltpu.SemaphoreType.DMA((5,))]
                       + group_sems(n_grp) * 2 + scatter_scratch(chunks, n // 2, rows, width),
        compiler_params=pltpu.CompilerParams(collective_id=2, has_side_effects=True, vmem_limit_bytes=62 << 20),
        cost_estimate=pl.CostEstimate(flops=2 * length * hw * width, bytes_accessed=1 << 23, transcendentals=0),
        name="attn_out",
    )(ctx.reshape(n, share, hw), w_out, b_out[None], gain[None], shift[None], x.reshape(n, share, width), up16, down16)


def front_kernel(x_hbm, w_qkv, w_out, w_up, w_down, gain, shift, bias_hbm, proj, n1_hbm, w_attn, w_proj, up16, down16,
                 xbuf, n1, acc, bias, xsem, osem, bsem, *sc, n, n_grp, parts):
    at = Place(n)
    width, hw = w_attn.shape
    block = width // n_grp
    length = n1.shape[0]
    rows = length // parts
    heads = hw // (3 * HD)

    def fetch(i):
        slot = lax.rem(i, 2)
        return pltpu.make_async_copy(x_hbm.at[chunk_rows(i, rows), :], xbuf.at[slot], xsem.at[slot])

    def put(i):
        r = chunk_rows(i, rows)
        return pltpu.make_async_copy(n1.at[r, :], n1_hbm.at[r, :], osem)

    get_bias = pltpu.make_async_copy(bias_hbm.at[at.t], bias, bsem)
    get_bias.start()
    fetch(0).start()
    own = chunk_rows(at.g, block)
    w_attn[own, :] = w_qkv[...].astype(BF)
    bar = pltpu.get_barrier_semaphore()
    pl.semaphore_wait(bar, grp_signal(at, n_grp))
    qkv, out = GroupGather(at, n_grp, w_attn, *sc[:2]), GroupGather(at, n_grp, w_proj, *sc[2:])
    qkv.start()
    w_proj[own, :] = w_out[...].astype(BF)
    out.start()
    up16[...] = w_up[...].astype(BF)
    down16[...] = w_down[...].astype(BF)

    def norm(i):
        fetch(i).wait()

        @pl.when(i + 1 < parts)
        def _():
            fetch(i + 1).start()
        y = rows_stats(xbuf[lax.rem(i, 2)].astype(F32))[0] * gain[...] + shift[...]
        n1[chunk_rows(i, rows), :] = y.astype(BF)
        put(i).start()
    tiles(parts, norm)

    def partial(b, first=False, last=False):
        r = chunk_rows(b, block)

        def tile(i):
            m = chunk_rows(i, 2 * rows)
            y = dg(n1[m, r], w_attn[r, :], 1, 0)
            if not first:
                y = y + acc[m, :]
            acc[m, :] = y
        tiles(parts // 2, tile)

    p, q, P = at.g // 2, lax.rem(at.g, 2), n_grp // 2
    partial(at.g, True)
    qkv.forward()
    partial(2 * p + 1 - q)
    for j in range(1, P):
        partial(2 * lax.rem(p + j, P) + q)
    out.forward()
    qkv.finish()
    for j in range(1, P):
        partial(2 * lax.rem(p + j, P) + 1 - q)
    get_bias.wait()

    def write(i):
        m = chunk_rows(i, rows)
        for h in range(heads):
            c = 3 * h * HD
            proj[m, c:c + HD] = (acc[m, c:c + HD] + bias[:, 2 * h * HD:(2 * h + 1) * HD]).astype(BF)
            c += HD
            proj[m, c:c + HD] = acc[m, c:c + HD].astype(BF)
            c += HD
            proj[m, c:c + HD] = (acc[m, c:c + HD] + bias[:, (2 * h + 1) * HD:(2 * h + 2) * HD]).astype(BF)
        put(i).wait()
    tiles(parts, write)
    out.finish()


def front(x, w_qkv, w_out, w_up, w_down, gain, shift, b_qv, n, n_grp):
    length, width = x.shape
    block, hw = w_qkv.shape
    pw, hid = w_out.shape[1], w_up.shape[1]
    parts = length // TILE
    vm, hbm = pl.BlockSpec(memory_space=pltpu.VMEM), pl.BlockSpec(memory_space=pl.ANY)
    S, dma = jax.ShapeDtypeStruct, pltpu.SemaphoreType.DMA
    return pl.pallas_call(
        functools.partial(front_kernel, n=n, n_grp=n_grp, parts=parts),
        in_specs=[hbm] + [vm] * 6 + [hbm], out_specs=[vm, hbm] + [vm] * 4,
        out_shape=[S((length, hw), BF), S((length, width), BF), S((width, hw), BF), S((width, pw), BF),
                   S((block, hid), BF), S((block, hid), BF)],
        scratch_shapes=[pltpu.VMEM((2, length // parts, width), BF), pltpu.VMEM((length, width), BF),
                        pltpu.VMEM((length, hw), F32), pltpu.VMEM((1, b_qv.shape[0] // n), F32),
                        dma((2,)), dma, dma] + group_sems(n_grp) * 2,
        compiler_params=pltpu.CompilerParams(collective_id=5, has_side_effects=True, vmem_limit_bytes=62 << 20),
        cost_estimate=pl.CostEstimate(flops=2 * length * hw * width, bytes_accessed=1 << 24, transcendentals=0),
        name="front",
    )(x, w_qkv, w_out, w_up, w_down, gain[None], shift[None], b_qv.reshape(n, 1, -1))


class AllSum:
    def __init__(self, at, n_grp, x, gbuf, tbuf, gs, gr, ts, tr):
        self.at, self.n_grp, self.x, self.gbuf, self.tbuf = at, n_grp, x, gbuf, tbuf
        self.gs, self.gr, self.ts, self.tr = gs, gr, ts, tr

    def over_grp(self, d):
        at = self.at
        return remote(self.x, self.gbuf.at[at.g], self.gs.at[d - 1], self.gr.at[d - 1],
                      (lax.rem(at.g + d, self.n_grp), at.t))

    def over_tp(self, d):
        at = self.at
        return remote(self.tbuf.at[at.t], self.tbuf.at[at.t], self.ts.at[d - 1], self.tr.at[d - 1],
                      (at.g, lax.rem(at.t + d, at.n)))

    def start(self):
        for d in range(1, self.n_grp):
            self.over_grp(d).start()
        self.gbuf[self.at.g] = self.x[...]

    def turn(self):
        for d in range(1, self.n_grp):
            self.over_grp(d).wait()
        total = self.gbuf[0]
        for i in range(1, self.n_grp):
            total = total + self.gbuf[i]
        self.tbuf[self.at.t] = total
        for d in range(1, self.at.n):
            self.over_tp(d).start()

    def finish(self):
        for d in range(1, self.at.n):
            self.over_tp(d).wait()

    def total(self, lo, hi):
        out = self.tbuf[0, lo:hi, :]
        for i in range(1, self.at.n):
            out = out + self.tbuf[i, lo:hi, :]
        return out


def all_sum_scratch(n_grp, n, shape):
    dma = pltpu.SemaphoreType.DMA
    return [pltpu.VMEM(shape, F32), pltpu.VMEM((n_grp,) + shape, F32), pltpu.VMEM((n,) + shape, F32),
            dma((n_grp - 1,)), dma((n_grp - 1,)), dma((n - 1,)), dma((n - 1,))]


def back_kernel(dproj, w_attn, n1_hbm, gw_proj, x_hbm, gain, stats, up_sum,
                grad_x, g_attn, g_proj, a_rest, p_rest, sums, owned,
                n1, x_share, gw, got, got_proj, total, qv, ln_sum, nsem, ws, wr, ps, pr, *scratch, n, n_grp, chunks, rows):
    at = Place(n)
    width, hw = w_attn.shape
    block = width // n_grp
    per = block // TILE
    heads = hw // (3 * HD)
    hid = up_sum.shape[1]
    load = pltpu.make_async_copy(n1_hbm, n1, nsem.at[0])
    load.start()
    load_x = pltpu.make_async_copy(x_hbm.at[at.t], x_share, nsem.at[1])
    load_x.start()
    rs, early, late = Scatter(at, *scratch[:7]), AllSum(at, n_grp, *scratch[7:14]), AllSum(at, n_grp, *scratch[14:])
    bar = pltpu.get_barrier_semaphore()
    for d in range(1, n_grp):
        pl.semaphore_signal(bar, inc=1, device_id=(lax.rem(at.g + d, n_grp), at.t), device_id_type=MESH)
    for d in range(1, n):
        pl.semaphore_signal(bar, inc=1, device_id=(at.g, lax.rem(at.t + d, n)), device_id_type=MESH)
    pl.semaphore_wait(bar, n_grp + n - 2)

    def owner(k):
        return lax.rem(at.g + 1 + k, n_grp)

    def send(k):
        r = chunk_rows(owner(k), block)
        return remote(gw.at[r, :], got.at[k], ws.at[k], wr.at[k], (owner(k), at.t))

    def send_proj(k):
        r = chunk_rows(owner(k), block)
        return remote(gw_proj.at[r, :], got_proj.at[k], ps.at[k], pr.at[k], (owner(k), at.t))

    for k in range(n_grp - 1):
        send_proj(k).start()
    qv[...] = jnp.zeros_like(qv)
    ln_sum[...] = jnp.zeros_like(ln_sum)

    def product(c):
        lhs = dproj[:, chunk_rows(c, rows), :].reshape(n * rows, hw)
        qv[...] += jnp.sum(lhs.astype(F32), 0, keepdims=True)

        def tile(i):
            y = dg(lhs, w_attn[cols(i, 1024), :], 1, 1)
            rs.parts[:, :, :, cols(i, 1024)] = y.astype(BF).reshape(at.Z, 2, rows, 1024)
        tiles(width // 1024, tile)
        rs.start(c)

    def weights(i):
        @pl.when(i == 0)
        def _():
            load.wait()
            load_x.wait()
        k = i // per
        first = pl.multiple_of(owner(k) * block + lax.rem(i, per) * TILE, TILE)
        y = dg(n1[:, pl.ds(first, TILE)], dproj[...].reshape(-1, hw), 0, 0)

        @pl.when(k < n_grp - 1)
        def _():
            gw[pl.ds(first, TILE), :] = y.astype(BF)

            @pl.when(lax.rem(i, per) == per - 1)
            def _():
                send(k).start()

        @pl.when(k == n_grp - 1)
        def _():
            g_attn[cols(lax.rem(i, per)), :] = y

    def norm_grad(c):
        r = chunk_rows(c, rows)
        xhat, inverse = rows_stats(x_share[r, :].astype(F32))
        dn = total[...]
        e = dn * gain[...]
        inner = jnp.mean(e, -1, keepdims=True) + xhat * jnp.mean(e * xhat, -1, keepdims=True)
        grad_x[r, :] = inverse * (e - inner)
        ln_sum[0:1, :] += jnp.sum(dn * xhat, 0, keepdims=True)
        ln_sum[1:2, :] += jnp.sum(dn, 0, keepdims=True)

    def tick(i, carry):
        c = i - 1

        @pl.when(inside(c, chunks))
        def _():
            rs.meet(c)
            rs.hop(c, 1)

        @pl.when(inside(i, chunks))
        def _():
            product(i)

        @pl.when(inside(c, chunks))
        def _():
            rs.hop(c, 2)

        @pl.when((i >= 2) & (i < width // TILE + 2))
        def _():
            weights(i - 2)

        @pl.when(inside(c, chunks))
        def _():
            for h in range(3, at.Z):
                rs.hop(c, h)

        @pl.when(i == chunks)
        def _():
            early.x[...] = stats[...]
            early.x[4:5, 0:hid] = up_sum[...]
            for h in range(heads):
                for j, src in ((0, 3 * h), (1, 3 * h + 2)):
                    early.x[4:5, hid + (2 * h + j) * HD:hid + (2 * h + j + 1) * HD] = qv[:, src * HD:(src + 1) * HD]
            early.start()

        @pl.when(i == chunks + 1)
        def _():
            early.turn()
        e = i - 2

        @pl.when(inside(e, chunks))
        def _():
            rs.finish(e, total)
            norm_grad(e)
        return carry

    lax.fori_loop(0, chunks + 2, tick, 0)
    part = width // 4
    for j in range(4):
        late.x[j:j + 1, :] = ln_sum[0:1, j * part:(j + 1) * part]
        late.x[j + 4:j + 5, :] = ln_sum[1:2, j * part:(j + 1) * part]
    late.start()
    mine = chunk_rows(at.g, block)
    g_proj[...] = gw_proj[mine, :].astype(F32)
    for k in range(n_grp - 1):
        send(k).wait()
        send_proj(k).wait()
    a_rest[...] = sum(got[k].astype(F32) for k in range(n_grp - 1))
    p_rest[...] = sum(got_proj[k].astype(F32) for k in range(n_grp - 1))
    late.turn()
    early.finish()
    sums[0:4, :] = early.total(0, 4)
    owned[...] = early.tbuf[:, 4, :]
    late.finish()
    ln = late.total(0, 8)
    for j in range(4):
        sums[4:5, j * part:(j + 1) * part] = ln[j:j + 1, :]
        sums[5:6, j * part:(j + 1) * part] = ln[j + 4:j + 5, :]
    sums[6:8, :] = jnp.zeros_like(sums[6:8, :])


def project_back(dproj, w_attn, n1, gw_proj, x, gain, stats, up_sum, n, n_grp, chunks):
    length, hw = dproj.shape
    width = w_attn.shape[0]
    share = length // n
    rows = share // chunks
    block = width // n_grp
    pw = gw_proj.shape[1]
    vm, hbm = pl.BlockSpec(memory_space=pltpu.VMEM), pl.BlockSpec(memory_space=pl.ANY)
    S, dma = jax.ShapeDtypeStruct, pltpu.SemaphoreType.DMA
    return pl.pallas_call(
        functools.partial(back_kernel, n=n, n_grp=n_grp, chunks=chunks, rows=rows),
        in_specs=[vm, vm, hbm, vm, hbm] + [vm] * 3, out_specs=[vm] * 7,
        out_shape=[S((share, width), F32), S((block, hw), F32), S((block, pw), F32), S((block, hw), F32),
                   S((block, pw), F32), S((8, width), F32),
                   S((n, width), F32)],
        scratch_shapes=[pltpu.VMEM((length, width), BF), pltpu.VMEM((share, width), BF), pltpu.VMEM((width, hw), BF),
                        pltpu.VMEM((n_grp - 1, block, hw), BF), pltpu.VMEM((n_grp - 1, block, pw), BF),
                        pltpu.VMEM((rows, width), F32), pltpu.VMEM((1, hw), F32), pltpu.VMEM((8, width), F32), dma((2,))]
                       + [dma((n_grp - 1,))] * 4 + scatter_scratch(chunks, n // 2, rows, width)
                       + all_sum_scratch(n_grp, n, (8, width)) + all_sum_scratch(n_grp, n, (8, width // 4)),
        compiler_params=pltpu.CompilerParams(collective_id=4, has_side_effects=True, vmem_limit_bytes=50 << 20),
        cost_estimate=pl.CostEstimate(flops=4 * length * hw * width, bytes_accessed=1 << 24, transcendentals=0),
        name="project_back",
    )(dproj.reshape(n, share, hw), w_attn, n1, gw_proj, x.reshape(n, share, width), gain, stats, up_sum)


def ffn_kernel(n2_hbm, gradb_hbm, bias_hbm, up_hbm, down_hbm, out_hbm, ctx_hbm, hidden_hbm, gain, b_down, groups, lens,
               gw_hbm, gwo, dctx, dh, res, stats, bsum,
               w_up, w_down, w_out, ctx, hidden, wsem, acc_out, gat, acc_up, acc_down, gbuf, actb, dbb, total, gshare, b_up, keep, lsem, gsem, msem, *scratch, n, chunks, rows):
    at = Place(n)
    ag1, ag2 = Gather(at, gat, rows, *scratch[:4]), Gather(at, gat, rows, *scratch[4:8])
    rs, mlp = Scatter(at, *scratch[8:15]), Scatter(at, *scratch[15:])
    width, hid = w_up.shape
    m = n * rows

    load = pltpu.make_async_copy(n2_hbm, gat.at[at.t], lsem)
    load.start()
    load_g = pltpu.make_async_copy(gradb_hbm.at[at.t], gshare, msem.at[0])
    load_g.start()
    big = [pltpu.make_async_copy(src, dst, wsem.at[j]) for j, (src, dst) in enumerate(
        ((up_hbm, w_up), (down_hbm, w_down), (hidden_hbm, hidden), (out_hbm, w_out), (ctx_hbm, ctx)))]
    for copy in big:
        copy.start()
    load_b = pltpu.make_async_copy(bias_hbm.at[at.t], b_up, msem.at[1])
    load_b.start()
    share = hidden.shape[0]
    tokens = jnp.sum(jnp.where(groups[...] == at.g, lens[...], 0), 1, keepdims=True)

    def alive(ranks, first, c):
        shape = (ranks, rows, 1)
        place = ((first + lax.broadcasted_iota(jnp.int32, shape, 0)) * share + c * rows
                 + lax.broadcasted_iota(jnp.int32, shape, 1))
        return jnp.where(place < tokens.reshape(1, 1, 1), 1.0, 0.0).reshape(ranks * rows, 1)

    def fetch(c):
        slot = lax.rem(c, 2)
        return pltpu.make_async_copy(gradb_hbm.at[:, chunk_rows(c, rows), :], gbuf.at[slot], gsem.at[slot])

    fetch(0).start()
    stats[...] = jnp.zeros_like(stats)
    bsum[...] = jnp.zeros_like(bsum)
    load.wait()
    load_g.wait()
    load_b.wait()
    at.barrier()

    a0, a1 = 0.7978845608028654, 0.044715

    def wide(c):
        return gat[:, chunk_rows(c, rows), :].reshape(m, width)

    def forward(c):
        @pl.when(c == 0)
        def _():
            for copy in big:
                copy.wait()
        fetch(c).wait()

        @pl.when(c + 1 < chunks)
        def _():
            fetch(c + 1).start()
        slot = lax.rem(c, 2)
        keep[...] = alive(n, 0, c)

        def tile(i):
            v = dg(wide(c), w_up[:, cols(i, 512)], 1, 0) + b_up[:, cols(i, 512)]
            ga = dg(gbuf[slot].reshape(m, width), w_down[:, cols(i, 512)], 1, 0)
            v2 = v * v
            th = jnp.tanh(a0 * (v + a1 * v2 * v))
            half = 0.5 * (1.0 + th)
            actb[:, cols(i, 512)] = (v * half * keep[...]).astype(BF)
            slope = half + 0.5 * v * (1.0 - th * th) * (a0 * (1.0 + 3.0 * a1 * v2))
            db = (ga * slope * keep[...]).astype(BF)
            dbb[:, cols(i, 512)] = db
            bsum[:, cols(i, 512)] += jnp.sum(db.astype(F32), 0, keepdims=True)
        tiles(hid // 512, tile)

    def back(c):
        def tile(i):
            y = dg(dbb[...], w_up[cols(i, 1024), :], 1, 1)
            rs.parts[:, :, :, cols(i, 1024)] = y.astype(BF).reshape(at.Z, 2, rows, 1024)
        tiles(width // 1024, tile)

    def down(c):
        def tile(i):
            y = dg(actb[...], w_down[cols(i, 1024), :], 1, 1)
            mlp.parts[:, :, :, cols(i, 1024)] = y.astype(BF).reshape(at.Z, 2, rows, 1024)
        tiles(width // 1024, tile)

    def weights(c):
        slot = lax.rem(c, 2)

        def tile(i):
            x = gat[:, chunk_rows(c, rows), cols(i, 512)].reshape(m, 512)
            acc_up[cols(i, 512), :] += dg(x, dbb[...], 0, 0)
            y = gbuf[slot, :, :, cols(i, 512)].reshape(m, 512)
            acc_down[cols(i, 512), :] += dg(y, actb[...], 0, 0)
        tiles(width // 512, tile)

    def norm_grad(c):
        r = chunk_rows(c, rows)
        xhat, inverse = rows_stats(hidden[r, :])
        dn2 = total[...]
        e = dn2 * gain[...]
        inner = jnp.mean(e, -1, keepdims=True) + xhat * jnp.mean(e * xhat, -1, keepdims=True)
        grad = gshare[r, :].astype(F32) * alive(1, at.t, c)
        d = grad + inverse * (e - inner)
        dh[r, :] = d
        gat[at.t, r, :] = d.astype(BF)
        stats[0:1, :] += jnp.sum(dn2 * xhat, 0, keepdims=True)
        stats[1:2, :] += jnp.sum(dn2, 0, keepdims=True)
        stats[2:3, :] += jnp.sum(d, 0, keepdims=True)
        stats[3:4, :] += jnp.sum(grad, 0, keepdims=True)

    def heads(c):
        def tile(i):
            x = gat[:, chunk_rows(c, rows), cols(i, 512)].reshape(m, 512)
            acc_out[cols(i, 512), :] += dg(x, ctx[:, chunk_rows(c, rows), :].reshape(m, -1), 0, 0)
        tiles(width // 512, tile)
        y = dg(wide(c), w_out[...], 1, 0)
        dctx[:, chunk_rows(c, rows), :] = y.astype(BF).reshape(n, rows, y.shape[1])

    def at_stage(c, fn):
        @pl.when(inside(c, chunks))
        def _():
            fn(c)

    def store_copies(j):
        r = chunk_rows(j, m)
        return (pltpu.make_async_copy(actb, gw_hbm.at[r, pl.ds(0, hid)], lsem),
                pltpu.make_async_copy(dbb, gw_hbm.at[r, pl.ds(hid, hid)], msem.at[0]))

    def store_wait(j):
        for copy in store_copies(j):
            copy.wait()

    def store(j):
        @pl.when((j >= 0) & (j < width // m))
        def _():
            @pl.when(j > 0)
            def _():
                store_wait(j - 1)
            r = chunk_rows(j, m)
            actb[...] = acc_up[r, :].astype(BF)
            dbb[...] = acc_down[r, :].astype(BF)
            for copy in store_copies(j):
                copy.start()

    per_slot = -(-(width // m) // (3 * (at.Z - 1)))

    def tick(i, carry):
        def stores(slot):
            for j in range(per_slot):
                store(((i - chunks - 2) * (at.Z - 1) + slot) * per_slot + j)
        at_stage(i, ag1.start)

        @pl.when(i == 0)
        def _():
            acc_up[...] = jnp.zeros_like(acc_up)
            acc_down[...] = jnp.zeros_like(acc_down)
            acc_out[...] = jnp.zeros_like(acc_out)
        at_stage(i - 3, rs.meet)
        for h in range(1, at.Z):
            at_stage(i - 3, lambda c: rs.hop(c, h))
            at_stage(i - 1, lambda c: ag1.hop(c, h))
            if h == 1:
                at_stage(i - 4, lambda c: mlp.hop(c, at.Z - 1))
                at_stage(i - 5, lambda c: ag2.hop(c, at.Z - 1))
                at_stage(i - 2, forward)
                stores(0)
            else:
                if h == 2:
                    def served(c):
                        mlp.finish(c, total)
                        r = chunk_rows(c, rows)
                        res[r, :] = (alive(1, at.t, c) * (hidden[r, :] + total[...] + b_down[...])).astype(BF)
                    at_stage(i - 4, served)
                    at_stage(i - 3, mlp.meet)
                at_stage(i - 3, lambda c: mlp.hop(c, h - 1))
                at_stage(i - 4, lambda c: ag2.hop(c, h - 1))
                stores(h - 1)
                if h == 2:
                    at_stage(i - 2, back)

                    def gathered(c):
                        ag2.finish(c)
                        heads(c)
                    at_stage(i - 5, gathered)

        def rest(c):
            weights(c)
            rs.start(c)
        at_stage(i - 2, rest)

        def reduced(c):
            rs.finish(c, total)
            norm_grad(c)
            ag2.start(c)
        at_stage(i - 3, reduced)
        at_stage(i - 1, ag1.finish)

        def send_mlp(c):
            down(c)
            mlp.start(c)
        at_stage(i - 2, send_mlp)

        return carry

    lax.fori_loop(0, chunks + 5, tick, 0)

    store_wait(width // m - 1)
    gwo[...] = acc_out[...].astype(BF)


def feed_forward(n2, gradb, b_up, w_up, w_down, w_out, ctx, hidden, gain, b_down, groups, lens, n, chunks):
    length, width = gradb.shape
    hid, hw = w_up.shape[1], w_out.shape[1]
    share = length // n
    rows = share // chunks
    Z = n // 2
    vm, hbm = pl.BlockSpec(memory_space=pltpu.VMEM), pl.BlockSpec(memory_space=pl.ANY)
    S = jax.ShapeDtypeStruct
    m = n * rows
    return pl.pallas_call(
        functools.partial(ffn_kernel, n=n, chunks=chunks, rows=rows),
        in_specs=[hbm] * 8 + [vm] * 4,
        out_specs=[hbm] + [vm] * 6,
        out_shape=[S((width, 2 * hid), BF), S((width, hw), BF), S((n, share, hw), BF), S((share, width), F32),
                   S((share, width), BF), S((8, width), F32), S((1, hid), F32)],
        scratch_shapes=[pltpu.VMEM((width, hid), BF), pltpu.VMEM((width, hid), BF), pltpu.VMEM((width, hw), BF),
                        pltpu.VMEM((n, share, hw), BF), pltpu.VMEM((share, width), F32), pltpu.SemaphoreType.DMA((5,)),
                        pltpu.VMEM((width, hw), F32), pltpu.VMEM((n, share, width), BF), pltpu.VMEM((width, hid), F32), pltpu.VMEM((width, hid), F32),
                        pltpu.VMEM((2, n, rows, width), BF),
                        pltpu.VMEM((m, hid), BF), pltpu.VMEM((m, hid), BF), pltpu.VMEM((rows, width), F32),
                        pltpu.VMEM((share, width), BF), pltpu.VMEM((1, hid), F32), pltpu.VMEM((m, 1), F32),
                        pltpu.SemaphoreType.DMA, pltpu.SemaphoreType.DMA((2,)), pltpu.SemaphoreType.DMA((2,))]
                       + gather_sems(chunks, Z) + gather_sems(chunks, Z) + scatter_scratch(chunks, Z, rows, width) * 2,
        compiler_params=pltpu.CompilerParams(collective_id=3, has_side_effects=True, vmem_limit_bytes=62 << 20),
        cost_estimate=pl.CostEstimate(flops=12 * length * hid * width, bytes_accessed=1 << 26, transcendentals=0),
        name="feed_forward",
    )(n2, gradb.reshape(n, share, width), b_up.reshape(n, 1, hid), w_up, w_down, w_out, ctx.reshape(n, share, hw),
      hidden, gain[None], b_down[None], groups[None], lens[None])


def on_device(layer_input, out_cotangent, seq_group, seq_len, w_qkv, b_qv, w_out, b_out, w_up, b_up,
              w_down, b_down, first_norm_gain, first_norm_bias, second_norm_gain, second_norm_bias):
    n_tp, n_grp = lax.axis_size("tp"), lax.axis_size("grp")
    length = layer_input.shape[0]
    hid, qv = w_up.shape[1], b_qv.shape[0] // n_tp

    proj, n1, w_attn, w_proj, up16, down16 = front(
        layer_input, w_qkv, w_out, w_up, w_down, first_norm_gain, first_norm_bias, b_qv, n_tp, n_grp)
    context, lse = attn_fwd(seq_group, seq_len, proj)
    hidden, n2, w_expand, w_reduce = attn_out(
        context, w_proj, b_out, second_norm_gain, second_norm_bias, layer_input, up16, down16,
        n_tp, n_grp, 8)
    gw_ffn, gw_proj, dcontext, dh, result, stats, up_sum = feed_forward(
        n2, out_cotangent, b_up, w_expand, w_reduce, w_proj, context, hidden,
        second_norm_gain, b_down, seq_group, seq_len, n_tp, 8)
    grads_ffn = lax.psum_scatter(gw_ffn, "grp", scatter_dimension=0, tiled=True).astype(F32)
    grads_expand, grads_reduce = grads_ffn[:, :hid], grads_ffn[:, hid:]

    dproj = attn_bwd(seq_group, seq_len, proj, context, dcontext.reshape(length, -1), lse)
    grad_x, grads_attn, grads_proj, attn_rest, proj_rest, sums, owned = project_back(
        dproj, w_attn, n1, gw_proj, layer_input, first_norm_gain[None], stats, up_sum, n_tp, n_grp, 8)
    grad_x, grads_attn, grads_proj = dh + grad_x, grads_attn + attn_rest, grads_proj + proj_rest
    return (result, grad_x, grads_attn, owned[:, hid:hid + qv].reshape(-1), grads_proj, sums[2],
            grads_expand, owned[:, :hid].reshape(-1), grads_reduce, sums[3], sums[4], sums[5],
            sums[0], sums[1])


def solution(mesh):
    rows, both, flat = P("grp", None), P("grp", "tp"), P()
    in_specs = (rows, rows, flat, flat, both, flat, both, flat, both, flat, both, flat, flat, flat, flat, flat)
    spread = P(("grp", "tp"), None)
    out_specs = (spread, spread, both, flat, both, flat, both, flat, both, flat, flat, flat, flat, flat)
    return jax.shard_map(on_device, mesh=mesh, in_specs=in_specs, out_specs=out_specs, check_vma=False)
```
